32 devices in a mesh: head: 4 (over y, x), blk: 8 (over z, core).
Axes of the slice: x: 2, y: 2, z: 4, core: 2. Of those that a mesh axis runs over, the one named last changes fastest.
Arguments:
- hidden: bfloat16 [4, 1024, 2048], P('head', 'blk'), may hold values from -6 to 6
- segment_ids: int32 [4, 1024], replicated, may hold values from 0 to 3, as said below
- block_ids: int32 [4, 1024], replicated, may hold values from 0 to 2, as said below
- positions: int32 [4, 1024], replicated, may hold values from 0 to 767, as said below
- attn_gain: bfloat16 [2048], P(('head', 'blk')), may hold values from 0.099609375 to 1.8984375
- w_query: bfloat16 [2048, 2048], P(('head', 'blk')), may hold values from -0.125 to 0.125
- key_weight_matrix: bfloat16 [2048, 1024], P(('head', 'blk')), may hold values from -0.125 to 0.125
- value_weight_matrix: bfloat16 [2048, 1024], P(('head', 'blk')), may hold values from -0.125 to 0.125
- q_gain: bfloat16 [128], P(('head', 'blk')), may hold values from 0.099609375 to 1.8984375
- k_gain: bfloat16 [128], P(('head', 'blk')), may hold values from 0.099609375 to 1.8984375
- w_head_gate: bfloat16 [2048, 16], P(('head', 'blk')), may hold values from -0.125 to 0.125
- w_out: bfloat16 [2048, 2048], P(('head', 'blk')), may hold values from -2 to 2
- mlp_gain: bfloat16 [2048], P(('head', 'blk')), may hold values from 0.099609375 to 1.8984375
- w_gate: bfloat16 [6144, 2048], P(('head', 'blk')), may hold values from -0.125 to 0.125
- w_up: bfloat16 [6144, 2048], P(('head', 'blk')), may hold values from -0.125 to 0.125
- w_down: bfloat16 [6144, 2048], P(('head', 'blk')), may hold values from -0.078125 to 0.078125
- cotangent: bfloat16 [4, 1024, 2048], P('head', 'blk'), may hold values from -6 to 6
Outputs:
- layer_output: bfloat16 [4, 1024, 2048], P('head', 'blk')
- input_grad: float32 [4, 1024, 2048], P('head', 'blk')
- attn_gain_grad: float32 [2048], P(('head', 'blk'))
- w_query_grad: float32 [2048, 2048], P(('head', 'blk'))
- w_key_grad: float32 [2048, 1024], P(('head', 'blk'))
- w_value_grad: float32 [2048, 1024], P(('head', 'blk'))
- q_gain_grad: float32 [128], P(('head', 'blk'))
- k_gain_grad: float32 [128], P(('head', 'blk'))
- w_head_gate_grad: float32 [2048, 16], P(('head', 'blk'))
- w_out_grad: float32 [2048, 2048], P(('head', 'blk'))
- mlp_gain_grad: float32 [2048], P(('head', 'blk'))
- w_gate_grad: float32 [6144, 2048], P(('head', 'blk'))
- w_up_grad: float32 [6144, 2048], P(('head', 'blk'))
- w_down_grad: float32 [6144, 2048], P(('head', 'blk'))
The draws below stay inside these ranges and needn't reach their ends.
Inputs may be any that keep to these rules, and one draw needn't show every extreme that they name: `segment_ids`: within a pack the ids never fall and each of the 4 documents is one nonempty run of positions. `positions`: A token's rotary position counts from 0 at its document's first position. block_ids equal positions // 256.
All inputs are finite; a program needn't handle non-finite values.
Results may differ from the reference program's by a relative error of at most 0.025.
Values may be sent and summed in bfloat16 or wider, within the bound.
A program may use at most 512 MiB of HBM per device.

```python
import math
import jax
import jax.numpy as jnp
from jax import lax

MODEL_WIDTH = 2048
HEADS = 16
KV_HEADS = 8
HEAD_DIM = 128
FF = 6144
DOCS = 4
BLOCK = 256
HQ = 2048
KEY_FEATURES = 1024
PACKS = 4
PACK = 1024


def document_starts(key):
    base_key = jax.random.fold_in(key, 11)
    cut_key, side_key = jax.random.split(base_key, 2)
    long_len = jnp.full((PACKS, 1), PACK * 3 // 4, jnp.int32)
    remaining = PACK - PACK * 3 // 4
    raw_cuts = jnp.sort(jax.random.randint(cut_key, (PACKS, DOCS - 2), 0, remaining - DOCS + 2), axis=1)
    cut_points = raw_cuts + jnp.arange(1, DOCS - 1, dtype=jnp.int32)[None, :]
    long_side = jax.random.randint(side_key, (PACKS, 1), 0, 2)
    zero_col = jnp.zeros((PACKS, 1), jnp.int32)
    remain_col = jnp.full((PACKS, 1), remaining, jnp.int32)
    long_first = jnp.concatenate([zero_col, long_len, long_len + cut_points], axis=1)
    long_last = jnp.concatenate([zero_col, cut_points, remain_col], axis=1)
    return jnp.where(long_side == 1, long_first, long_last).astype(jnp.int32)


def doc_positions(key):
    starts = document_starts(key)
    places = jnp.arange(PACK, dtype=jnp.int32)
    reached = places[None, None, :] >= starts[:, :, None]
    doc_start = jnp.max(jnp.where(reached, starts[:, :, None], 0), axis=1)
    return (places[None, :] - doc_start).astype(jnp.int32)


def draw_segment_ids(key, part):
    starts = document_starts(key)
    places = jnp.arange(PACK, dtype=jnp.int32)
    reached = (places[None, None, :] >= starts[:, :, None]).astype(jnp.int32)
    return (jnp.sum(reached, axis=1) - 1).astype(jnp.int32)


def draw_positions(key, part):
    return doc_positions(key)


def draw_block_ids(key, part):
    return (doc_positions(key) // BLOCK).astype(jnp.int32)


def shard_levels(rng, dims, cuts, least, top_value):
    gain, own = 1.0, jax.random.fold_in(rng, 6)
    for axis_at, blocks in cuts:
        steps = jnp.exp(jax.random.uniform(jax.random.fold_in(own, axis_at), (blocks,), jnp.float32, least / len(cuts), top_value / len(cuts)))
        gain = gain * jnp.repeat(steps, dims[axis_at] // blocks).reshape([-1 if axis == axis_at else 1 for axis in range(len(dims))])
    return gain


def bell_draw(key, extent, spread, limit, cuts=(), held_as=jnp.bfloat16):
    result = jax.random.normal(key, extent, jnp.float32) * spread
    if len(cuts) > 0:
        result = shard_levels(key, extent, cuts, -0.22, 0.18) * result
    return jnp.clip(result, min=-limit, max=limit).astype(held_as)


def setup_inputs(seed: int = 0) -> dict:
    key_of = jax.random.split(jax.random.key(seed), 18)
    hidden = bell_draw(key_of[0], (PACKS, PACK, MODEL_WIDTH), 1.0, 6.0, ((0, 4), (1, 8)))
    segment_ids = draw_segment_ids(jax.random.fold_in(key_of[17], 71), 0)
    block_ids = draw_block_ids(jax.random.fold_in(key_of[17], 71), 0)
    positions = draw_positions(jax.random.fold_in(key_of[17], 71), 0)
    attn_gain = jnp.clip(1.0 + 0.18 * jax.random.normal(key_of[4], (MODEL_WIDTH,), jnp.float32), 0.099609375, 1.8984375).astype(jnp.bfloat16)
    w_query = bell_draw(key_of[5], (MODEL_WIDTH, HQ), MODEL_WIDTH ** -0.5, 0.125, ((0, 32),))
    key_weight_matrix = bell_draw(key_of[6], (MODEL_WIDTH, KEY_FEATURES), MODEL_WIDTH ** -0.5, 0.125, ((0, 32),))
    value_weight_matrix = bell_draw(key_of[7], (MODEL_WIDTH, KEY_FEATURES), MODEL_WIDTH ** -0.5, 0.125, ((0, 32),))
    q_gain = jnp.clip(1.0 + 0.18 * jax.random.normal(key_of[8], (HEAD_DIM,), jnp.float32), 0.099609375, 1.8984375).astype(jnp.bfloat16)
    k_gain = jnp.clip(1.0 + 0.18 * jax.random.normal(key_of[9], (HEAD_DIM,), jnp.float32), 0.099609375, 1.8984375).astype(jnp.bfloat16)
    w_head_gate = bell_draw(key_of[10], (MODEL_WIDTH, HEADS), MODEL_WIDTH ** -0.5, 0.125, ((0, 32),))
    w_out = bell_draw(key_of[11], (HQ, MODEL_WIDTH), (HQ // 256) ** -0.5, 2.0, ((0, 32),))
    mlp_gain = jnp.clip(1.0 + 0.18 * jax.random.normal(key_of[12], (MODEL_WIDTH,), jnp.float32), 0.099609375, 1.8984375).astype(jnp.bfloat16)
    w_gate = bell_draw(key_of[13], (FF, MODEL_WIDTH), MODEL_WIDTH ** -0.5, 0.125, ((0, 32),))
    w_up = bell_draw(key_of[14], (FF, MODEL_WIDTH), MODEL_WIDTH ** -0.5, 0.125, ((0, 32),))
    w_down = bell_draw(key_of[15], (FF, MODEL_WIDTH), FF ** -0.5, 0.078125, ((0, 32),))
    cotangent = bell_draw(key_of[16], (PACKS, PACK, MODEL_WIDTH), 1.0, 6.0, ((0, 4), (1, 8)))
    return dict(hidden=hidden, segment_ids=segment_ids, block_ids=block_ids, positions=positions, attn_gain=attn_gain, w_query=w_query, key_weight_matrix=key_weight_matrix, value_weight_matrix=value_weight_matrix, q_gain=q_gain, k_gain=k_gain, w_head_gate=w_head_gate, w_out=w_out, mlp_gain=mlp_gain, w_gate=w_gate, w_up=w_up, w_down=w_down, cotangent=cotangent)


@jax.custom_vjp
def lowered_values(v):
    return lax.optimization_barrier(v.astype(jnp.bfloat16)).astype(jnp.float32)

@jax.custom_vjp
def lowered_backward(v):
    return v

def low_keep(v):
    return (lowered_values(v), None)

def low_pass(kept, grad):
    return (grad,)

def back_keep(v):
    return (v, None)

def back_low(kept, grad):
    return (lowered_values(grad),)
lowered_values.defvjp(low_keep, low_pass)
lowered_backward.defvjp(back_keep, back_low)
EPSILON = 1e-06
ROPE_BASE = 1000000.0
MASKED = -1e+30

def dot_high(left_side, right_side):
    return jnp.dot(left_side, right_side, precision=lax.Precision.HIGHEST, preferred_element_type=jnp.float32)

def rms_normed(values, gain_vec):
    factor = lax.rsqrt(lax.optimization_barrier(jnp.mean(values * values, axis=-1, keepdims=True)) + EPSILON)
    return values * factor * gain_vec

def angle_tables(position_row):
    frequencies = jnp.exp(jnp.arange(HEAD_DIM // 2, dtype=jnp.float32) * (-2.0 * math.log(ROPE_BASE) / HEAD_DIM))
    angles = position_row.astype(jnp.float32)[:, None] * frequencies[None, :]
    return (jnp.cos(angles)[:, None, :], jnp.sin(angles)[:, None, :])

def rotary(values, cosine, sine_table):
    half_dim = values.shape[-1] // 2
    first_half = values[..., :half_dim]
    second_half = values[..., half_dim:]
    return jnp.concatenate([first_half * cosine - second_half * sine_table, second_half * cosine + first_half * sine_table], axis=-1)

def layer_pack(hidden_row, weights, segment_row, block_row, position_row):
    attn_gain, w_query, key_weight_matrix, value_weight_matrix, q_gain, k_gain, w_head_gate, w_out, mlp_gain, w_gate, w_up, w_down = weights
    seq_len = hidden_row.shape[0]
    groups = HEADS // KV_HEADS
    inverse_square_root = 1.0 / math.sqrt(HEAD_DIM)
    normed_x = lowered_values(rms_normed(hidden_row, attn_gain))
    q_lin = lowered_backward(dot_high(normed_x, w_query))
    k_lin = lowered_backward(dot_high(normed_x, key_weight_matrix))
    value_head_rows = lowered_backward(lowered_values(dot_high(normed_x, value_weight_matrix))).reshape(seq_len, KV_HEADS, HEAD_DIM)
    gate_lin = lowered_backward(dot_high(normed_x, w_head_gate))
    cosine, sine_table = angle_tables(position_row)
    q_heads = lowered_backward(lowered_values(rotary(rms_normed(q_lin.reshape(seq_len, HEADS, HEAD_DIM), q_gain), cosine, sine_table)))
    key_head_rows = lowered_backward(lowered_values(rotary(rms_normed(k_lin.reshape(seq_len, KV_HEADS, HEAD_DIM), k_gain), cosine, sine_table)))
    block_rows = math.gcd(seq_len, 512)
    n_blocks = seq_len // block_rows
    q_blocks = q_heads.reshape(n_blocks, block_rows, KV_HEADS, groups, HEAD_DIM)

    def attend(block_items):
        query_block_rows, seg_block, blk_block = block_items
        logit_scores = lowered_backward(jnp.einsum('kjez,fjz->jekf', query_block_rows, key_head_rows, precision=lax.Precision.HIGHEST, preferred_element_type=jnp.float32) * inverse_square_root)
        visible = (seg_block[:, None] == segment_row[None, :]) & (block_row[None, :] <= blk_block[:, None])
        masked = jnp.where(visible, logit_scores, MASKED)
        row_top = lax.optimization_barrier(jnp.max(masked, axis=-1, keepdims=True))
        log_total = row_top + jnp.log(lax.optimization_barrier(jnp.sum(jnp.where(visible, jnp.exp(masked - row_top), 0.0), axis=-1, keepdims=True)))
        attention_probabilities = jnp.where(visible, jnp.exp(masked - log_total), 0.0)
        return jnp.einsum('fzuc,cfi->ufzi', lowered_values(attention_probabilities), value_head_rows, precision=lax.Precision.HIGHEST, preferred_element_type=jnp.float32)
    attended = lax.map(jax.checkpoint(attend), (q_blocks, segment_row.reshape(n_blocks, block_rows), block_row.reshape(n_blocks, block_rows)))
    out_heads = lowered_backward(lowered_values(attended.reshape(seq_len, HEADS, HEAD_DIM)))
    gated_out = out_heads * jax.nn.sigmoid(gate_lin)[:, :, None]
    attn_out = lowered_backward(dot_high(lowered_values(gated_out.reshape(seq_len, HEADS * HEAD_DIM)), w_out))
    middle = hidden_row + attn_out
    normed_mid = lowered_values(rms_normed(middle, mlp_gain))
    gate_act = lowered_backward(dot_high(normed_mid, w_gate.T))
    up_act = lowered_backward(dot_high(normed_mid, w_up.T))
    unit_values = lowered_values(jax.nn.silu(gate_act) * up_act)
    return middle + lowered_backward(dot_high(unit_values, w_down))

def reference(hidden, segment_ids, block_ids, positions, attn_gain, w_query, key_weight_matrix, value_weight_matrix, q_gain, k_gain, w_head_gate, w_out, mlp_gain, w_gate, w_up, w_down, cotangent):
    weights = tuple((tensor.astype(jnp.float32) for tensor in (attn_gain, w_query, key_weight_matrix, value_weight_matrix, q_gain, k_gain, w_head_gate, w_out, mlp_gain, w_gate, w_up, w_down)))

    def one_pack(totals, pack_items):
        hidden_row, cot_row, segment_row, block_row, position_row = pack_items

        def forward(inputs_row, params):
            return layer_pack(inputs_row, params, segment_row, block_row, position_row)
        output_row, pullback = jax.vjp(forward, hidden_row.astype(jnp.float32), weights)
        grad_row, grad_weights = pullback(cot_row.astype(jnp.float32))
        totals = jax.tree.map(jnp.add, totals, grad_weights)
        return (totals, (output_row.astype(jnp.bfloat16), grad_row))
    zeros_init = jax.tree.map(jnp.zeros_like, weights)
    totals, (outputs, input_grad) = lax.scan(one_pack, zeros_init, (hidden, cotangent, segment_ids, block_ids, positions))
    return (outputs, input_grad, totals[0], totals[1], totals[2], totals[3], totals[4], totals[5], totals[6], totals[7], totals[8], totals[9], totals[10], totals[11])
```

```python
import math

import jax
import jax.numpy as jnp
from jax import lax
from jax.experimental import pallas as pl
from jax.experimental.pallas import tpu as pltpu
from jax.sharding import PartitionSpec as P

MODEL_WIDTH = 2048
HEADS = 16
KV_HEADS = 8
HEAD_DIM = 128
GATE_PAD = 128
EPSILON = 1e-06
ROPE_BASE = 1000000.0
MASKED = -1e30
F32 = jnp.float32
BF16 = jnp.bfloat16
MESH = pl.DeviceIdType.MESH


def mm(a, b):
    return jnp.dot(a, b, preferred_element_type=F32)


def mm_nt(a, b):
    return lax.dot_general(a, b, (((1,), (1,)), ((), ())), preferred_element_type=F32)


def mm_tn(a, b):
    return lax.dot_general(a, b, (((0,), (0,)), ((), ())), preferred_element_type=F32)


def unit_of(values):
    factor = lax.rsqrt(jnp.mean(values * values, axis=-1, keepdims=True) + EPSILON)
    return values * factor, factor


def unit_back(scaled, unit, factor):
    return factor * (scaled - unit * jnp.mean(scaled * unit, axis=-1, keepdims=True))


def signal_to(semaphore, target):
    pl.semaphore_signal(semaphore, inc=1, device_id=target, device_id_type=MESH)


class Line:
    def __init__(self, n_blk):
        self.me = lax.axis_index("blk")
        self.chips = n_blk // 2
        self.i = self.me // 2
        self.c = self.me % 2
        self.right = {"blk": self.me + 2}
        self.left = {"blk": self.me - 2}
        self.sibling = {"blk": self.me + 1 - 2 * self.c}
        self.has_right = self.i < self.chips - 1
        self.has_left = self.i > 0

    def greet(self, barrier):
        signal_to(barrier, self.sibling)

        @pl.when(self.has_right)
        def _():
            signal_to(barrier, self.right)

        @pl.when(self.has_left)
        def _():
            signal_to(barrier, self.left)

        return 1 + self.has_right.astype(jnp.int32) + self.has_left.astype(jnp.int32)


class Gather:
    def __init__(self, line, src, out, sems):
        self.line, self.src, self.out, self.sems = line, src, out, sems
        self.pieces = sems.shape[2]
        self.rows = src.shape[0] // self.pieces

    def part(self, p):
        return pl.ds(p * self.rows, self.rows)

    def move(self, kind, src, j, p, target):
        return pltpu.make_async_remote_copy(
            src_ref=src.at[self.part(p)],
            dst_ref=self.out.at[j, self.line.c, self.part(p)],
            send_sem=self.sems.at[kind, j, p],
            recv_sem=self.sems.at[3 + kind, j, p],
            device_id=target,
            device_id_type=MESH,
        )

    def arrived(self, kind, j, p, core):
        there = self.out.at[j, core, self.part(p)]
        pltpu.make_async_remote_copy(
            src_ref=there,
            dst_ref=there,
            send_sem=self.sems.at[kind, j, p],
            recv_sem=self.sems.at[3 + kind, j, p],
            device_id=self.line.sibling,
            device_id_type=MESH,
        ).wait_recv()

    def send(self, src, j, p, right, left):
        line = self.line
        if right is not None:

            @pl.when(right)
            def _():
                self.move(0, src, j, p, line.right).start()

        if left is not None:

            @pl.when(left)
            def _():
                self.move(1, src, j, p, line.left).start()

        self.move(2, src, j, p, line.sibling).start()

    def own_copy(self):
        return pltpu.make_async_copy(
            self.src, self.out.at[self.line.i, self.line.c], self.sems.at[6, 0, 0]
        )

    def start(self):
        line = self.line
        for p in range(self.pieces):
            self.send(self.src, line.i, p, line.has_right, line.has_left)
        self.own_copy().start()

    def step(self, s):
        line = self.line
        from_left, from_right = line.i - s, line.i + s
        for p in range(self.pieces):

            @pl.when(from_left >= 0)
            def _(p=p):
                self.arrived(0, from_left, p, line.c)
                self.send(self.out.at[from_left, line.c], from_left, p, line.has_right, None)

            @pl.when(from_right < line.chips)
            def _(p=p):
                self.arrived(1, from_right, p, line.c)
                self.send(self.out.at[from_right, line.c], from_right, p, None, line.has_left)

    def finish(self):
        line = self.line
        for j in range(line.chips):
            mine = self.out.at[j, line.c]
            for p in range(self.pieces):
                self.arrived(2, j, p, 1 - line.c)
                self.move(2, mine, j, p, line.sibling).wait_send()

                @pl.when((line.i >= j) & line.has_right)
                def _(j=j, p=p, mine=mine):
                    self.move(0, mine, j, p, line.right).wait_send()

                @pl.when((line.i <= j) & line.has_left)
                def _(j=j, p=p, mine=mine):
                    self.move(1, mine, j, p, line.left).wait_send()

        self.own_copy().wait()

    def run(self):
        self.start()
        for s in range(1, self.line.chips):
            self.step(s)
        self.finish()


def by_rows(rows, step, body):
    def one(k, carry):
        body(pl.ds(pl.multiple_of(k * step, step), step))
        return carry

    lax.fori_loop(0, rows // step, one, 0)


class Scatter:
    def __init__(self, line, part, bufs, sems):
        self.line, self.part, self.sems = line, part, sems
        self.own, self.sib, self.inn, self.out = bufs

    def copy(self, kind, src, dst, j, target):
        return pltpu.make_async_remote_copy(
            src_ref=src,
            dst_ref=dst,
            send_sem=self.sems.at[kind, j],
            recv_sem=self.sems.at[3 + kind, j],
            device_id=target,
            device_id_type=MESH,
        )

    def to_sibling(self, j):
        line = self.line
        return self.copy(2, self.part.at[j, 1 - line.c], self.sib.at[j], j, line.sibling)

    def to_own(self, j):
        return pltpu.make_async_copy(
            self.part.at[j, self.line.c], self.own.at[j], self.sems.at[6, j]
        )

    def along(self, way, j):
        line = self.line
        target = line.left if way else line.right
        return self.copy(way, self.out.at[j], self.inn.at[way, j], j, target)

    def start(self):
        chips = self.line.chips
        order = []
        for k in range((chips + 1) // 2):
            order += [chips - 1 - k, k]
        for j in order[:chips]:
            self.to_sibling(j).start()
            self.to_own(j).start()

    def ready(self, j):
        self.to_sibling(j).wait_recv()
        self.to_own(j).wait()

    def pass_on(self, way, j, first):
        self.ready(j)
        rows = self.own.shape[1]

        @pl.when(first)
        def _():
            def body(r):
                total = self.own[j, r, :].astype(F32) + self.sib[j, r, :].astype(F32)
                self.out[j, r, :] = total.astype(BF16)

            by_rows(rows, 16, body)

        @pl.when(jnp.logical_not(first))
        def _():
            self.along(way, j).wait_recv()

            def body(r):
                total = self.own[j, r, :].astype(F32) + self.sib[j, r, :].astype(F32)
                self.out[j, r, :] = (total + self.inn[way, j, r, :].astype(F32)).astype(BF16)

            by_rows(rows, 16, body)

        self.along(way, j).start()

    def step(self, tau):
        line = self.line

        @pl.when((line.i <= tau) & line.has_right)
        def _():
            self.pass_on(0, line.chips - 1 - tau + line.i, line.i == 0)

        @pl.when((line.chips - 1 - line.i <= tau) & line.has_left)
        def _():
            self.pass_on(1, tau - (line.chips - 1 - line.i), line.i == line.chips - 1)

    def total(self, consume):
        line, i = self.line, self.line.i
        self.ready(i)

        @pl.when(line.has_left)
        def _():
            self.along(0, i).wait_recv()

        @pl.when(line.has_right)
        def _():
            self.along(1, i).wait_recv()

        rows = self.own.shape[1]

        def add(r, with_left, with_right):
            total = self.own[i, r, :].astype(F32) + self.sib[i, r, :].astype(F32)
            if with_left:
                total += self.inn[0, i, r, :].astype(F32)
            if with_right:
                total += self.inn[1, i, r, :].astype(F32)
            consume(r, total)

        @pl.when(line.has_left & line.has_right)
        def _():
            by_rows(rows, 16, lambda r: add(r, True, True))

        @pl.when(line.has_left & jnp.logical_not(line.has_right))
        def _():
            by_rows(rows, 16, lambda r: add(r, True, False))

        @pl.when(line.has_right & jnp.logical_not(line.has_left))
        def _():
            by_rows(rows, 16, lambda r: add(r, False, True))

    def finish(self):
        line = self.line
        for j in range(line.chips):
            self.to_sibling(j).wait_send()

            @pl.when(j > line.i)
            def _(j=j):
                self.along(0, j).wait_send()

            @pl.when(j < line.i)
            def _(j=j):
                self.along(1, j).wait_send()

    def run(self, consume):
        self.start()
        for tau in range(self.line.chips - 1):
            self.step(tau)
        self.total(consume)
        self.finish()


PIECES = 2


def gather_sems(chips):
    return pltpu.SemaphoreType.DMA((7, chips, PIECES))


def scatter_bufs(chips, rows, width):
    return [
        pltpu.VMEM((chips, rows, width), BF16),
        pltpu.VMEM((chips, rows, width), BF16),
        pltpu.VMEM((2, chips, rows, width), BF16),
        pltpu.VMEM((chips, rows, width), BF16),
        pltpu.SemaphoreType.DMA((7, chips)),
    ]


ANYWHERE = pl.BlockSpec(memory_space=pl.ANY)
IN_VMEM = pl.BlockSpec(memory_space=pltpu.VMEM)


def params(collective_id):
    return pltpu.CompilerParams(
        collective_id=collective_id, has_side_effects=True, vmem_limit_bytes=56 * 2**20
    )


def comm_cost(byte_count):
    return pl.CostEstimate(flops=0, transcendentals=0, bytes_accessed=40 * byte_count)


class Exchange:
    def __init__(self, axis, size):
        self.axis, self.size = axis, size
        self.me = lax.axis_index(axis)

    def peer(self, k):
        return lax.rem(self.me + k, self.size)

    def greet(self, barrier):
        for k in range(1, self.size):
            signal_to(barrier, {self.axis: self.peer(k)})

    def copy(self, k, src, dst, sems):
        return pltpu.make_async_remote_copy(
            src_ref=src,
            dst_ref=dst,
            send_sem=sems.at[0, k],
            recv_sem=sems.at[1, k],
            device_id={self.axis: self.peer(k)},
            device_id_type=MESH,
        )

    def sems(self):
        return pltpu.SemaphoreType.DMA((2, self.size))


def pair_sems(size):
    return pltpu.SemaphoreType.DMA((2, size))


def greet_all(exchanges, line=None, moves=None):
    barrier = pltpu.get_barrier_semaphore()
    count = 0
    for exchange in exchanges:
        exchange.greet(barrier)
        count += exchange.size - 1
    if line is not None:
        count += line.greet(barrier)
    if moves is not None:
        whether, source = moves

        @pl.when(whether)
        def _():
            signal_to(barrier, source)

        count += whether.astype(jnp.int32)
    pl.semaphore_wait(barrier, count)


def flip_copy(src, dst, bit, sems, *index):
    return pltpu.make_async_remote_copy(
        src_ref=src,
        dst_ref=dst,
        send_sem=sems.at[(0, *index)],
        recv_sem=sems.at[(1, *index)],
        device_id={"head": lax.axis_index("head") ^ (1 << bit)},
        device_id_type=MESH,
    )


def ff_entries(rows, n_head):
    bits = tuple(range(n_head.bit_length() - 1))
    back, half = bits[::-1], rows // 2
    return (
        (0, pl.ds(0, rows), bits),
        (1, pl.ds(0, rows), back),
        (2, pl.ds(0, half), bits),
        (2, pl.ds(half, half), back),
    )


def place_of_out_rows(n_head, n_blk):
    h, b = lax.axis_index("head"), lax.axis_index("blk")
    d = h * n_blk + b
    source = b * n_head + h
    return (d % n_head, d // n_head), (source // n_blk, source % n_blk)


PACK_ROWS = 24


def weight_pieces(b, q_cols, copies):
    kv = b // copies * HEAD_DIM
    return (
        (0, pl.ds(pl.multiple_of(b * q_cols, HEAD_DIM), q_cols), pl.ds(0, q_cols)),
        (1, pl.ds(pl.multiple_of(kv, HEAD_DIM), HEAD_DIM), pl.ds(q_cols, HEAD_DIM)),
        (2, pl.ds(pl.multiple_of(kv, HEAD_DIM), HEAD_DIM), pl.ds(q_cols + HEAD_DIM, HEAD_DIM)),
    )


def first_gather(rows, weights, pack, w_out, ids, q_cols, copies, n_head, n_blk, collective_id):
    count, width = rows.shape
    chips, length = n_blk // 2, n_blk * count
    rows_here = weights[0].shape[0]
    columns = q_cols + 2 * HEAD_DIM
    together = 128 // rows_here
    chunk = 256

    def kernel(src, *refs):
        w_src, (pack_src, out_src), (pos, seg, blk) = refs[:3], refs[3:5], refs[5:8]
        out, w_all, moved_out, vec, gates, cos_ref, sin_ref, low_ref, code_ref, key_ref = refs[8:18]
        g_all, sems, block_sems, w_sems, pack_sems, g_sems, moved, local = refs[18:]
        line = Line(n_blk)
        across, along = Exchange("head", n_head), Exchange("blk", n_blk)
        h, b = across.me, along.me
        (th, tb), (sh, sb) = place_of_out_rows(n_head, n_blk)
        stays = (th == h) & (tb == b)
        moves = jnp.logical_not(stays)
        greet_all((across, along), moves=(moves, {"head": sh, "blk": sb}))

        def block_copies(k):
            for w, there, here in weight_pieces(along.peer(k), q_cols, copies):
                yield along.copy(
                    k, w_src[w].at[:, there], w_all.at[h, b, :, here], block_sems.at[w]
                )

        def pack_copy(k):
            return along.copy(k, pack_src, g_all.at[h, b], pack_sems)

        def w_copy(k):
            return across.copy(k, w_all.at[h], w_all.at[h], w_sems)

        def g_copy(k):
            return across.copy(k, g_all.at[h], g_all.at[h], g_sems)

        move_out = pltpu.make_async_remote_copy(
            src_ref=out_src,
            dst_ref=moved_out,
            send_sem=moved.at[0],
            recv_sem=moved.at[1],
            device_id={"head": th, "blk": tb},
            device_id_type=MESH,
        )
        keep_out = pltpu.make_async_copy(out_src, moved_out, moved.at[2])
        locals_ = [
            pltpu.make_async_copy(w_src[w].at[:, there], w_all.at[h, b, :, here], local.at[w])
            for w, there, here in weight_pieces(b, q_cols, copies)
        ] + [pltpu.make_async_copy(pack_src, g_all.at[h, b], local.at[3])]
        for k in range(1, n_blk):
            for copy in block_copies(k):
                copy.start()
        gather = Gather(line, src, out, sems)
        gather.start()
        for k in range(1, n_blk):
            pack_copy(k).start()
        for one in locals_:
            one.start()

        @pl.when(stays)
        def _():
            keep_out.start()

        @pl.when(moves)
        def _():
            move_out.start()

        half = HEAD_DIM // 2
        index = lax.broadcasted_iota(jnp.int32, (half, chunk), 0).astype(F32)
        frequency = jnp.exp(index * (-2.0 * math.log(ROPE_BASE) / HEAD_DIM))
        key_ref[...] = (seg[...] * length + blk[...]).astype(F32)

        def tables(n, carry):
            r = block_of(n, chunk)
            angles = frequency * pos[:, r].astype(F32)
            cosine, sine = jnp.cos(angles), jnp.sin(angles)
            cos_ref[r, :] = jnp.concatenate([cosine, cosine], axis=0).T
            sin_ref[r, :] = jnp.concatenate([-sine, sine], axis=0).T
            low_ref[r, :] = jnp.broadcast_to((seg[:, r] * length).astype(F32), (128, chunk)).T
            code_ref[r, :] = jnp.broadcast_to(key_ref[:, r], (128, chunk)).T
            return carry

        lax.fori_loop(0, length // chunk, tables, 0)
        for one in locals_:
            one.wait()
        for k in range(1, n_blk):
            pack_copy(k).wait_recv()
        for k in range(1, n_head):
            g_copy(k).start()
        gather.step(1)
        for k in range(1, n_blk):
            for copy in block_copies(k):
                copy.wait_recv()
        for k in range(1, n_head):
            w_copy(k).start()
        for s in range(2, chips):
            gather.step(s)
        for k in range(1, n_head):
            g_copy(k).wait()
        everyone = [g_all.at[d // n_blk, d % n_blk] for d in range(n_head * n_blk)]
        vec[...] = jnp.zeros_like(vec)
        for t in range(width // 128):
            tile = sum(one[...] for one in everyone[t * together : (t + 1) * together])
            vec[0:2, t * 128 : (t + 1) * 128] = tile[0:2]
            gates[:, t * 128 : (t + 1) * 128] = tile[8:].astype(BF16)
        vec[2:4, 0:128] = sum(one[2:4, :] for one in everyone)
        gather.finish()
        for k in range(1, n_head):
            w_copy(k).wait()
        for k in range(1, n_blk):
            pack_copy(k).wait_send()
            for copy in block_copies(k):
                copy.wait_send()

        @pl.when(stays)
        def _():
            keep_out.wait()

        @pl.when(moves)
        def _():
            move_out.wait()

    dma = pltpu.SemaphoreType.DMA
    out, w_attn, *rest = pl.pallas_call(
        kernel,
        out_shape=(
            jax.ShapeDtypeStruct((chips, 2, count, width), rows.dtype),
            jax.ShapeDtypeStruct((n_head, n_blk, rows_here, columns), BF16),
            jax.ShapeDtypeStruct(w_out.shape, w_out.dtype),
            jax.ShapeDtypeStruct((8, width), F32),
            jax.ShapeDtypeStruct((HEADS, width), BF16),
            *[jax.ShapeDtypeStruct((length, 128), F32)] * 4,
            jax.ShapeDtypeStruct((1, length), F32),
        ),
        in_specs=[IN_VMEM] + [ANYWHERE] * 5 + [IN_VMEM] * 3,
        out_specs=[ANYWHERE] * 3 + [IN_VMEM] * 7,
        scratch_shapes=[
            pltpu.VMEM((n_head, n_blk, PACK_ROWS, 128), F32),
            gather_sems(chips),
            dma((3, 2, n_blk)),
            pair_sems(n_head),
            pair_sems(n_blk),
            pair_sems(n_head),
            dma((3,)),
            dma((4,)),
        ],
        compiler_params=params(collective_id),
        cost_estimate=comm_cost(n_blk * count * width),
        name="first_gather",
    )(rows, *weights, pack, w_out, *ids)
    return (
        out.reshape(length, width),
        w_attn.reshape(n_head * n_blk * rows_here, columns),
        *rest,
    )


class Spread:
    def __init__(self, full, entries, n_head, sems):
        self.full, self.entries, self.n_head, self.sems = full, entries, n_head, sems

    def copies(self, e, level):
        weight, part, order = self.entries[e]
        full = self.full[weight]
        bit = order[level]
        keys = [0]
        for low in order[:level]:
            keys += [key ^ (1 << low) for key in keys]
        for key in keys:
            there = key ^ (1 << bit)
            yield flip_copy(
                full.at[key, part], full.at[there, part], bit, self.sems, e, there
            )

    def level(self, level):
        for e in range(len(self.entries)):
            if level > 1:
                for copy in self.copies(e, level - 1):
                    copy.wait_recv()
            for copy in self.copies(e, level):
                copy.start()

    def start(self):
        self.level(1)

    def finish(self):
        levels = self.n_head.bit_length() - 1
        for level in range(2, levels):
            self.level(level)
        for e in range(len(self.entries)):
            for level in range(1, levels):
                for copy in self.copies(e, level):
                    copy.wait_send()
                    if level == levels - 1:
                        copy.wait_recv()

    @staticmethod
    def sem_shape(n_head):
        return pltpu.SemaphoreType.DMA((2, 4, n_head))


class Collect:
    def __init__(self, have, kept, inbox, total, entries, n_head, sems):
        self.have, self.kept, self.inbox, self.total = have, kept, inbox, total
        self.entries, self.n_head, self.sems = entries, n_head, sems

    def keys(self, order, level):
        keys = [0]
        for low in order[: len(order) - 1 - level]:
            keys += [key ^ (1 << low) for key in keys]
        return keys

    def slot(self, order, key):
        return self.keys(order, 0).index(key)

    def copies(self, e, level):
        weight, part, order = self.entries[e]
        bit = order[len(order) - 1 - level]
        for key in self.keys(order, level):
            slot = self.slot(order, key)
            if level == 0:
                src = self.have[weight].at[key ^ (1 << bit), part]
            else:
                src = self.kept[weight].at[self.slot(order, key ^ (1 << bit)), part]
            yield flip_copy(src, self.inbox[weight].at[level, slot, part], bit, self.sems, e, level, slot)

    def locals_(self):
        for e, (weight, part, order) in enumerate(self.entries):
            for key in self.keys(order, 0):
                slot = self.slot(order, key)
                yield pltpu.make_async_copy(
                    self.have[weight].at[key, part],
                    self.kept[weight].at[slot, part],
                    self.sems.at[2, e, 0, slot],
                )

    def start(self):
        for copy in self.locals_():
            copy.start()
        for e in range(len(self.entries)):
            for copy in self.copies(e, 0):
                copy.start()

    def finish(self):
        for copy in self.locals_():
            copy.wait()
        levels = self.n_head.bit_length() - 2
        for level in range(levels):
            last = level == levels - 1
            for e, (weight, part, order) in enumerate(self.entries):
                for copy in self.copies(e, level):
                    copy.wait_recv()
                for at, key in enumerate(self.keys(order, level)):
                    slot = self.slot(order, key)
                    kept, inbox = self.kept[weight], self.inbox[weight]
                    into = self.total[weight] if last else kept
                    where = at if last else slot

                    def body(r, part=part, slot=slot, kept=kept, inbox=inbox, into=into, where=where):
                        r = pl.ds(pl.multiple_of(r.start + part.start, 16), r.size)
                        value = kept[slot, r, :].astype(F32) + inbox[level, slot, r, :].astype(F32)
                        into[where, r, :] = value.astype(BF16)

                    by_rows(part.size, 16, body)
            for e in range(len(self.entries)):
                if not last:
                    for copy in self.copies(e, level + 1):
                        copy.start()
        for level in range(levels):
            for e in range(len(self.entries)):
                for copy in self.copies(e, level):
                    copy.wait_send()

    @staticmethod
    def sem_shape(n_head):
        levels = n_head.bit_length() - 2
        return pltpu.SemaphoreType.DMA((3, 4, levels, n_head // 2))


def last_scatter(
    partial_rows, w_grad, out_grad, pack, sums, hidden, gain, q_cols, copies, n_head, n_blk, collective_id
):
    total_rows, width = partial_rows.shape
    chips, count = n_blk // 2, total_rows // n_blk
    _, _, rows_here, columns = w_grad.shape
    n_sums = len(sums)
    entries = ff_entries(sums[0].shape[1], n_head) if sums else ()

    def kernel(part, w_src, o_src, g_src, *refs):
        ff_src, (x_ref, gain_ref), refs = refs[:n_sums], refs[n_sums : n_sums + 2], refs[n_sums + 2 :]
        out, wq_out, wk_out, wv_out, o_out, g_out = refs[:6]
        ff_out, refs = refs[6 : 6 + n_sums], refs[6 + n_sums :]
        bufs, sems = refs[:4], refs[4]
        w_in, w_sum, o_in, o_sum, g_in, g_sum, g_last = refs[5:12]
        w_sems, block_sems, o_sems, g_sems, pack_sems, moved, ff_sems, local = refs[12:]
        line = Line(n_blk)
        across, along = Exchange("head", n_head), Exchange("blk", n_blk)
        h, b = across.me, along.me
        (sh, sb), (th, tb) = place_of_out_rows(n_head, n_blk)
        stays = (th == h) & (tb == b)
        moves = jnp.logical_not(stays)
        greet_all((across, along), moves=(moves, {"head": sh, "blk": sb}))

        def w_copy(k):
            return across.copy(k, w_src.at[across.peer(k)], w_in.at[k], w_sems)

        def o_copy(k):
            return across.copy(k, o_src.at[across.peer(k)], o_in.at[k], o_sems)

        lanes = n_blk * rows_here

        def g_part(head):
            return g_src.at[:, pl.ds(pl.multiple_of(head * lanes, 128), lanes)]

        def g_copy(k):
            return across.copy(k, g_part(across.peer(k)), g_in.at[k], g_sems)

        def landings():
            kv = pl.ds(pl.multiple_of(b // copies * HEAD_DIM, HEAD_DIM), HEAD_DIM)
            return (
                wq_out.at[:, pl.ds(pl.multiple_of(b * q_cols, HEAD_DIM), q_cols)],
                wk_out.at[b % copies, :, kv],
                wv_out.at[b % copies, :, kv],
            )

        spans = (
            pl.ds(0, q_cols),
            pl.ds(q_cols, HEAD_DIM),
            pl.ds(q_cols + HEAD_DIM, HEAD_DIM),
        )

        def block_copies(k):
            for w, there in enumerate(landings()):
                yield along.copy(
                    k, w_sum.at[along.peer(k), :, spans[w]], there, block_sems.at[w]
                )

        def pack_copy(k):
            tile = along.peer(k) * rows_here // 128 * 128
            part = g_sum.at[:, pl.ds(pl.multiple_of(tile, 128), 128)]
            return along.copy(k, part, g_last.at[b], pack_sems)

        move_out = pltpu.make_async_remote_copy(
            src_ref=o_sum,
            dst_ref=o_out,
            send_sem=moved.at[0],
            recv_sem=moved.at[1],
            device_id={"head": th, "blk": tb},
            device_id_type=MESH,
        )
        keep_out = pltpu.make_async_copy(o_sum, o_out, moved.at[2])

        def hop(e):
            weight, part, order = entries[e]
            return flip_copy(
                ff_src[weight].at[1, part], ff_out[weight].at[part], order[0], ff_sems, e
            )

        own_w = pltpu.make_async_copy(w_src.at[h], w_in.at[0], local.at[0])
        own_g = pltpu.make_async_copy(g_part(h), g_in.at[0], local.at[1])
        own_blocks = [
            pltpu.make_async_copy(w_sum.at[b, :, spans[w]], there, local.at[4 + w])
            for w, there in enumerate(landings())
        ]
        own_o = pltpu.make_async_copy(o_src.at[h], o_in.at[0], local.at[3])
        scatter = Scatter(line, part, bufs, sems)
        scatter.start()
        own_w.start()
        own_g.start()
        own_o.start()
        for k in range(1, n_head):
            g_copy(k).start()
            w_copy(k).start()
        for k in range(1, n_head):
            o_copy(k).start()
        for e in range(len(entries)):
            hop(e).start()
        scatter.step(0)
        own_g.wait()
        for k in range(1, n_head):
            g_copy(k).wait_recv()
        g_sum[...] = sum(g_in[k] for k in range(n_head))
        own_tile = b * rows_here // 128 * 128
        g_last[b] = g_sum[:, pl.ds(pl.multiple_of(own_tile, 128), 128)]
        for k in range(1, n_blk):
            pack_copy(k).start()
        for tau in range(1, chips - 2):
            scatter.step(tau)
        own_w.wait()
        for k in range(1, n_head):
            w_copy(k).wait_recv()

        def add(j, carry):
            total = w_in[0, j].astype(F32)
            for k in range(1, n_head):
                total += w_in[k, j].astype(F32)
            w_sum[j] = total.astype(BF16)
            return carry

        lax.fori_loop(0, n_blk, add, 0)
        for one in own_blocks:
            one.start()
        for k in range(1, n_blk):
            for copy in block_copies(k):
                copy.start()

        scatter.step(chips - 2)
        own_o.wait()
        for k in range(1, n_head):
            o_copy(k).wait_recv()

        def add_out(r):
            total = o_in[0, r, :].astype(F32)
            for k in range(1, n_head):
                total += o_in[k, r, :].astype(F32)
            o_sum[r, :] = total.astype(BF16)

        by_rows(rows_here, 16, add_out)

        @pl.when(stays)
        def _():
            keep_out.start()

        @pl.when(jnp.logical_not(stays))
        def _():
            move_out.start()

        def consume(r, dxn):
            unit, factor = unit_of(x_ref[r, :].astype(F32))
            out[r, :] = unit_back(dxn * gain_ref[0:1, :], unit, factor)

        scatter.total(consume)
        for k in range(1, n_blk):
            pack_copy(k).wait_recv()
        g_out[...] = sum(g_last[k] for k in range(n_blk))
        scatter.finish()
        for one in own_blocks:
            one.wait()
        for k in range(1, n_head):
            g_copy(k).wait_send()
            o_copy(k).wait_send()
            w_copy(k).wait_send()
        for k in range(1, n_blk):
            pack_copy(k).wait_send()
            for copy in block_copies(k):
                copy.wait()
        for e in range(len(entries)):
            hop(e).wait()

        @pl.when(stays)
        def _():
            keep_out.wait()

        @pl.when(jnp.logical_not(stays))
        def _():
            move_out.wait()

    return pl.pallas_call(
        kernel,
        out_shape=(
            jax.ShapeDtypeStruct((count, width), F32),
            jax.ShapeDtypeStruct((rows_here, n_blk * q_cols), BF16),
            *[jax.ShapeDtypeStruct((copies, rows_here, n_blk // copies * HEAD_DIM), BF16)] * 2,
            jax.ShapeDtypeStruct((rows_here, width), BF16),
            jax.ShapeDtypeStruct((pack.shape[0], 128), F32),
            *(jax.ShapeDtypeStruct(one.shape[1:], BF16) for one in sums),
        ),
        in_specs=[ANYWHERE] * (4 + n_sums) + [IN_VMEM] * 2,
        out_specs=[IN_VMEM] + [ANYWHERE] * 4 + [IN_VMEM] + [ANYWHERE] * n_sums,
        scratch_shapes=[
            *scatter_bufs(chips, count, width),
            pltpu.VMEM((n_head, n_blk, rows_here, columns), BF16),
            pltpu.VMEM((n_blk, rows_here, columns), BF16),
            pltpu.VMEM((n_head, rows_here, width), BF16),
            pltpu.VMEM((rows_here, width), BF16),
            pltpu.VMEM((n_head, pack.shape[0], n_blk * rows_here), F32),
            pltpu.VMEM((pack.shape[0], n_blk * rows_here), F32),
            pltpu.VMEM((n_blk, pack.shape[0], 128), F32),
            pair_sems(n_head),
            pltpu.SemaphoreType.DMA((3, 2, n_blk)),
            pair_sems(n_head),
            pair_sems(n_head),
            pair_sems(n_blk),
            pltpu.SemaphoreType.DMA((3,)),
            pair_sems(max(1, len(entries))),
            pltpu.SemaphoreType.DMA((7,)),
        ],
        compiler_params=params(collective_id),
        cost_estimate=comm_cost(total_rows * width),
        name="last_scatter",
    )(
        partial_rows.astype(BF16).reshape(chips, 2, count, width),
        w_grad,
        out_grad.reshape(n_head, rows_here, width),
        pack,
        *sums,
        hidden,
        gain,
    )


ROWS = 256
CHUNKS = 2


def block_of(k, size=ROWS):
    return pl.ds(pl.multiple_of(k * size, size), size)


class View:
    def __init__(self, ref, rows):
        self.ref, self.rows = ref, rows
        self.at = self

    def __getitem__(self, index):
        if len(index) == 3:
            j, core, inner = index
            return self.ref.at[j, core, pl.ds(self.rows.start + inner.start, inner.size)]
        j, core = index
        return self.ref.at[j, core, self.rows]


def scatter_gather(
    partial_rows, prepare, between, inputs, outputs, beside, n_head, n_blk, collective_id
):
    total_rows, width = partial_rows.shape
    chips, count = n_blk // 2, total_rows // n_blk
    size = count // CHUNKS
    operands, results, result_specs, more_scratch, aliases, make = beside
    n_in, n_out, n_op, n_res = len(inputs), len(outputs), len(operands), len(results)

    def kernel(part, *refs):
        refs = list(refs)

        def take(n):
            taken = refs[:n]
            del refs[:n]
            return taken

        ins, ops, outs = take(n_in), take(n_op), take(n_out)
        (gathered,) = take(1)
        ress = take(n_res)
        (made,) = take(1)
        chunk_scratch = [take(6) for _ in range(CHUNKS)]
        line = Line(n_blk)
        across = Exchange("head", n_head)
        greet_all((across,), line)
        prepare(outs)
        other = make(ops, ress, refs)
        scatters, gathers = [], []
        for q in range(CHUNKS):
            own, sib, inn, outgoing, sems, g_sems = chunk_scratch[q]
            rows = pl.ds(q * size, size)
            scatters.append(Scatter(line, View(part, rows), (own, sib, inn, outgoing), sems))
            gathers.append(Gather(line, made.at[rows], View(gathered, rows), g_sems))

        def turn(q):
            def consume(r, value):
                r = pl.ds(pl.multiple_of(r.start + q * size, 16), r.size)
                made[r, :] = between(r, value, ins, outs).astype(BF16)

            scatters[q].total(consume)
            gathers[q].start()

        scatters[0].start()
        other.start()
        for q in range(1, CHUNKS):
            scatters[q].start()
        for q in range(CHUNKS):
            for tau in range(chips - 1):
                scatters[q].step(tau)
                if q:
                    gathers[q - 1].step(tau + 1)
            turn(q)
        for s in range(1, chips):
            gathers[-1].step(s)
        for q in range(CHUNKS):
            scatters[q].finish()
            gathers[q].finish()
        other.finish()

    per_chunk = []
    for _ in range(CHUNKS):
        per_chunk += [*scatter_bufs(chips, size, width), gather_sems(chips)]
    given = pl.pallas_call(
        kernel,
        out_shape=(
            *outputs,
            jax.ShapeDtypeStruct((chips, 2, count, width), BF16),
            *results,
        ),
        in_specs=[ANYWHERE] + [IN_VMEM] * n_in + [ANYWHERE] * n_op,
        out_specs=[IN_VMEM] * n_out + [ANYWHERE] + list(result_specs),
        scratch_shapes=[pltpu.VMEM((count, width), BF16), *per_chunk, *more_scratch],
        input_output_aliases={1 + n_in + i: n_out + 1 + o for i, o in aliases.items()},
        compiler_params=params(collective_id),
        cost_estimate=comm_cost(2 * total_rows * width),
        name="scatter_gather",
    )(partial_rows.astype(BF16).reshape(chips, 2, count, width), *inputs, *operands)
    return (
        *given[:n_out],
        given[n_out].reshape(total_rows, width),
        *given[n_out + 1 :],
    )


def spread_beside(full, n_head):
    entries = ff_entries(full[0].shape[1], n_head)

    def make(ops, ress, scratch):
        return Spread(ress, entries, n_head, scratch[0])

    return (
        tuple(full),
        tuple(jax.ShapeDtypeStruct(w.shape, w.dtype) for w in full),
        [ANYWHERE] * 3,
        [Spread.sem_shape(n_head)],
        {0: 0, 1: 1, 2: 2},
        make,
    )


def collect_beside(have, carried, n_head):
    entries = ff_entries(have[0].shape[1], n_head)
    levels = n_head.bit_length() - 2
    shapes = [(n_head // 2, *one.shape[1:]) for one in have]

    def make(ops, ress, scratch):
        kept, inbox = scratch[0:3], scratch[3:6]
        return Collect(ops[:3], kept, inbox, ress[:3], entries, n_head, scratch[6])

    return (
        (*have, carried),
        (
            *(jax.ShapeDtypeStruct((2, *one.shape[1:]), BF16) for one in have),
            jax.ShapeDtypeStruct(carried.shape, carried.dtype),
        ),
        [IN_VMEM] * 3 + [ANYWHERE],
        [
            *(pltpu.VMEM(shape, BF16) for shape in shapes),
            *(pltpu.VMEM((levels, *shape), BF16) for shape in shapes),
            Collect.sem_shape(n_head),
        ],
        {3: 3},
        make,
    )


def turned(values, cosine, sine):
    return values * cosine + pltpu.roll(values, HEAD_DIM // 2, 1) * sine


def local_params(collective_id):
    if collective_id is None:
        return pltpu.CompilerParams(vmem_limit_bytes=60 * 2**20)
    return pltpu.CompilerParams(
        collective_id=collective_id, has_side_effects=True, vmem_limit_bytes=60 * 2**20
    )


def spec_of(shape, dtype):
    return jax.ShapeDtypeStruct(shape, dtype)


def attention_forward(
    x_all, w_attn, vec, gates, tables, out_moved, cot, ff, q_here, n_head, n_blk, collective_id
):
    pack, width = x_all.shape
    chips, count = n_blk // 2, cot.shape[0]
    rows_here, rows_ff = out_moved.shape[0], ff[0].shape[0]
    entries = ff_entries(rows_ff, n_head)
    columns = w_attn.shape[1]
    q_cols = q_here * HEAD_DIM
    blocks = pack // ROWS
    scale = 1.0 / math.sqrt(HEAD_DIM)

    def kernel(x_hbm, moved_hbm, *refs):
        ff_src, (cot_ref, w_ref, vec_ref, gate_ref) = refs[:3], refs[3:7]
        cos_ref, sin_ref, low_ref, code_ref, key_ref = refs[7:12]
        part_hbm, xn_hbm, p_hbm, cot_hbm = refs[12:16]
        ff_out, refs = refs[16:19], refs[19:]
        lin_ref, q_ref, k_ref, v_ref, sig_ref, o_ref, gated_ref, o_rows = refs[:8]
        x_s, xn_s, p_s, in_sem, xn_sem, p_sem, part_sem = refs[8:15]
        cot_sems, out_sems, ff_sems, own_sem = refs[15:]
        line = Line(n_blk)
        across = Exchange("head", n_head)
        h_me, b_me = across.me, line.me
        greet_all((across,), line)
        mine = pl.ds(pl.multiple_of(h_me * rows_here, rows_here), rows_here)

        def out_copy(k):
            return across.copy(k, moved_hbm, o_rows.at[mine], out_sems)

        def hop(e):
            weight, part, order = entries[e]
            return flip_copy(
                ff_src[weight].at[part], ff_out[weight].at[part], order[0], ff_sems, e
            )

        own_out = pltpu.make_async_copy(moved_hbm, o_rows.at[mine], own_sem)
        gather = Gather(line, cot_ref, cot_hbm, cot_sems)
        for k in range(1, n_head):
            out_copy(k).start()
        own_out.start()
        gather.start()
        for e in range(len(entries)):
            hop(e).start()

        def load(n):
            return pltpu.make_async_copy(x_hbm.at[block_of(n)], x_s.at[block_of(n)], in_sem.at[n])

        def xn_store(n):
            return pltpu.make_async_copy(
                xn_s.at[block_of(n)], xn_hbm.at[block_of(n)], xn_sem.at[n]
            )

        def p_store(h, n):
            return pltpu.make_async_copy(
                p_s.at[h, block_of(n)], p_hbm.at[h, block_of(n)], p_sem.at[h, n]
            )

        def part_store(n):
            return pltpu.make_async_copy(
                x_s.at[block_of(n)], part_hbm.at[block_of(n)], part_sem.at[n]
            )

        for n in range(blocks):
            load(n).start()

        def project(n, carry):
            r = block_of(n)
            load(n).wait()
            unit, _ = unit_of(x_s[r, :].astype(F32))
            xn = (unit * vec_ref[0:1, :]).astype(BF16)
            xn_s[r, :] = xn
            xn_store(n).start()
            lin = mm(xn, w_ref[...])
            lin_ref[r, :] = lin
            gate = mm_nt(xn, gate_ref[...])
            one_of = lax.broadcasted_iota(jnp.int32, (ROWS, HEADS), 1)
            lane = lax.broadcasted_iota(jnp.int32, (ROWS, GATE_PAD), 1)
            sigs = jnp.zeros((ROWS, GATE_PAD), F32)
            for h in range(q_here):
                own = jnp.where(one_of == b_me * q_here + h, gate, 0.0)
                own = jax.nn.sigmoid(jnp.sum(own, axis=1, keepdims=True))
                sigs = jnp.where(lane == h, own, sigs)
            sig_ref[r, :] = sigs
            cosine, sine = cos_ref[r, :], sin_ref[r, :]
            for h in range(q_here):
                at = slice(h * HEAD_DIM, (h + 1) * HEAD_DIM)
                unit_q, _ = unit_of(lin[:, at])
                q_ref[r, at] = turned(unit_q * vec_ref[2:3, :HEAD_DIM], cosine, sine).astype(BF16)
            unit_k, _ = unit_of(lin[:, q_cols : q_cols + HEAD_DIM])
            k_ref[r, :] = turned(unit_k * vec_ref[3:4, :HEAD_DIM], cosine, sine).astype(BF16)
            v_ref[r, :] = lin[:, q_cols + HEAD_DIM :].astype(BF16)
            return carry

        lax.fori_loop(0, blocks, project, 0)
        gather.step(1)
        own_out.wait()
        for k in range(1, n_head):
            out_copy(k).wait_recv()

        def attend(n, carry):
            r = block_of(n)
            visible = (key_ref[...] >= low_ref[r, 0:1]) & (key_ref[...] <= code_ref[r, 0:1])
            for h in range(q_here):
                at = slice(h * HEAD_DIM, (h + 1) * HEAD_DIM)
                scores = mm_nt(q_ref[r, at], k_ref[...]) * scale
                scores = jnp.where(visible, scores, MASKED)
                top = jnp.max(scores, axis=-1, keepdims=True)
                weights = jnp.exp(scores - top)
                weights = weights * (1.0 / jnp.sum(weights, axis=-1, keepdims=True))
                prob = weights.astype(BF16)
                p_s[h, r, :] = prob
                p_store(h, n).start()
                out = mm(prob, v_ref[...]).astype(BF16)
                o_ref[r, at] = out
                gated_ref[r, at] = (out.astype(F32) * sig_ref[r, h : h + 1]).astype(BF16)
            x_s[r, :] = mm(gated_ref[r, :], o_rows[...]).astype(BF16)
            part_store(n).start()
            return carry

        lax.fori_loop(0, blocks - 1, attend, 0)
        gather.step(2)
        lax.fori_loop(blocks - 1, blocks, attend, 0)
        for s in range(3, chips):
            gather.step(s)
        gather.finish()
        for k in range(1, n_head):
            out_copy(k).wait_send()
        for e in range(len(entries)):
            hop(e).wait()
        for n in range(blocks):
            xn_store(n).wait()
            part_store(n).wait()
            for h in range(q_here):
                p_store(h, n).wait()

    dma = pltpu.SemaphoreType.DMA
    return pl.pallas_call(
        kernel,
        out_shape=(
            spec_of((pack, width), BF16),
            spec_of((pack, width), BF16),
            spec_of((q_here, pack, pack), BF16),
            spec_of((chips, 2, count, width), BF16),
            *(spec_of(w.shape, BF16) for w in ff),
            spec_of((pack, columns), F32),
            spec_of((pack, q_cols), BF16),
            spec_of((pack, HEAD_DIM), BF16),
            spec_of((pack, HEAD_DIM), BF16),
            spec_of((pack, GATE_PAD), F32),
            spec_of((pack, q_cols), BF16),
            spec_of((pack, q_cols), BF16),
            spec_of((q_cols, width), BF16),
        ),
        in_specs=[ANYWHERE] * 5 + [IN_VMEM] * 9,
        out_specs=[ANYWHERE] * 7 + [IN_VMEM] * 8,
        scratch_shapes=[
            pltpu.VMEM((pack, width), BF16),
            pltpu.VMEM((pack, width), BF16),
            pltpu.VMEM((q_here, pack, pack), BF16),
            dma((blocks,)),
            dma((blocks,)),
            dma((q_here, blocks)),
            dma((blocks,)),
            gather_sems(chips),
            pair_sems(n_head),
            pair_sems(len(entries)),
            dma,
        ],
        compiler_params=local_params(collective_id),
        cost_estimate=comm_cost(pack * width),
        name="attention_forward",
    )(x_all, out_moved, *ff, cot, w_attn, vec, gates, *tables)


def attention_backward(
    dy, xn, p, saved, w_attn, vec, gates, tables, mlp_gain_part, q_here, beside=None
):
    pack, width = dy.shape
    columns = w_attn.shape[1]
    q_cols = q_here * HEAD_DIM
    blocks = pack // ROWS
    scale = 1.0 / math.sqrt(HEAD_DIM)

    have, n_head, collective_id = beside or ((), 0, None)
    n_have = len(have)
    sum_scratch = []
    if have:
        entries = ff_entries(have[0].shape[1], n_head)
        sum_scratch = [pair_sems(len(entries))]

    def kernel(dy_hbm, xn_hbm, p_hbm, *refs):
        have_refs, refs = refs[:n_have], refs[n_have:]
        n_plain = 14 + 4
        plain, more = refs[:n_plain], refs[n_plain:]
        got, more = more[:n_have], more[n_have:]
        plain_scratch, sems = more[:14], more[14:]
        if not have:
            return local(dy_hbm, xn_hbm, p_hbm, *plain, *plain_scratch)
        greet_all((Exchange("head", n_head),))
        copies = [
            flip_copy(have_refs[w].at[1, part], got[w].at[part], order[0], sems[0], e)
            for e, (w, part, order) in enumerate(entries)
        ]
        for copy in copies:
            copy.start()
        local(dy_hbm, xn_hbm, p_hbm, *plain, *plain_scratch)
        for copy in copies:
            copy.wait()

    def local(dy_hbm, xn_hbm, p_hbm, lin_ref, q_ref, k_ref, v_ref, sig_ref, o_ref, *refs):
        gated_ref, o_rows, w_ref, vec_ref, gate_ref, cos_ref, sin_ref, mlp_ref = refs[:8]
        dxn_hbm, dw_ref, pack_ref, dout_ref = refs[8:12]
        dy_s, xn_s, p_s, do_s, delta_s, dgate_s, dlin_s, dk_s, dv_s, dgq_s = refs[12:22]
        dy_sem, xn_sem, p_sem, out_sem = refs[22:]
        first_head = lax.axis_index("blk") * q_here

        def dy_load(n):
            return pltpu.make_async_copy(
                dy_hbm.at[block_of(n)], dy_s.at[block_of(n)], dy_sem.at[n]
            )

        def p_load(h, n):
            return pltpu.make_async_copy(
                p_hbm.at[h, block_of(n)], p_s.at[h, block_of(n)], p_sem.at[h, n]
            )

        def dxn_store(n):
            return pltpu.make_async_copy(
                dy_s.at[block_of(n)], dxn_hbm.at[block_of(n)], out_sem.at[n]
            )

        xn_load = pltpu.make_async_copy(xn_hbm, xn_s, xn_sem)
        for n in range(blocks):
            dy_load(n).start()
        for n in range(blocks):
            for h in range(q_here):
                p_load(h, n).start()
        xn_load.start()

        def through_gate(n, carry):
            r = block_of(n)
            dy_load(n).wait()
            dgated = mm_nt(dy_s[r, :], o_rows[...])
            lane = lax.broadcasted_iota(jnp.int32, (ROWS, GATE_PAD), 1)
            dgates = jnp.zeros((ROWS, GATE_PAD), F32)
            deltas = jnp.zeros((ROWS, GATE_PAD), F32)
            for h in range(q_here):
                at = slice(h * HEAD_DIM, (h + 1) * HEAD_DIM)
                sig = sig_ref[r, h : h + 1]
                out = o_ref[r, at].astype(F32)
                do = (dgated[:, at] * sig).astype(BF16)
                do_s[r, at] = do
                dgate = jnp.sum(dgated[:, at] * out, axis=-1, keepdims=True) * sig * (1.0 - sig)
                delta = jnp.sum(do.astype(F32) * out, axis=-1, keepdims=True)
                dgates = jnp.where(lane == first_head + h, dgate, dgates)
                deltas = jnp.where(lane == h, delta, deltas)
            dgate_s[r, :] = dgates.astype(BF16)
            delta_s[r, :] = deltas
            return carry

        lax.fori_loop(0, blocks, through_gate, 0)

        def out_grad(n, carry):
            c = block_of(n)
            dout_ref[:, c] = mm_tn(gated_ref[...], dy_s[:, c]).astype(BF16)
            return carry

        lax.fori_loop(0, width // ROWS, out_grad, 0)
        dk_s[...] = jnp.zeros_like(dk_s)
        dv_s[...] = jnp.zeros_like(dv_s)
        dgq_s[...] = jnp.zeros_like(dgq_s)

        def into_lin(grad, lin, gain, r):
            grad = turned(grad.astype(BF16).astype(F32), cos_ref[r, :], -sin_ref[r, :])
            unit, factor = unit_of(lin)
            return unit_back(grad * gain, unit, factor).astype(BF16), grad * unit

        def attend(n, carry):
            r = block_of(n)
            for h in range(q_here):
                at = slice(h * HEAD_DIM, (h + 1) * HEAD_DIM)
                p_load(h, n).wait()
                do, prob, q = do_s[r, at], p_s[h, r, :], q_ref[r, at]
                dp = mm_nt(do, v_ref[...])
                ds = (prob.astype(F32) * (dp - delta_s[r, h : h + 1])).astype(BF16)
                dq = mm(ds, k_ref[...]) * scale
                dk_s[...] += mm(q.T, ds)
                dv_s[...] += mm(do.T, prob)
                dlin, part = into_lin(dq, lin_ref[r, at], vec_ref[2:3, :HEAD_DIM], r)
                dlin_s[r, at] = dlin
                dgq_s[...] += jnp.sum(part.reshape(ROWS // 8, 8, HEAD_DIM), axis=0)
            return carry

        lax.fori_loop(0, blocks, attend, 0)
        every = pl.ds(0, pack)
        k_cols = slice(q_cols, q_cols + HEAD_DIM)
        dlin, part = into_lin(
            dk_s[...].T * scale, lin_ref[:, k_cols], vec_ref[3:4, :HEAD_DIM], every
        )
        dlin_s[:, k_cols] = dlin
        dgk = jnp.sum(part, axis=0, keepdims=True)
        dgq = jnp.sum(dgq_s[...], axis=0, keepdims=True)
        pack_ref[HEADS:, :] = jnp.zeros((PACK_ROWS - HEADS, width), F32)
        pack_ref[HEADS : HEADS + 1, :] = jnp.sum(mlp_ref[...], axis=0, keepdims=True)
        for t in range(width // HEAD_DIM):
            lanes = slice(t * HEAD_DIM, (t + 1) * HEAD_DIM)
            pack_ref[HEADS + 1 : HEADS + 2, lanes] = dgq
            pack_ref[HEADS + 2 : HEADS + 3, lanes] = dgk
        dlin_s[:, q_cols + HEAD_DIM :] = dv_s[...].T.astype(BF16)

        def into_x(n, carry):
            r = block_of(n)
            dxn = mm_nt(dlin_s[r, :], w_ref[...]) + mm(dgate_s[r, :HEADS], gate_ref[...])
            dy_s[r, :] = dxn.astype(BF16)
            dxn_store(n).start()
            return carry

        lax.fori_loop(0, blocks, into_x, 0)
        xn_load.wait()
        dgate_t = dgate_s[...].astype(F32).T[:HEADS].astype(BF16)

        def weights(n, carry):
            c = block_of(n)
            xn_cols = xn_s[:, c]
            dw_ref[c, :] = mm_tn(xn_cols, dlin_s[...]).astype(BF16)
            pack_ref[:HEADS, c] = mm(dgate_t, xn_cols)
            return carry

        lax.fori_loop(0, width // ROWS, weights, 0)
        for n in range(blocks):
            dxn_store(n).wait()

    return pl.pallas_call(
        kernel,
        out_shape=(
            spec_of((pack, width), BF16),
            spec_of((width, columns), BF16),
            spec_of((PACK_ROWS, width), F32),
            spec_of((q_cols, width), BF16),
            *(spec_of(one.shape[1:], BF16) for one in have),
        ),
        in_specs=[ANYWHERE] * (3 + n_have) + [IN_VMEM] * 14,
        out_specs=[ANYWHERE] + [IN_VMEM] * 3 + [ANYWHERE] * n_have,
        scratch_shapes=[
            pltpu.VMEM((pack, width), BF16),
            pltpu.VMEM((pack, width), BF16),
            pltpu.VMEM((q_here, pack, pack), BF16),
            pltpu.VMEM((pack, q_cols), BF16),
            pltpu.VMEM((pack, GATE_PAD), F32),
            pltpu.VMEM((pack, GATE_PAD), BF16),
            pltpu.VMEM((pack, columns), BF16),
            pltpu.VMEM((HEAD_DIM, pack), F32),
            pltpu.VMEM((HEAD_DIM, pack), F32),
            pltpu.VMEM((8, HEAD_DIM), F32),
            pltpu.SemaphoreType.DMA((blocks,)),
            pltpu.SemaphoreType.DMA,
            pltpu.SemaphoreType.DMA((q_here, blocks)),
            pltpu.SemaphoreType.DMA((blocks,)),
            *sum_scratch,
        ],
        compiler_params=local_params(collective_id),
        name="attention_backward",
    )(dy, xn, p, *have, *saved, w_attn, vec, gates, *tables, mlp_gain_part)


class Rows:
    def __init__(self, ref, q, size, chips):
        self.ref, self.base, self.size = ref, q * size * chips * 2, size
        self.at = self

    def rows(self, j, core, start=0, count=None):
        first = self.base + (j * 2 + core) * self.size + start
        return pl.ds(pl.multiple_of(first, 16), count or self.size)

    def __getitem__(self, index):
        j, core, *inner = index
        if inner:
            return self.ref.at[self.rows(j, core, inner[0].start, inner[0].size)]
        return self.ref.at[self.rows(j, core)]


class OwnRows:
    def __init__(self, rows, core):
        self.view, self.core = rows, core
        self.shape = (0, rows.size)

    def __getitem__(self, index):
        j, r, _ = index
        return self.view.ref[self.view.rows(j, self.core, r.start, r.size), :]


class LocalScatter(Scatter):
    def __init__(self, line, part, bufs, sems):
        super().__init__(line, part, (OwnRows(part, line.c), *bufs), sems)

    def start(self):
        chips = self.line.chips
        order = []
        for k in range((chips + 1) // 2):
            order += [chips - 1 - k, k]
        for j in order[:chips]:
            self.to_sibling(j).start()

    def ready(self, j):
        self.to_sibling(j).wait_recv()


def feed_forward(attn_part, ff, halfway, cot, inputs, to_mlp, to_attention, n_head, n_blk, collective_id):
    total_rows, width = attn_part.shape
    chips, count = n_blk // 2, total_rows // n_blk
    size, half = count // CHUNKS, total_rows // CHUNKS
    rows_ff = ff[0].shape[0]
    units = n_head * rows_ff
    entries = ff_entries(rows_ff, n_head)
    n_in = len(inputs)

    def kernel(part, cot_hbm, *refs):
        refs = list(refs)

        def take(n):
            taken = refs[:n]
            del refs[:n]
            return taken

        sources = take(3), take(3)
        ins = take(n_in)
        middle, dmid, gain_part, dy_hbm, mlp_hbm, *sum_hbm = take(8)
        made, hn_s, cot_s, dhn_s, u_s, da_s, db_s, stage = take(8)
        inboxes, weights = take(3), take(3)
        chunk_scratch = [take(8) for _ in range(CHUNKS)]
        load_sems, hop_sems, cot_sems, stage_sems, sum_sems, grad_sems = refs
        line = Line(n_blk)
        across = Exchange("head", n_head)
        greet_all((across,), line)
        gain_part[...] = jnp.zeros_like(gain_part)

        def place(key, span):
            return pl.ds(key * rows_ff + span.start, span.size)

        loads, hops = [], []
        for e, (w, span, order) in enumerate(entries):
            first, second = 1 << order[0], 1 << order[1]
            for at, key in enumerate((0, first)):
                src = sources[at][w].at[span]
                loads.append(
                    pltpu.make_async_copy(src, weights[w].at[place(key, span)], load_sems.at[e, at])
                )
                there = weights[w].at[place(key ^ second, span)]
                hops.append(flip_copy(src, there, order[1], hop_sems, e, at))

        def cot_loads(q):
            for j in range(chips):
                for c in range(2):
                    yield pltpu.make_async_copy(
                        cot_hbm.at[j, c, pl.ds(q * size, size)],
                        Rows(cot_s, q, size, chips)[j, c],
                        cot_sems.at[q, 2 * j + c],
                    )

        first, gather1, second, gather2 = [], [], [], []
        for q in range(CHUNKS):
            own, sib, inn, outgoing, sems, g_sems, sems2, g_sems2 = chunk_scratch[q]
            rows = pl.ds(q * size, size)
            first.append(Scatter(line, View(part, rows), (own, sib, inn, outgoing), sems))
            gather1.append(Gather(line, made.at[rows], Rows(hn_s, q, size, chips), g_sems))
            second.append(
                LocalScatter(line, Rows(dhn_s, q, size, chips), (sib, inn, outgoing), sems2)
            )
            gather2.append(Gather(line, made.at[rows], View(dy_hbm, rows), g_sems2))

        def turn(q, scatter, between, outs, gather):
            def consume(r, value):
                r = pl.ds(pl.multiple_of(r.start + q * size, 16), r.size)
                made[r, :] = between(r, value, ins, outs).astype(BF16)

            scatter[q].total(consume)
            gather[q].start()

        def loop(steps, body):
            lax.fori_loop(0, steps, lambda k, carry: body(k) or carry, 0)

        def span_of(q):
            return pl.ds(q * half, half)

        def unit_block(q, f):
            r, fr = span_of(q), block_of(f)
            a = mm_nt(hn_s[r, :], weights[0][fr, :])
            b = mm_nt(hn_s[r, :], weights[1][fr, :])
            du = mm_nt(cot_s[r, :], weights[2][fr, :])
            sig = jax.nn.sigmoid(a)
            silu = a * sig
            u_s[r, fr] = (silu * b).astype(BF16)
            da_s[r, fr] = (du * b * sig * (1.0 + a * (1.0 - sig))).astype(BF16)
            db_s[r, fr] = (du * silu).astype(BF16)

        def back(q):
            r = span_of(q)

            def body(n):
                cols = block_of(n, 512)
                dhn = mm(da_s[r, :], weights[0][:, cols]) + mm(db_s[r, :], weights[1][:, cols])
                dhn_s[r, cols] = dhn.astype(BF16)

            loop(width // 512, body)

        def stage_stores(q):
            for j in range(chips):
                for c in range(2):
                    yield pltpu.make_async_copy(
                        Rows(stage, 0, size, chips)[j, c],
                        mlp_hbm.at[j, c, pl.ds(q * size, size)],
                        stage_sems.at[2 * j + c],
                    )

        def mlp_out(q):
            if q:
                for store in stage_stores(q - 1):
                    store.wait()
            r = span_of(q)

            def body(n):
                cols = block_of(n, 512)
                stage[:, cols] = mm(u_s[r, :], weights[2][:, cols]).astype(BF16)

            loop(width // 512, body)
            for store in stage_stores(q):
                store.start()

        def grad(w):
            left, right = ((da_s, hn_s), (db_s, hn_s), (u_s, cot_s))[w]

            def body(f):
                fr = block_of(f)
                weights[w][fr, :] = mm_tn(left[:, fr], right[...]).astype(BF16)

            loop(units // ROWS, body)

        def sum_copies(w):
            for e, (weight, span, order) in enumerate(entries):
                if weight == w:
                    for at, key in enumerate((0, 1 << order[0])):
                        yield flip_copy(
                            weights[w].at[place(key ^ (1 << order[1]), span)],
                            inboxes[w].at[at, span],
                            order[1],
                            sum_sems,
                            e,
                            at,
                        )

        def sum_stores(w):
            for e, (weight, span, order) in enumerate(entries):
                if weight == w:
                    for at, key in enumerate((0, 1 << order[0])):
                        yield pltpu.make_async_copy(
                            weights[w].at[place(key, span)],
                            sum_hbm[w].at[at, span],
                            grad_sems.at[e, at],
                        )

        def send_grad(w):
            grad(w)
            for copy in sum_copies(w):
                copy.start()

        def add_grad(w):
            for copy in sum_copies(w):
                copy.wait()
            for weight, span, order in entries:
                if weight == w:
                    for at, key in enumerate((0, 1 << order[0])):

                        def body(r, span=span, at=at, key=key):
                            r = pl.ds(pl.multiple_of(r.start + span.start, 16), r.size)
                            mine = pl.ds(pl.multiple_of(r.start + key * rows_ff, 16), r.size)
                            value = weights[w][mine, :].astype(F32)
                            value += inboxes[w][at, r, :].astype(F32)
                            weights[w][mine, :] = value.astype(BF16)

                        by_rows(span.size, 16, body)
            for store in sum_stores(w):
                store.start()

        first[0].start()
        for hop in hops:
            hop.start()
        for q in range(1, CHUNKS):
            first[q].start()
        for load in loads:
            load.start()
        for q in range(CHUNKS):
            for load in cot_loads(q):
                load.start()
        steps = chips - 1
        for tau in range(steps):
            first[0].step(tau)
        turn(0, first, to_mlp, (middle,), gather1)
        for tau in range(steps):
            first[1].step(tau)
            gather1[0].step(tau + 1)
        turn(1, first, to_mlp, (middle,), gather1)
        for q in range(CHUNKS):
            first[q].finish()
        gather1[0].finish()
        gather1[1].step(1)
        for load in loads:
            load.wait()
        for load in cot_loads(0):
            load.wait()
        for hop in hops:
            hop.wait()
        blocks = units // ROWS
        unit_block(0, 0)
        for s in range(2, chips):
            gather1[1].step(s)
            if s == 2:
                unit_block(0, 1)
        for f in range(2, blocks):
            unit_block(0, f)
        back(0)
        second[0].start()
        gather1[1].finish()
        for load in cot_loads(1):
            load.wait()
        second[0].step(0)
        loop(blocks, lambda f: unit_block(1, f))
        second[0].step(1)
        back(1)
        second[1].start()
        send_grad(0)
        for tau in range(2, steps):
            second[0].step(tau)
        second[1].step(0)
        send_grad(1)
        turn(0, second, to_attention, (middle, dmid, gain_part), gather2)
        second[1].step(1)
        mlp_out(0)
        mlp_out(1)
        gather2[0].step(1)
        send_grad(2)
        for tau in range(2, steps):
            second[1].step(tau)
            gather2[0].step(tau)
        turn(1, second, to_attention, (middle, dmid, gain_part), gather2)
        gather2[0].step(chips - 1)
        for s in range(1, chips):
            gather2[1].step(s)
        for w in range(3):
            add_grad(w)
        for q in range(CHUNKS):
            second[q].finish()
            gather2[q].finish()
        for store in stage_stores(CHUNKS - 1):
            store.wait()
        for w in range(3):
            for store in sum_stores(w):
                store.wait()

    per_chunk = []
    for _ in range(CHUNKS):
        own, sib, inn, outgoing, sems = scatter_bufs(chips, size, width)
        per_chunk += [own, sib, inn, outgoing, sems, gather_sems(chips), sems, gather_sems(chips)]
    sums = jax.ShapeDtypeStruct((2, rows_ff, width), BF16)
    shards_ = jax.ShapeDtypeStruct((chips, 2, count, width), BF16)
    dma = pltpu.SemaphoreType.DMA
    middle, dmid, gain_part, dy, mlp_part, *ff_sums = pl.pallas_call(
        kernel,
        out_shape=(
            jax.ShapeDtypeStruct((count, width), F32),
            jax.ShapeDtypeStruct((count, width), F32),
            jax.ShapeDtypeStruct((8, width), F32),
            shards_,
            shards_,
            *[sums] * 3,
        ),
        in_specs=[ANYWHERE] * 8 + [IN_VMEM] * n_in,
        out_specs=[IN_VMEM] * 3 + [ANYWHERE] * 5,
        scratch_shapes=[
            pltpu.VMEM((count, width), BF16),
            *[pltpu.VMEM((total_rows, width), BF16)] * 3,
            *[pltpu.VMEM((total_rows, units), BF16)] * 3,
            pltpu.VMEM((half, width), BF16),
            *[pltpu.VMEM((2, rows_ff, width), BF16)] * 3,
            *[pltpu.VMEM((units, width), BF16)] * 3,
            *per_chunk,
            dma((len(entries), 2)),
            dma((2, len(entries), 2)),
            dma((CHUNKS, n_blk)),
            dma((n_blk,)),
            dma((2, len(entries), 2)),
            dma((len(entries), 2)),
        ],
        compiler_params=pltpu.CompilerParams(
            collective_id=collective_id, has_side_effects=True, vmem_limit_bytes=62 * 2**20
        ),
        cost_estimate=comm_cost(2 * total_rows * width),
        name="feed_forward",
    )(
        attn_part.reshape(chips, 2, count, width),
        cot.reshape(chips, 2, count, width),
        *ff,
        *halfway,
        *inputs,
    )
    return (
        middle,
        dmid,
        gain_part,
        dy.reshape(total_rows, width),
        mlp_part.reshape(total_rows, width),
        ff_sums,
    )


def padded(values, size):
    return jnp.pad(values, [(0, 0)] * (values.ndim - 1) + [(0, size - values.shape[-1])])


def shards(
    hidden,
    segment_ids,
    block_ids,
    positions,
    attn_gain,
    w_query,
    key_weight_matrix,
    value_weight_matrix,
    q_gain,
    k_gain,
    w_head_gate,
    w_out,
    mlp_gain,
    w_gate,
    w_up,
    w_down,
    cotangent,
):
    n_head = lax.axis_size("head")
    n_blk = lax.axis_size("blk")
    n_all = n_head * n_blk
    my_head = lax.axis_index("head")
    my_blk = lax.axis_index("blk")
    tokens = hidden.shape[1]
    pack = tokens * n_blk
    rows_here = w_query.shape[0]
    rows_ff = w_gate.shape[0]
    q_here = HEADS // n_blk
    q_cols = q_here * HEAD_DIM
    kv_copies = max(1, n_blk // KV_HEADS)
    kv_here = max(1, KV_HEADS // n_blk)
    kv_cols = kv_here * HEAD_DIM
    device = my_head * n_blk + my_blk
    together = 128 // rows_here
    lane = jnp.arange(128)
    here = (lane // rows_here == device % together)[None]
    mine = jnp.concatenate(
        [
            attn_gain[None],
            mlp_gain[None],
            jnp.zeros((6, rows_here), BF16),
            w_head_gate.T,
        ]
    )
    small = jnp.where(here, jnp.tile(mine, (1, together)), 0).astype(F32)
    share = q_gain.shape[0]
    head_gains = jnp.stack([jnp.tile(q_gain, n_all), jnp.tile(k_gain, n_all)]).astype(F32)
    head_gains = jnp.where(lane // share == device, head_gains, 0)
    small = small + jnp.pad(head_gains, ((2, PACK_ROWS - 4), (0, 0)))
    ids = [
        lax.dynamic_slice_in_dim(ids_, my_head, 1, 0) for ids_ in (positions, segment_ids, block_ids)
    ]
    x_all, w_attn, out_moved, vec, gates, *tables = first_gather(
        hidden[0],
        (w_query, key_weight_matrix, value_weight_matrix),
        small,
        w_out,
        ids,
        q_cols,
        kv_copies,
        n_head,
        n_blk,
        0,
    )
    ff = (w_gate, w_up, w_down)
    attn_part, xn, prob, cot, *rest = attention_forward(
        x_all, w_attn, vec, gates, tables, out_moved, cotangent[0], ff, q_here, n_head, n_blk, 4
    )
    halfway, saved = rest[:3], rest[3:]

    def to_mlp(r, total, ins, outs):
        x_ref, gain_ref = ins
        mid = x_ref[r, :].astype(F32) + total
        outs[0][r, :] = mid
        unit, _ = unit_of(mid)
        return unit * gain_ref[1:2, :]

    def to_attention(r, dhn, ins, outs):
        mid_ref, cot_ref, gain_ref = ins
        unit, factor = unit_of(mid_ref[r, :])
        product = dhn * unit
        seen = outs[1]
        seen[...] += product[:8] + product[8:]
        back = cot_ref[r, :].astype(F32) + unit_back(dhn * gain_ref[1:2, :], unit, factor)
        outs[0][r, :] = back
        return back

    fused = n_head == 4 and pack <= 1024
    if fused:

        def into_mlp(r, total, ins, outs):
            return to_mlp(r, total, (ins[0], ins[2]), outs)

        def into_attention(r, dhn, ins, outs):
            return to_attention(r, dhn, (outs[0], ins[1], ins[2]), outs[1:])

        middle, dmid, mlp_gain_part, dy, mlp_part, ff_sums = feed_forward(
            attn_part,
            ff,
            halfway,
            cot,
            (hidden[0], cotangent[0], vec),
            into_mlp,
            into_attention,
            n_head,
            n_blk,
            1,
        )
    else:
        cot = cot.reshape(pack, MODEL_WIDTH)
        ff_full = []
        for w, (own, other) in enumerate(zip(ff, halfway)):
            full = jnp.zeros((n_head, *own.shape), BF16).at[0].set(own)
            for weight, part, order in ff_entries(rows_ff, n_head):
                if weight == w:
                    span = slice(part.start, part.start + part.size)
                    full = full.at[1 << order[0], span].set(other[span])
            ff_full.append(full)
        middle, hn, *ff_rows = scatter_gather(
            attn_part,
            lambda outs: None,
            to_mlp,
            (hidden[0], vec),
            (jax.ShapeDtypeStruct(hidden.shape[1:], F32),),
            spread_beside(ff_full, n_head),
            n_head,
            n_blk,
            1,
        )
        gate_rows, up_rows, down_rows = (one.reshape(n_head * rows_ff, MODEL_WIDTH) for one in ff_rows)

        a = mm_nt(hn, gate_rows)
        b = mm_nt(hn, up_rows)
        sig = jax.nn.sigmoid(a)
        silu = a * sig
        u = (silu * b).astype(BF16)
        mlp_part = mm(u, down_rows).astype(BF16)
        du = mm_nt(cot, down_rows)
        da = (du * b * sig * (1.0 + a * (1.0 - sig))).astype(BF16)
        db = (du * silu).astype(BF16)
        ff_parts = [
            mm_tn(left, right).astype(BF16).reshape(n_head, rows_ff, MODEL_WIDTH)
            for left, right in ((da, hn), (db, hn), (u, cot))
        ]

        def clear(outs):
            outs[1][...] = jnp.zeros_like(outs[1])

        dmid, mlp_gain_part, dy, *ff_sums, mlp_part = scatter_gather(
            mm(da, gate_rows) + mm(db, up_rows),
            clear,
            to_attention,
            (middle, cotangent[0], vec),
            (
                jax.ShapeDtypeStruct(hidden.shape[1:], F32),
                jax.ShapeDtypeStruct((8, MODEL_WIDTH), F32),
            ),
            collect_beside(ff_parts, mlp_part, n_head),
            n_head,
            n_blk,
            2,
        )

    layer_output = (
        middle + lax.psum_scatter(mlp_part, "blk", scatter_dimension=0, tiled=True).astype(F32)
    ).astype(BF16)[None]
    dxn_part, attn_grad, small_parts, out_grad, *ff_last = attention_backward(
        dy,
        xn,
        prob,
        saved,
        w_attn,
        vec,
        gates,
        tables[:2],
        mlp_gain_part,
        q_here,
        (ff_sums, n_head, 2) if fused else None,
    )
    back_x, query_grad, key_grad, value_grad, out_grad, small_sums, *ff_rest = last_scatter(
        dxn_part,
        attn_grad.reshape(n_head, n_blk, rows_here, -1),
        out_grad,
        small_parts,
        () if fused else ff_sums,
        hidden[0],
        vec,
        q_cols,
        kv_copies,
        n_head,
        n_blk,
        3,
    )
    ff_last = ff_last or ff_rest
    input_grad = (dmid + back_x)[None]
    ff_grads = [one[0].astype(F32) + two.astype(F32) for one, two in zip(ff_sums, ff_last)]

    query_grad = query_grad.astype(F32)
    key_grad = jnp.sum(key_grad.astype(F32), axis=0)
    value_grad = jnp.sum(value_grad.astype(F32), axis=0)
    small_sums = jnp.sum(
        jnp.where(
            jnp.arange(together)[None, :, None] == device % together,
            small_sums.reshape(PACK_ROWS, together, rows_here),
            0.0,
        ),
        axis=1,
    ), small_sums[HEADS + 1 : HEADS + 3]
    small_sums, head_sums = small_sums
    head_sums = lax.dynamic_slice_in_dim(head_sums, device * share, share, 1)
    head_gate_grad = small_sums[:HEADS].T
    attn_gain_grad = (
        jnp.sum(w_query.astype(F32) * query_grad, axis=1)
        + jnp.sum(key_weight_matrix.astype(F32) * key_grad, axis=1)
        + jnp.sum(value_weight_matrix.astype(F32) * value_grad, axis=1)
        + jnp.sum(w_head_gate.astype(F32) * head_gate_grad, axis=1)
    ) / attn_gain.astype(F32)
    return (
        layer_output,
        input_grad,
        attn_gain_grad,
        query_grad,
        key_grad,
        value_grad,
        head_sums[0],
        head_sums[1],
        head_gate_grad,
        out_grad.astype(F32),
        small_sums[HEADS],
        ff_grads[0],
        ff_grads[1],
        ff_grads[2],
    )


def solution(mesh):
    rows = P(("head", "blk"), None)
    vector = P(("head", "blk"))
    token = P("head", "blk", None)
    return jax.shard_map(
        shards,
        mesh=mesh,
        in_specs=(
            token, P(), P(), P(), vector, rows, rows, rows, vector, vector, rows, rows, vector,
            rows, rows, rows, token,
        ),
        out_specs=(
            token, token, vector, rows, rows, rows, vector, vector, rows, rows, vector,
            rows, rows, rows,
        ),
        check_vma=False,
    )
```

```python
import math

import jax
import jax.numpy as jnp
from jax import lax
from jax.experimental import pallas as pl
from jax.experimental.pallas import tpu as pltpu
from jax.sharding import PartitionSpec as P

MODEL_WIDTH = 2048
HEADS = 16
KV_HEADS = 8
HEAD_DIM = 128
GATE_PAD = 128
EPSILON = 1e-06
ROPE_BASE = 1000000.0
MASKED = -1e30
F32 = jnp.float32
BF16 = jnp.bfloat16
MESH = pl.DeviceIdType.MESH


def mm(a, b):
    return jnp.dot(a, b, preferred_element_type=F32)


def mm_nt(a, b):
    return lax.dot_general(a, b, (((1,), (1,)), ((), ())), preferred_element_type=F32)


def mm_tn(a, b):
    return lax.dot_general(a, b, (((0,), (0,)), ((), ())), preferred_element_type=F32)


def unit_of(values):
    factor = lax.rsqrt(jnp.mean(values * values, axis=-1, keepdims=True) + EPSILON)
    return values * factor, factor


def unit_back(scaled, unit, factor):
    return factor * (scaled - unit * jnp.mean(scaled * unit, axis=-1, keepdims=True))


def signal_to(semaphore, target):
    pl.semaphore_signal(semaphore, inc=1, device_id=target, device_id_type=MESH)


class Line:
    def __init__(self, n_blk):
        self.me = lax.axis_index("blk")
        self.chips = n_blk // 2
        self.i = self.me // 2
        self.c = self.me % 2
        self.right = {"blk": self.me + 2}
        self.left = {"blk": self.me - 2}
        self.sibling = {"blk": self.me + 1 - 2 * self.c}
        self.has_right = self.i < self.chips - 1
        self.has_left = self.i > 0

    def greet(self, barrier):
        signal_to(barrier, self.sibling)

        @pl.when(self.has_right)
        def _():
            signal_to(barrier, self.right)

        @pl.when(self.has_left)
        def _():
            signal_to(barrier, self.left)

        return 1 + self.has_right.astype(jnp.int32) + self.has_left.astype(jnp.int32)


class Gather:
    def __init__(self, line, src, out, sems):
        self.line, self.src, self.out, self.sems = line, src, out, sems
        self.pieces = sems.shape[2]
        self.rows = src.shape[0] // self.pieces

    def part(self, p):
        return pl.ds(p * self.rows, self.rows)

    def move(self, kind, src, j, p, target):
        return pltpu.make_async_remote_copy(
            src_ref=src.at[self.part(p)],
            dst_ref=self.out.at[j, self.line.c, self.part(p)],
            send_sem=self.sems.at[kind, j, p],
            recv_sem=self.sems.at[3 + kind, j, p],
            device_id=target,
            device_id_type=MESH,
        )

    def arrived(self, kind, j, p, core):
        there = self.out.at[j, core, self.part(p)]
        pltpu.make_async_remote_copy(
            src_ref=there,
            dst_ref=there,
            send_sem=self.sems.at[kind, j, p],
            recv_sem=self.sems.at[3 + kind, j, p],
            device_id=self.line.sibling,
            device_id_type=MESH,
        ).wait_recv()

    def send(self, src, j, p, right, left):
        line = self.line
        if right is not None:

            @pl.when(right)
            def _():
                self.move(0, src, j, p, line.right).start()

        if left is not None:

            @pl.when(left)
            def _():
                self.move(1, src, j, p, line.left).start()

        self.move(2, src, j, p, line.sibling).start()

    def own_copy(self):
        return pltpu.make_async_copy(
            self.src, self.out.at[self.line.i, self.line.c], self.sems.at[6, 0, 0]
        )

    def start(self):
        line = self.line
        for p in range(self.pieces):
            self.send(self.src, line.i, p, line.has_right, line.has_left)
        self.own_copy().start()

    def step(self, s):
        line = self.line
        from_left, from_right = line.i - s, line.i + s
        for p in range(self.pieces):

            @pl.when(from_left >= 0)
            def _(p=p):
                self.arrived(0, from_left, p, line.c)
                self.send(self.out.at[from_left, line.c], from_left, p, line.has_right, None)

            @pl.when(from_right < line.chips)
            def _(p=p):
                self.arrived(1, from_right, p, line.c)
                self.send(self.out.at[from_right, line.c], from_right, p, None, line.has_left)

    def finish(self):
        line = self.line
        for j in range(line.chips):
            mine = self.out.at[j, line.c]
            for p in range(self.pieces):
                self.arrived(2, j, p, 1 - line.c)
                self.move(2, mine, j, p, line.sibling).wait_send()

                @pl.when((line.i >= j) & line.has_right)
                def _(j=j, p=p, mine=mine):
                    self.move(0, mine, j, p, line.right).wait_send()

                @pl.when((line.i <= j) & line.has_left)
                def _(j=j, p=p, mine=mine):
                    self.move(1, mine, j, p, line.left).wait_send()

        self.own_copy().wait()

    def run(self):
        self.start()
        for s in range(1, self.line.chips):
            self.step(s)
        self.finish()


def by_rows(rows, step, body):
    def one(k, carry):
        body(pl.ds(pl.multiple_of(k * step, step), step))
        return carry

    lax.fori_loop(0, rows // step, one, 0)


SUMS = 2


class Scatter:
    def __init__(self, line, part, bufs, sems):
        self.line, self.part, self.sems = line, part, sems
        self.own, self.sib, self.inn, self.out = bufs

    def copy(self, kind, src, dst, slot, target):
        return pltpu.make_async_remote_copy(
            src_ref=src,
            dst_ref=dst,
            send_sem=self.sems.at[(kind, *slot)],
            recv_sem=self.sems.at[(3 + kind, *slot)],
            device_id=target,
            device_id_type=MESH,
        )

    def to_sibling(self, j):
        line = self.line
        return self.copy(2, self.part.at[j, 1 - line.c], self.sib.at[j], (j, 0), line.sibling)

    def to_own(self, j):
        return pltpu.make_async_copy(
            self.part.at[j, self.line.c], self.own.at[j], self.sems.at[6, j, 0]
        )

    @property
    def size(self):
        return self.own.shape[1] // SUMS

    def along(self, way, j, p):
        line = self.line
        target = line.left if way else line.right
        span = pl.ds(p * self.size, self.size)
        return self.copy(way, self.out.at[j, span], self.inn.at[way, j, span], (j, p), target)

    def start(self):
        chips = self.line.chips
        order = []
        for k in range((chips + 1) // 2):
            order += [chips - 1 - k, k]
        for j in order[:chips]:
            self.to_sibling(j).start()
            self.to_own(j).start()

    def ready(self, j):
        self.to_sibling(j).wait_recv()
        self.to_own(j).wait()

    def rows_of(self, p, body):
        def shifted(r):
            body(pl.ds(pl.multiple_of(r.start + p * self.size, 16), r.size))

        by_rows(self.size, 16, shifted)

    def pass_on(self, way, j, first):
        self.ready(j)
        for p in range(SUMS):

            @pl.when(first)
            def _(p=p):
                def body(r):
                    total = self.own[j, r, :].astype(F32) + self.sib[j, r, :].astype(F32)
                    self.out[j, r, :] = total.astype(BF16)

                self.rows_of(p, body)

            @pl.when(jnp.logical_not(first))
            def _(p=p):
                self.along(way, j, p).wait_recv()

                def body(r):
                    total = self.own[j, r, :].astype(F32) + self.sib[j, r, :].astype(F32)
                    total += self.inn[way, j, r, :].astype(F32)
                    self.out[j, r, :] = total.astype(BF16)

                self.rows_of(p, body)

            self.along(way, j, p).start()

    def step(self, tau):
        line = self.line

        @pl.when((line.i <= tau) & line.has_right)
        def _():
            self.pass_on(0, line.chips - 1 - tau + line.i, line.i == 0)

        @pl.when((line.chips - 1 - line.i <= tau) & line.has_left)
        def _():
            self.pass_on(1, tau - (line.chips - 1 - line.i), line.i == line.chips - 1)

    def total(self, consume):
        line, i = self.line, self.line.i
        self.ready(i)
        for p in range(SUMS):

            @pl.when(line.has_left)
            def _(p=p):
                self.along(0, i, p).wait_recv()

            @pl.when(line.has_right)
            def _(p=p):
                self.along(1, i, p).wait_recv()

        rows = self.own.shape[1]

        def add(r, with_left, with_right):
            total = self.own[i, r, :].astype(F32) + self.sib[i, r, :].astype(F32)
            if with_left:
                total += self.inn[0, i, r, :].astype(F32)
            if with_right:
                total += self.inn[1, i, r, :].astype(F32)
            consume(r, total)

        @pl.when(line.has_left & line.has_right)
        def _():
            by_rows(rows, 16, lambda r: add(r, True, True))

        @pl.when(line.has_left & jnp.logical_not(line.has_right))
        def _():
            by_rows(rows, 16, lambda r: add(r, True, False))

        @pl.when(line.has_right & jnp.logical_not(line.has_left))
        def _():
            by_rows(rows, 16, lambda r: add(r, False, True))

    def finish(self):
        line = self.line
        for j in range(line.chips):
            self.to_sibling(j).wait_send()
            for p in range(SUMS):

                @pl.when(j > line.i)
                def _(j=j, p=p):
                    self.along(0, j, p).wait_send()

                @pl.when(j < line.i)
                def _(j=j, p=p):
                    self.along(1, j, p).wait_send()


PIECES = 2


def gather_sems(chips):
    return pltpu.SemaphoreType.DMA((7, chips, PIECES))


def scatter_bufs(chips, rows, width):
    return [
        pltpu.VMEM((chips, rows, width), BF16),
        pltpu.VMEM((chips, rows, width), BF16),
        pltpu.VMEM((2, chips, rows, width), BF16),
        pltpu.VMEM((chips, rows, width), BF16),
        pltpu.SemaphoreType.DMA((7, chips, SUMS)),
    ]


ANYWHERE = pl.BlockSpec(memory_space=pl.ANY)
IN_VMEM = pl.BlockSpec(memory_space=pltpu.VMEM)


def params(collective_id):
    return pltpu.CompilerParams(
        collective_id=collective_id, has_side_effects=True, vmem_limit_bytes=56 * 2**20
    )


def comm_cost(byte_count):
    return pl.CostEstimate(flops=0, transcendentals=0, bytes_accessed=40 * byte_count)


class Exchange:
    def __init__(self, axis, size):
        self.axis, self.size = axis, size
        self.me = lax.axis_index(axis)

    def peer(self, k):
        return lax.rem(self.me + k, self.size)

    def greet(self, barrier):
        for k in range(1, self.size):
            signal_to(barrier, {self.axis: self.peer(k)})

    def copy(self, k, src, dst, sems):
        return pltpu.make_async_remote_copy(
            src_ref=src,
            dst_ref=dst,
            send_sem=sems.at[0, k],
            recv_sem=sems.at[1, k],
            device_id={self.axis: self.peer(k)},
            device_id_type=MESH,
        )

    def sems(self):
        return pltpu.SemaphoreType.DMA((2, self.size))


def pair_sems(size):
    return pltpu.SemaphoreType.DMA((2, size))


def greet_all(exchanges, line=None, moves=None):
    barrier = pltpu.get_barrier_semaphore()
    count = 0
    for exchange in exchanges:
        exchange.greet(barrier)
        count += exchange.size - 1
    if line is not None:
        count += line.greet(barrier)
    if moves is not None:
        whether, source = moves

        @pl.when(whether)
        def _():
            signal_to(barrier, source)

        count += whether.astype(jnp.int32)
    pl.semaphore_wait(barrier, count)


def flip_copy(src, dst, bit, sems, *index):
    return pltpu.make_async_remote_copy(
        src_ref=src,
        dst_ref=dst,
        send_sem=sems.at[(0, *index)],
        recv_sem=sems.at[(1, *index)],
        device_id={"head": lax.axis_index("head") ^ (1 << bit)},
        device_id_type=MESH,
    )


def ff_entries(rows, n_head):
    bits = tuple(range(n_head.bit_length() - 1))
    back, half = bits[::-1], rows // 2
    return (
        (0, pl.ds(0, rows), bits),
        (1, pl.ds(0, rows), back),
        (2, pl.ds(0, half), bits),
        (2, pl.ds(half, half), back),
    )


def place_of_out_rows(n_head, n_blk):
    h, b = lax.axis_index("head"), lax.axis_index("blk")
    d = h * n_blk + b
    source = b * n_head + h
    return (d % n_head, d // n_head), (source // n_blk, source % n_blk)


PACK_ROWS = 24


def weight_pieces(b, q_cols, copies):
    kv = b // copies * HEAD_DIM
    return (
        (0, pl.ds(pl.multiple_of(b * q_cols, HEAD_DIM), q_cols), pl.ds(0, q_cols)),
        (1, pl.ds(pl.multiple_of(kv, HEAD_DIM), HEAD_DIM), pl.ds(q_cols, HEAD_DIM)),
        (2, pl.ds(pl.multiple_of(kv, HEAD_DIM), HEAD_DIM), pl.ds(q_cols + HEAD_DIM, HEAD_DIM)),
    )


PACK_ROWS = 24


def weight_pieces(b, q_cols, copies):
    kv = b // copies * HEAD_DIM
    return (
        (0, pl.ds(pl.multiple_of(b * q_cols, HEAD_DIM), q_cols), pl.ds(0, q_cols)),
        (1, pl.ds(pl.multiple_of(kv, HEAD_DIM), HEAD_DIM), pl.ds(q_cols, HEAD_DIM)),
        (2, pl.ds(pl.multiple_of(kv, HEAD_DIM), HEAD_DIM), pl.ds(q_cols + HEAD_DIM, HEAD_DIM)),
    )


class Spread:
    def __init__(self, full, entries, n_head, sems):
        self.full, self.entries, self.n_head, self.sems = full, entries, n_head, sems

    def copies(self, e, level):
        weight, part, order = self.entries[e]
        full = self.full[weight]
        bit = order[level]
        keys = [0]
        for low in order[:level]:
            keys += [key ^ (1 << low) for key in keys]
        for key in keys:
            there = key ^ (1 << bit)
            yield flip_copy(
                full.at[key, part], full.at[there, part], bit, self.sems, e, there
            )

    def level(self, level):
        for e in range(len(self.entries)):
            if level > 1:
                for copy in self.copies(e, level - 1):
                    copy.wait_recv()
            for copy in self.copies(e, level):
                copy.start()

    def start(self):
        self.level(1)

    def finish(self):
        levels = self.n_head.bit_length() - 1
        for level in range(2, levels):
            self.level(level)
        for e in range(len(self.entries)):
            for level in range(1, levels):
                for copy in self.copies(e, level):
                    copy.wait_send()
                    if level == levels - 1:
                        copy.wait_recv()

    @staticmethod
    def sem_shape(n_head):
        return pltpu.SemaphoreType.DMA((2, 4, n_head))


class Collect:
    def __init__(self, have, kept, inbox, total, entries, n_head, sems):
        self.have, self.kept, self.inbox, self.total = have, kept, inbox, total
        self.entries, self.n_head, self.sems = entries, n_head, sems

    def keys(self, order, level):
        keys = [0]
        for low in order[: len(order) - 1 - level]:
            keys += [key ^ (1 << low) for key in keys]
        return keys

    def slot(self, order, key):
        return self.keys(order, 0).index(key)

    def copies(self, e, level):
        weight, part, order = self.entries[e]
        bit = order[len(order) - 1 - level]
        for key in self.keys(order, level):
            slot = self.slot(order, key)
            if level == 0:
                src = self.have[weight].at[key ^ (1 << bit), part]
            else:
                src = self.kept[weight].at[self.slot(order, key ^ (1 << bit)), part]
            yield flip_copy(src, self.inbox[weight].at[level, slot, part], bit, self.sems, e, level, slot)

    def locals_(self):
        for e, (weight, part, order) in enumerate(self.entries):
            for key in self.keys(order, 0):
                slot = self.slot(order, key)
                yield pltpu.make_async_copy(
                    self.have[weight].at[key, part],
                    self.kept[weight].at[slot, part],
                    self.sems.at[2, e, 0, slot],
                )

    def start(self):
        for copy in self.locals_():
            copy.start()
        for e in range(len(self.entries)):
            for copy in self.copies(e, 0):
                copy.start()

    def finish(self):
        for copy in self.locals_():
            copy.wait()
        levels = self.n_head.bit_length() - 2
        for level in range(levels):
            last = level == levels - 1
            for e, (weight, part, order) in enumerate(self.entries):
                for copy in self.copies(e, level):
                    copy.wait_recv()
                for at, key in enumerate(self.keys(order, level)):
                    slot = self.slot(order, key)
                    kept, inbox = self.kept[weight], self.inbox[weight]
                    into = self.total[weight] if last else kept
                    where = at if last else slot

                    def body(r, part=part, slot=slot, kept=kept, inbox=inbox, into=into, where=where):
                        r = pl.ds(pl.multiple_of(r.start + part.start, 16), r.size)
                        value = kept[slot, r, :].astype(F32) + inbox[level, slot, r, :].astype(F32)
                        into[where, r, :] = value.astype(BF16)

                    by_rows(part.size, 16, body)
            for e in range(len(self.entries)):
                if not last:
                    for copy in self.copies(e, level + 1):
                        copy.start()
        for level in range(levels):
            for e in range(len(self.entries)):
                for copy in self.copies(e, level):
                    copy.wait_send()

    @staticmethod
    def sem_shape(n_head):
        levels = n_head.bit_length() - 2
        return pltpu.SemaphoreType.DMA((3, 4, levels, n_head // 2))


def last_scatter(
    partial_rows, w_grad, out_grad, pack, sums, hidden, gain, q_cols, copies, n_head, n_blk, collective_id
):
    total_rows, width = partial_rows.shape
    chips, count = n_blk // 2, total_rows // n_blk
    _, _, rows_here, columns = w_grad.shape
    n_sums = len(sums)
    entries = ff_entries(sums[0].shape[1], n_head) if sums else ()

    def kernel(part, w_src, o_src, g_src, *refs):
        ff_src, (x_ref, gain_ref), refs = refs[:n_sums], refs[n_sums : n_sums + 2], refs[n_sums + 2 :]
        out, wq_out, wk_out, wv_out, o_out, g_out = refs[:6]
        ff_out, refs = refs[6 : 6 + n_sums], refs[6 + n_sums :]
        bufs, sems = refs[:4], refs[4]
        w_in, w_sum, o_in, o_sum, g_in, g_sum, g_last = refs[5:12]
        w_sems, block_sems, o_sems, g_sems, pack_sems, moved, ff_sems, local = refs[12:]
        line = Line(n_blk)
        across, along = Exchange("head", n_head), Exchange("blk", n_blk)
        h, b = across.me, along.me
        (sh, sb), (th, tb) = place_of_out_rows(n_head, n_blk)
        stays = (th == h) & (tb == b)
        moves = jnp.logical_not(stays)
        greet_all((across, along), moves=(moves, {"head": sh, "blk": sb}))

        def w_copy(k):
            return across.copy(k, w_src.at[across.peer(k)], w_in.at[k], w_sems)

        def o_copy(k):
            return across.copy(k, o_src.at[across.peer(k)], o_in.at[k], o_sems)

        lanes = n_blk * rows_here

        def g_part(head):
            return g_src.at[:, pl.ds(pl.multiple_of(head * lanes, 128), lanes)]

        def g_copy(k):
            return across.copy(k, g_part(across.peer(k)), g_in.at[k], g_sems)

        def landings():
            kv = pl.ds(pl.multiple_of(b // copies * HEAD_DIM, HEAD_DIM), HEAD_DIM)
            return (
                wq_out.at[:, pl.ds(pl.multiple_of(b * q_cols, HEAD_DIM), q_cols)],
                wk_out.at[b % copies, :, kv],
                wv_out.at[b % copies, :, kv],
            )

        spans = (
            pl.ds(0, q_cols),
            pl.ds(q_cols, HEAD_DIM),
            pl.ds(q_cols + HEAD_DIM, HEAD_DIM),
        )

        def block_copies(k):
            for w, there in enumerate(landings()):
                yield along.copy(
                    k, w_sum.at[along.peer(k), :, spans[w]], there, block_sems.at[w]
                )

        def pack_copy(k):
            tile = along.peer(k) * rows_here // 128 * 128
            part = g_sum.at[:, pl.ds(pl.multiple_of(tile, 128), 128)]
            return along.copy(k, part, g_last.at[b], pack_sems)

        move_out = pltpu.make_async_remote_copy(
            src_ref=o_sum,
            dst_ref=o_out,
            send_sem=moved.at[0],
            recv_sem=moved.at[1],
            device_id={"head": th, "blk": tb},
            device_id_type=MESH,
        )
        keep_out = pltpu.make_async_copy(o_sum, o_out, moved.at[2])

        def hop(e):
            weight, part, order = entries[e]
            return flip_copy(
                ff_src[weight].at[1, part], ff_out[weight].at[part], order[0], ff_sems, e
            )

        own_w = pltpu.make_async_copy(w_src.at[h], w_in.at[0], local.at[0])
        own_g = pltpu.make_async_copy(g_part(h), g_in.at[0], local.at[1])
        own_blocks = [
            pltpu.make_async_copy(w_sum.at[b, :, spans[w]], there, local.at[4 + w])
            for w, there in enumerate(landings())
        ]
        own_o = pltpu.make_async_copy(o_src.at[h], o_in.at[0], local.at[3])
        scatter = Scatter(line, part, bufs, sems)
        scatter.start()
        own_w.start()
        own_g.start()
        own_o.start()
        for k in range(1, n_head):
            g_copy(k).start()
            w_copy(k).start()
        for k in range(1, n_head):
            o_copy(k).start()
        for e in range(len(entries)):
            hop(e).start()
        scatter.step(0)
        own_g.wait()
        for k in range(1, n_head):
            g_copy(k).wait_recv()
        g_sum[...] = sum(g_in[k] for k in range(n_head))
        own_tile = b * rows_here // 128 * 128
        g_last[b] = g_sum[:, pl.ds(pl.multiple_of(own_tile, 128), 128)]
        for k in range(1, n_blk):
            pack_copy(k).start()
        for tau in range(1, chips - 2):
            scatter.step(tau)
        own_w.wait()
        for k in range(1, n_head):
            w_copy(k).wait_recv()

        def add(j, carry):
            total = w_in[0, j].astype(F32)
            for k in range(1, n_head):
                total += w_in[k, j].astype(F32)
            w_sum[j] = total.astype(BF16)
            return carry

        lax.fori_loop(0, n_blk, add, 0)
        for one in own_blocks:
            one.start()
        for k in range(1, n_blk):
            for copy in block_copies(k):
                copy.start()

        scatter.step(chips - 2)
        own_o.wait()
        for k in range(1, n_head):
            o_copy(k).wait_recv()

        def add_out(r):
            total = o_in[0, r, :].astype(F32)
            for k in range(1, n_head):
                total += o_in[k, r, :].astype(F32)
            o_sum[r, :] = total.astype(BF16)

        by_rows(rows_here, 16, add_out)

        @pl.when(stays)
        def _():
            keep_out.start()

        @pl.when(jnp.logical_not(stays))
        def _():
            move_out.start()

        def consume(r, dxn):
            unit, factor = unit_of(x_ref[r, :].astype(F32))
            out[r, :] = unit_back(dxn * gain_ref[0:1, :], unit, factor)

        scatter.total(consume)
        for k in range(1, n_blk):
            pack_copy(k).wait_recv()
        g_out[...] = sum(g_last[k] for k in range(n_blk))
        scatter.finish()
        for one in own_blocks:
            one.wait()
        for k in range(1, n_head):
            g_copy(k).wait_send()
            o_copy(k).wait_send()
            w_copy(k).wait_send()
        for k in range(1, n_blk):
            pack_copy(k).wait_send()
            for copy in block_copies(k):
                copy.wait()
        for e in range(len(entries)):
            hop(e).wait()

        @pl.when(stays)
        def _():
            keep_out.wait()

        @pl.when(jnp.logical_not(stays))
        def _():
            move_out.wait()

    return pl.pallas_call(
        kernel,
        out_shape=(
            jax.ShapeDtypeStruct((count, width), F32),
            jax.ShapeDtypeStruct((rows_here, n_blk * q_cols), BF16),
            *[jax.ShapeDtypeStruct((copies, rows_here, n_blk // copies * HEAD_DIM), BF16)] * 2,
            jax.ShapeDtypeStruct((rows_here, width), BF16),
            jax.ShapeDtypeStruct((pack.shape[0], 128), F32),
            *(jax.ShapeDtypeStruct(one.shape[1:], BF16) for one in sums),
        ),
        in_specs=[ANYWHERE] * (4 + n_sums) + [IN_VMEM] * 2,
        out_specs=[IN_VMEM] + [ANYWHERE] * 4 + [IN_VMEM] + [ANYWHERE] * n_sums,
        scratch_shapes=[
            *scatter_bufs(chips, count, width),
            pltpu.VMEM((n_head, n_blk, rows_here, columns), BF16),
            pltpu.VMEM((n_blk, rows_here, columns), BF16),
            pltpu.VMEM((n_head, rows_here, width), BF16),
            pltpu.VMEM((rows_here, width), BF16),
            pltpu.VMEM((n_head, pack.shape[0], n_blk * rows_here), F32),
            pltpu.VMEM((pack.shape[0], n_blk * rows_here), F32),
            pltpu.VMEM((n_blk, pack.shape[0], 128), F32),
            pair_sems(n_head),
            pltpu.SemaphoreType.DMA((3, 2, n_blk)),
            pair_sems(n_head),
            pair_sems(n_head),
            pair_sems(n_blk),
            pltpu.SemaphoreType.DMA((3,)),
            pair_sems(max(1, len(entries))),
            pltpu.SemaphoreType.DMA((7,)),
        ],
        compiler_params=params(collective_id),
        cost_estimate=comm_cost(total_rows * width),
        name="last_scatter",
    )(
        partial_rows.astype(BF16).reshape(chips, 2, count, width),
        w_grad,
        out_grad.reshape(n_head, rows_here, width),
        pack,
        *sums,
        hidden,
        gain,
    )


ROWS = 256
CHUNKS = 2


def block_of(k, size=ROWS):
    return pl.ds(pl.multiple_of(k * size, size), size)


class View:
    def __init__(self, ref, rows):
        self.ref, self.rows = ref, rows
        self.at = self

    def __getitem__(self, index):
        if len(index) == 3:
            j, core, inner = index
            return self.ref.at[j, core, pl.ds(self.rows.start + inner.start, inner.size)]
        j, core = index
        return self.ref.at[j, core, self.rows]


def scatter_gather(
    partial_rows, prepare, between, inputs, outputs, beside, n_head, n_blk, collective_id
):
    total_rows, width = partial_rows.shape
    chips, count = n_blk // 2, total_rows // n_blk
    size = count // CHUNKS
    operands, results, result_specs, more_scratch, aliases, make = beside
    n_in, n_out, n_op, n_res = len(inputs), len(outputs), len(operands), len(results)

    def kernel(part, *refs):
        refs = list(refs)

        def take(n):
            taken = refs[:n]
            del refs[:n]
            return taken

        ins, ops, outs = take(n_in), take(n_op), take(n_out)
        (gathered,) = take(1)
        ress = take(n_res)
        (made,) = take(1)
        chunk_scratch = [take(6) for _ in range(CHUNKS)]
        line = Line(n_blk)
        across = Exchange("head", n_head)
        greet_all((across,), line)
        prepare(outs)
        other = make(ops, ress, refs)
        scatters, gathers = [], []
        for q in range(CHUNKS):
            own, sib, inn, outgoing, sems, g_sems = chunk_scratch[q]
            rows = pl.ds(q * size, size)
            scatters.append(Scatter(line, View(part, rows), (own, sib, inn, outgoing), sems))
            gathers.append(Gather(line, made.at[rows], View(gathered, rows), g_sems))

        def turn(q):
            def consume(r, value):
                r = pl.ds(pl.multiple_of(r.start + q * size, 16), r.size)
                made[r, :] = between(r, value, ins, outs).astype(BF16)

            scatters[q].total(consume)
            gathers[q].start()

        scatters[0].start()
        other.start()
        for q in range(1, CHUNKS):
            scatters[q].start()
        for q in range(CHUNKS):
            for tau in range(chips - 1):
                scatters[q].step(tau)
                if q:
                    gathers[q - 1].step(tau + 1)
            turn(q)
        for s in range(1, chips):
            gathers[-1].step(s)
        for q in range(CHUNKS):
            scatters[q].finish()
            gathers[q].finish()
        other.finish()

    per_chunk = []
    for _ in range(CHUNKS):
        per_chunk += [*scatter_bufs(chips, size, width), gather_sems(chips)]
    given = pl.pallas_call(
        kernel,
        out_shape=(
            *outputs,
            jax.ShapeDtypeStruct((chips, 2, count, width), BF16),
            *results,
        ),
        in_specs=[ANYWHERE] + [IN_VMEM] * n_in + [ANYWHERE] * n_op,
        out_specs=[IN_VMEM] * n_out + [ANYWHERE] + list(result_specs),
        scratch_shapes=[pltpu.VMEM((count, width), BF16), *per_chunk, *more_scratch],
        input_output_aliases={1 + n_in + i: n_out + 1 + o for i, o in aliases.items()},
        compiler_params=params(collective_id),
        cost_estimate=comm_cost(2 * total_rows * width),
        name="scatter_gather",
    )(partial_rows.astype(BF16).reshape(chips, 2, count, width), *inputs, *operands)
    return (
        *given[:n_out],
        given[n_out].reshape(total_rows, width),
        *given[n_out + 1 :],
    )


def spread_beside(full, n_head):
    entries = ff_entries(full[0].shape[1], n_head)

    def make(ops, ress, scratch):
        return Spread(ress, entries, n_head, scratch[0])

    return (
        tuple(full),
        tuple(jax.ShapeDtypeStruct(w.shape, w.dtype) for w in full),
        [ANYWHERE] * 3,
        [Spread.sem_shape(n_head)],
        {0: 0, 1: 1, 2: 2},
        make,
    )


def collect_beside(have, carried, n_head):
    entries = ff_entries(have[0].shape[1], n_head)
    levels = n_head.bit_length() - 2
    shapes = [(n_head // 2, *one.shape[1:]) for one in have]

    def make(ops, ress, scratch):
        kept, inbox = scratch[0:3], scratch[3:6]
        return Collect(ops[:3], kept, inbox, ress[:3], entries, n_head, scratch[6])

    return (
        (*have, carried),
        (
            *(jax.ShapeDtypeStruct((2, *one.shape[1:]), BF16) for one in have),
            jax.ShapeDtypeStruct(carried.shape, carried.dtype),
        ),
        [IN_VMEM] * 3 + [ANYWHERE],
        [
            *(pltpu.VMEM(shape, BF16) for shape in shapes),
            *(pltpu.VMEM((levels, *shape), BF16) for shape in shapes),
            Collect.sem_shape(n_head),
        ],
        {3: 3},
        make,
    )


class Rows:
    def __init__(self, ref, q, size, chips):
        self.ref, self.base, self.size = ref, q * size * chips * 2, size
        self.at = self

    def rows(self, j, core, start=0, count=None):
        first = self.base + (j * 2 + core) * self.size + start
        return pl.ds(pl.multiple_of(first, 16), count or self.size)

    def __getitem__(self, index):
        j, core, *inner = index
        if inner:
            return self.ref.at[self.rows(j, core, inner[0].start, inner[0].size)]
        return self.ref.at[self.rows(j, core)]


class OwnRows:
    def __init__(self, rows, core):
        self.view, self.core = rows, core
        self.shape = (0, rows.size)

    def __getitem__(self, index):
        j, r, _ = index
        return self.view.ref[self.view.rows(j, self.core, r.start, r.size), :]


class LocalScatter(Scatter):
    def __init__(self, line, part, bufs, sems):
        super().__init__(line, part, (OwnRows(part, line.c), *bufs), sems)

    def start(self):
        chips = self.line.chips
        order = []
        for k in range((chips + 1) // 2):
            order += [chips - 1 - k, k]
        for j in order[:chips]:
            self.to_sibling(j).start()

    def ready(self, j):
        self.to_sibling(j).wait_recv()


def turned(values, cosine, sine):
    return values * cosine + pltpu.roll(values, HEAD_DIM // 2, 1) * sine


def local_params(collective_id):
    if collective_id is None:
        return pltpu.CompilerParams(vmem_limit_bytes=60 * 2**20)
    return pltpu.CompilerParams(
        collective_id=collective_id, has_side_effects=True, vmem_limit_bytes=60 * 2**20
    )


def spec_of(shape, dtype):
    return jax.ShapeDtypeStruct(shape, dtype)


def attention_forward(
    rows, weights, small, w_out, ids, cot, ff, q_cols, copies, n_head, n_blk, collective_id
):
    count, width = rows.shape
    chips, pack = n_blk // 2, n_blk * count
    rows_here, rows_ff = w_out.shape[0], ff[0].shape[0]
    entries = ff_entries(rows_ff, n_head)
    columns, q_here = q_cols + 2 * HEAD_DIM, q_cols // HEAD_DIM
    together, n_all = 128 // rows_here, n_head * n_blk
    blocks = pack // ROWS
    scale = 1.0 / math.sqrt(HEAD_DIM)

    def kernel(src, cot_ref, *refs):
        w_src, (pack_src, out_src), ff_src = refs[:3], refs[3:5], refs[5:8]
        pos, seg, blk_ids = refs[8:11]
        part_hbm, xn_hbm, p_hbm, cot_hbm = refs[11:15]
        ff_out, refs = refs[15:18], refs[18:]
        w_ref, vec_ref, gate_ref, cos_ref, sin_ref = refs[:5]
        lin_ref, q_ref, k_ref, v_ref, sig_ref, o_ref, gated_ref, o_rows = refs[5:13]
        x_s, xn_s, p_s, low_ref, code_ref, key_ref, g_all, xn_sem, p_sem, part_sem = refs[13:23]
        sems, block_sems, w_sems, pack_sems, g_sems, moved, local = refs[23:30]
        cot_sems, out_sems, ff_sems = refs[30:]
        line = Line(n_blk)
        across, along = Exchange("head", n_head), Exchange("blk", n_blk)
        h, b = across.me, along.me
        h_me, b_me = h, b
        (th, tb), (sh, sb) = place_of_out_rows(n_head, n_blk)
        stays = (th == h) & (tb == b)
        moves = jnp.logical_not(stays)
        greet_all((across, along), moves=(moves, {"head": sh, "blk": sb}))

        def at_rows(head, blk):
            first = (head * n_blk + blk) * rows_here
            return pl.ds(pl.multiple_of(first, rows_here), rows_here)

        def of_head(head):
            size = n_blk * rows_here
            return pl.ds(pl.multiple_of(head * size, size), size)

        def out_rows_of(head):
            return o_rows.at[pl.ds(pl.multiple_of(head * rows_here, rows_here), rows_here)]

        def block_copies(k):
            for w, there, here in weight_pieces(along.peer(k), q_cols, copies):
                yield along.copy(
                    k, w_src[w].at[:, there], w_ref.at[at_rows(h, b), here], block_sems.at[w]
                )

        def pack_copy(k):
            return along.copy(k, pack_src, g_all.at[h, b], pack_sems)

        def w_copy(k):
            return across.copy(k, w_ref.at[of_head(h)], w_ref.at[of_head(h)], w_sems)

        def g_copy(k):
            return across.copy(k, g_all.at[h], g_all.at[h], g_sems)

        def out_copy(k):
            return across.copy(k, out_rows_of(h), out_rows_of(h), out_sems)

        def hop(e):
            weight, part, order = entries[e]
            return flip_copy(
                ff_src[weight].at[part], ff_out[weight].at[part], order[0], ff_sems, e
            )

        move_out = pltpu.make_async_remote_copy(
            src_ref=out_src,
            dst_ref=out_rows_of(th),
            send_sem=moved.at[0],
            recv_sem=moved.at[1],
            device_id={"head": th, "blk": tb},
            device_id_type=MESH,
        )
        keep_out = pltpu.make_async_copy(out_src, out_rows_of(h), moved.at[2])
        locals_ = [
            pltpu.make_async_copy(
                w_src[w].at[:, there], w_ref.at[at_rows(h, b), here], local.at[w]
            )
            for w, there, here in weight_pieces(b, q_cols, copies)
        ] + [pltpu.make_async_copy(pack_src, g_all.at[h, b], local.at[3])]
        for k in range(1, n_blk):
            for copy in block_copies(k):
                copy.start()
        tokens = Gather(line, src, Rows(x_s, 0, count, chips), sems)
        gather = Gather(line, cot_ref, cot_hbm, cot_sems)
        for k in range(1, n_blk):
            pack_copy(k).start()
        for one in locals_:
            one.start()

        @pl.when(stays)
        def _():
            keep_out.start()

        @pl.when(moves)
        def _():
            move_out.start()

        for e in (2, 3):
            hop(e).start()
        half = HEAD_DIM // 2
        index = lax.broadcasted_iota(jnp.int32, (half, ROWS), 0).astype(F32)
        frequency = jnp.exp(index * (-2.0 * math.log(ROPE_BASE) / HEAD_DIM))
        key_ref[...] = (seg[...] * pack + blk_ids[...]).astype(F32)

        def tables(n, carry):
            r = block_of(n)
            angles = frequency * pos[:, r].astype(F32)
            cosine, sine = jnp.cos(angles), jnp.sin(angles)
            cos_ref[r, :] = jnp.concatenate([cosine, cosine], axis=0).T
            sin_ref[r, :] = jnp.concatenate([-sine, sine], axis=0).T
            low_ref[r, :] = jnp.broadcast_to((seg[:, r] * pack).astype(F32), (128, ROWS)).T
            code_ref[r, :] = jnp.broadcast_to(key_ref[:, r], (128, ROWS)).T
            return carry

        lax.fori_loop(0, pack // ROWS, tables, 0)
        for one in locals_:
            one.wait()
        for k in range(1, n_blk):
            pack_copy(k).wait_recv()
        for k in range(1, n_head):
            g_copy(k).start()
        for k in range(1, n_blk):
            for copy in block_copies(k):
                copy.wait_recv()
        tokens.start()
        for k in range(1, n_head):
            w_copy(k).start()

        @pl.when(stays)
        def _():
            keep_out.wait()

        @pl.when(moves)
        def _():
            move_out.wait_recv()

        for k in range(1, n_head):
            out_copy(k).start()
        for s in range(1, chips):
            tokens.step(s)
        gather.start()
        for e in (0, 1):
            hop(e).start()
        for k in range(1, n_head):
            g_copy(k).wait()
        everyone = [g_all.at[d // n_blk, d % n_blk] for d in range(n_all)]
        vec_ref[...] = jnp.zeros_like(vec_ref)
        for t in range(width // 128):
            tile = sum(one[...] for one in everyone[t * together : (t + 1) * together])
            vec_ref[0:2, t * 128 : (t + 1) * 128] = tile[0:2]
            gate_ref[:, t * 128 : (t + 1) * 128] = tile[8:].astype(BF16)
        vec_ref[2:4, 0:128] = sum(one[2:4, :] for one in everyone)
        tokens.finish()
        for k in range(1, n_head):
            w_copy(k).wait()

        def xn_store(n):
            return pltpu.make_async_copy(
                xn_s.at[block_of(n)], xn_hbm.at[block_of(n)], xn_sem.at[n]
            )

        def p_store(h, n):
            return pltpu.make_async_copy(
                p_s.at[h, block_of(n)], p_hbm.at[h, block_of(n)], p_sem.at[h, n]
            )

        def part_store(n):
            return pltpu.make_async_copy(
                x_s.at[block_of(n)], part_hbm.at[block_of(n)], part_sem.at[n]
            )

        def project(n, carry):
            r = block_of(n)
            unit, _ = unit_of(x_s[r, :].astype(F32))
            xn = (unit * vec_ref[0:1, :]).astype(BF16)
            xn_s[r, :] = xn
            xn_store(n).start()
            lin = mm(xn, w_ref[...])
            lin_ref[r, :] = lin
            gate = mm_nt(xn, gate_ref[...])
            one_of = lax.broadcasted_iota(jnp.int32, (ROWS, HEADS), 1)
            lane = lax.broadcasted_iota(jnp.int32, (ROWS, GATE_PAD), 1)
            sigs = jnp.zeros((ROWS, GATE_PAD), F32)
            for h in range(q_here):
                own = jnp.where(one_of == b_me * q_here + h, gate, 0.0)
                own = jax.nn.sigmoid(jnp.sum(own, axis=1, keepdims=True))
                sigs = jnp.where(lane == h, own, sigs)
            sig_ref[r, :] = sigs
            cosine, sine = cos_ref[r, :], sin_ref[r, :]
            for h in range(q_here):
                at = slice(h * HEAD_DIM, (h + 1) * HEAD_DIM)
                unit_q, _ = unit_of(lin[:, at])
                q_ref[r, at] = turned(unit_q * vec_ref[2:3, :HEAD_DIM], cosine, sine).astype(BF16)
            unit_k, _ = unit_of(lin[:, q_cols : q_cols + HEAD_DIM])
            k_ref[r, :] = turned(unit_k * vec_ref[3:4, :HEAD_DIM], cosine, sine).astype(BF16)
            v_ref[r, :] = lin[:, q_cols + HEAD_DIM :].astype(BF16)
            return carry

        lax.fori_loop(0, blocks, project, 0)
        gather.step(1)
        for k in range(1, n_head):
            out_copy(k).wait_recv()

        def attend(n, carry):
            r = block_of(n)
            visible = (key_ref[...] >= low_ref[r, 0:1]) & (key_ref[...] <= code_ref[r, 0:1])
            for h in range(q_here):
                at = slice(h * HEAD_DIM, (h + 1) * HEAD_DIM)
                scores = mm_nt(q_ref[r, at], k_ref[...]) * scale
                scores = jnp.where(visible, scores, MASKED)
                top = jnp.max(scores, axis=-1, keepdims=True)
                weights = jnp.exp(scores - top)
                weights = weights * (1.0 / jnp.sum(weights, axis=-1, keepdims=True))
                prob = weights.astype(BF16)
                p_s[h, r, :] = prob
                p_store(h, n).start()
                out = mm(prob, v_ref[...]).astype(BF16)
                o_ref[r, at] = out
                gated_ref[r, at] = (out.astype(F32) * sig_ref[r, h : h + 1]).astype(BF16)
            x_s[r, :] = mm(gated_ref[r, :], o_rows[...]).astype(BF16)
            part_store(n).start()
            return carry

        lax.fori_loop(0, blocks - 1, attend, 0)
        gather.step(2)
        lax.fori_loop(blocks - 1, blocks, attend, 0)
        for s in range(3, chips):
            gather.step(s)
        gather.finish()
        for k in range(1, n_head):
            out_copy(k).wait_send()
        for e in range(len(entries)):
            hop(e).wait()
        for k in range(1, n_blk):
            pack_copy(k).wait_send()
            for copy in block_copies(k):
                copy.wait_send()

        @pl.when(moves)
        def _():
            move_out.wait_send()

        for n in range(blocks):
            xn_store(n).wait()
            part_store(n).wait()
            for h in range(q_here):
                p_store(h, n).wait()

    dma = pltpu.SemaphoreType.DMA
    return pl.pallas_call(
        kernel,
        out_shape=(
            spec_of((pack, width), BF16),
            spec_of((pack, width), BF16),
            spec_of((q_here, pack, pack), BF16),
            spec_of((chips, 2, *cot.shape), BF16),
            *(spec_of(w.shape, BF16) for w in ff),
            spec_of((width, columns), BF16),
            spec_of((8, width), F32),
            spec_of((HEADS, width), BF16),
            spec_of((pack, HEAD_DIM), F32),
            spec_of((pack, HEAD_DIM), F32),
            spec_of((pack, columns), F32),
            spec_of((pack, q_cols), BF16),
            spec_of((pack, HEAD_DIM), BF16),
            spec_of((pack, HEAD_DIM), BF16),
            spec_of((pack, GATE_PAD), F32),
            spec_of((pack, q_cols), BF16),
            spec_of((pack, q_cols), BF16),
            spec_of((q_cols, width), BF16),
        ),
        in_specs=[IN_VMEM] * 2 + [ANYWHERE] * 8 + [IN_VMEM] * 3,
        out_specs=[ANYWHERE] * 7 + [IN_VMEM] * 13,
        scratch_shapes=[
            pltpu.VMEM((pack, width), BF16),
            pltpu.VMEM((pack, width), BF16),
            pltpu.VMEM((q_here, pack, pack), BF16),
            pltpu.VMEM((pack, 128), F32),
            pltpu.VMEM((pack, 128), F32),
            pltpu.VMEM((1, pack), F32),
            pltpu.VMEM((n_head, n_blk, PACK_ROWS, 128), F32),
            dma((blocks,)),
            dma((q_here, blocks)),
            dma((blocks,)),
            gather_sems(chips),
            dma((3, 2, n_blk)),
            pair_sems(n_head),
            pair_sems(n_blk),
            pair_sems(n_head),
            dma((3,)),
            dma((4,)),
            gather_sems(chips),
            pair_sems(n_head),
            pair_sems(len(entries)),
        ],
        compiler_params=local_params(collective_id),
        cost_estimate=comm_cost(pack * width),
        name="attention_forward",
    )(rows, cot, *weights, small, w_out, *ff, *ids)


def attention_backward(
    dy, xn, p, saved, w_attn, vec, gates, tables, mlp_gain_part, q_here, beside=None
):
    pack, width = dy.shape
    columns = w_attn.shape[1]
    q_cols = q_here * HEAD_DIM
    blocks = pack // ROWS
    scale = 1.0 / math.sqrt(HEAD_DIM)

    have, n_head, collective_id = beside or ((), 0, None)
    n_have = len(have)
    sum_scratch = []
    if have:
        entries = ff_entries(have[0].shape[1], n_head)
        sum_scratch = [pair_sems(len(entries))]

    def kernel(dy_hbm, xn_hbm, p_hbm, *refs):
        have_refs, refs = refs[:n_have], refs[n_have:]
        n_plain = 14 + 4
        plain, more = refs[:n_plain], refs[n_plain:]
        got, more = more[:n_have], more[n_have:]
        plain_scratch, sems = more[:14], more[14:]
        if not have:
            return local(dy_hbm, xn_hbm, p_hbm, *plain, *plain_scratch)
        greet_all((Exchange("head", n_head),))
        copies = [
            flip_copy(have_refs[w].at[1, part], got[w].at[part], order[0], sems[0], e)
            for e, (w, part, order) in enumerate(entries)
        ]
        for copy in copies:
            copy.start()
        local(dy_hbm, xn_hbm, p_hbm, *plain, *plain_scratch)
        for copy in copies:
            copy.wait()

    def local(dy_hbm, xn_hbm, p_hbm, lin_ref, q_ref, k_ref, v_ref, sig_ref, o_ref, *refs):
        gated_ref, o_rows, w_ref, vec_ref, gate_ref, cos_ref, sin_ref, mlp_ref = refs[:8]
        dxn_hbm, dw_ref, pack_ref, dout_ref = refs[8:12]
        dy_s, xn_s, p_s, do_s, delta_s, dgate_s, dlin_s, dk_s, dv_s, dgq_s = refs[12:22]
        dy_sem, xn_sem, p_sem, out_sem = refs[22:]
        first_head = lax.axis_index("blk") * q_here

        def dy_load(n):
            return pltpu.make_async_copy(
                dy_hbm.at[block_of(n)], dy_s.at[block_of(n)], dy_sem.at[n]
            )

        def p_load(h, n):
            return pltpu.make_async_copy(
                p_hbm.at[h, block_of(n)], p_s.at[h, block_of(n)], p_sem.at[h, n]
            )

        def dxn_store(n):
            return pltpu.make_async_copy(
                dy_s.at[block_of(n)], dxn_hbm.at[block_of(n)], out_sem.at[n]
            )

        xn_load = pltpu.make_async_copy(xn_hbm, xn_s, xn_sem)
        for n in range(blocks):
            dy_load(n).start()
        for n in range(blocks):
            for h in range(q_here):
                p_load(h, n).start()
        xn_load.start()

        def through_gate(n, carry):
            r = block_of(n)
            dy_load(n).wait()
            dgated = mm_nt(dy_s[r, :], o_rows[...])
            lane = lax.broadcasted_iota(jnp.int32, (ROWS, GATE_PAD), 1)
            dgates = jnp.zeros((ROWS, GATE_PAD), F32)
            deltas = jnp.zeros((ROWS, GATE_PAD), F32)
            for h in range(q_here):
                at = slice(h * HEAD_DIM, (h + 1) * HEAD_DIM)
                sig = sig_ref[r, h : h + 1]
                out = o_ref[r, at].astype(F32)
                do = (dgated[:, at] * sig).astype(BF16)
                do_s[r, at] = do
                dgate = jnp.sum(dgated[:, at] * out, axis=-1, keepdims=True) * sig * (1.0 - sig)
                delta = jnp.sum(do.astype(F32) * out, axis=-1, keepdims=True)
                dgates = jnp.where(lane == first_head + h, dgate, dgates)
                deltas = jnp.where(lane == h, delta, deltas)
            dgate_s[r, :] = dgates.astype(BF16)
            delta_s[r, :] = deltas
            return carry

        lax.fori_loop(0, blocks, through_gate, 0)

        def out_grad(n, carry):
            c = block_of(n)
            dout_ref[:, c] = mm_tn(gated_ref[...], dy_s[:, c]).astype(BF16)
            return carry

        lax.fori_loop(0, width // ROWS, out_grad, 0)
        dk_s[...] = jnp.zeros_like(dk_s)
        dv_s[...] = jnp.zeros_like(dv_s)
        dgq_s[...] = jnp.zeros_like(dgq_s)

        def into_lin(grad, lin, gain, r):
            grad = turned(grad.astype(BF16).astype(F32), cos_ref[r, :], -sin_ref[r, :])
            unit, factor = unit_of(lin)
            return unit_back(grad * gain, unit, factor).astype(BF16), grad * unit

        def attend(n, carry):
            r = block_of(n)
            for h in range(q_here):
                at = slice(h * HEAD_DIM, (h + 1) * HEAD_DIM)
                p_load(h, n).wait()
                do, prob, q = do_s[r, at], p_s[h, r, :], q_ref[r, at]
                dp = mm_nt(do, v_ref[...])
                ds = (prob.astype(F32) * (dp - delta_s[r, h : h + 1])).astype(BF16)
                dq = mm(ds, k_ref[...]) * scale
                dk_s[...] += mm(q.T, ds)
                dv_s[...] += mm(do.T, prob)
                dlin, part = into_lin(dq, lin_ref[r, at], vec_ref[2:3, :HEAD_DIM], r)
                dlin_s[r, at] = dlin
                dgq_s[...] += jnp.sum(part.reshape(ROWS // 8, 8, HEAD_DIM), axis=0)
            return carry

        lax.fori_loop(0, blocks, attend, 0)
        every = pl.ds(0, pack)
        k_cols = slice(q_cols, q_cols + HEAD_DIM)
        dlin, part = into_lin(
            dk_s[...].T * scale, lin_ref[:, k_cols], vec_ref[3:4, :HEAD_DIM], every
        )
        dlin_s[:, k_cols] = dlin
        dgk = jnp.sum(part, axis=0, keepdims=True)
        dgq = jnp.sum(dgq_s[...], axis=0, keepdims=True)
        pack_ref[HEADS:, :] = jnp.zeros((PACK_ROWS - HEADS, width), F32)
        pack_ref[HEADS : HEADS + 1, :] = jnp.sum(mlp_ref[...], axis=0, keepdims=True)
        for t in range(width // HEAD_DIM):
            lanes = slice(t * HEAD_DIM, (t + 1) * HEAD_DIM)
            pack_ref[HEADS + 1 : HEADS + 2, lanes] = dgq
            pack_ref[HEADS + 2 : HEADS + 3, lanes] = dgk
        dlin_s[:, q_cols + HEAD_DIM :] = dv_s[...].T.astype(BF16)

        def into_x(n, carry):
            r = block_of(n)
            dxn = mm_nt(dlin_s[r, :], w_ref[...]) + mm(dgate_s[r, :HEADS], gate_ref[...])
            dy_s[r, :] = dxn.astype(BF16)
            dxn_store(n).start()
            return carry

        lax.fori_loop(0, blocks, into_x, 0)
        xn_load.wait()
        dgate_t = dgate_s[...].astype(F32).T[:HEADS].astype(BF16)

        def weights(n, carry):
            c = block_of(n)
            xn_cols = xn_s[:, c]
            dw_ref[c, :] = mm_tn(xn_cols, dlin_s[...]).astype(BF16)
            pack_ref[:HEADS, c] = mm(dgate_t, xn_cols)
            return carry

        lax.fori_loop(0, width // ROWS, weights, 0)
        for n in range(blocks):
            dxn_store(n).wait()

    return pl.pallas_call(
        kernel,
        out_shape=(
            spec_of((pack, width), BF16),
            spec_of((width, columns), BF16),
            spec_of((PACK_ROWS, width), F32),
            spec_of((q_cols, width), BF16),
            *(spec_of(one.shape[1:], BF16) for one in have),
        ),
        in_specs=[ANYWHERE] * (3 + n_have) + [IN_VMEM] * 14,
        out_specs=[ANYWHERE] + [IN_VMEM] * 3 + [ANYWHERE] * n_have,
        scratch_shapes=[
            pltpu.VMEM((pack, width), BF16),
            pltpu.VMEM((pack, width), BF16),
            pltpu.VMEM((q_here, pack, pack), BF16),
            pltpu.VMEM((pack, q_cols), BF16),
            pltpu.VMEM((pack, GATE_PAD), F32),
            pltpu.VMEM((pack, GATE_PAD), BF16),
            pltpu.VMEM((pack, columns), BF16),
            pltpu.VMEM((HEAD_DIM, pack), F32),
            pltpu.VMEM((HEAD_DIM, pack), F32),
            pltpu.VMEM((8, HEAD_DIM), F32),
            pltpu.SemaphoreType.DMA((blocks,)),
            pltpu.SemaphoreType.DMA,
            pltpu.SemaphoreType.DMA((q_here, blocks)),
            pltpu.SemaphoreType.DMA((blocks,)),
            *sum_scratch,
        ],
        compiler_params=local_params(collective_id),
        name="attention_backward",
    )(dy, xn, p, *have, *saved, w_attn, vec, gates, *tables, mlp_gain_part)


def attention_end(
    dy, xn, p, mlp_part, ff_sums, saved, w_attn, vec, gates, tables, token_rows, q_here, copies,
    n_head, n_blk, collective_id
):
    pack, width = dy.shape
    columns = w_attn.shape[1]
    q_cols = q_here * HEAD_DIM
    blocks = pack // ROWS
    scale = 1.0 / math.sqrt(HEAD_DIM)
    chips, count = n_blk // 2, pack // n_blk
    rows_here = width // (n_head * n_blk)
    lanes = n_blk * rows_here
    entries = ff_entries(ff_sums[0].shape[1], n_head)

    def kernel(dy_hbm, xn_hbm, p_hbm, mlp_hbm, *refs):
        refs = list(refs)

        def take(n):
            taken = refs[:n]
            del refs[:n]
            return taken

        ff_src = take(3)
        lin_ref, q_ref, k_ref, v_ref, sig_ref, o_ref, gated_ref, o_rows = take(8)
        w_ref, vec_ref, gate_ref, cos_ref, sin_ref = take(5)
        x_ref, middle_ref, dmid_ref, mlp_gain_ref = take(4)
        layer_out, input_grad, g_out, wq_out, wk_out, wv_out, o_out = take(7)
        ff_out = take(3)
        dy_s, xn_s, p_s, do_s, delta_s, dgate_s, dlin_s, dk_s, dv_s, dgq_s = take(10)
        dw_s, pack_s, dout_s, w_in, w_sum, o_in, o_sum, g_in, g_sum, g_last = take(10)
        mlp_scratch, dxn_scratch = take(5), take(4)
        dy_sem, xn_sem, p_sem = take(3)
        w_sems, block_sems, o_sems, g_sems, pack_sems, moved, ff_sems, local = refs
        line = Line(n_blk)
        across, along = Exchange("head", n_head), Exchange("blk", n_blk)
        h, b = across.me, along.me
        first_head = b * q_here
        (sh, sb), (th, tb) = place_of_out_rows(n_head, n_blk)
        stays = (th == h) & (tb == b)
        moves = jnp.logical_not(stays)
        greet_all((across, along), moves=(moves, {"head": sh, "blk": sb}))

        def dy_load(n):
            return pltpu.make_async_copy(
                dy_hbm.at[block_of(n)], dy_s.at[block_of(n)], dy_sem.at[n]
            )

        def p_load(head, n):
            return pltpu.make_async_copy(
                p_hbm.at[head, block_of(n)], p_s.at[head, block_of(n)], p_sem.at[head, n]
            )

        def of_head(head):
            return pl.ds(pl.multiple_of(head * lanes, lanes), lanes)

        def of_blk(blk):
            return pl.ds(pl.multiple_of(blk * rows_here, rows_here), rows_here)

        def out_of(head):
            return dout_s.at[pl.ds(pl.multiple_of(head * rows_here, rows_here), rows_here)]

        def w_copy(k):
            return across.copy(k, dw_s.at[of_head(across.peer(k))], w_in.at[k], w_sems)

        def o_copy(k):
            return across.copy(k, out_of(across.peer(k)), o_in.at[k], o_sems)

        def g_part(head):
            return pack_s.at[:, pl.ds(pl.multiple_of(head * lanes, 128), lanes)]

        def g_copy(k):
            return across.copy(k, g_part(across.peer(k)), g_in.at[k], g_sems)

        def landings():
            kv = pl.ds(pl.multiple_of(b // copies * HEAD_DIM, HEAD_DIM), HEAD_DIM)
            return (
                wq_out.at[:, pl.ds(pl.multiple_of(b * q_cols, HEAD_DIM), q_cols)],
                wk_out.at[b % copies, :, kv],
                wv_out.at[b % copies, :, kv],
            )

        spans = (
            pl.ds(0, q_cols),
            pl.ds(q_cols, HEAD_DIM),
            pl.ds(q_cols + HEAD_DIM, HEAD_DIM),
        )

        def block_copies(k):
            for w, there in enumerate(landings()):
                src = w_sum.at[of_blk(along.peer(k)), spans[w]]
                yield along.copy(k, src, there, block_sems.at[w])

        def tile_of(blk):
            return pl.ds(pl.multiple_of(blk * rows_here // 128 * 128, 128), 128)

        def pack_copy(k):
            return along.copy(k, g_sum.at[:, tile_of(along.peer(k))], g_last.at[b], pack_sems)

        move_out = pltpu.make_async_remote_copy(
            src_ref=o_sum,
            dst_ref=o_out,
            send_sem=moved.at[0],
            recv_sem=moved.at[1],
            device_id={"head": th, "blk": tb},
            device_id_type=MESH,
        )
        keep_out = pltpu.make_async_copy(o_sum, o_out, moved.at[2])
        hops = [
            flip_copy(ff_src[w].at[1, part], ff_out[w].at[part], order[0], ff_sems, e)
            for e, (w, part, order) in enumerate(entries)
        ]
        own_blocks = [
            pltpu.make_async_copy(w_sum.at[of_blk(b), spans[w]], there, local.at[w])
            for w, there in enumerate(landings())
        ]
        mlp = Scatter(line, mlp_hbm, mlp_scratch[:4], mlp_scratch[4])
        dxn = LocalScatter(
            line, Rows(dy_s, 0, count, chips), dxn_scratch[:3], dxn_scratch[3]
        )
        xn_load = pltpu.make_async_copy(xn_hbm, xn_s, xn_sem)
        for n in range(blocks):
            dy_load(n).start()
        mlp.start()
        for n in range(blocks):
            for head in range(q_here):
                p_load(head, n).start()
        xn_load.start()
        for hop in hops:
            hop.start()

        def through_gate(n, carry):
            r = block_of(n)
            dy_load(n).wait()
            dgated = mm_nt(dy_s[r, :], o_rows[...])
            lane = lax.broadcasted_iota(jnp.int32, (ROWS, GATE_PAD), 1)
            dgates = jnp.zeros((ROWS, GATE_PAD), F32)
            deltas = jnp.zeros((ROWS, GATE_PAD), F32)
            for head in range(q_here):
                at = slice(head * HEAD_DIM, (head + 1) * HEAD_DIM)
                sig = sig_ref[r, head : head + 1]
                out = o_ref[r, at].astype(F32)
                do = (dgated[:, at] * sig).astype(BF16)
                do_s[r, at] = do
                dgate = jnp.sum(dgated[:, at] * out, axis=-1, keepdims=True) * sig * (1.0 - sig)
                delta = jnp.sum(do.astype(F32) * out, axis=-1, keepdims=True)
                dgates = jnp.where(lane == first_head + head, dgate, dgates)
                deltas = jnp.where(lane == head, delta, deltas)
            dgate_s[r, :] = dgates.astype(BF16)
            delta_s[r, :] = deltas
            return carry

        lax.fori_loop(0, blocks, through_gate, 0)
        mlp.step(0)

        def out_grad(n, carry):
            c = block_of(n)
            dout_s[:, c] = mm_tn(gated_ref[...], dy_s[:, c]).astype(BF16)
            return carry

        lax.fori_loop(0, width // ROWS, out_grad, 0)
        dk_s[...] = jnp.zeros_like(dk_s)
        dv_s[...] = jnp.zeros_like(dv_s)
        dgq_s[...] = jnp.zeros_like(dgq_s)
        o_in[0] = dout_s[pl.ds(pl.multiple_of(h * rows_here, rows_here), rows_here), :]
        for k in range(1, n_head):
            o_copy(k).start()

        def into_lin(grad, lin, gain, r):
            grad = turned(grad.astype(BF16).astype(F32), cos_ref[r, :], -sin_ref[r, :])
            unit, factor = unit_of(lin)
            return unit_back(grad * gain, unit, factor).astype(BF16), grad * unit

        def attend(n, carry):
            r = block_of(n)
            for head in range(q_here):
                at = slice(head * HEAD_DIM, (head + 1) * HEAD_DIM)
                p_load(head, n).wait()
                do, prob, q = do_s[r, at], p_s[head, r, :], q_ref[r, at]
                dp = mm_nt(do, v_ref[...])
                ds = (prob.astype(F32) * (dp - delta_s[r, head : head + 1])).astype(BF16)
                dq = mm(ds, k_ref[...]) * scale
                dk_s[...] += mm(q.T, ds)
                dv_s[...] += mm(do.T, prob)
                dlin, part = into_lin(dq, lin_ref[r, at], vec_ref[2:3, :HEAD_DIM], r)
                dlin_s[r, at] = dlin
                dgq_s[...] += jnp.sum(part.reshape(ROWS // 8, 8, HEAD_DIM), axis=0)
            return carry

        lax.fori_loop(0, blocks // 2, attend, 0)
        mlp.step(1)
        lax.fori_loop(blocks // 2, blocks, attend, 0)
        every = pl.ds(0, pack)
        k_cols = slice(q_cols, q_cols + HEAD_DIM)
        dlin, part = into_lin(
            dk_s[...].T * scale, lin_ref[:, k_cols], vec_ref[3:4, :HEAD_DIM], every
        )
        dlin_s[:, k_cols] = dlin
        dlin_s[:, q_cols + HEAD_DIM :] = dv_s[...].T.astype(BF16)

        def into_x(n, carry):
            r = block_of(n)
            back = mm_nt(dlin_s[r, :], w_ref[...]) + mm(dgate_s[r, :HEADS], gate_ref[...])
            dy_s[r, :] = back.astype(BF16)
            return carry

        lax.fori_loop(0, blocks, into_x, 0)
        dxn.start()
        for tau in range(2, chips - 1):
            mlp.step(tau)
        dxn.step(0)
        dgk = jnp.sum(part, axis=0, keepdims=True)
        dgq = jnp.sum(dgq_s[...], axis=0, keepdims=True)
        pack_s[HEADS:, :] = jnp.zeros((PACK_ROWS - HEADS, width), F32)
        pack_s[HEADS : HEADS + 1, :] = jnp.sum(mlp_gain_ref[...], axis=0, keepdims=True)
        for t in range(width // HEAD_DIM):
            at = slice(t * HEAD_DIM, (t + 1) * HEAD_DIM)
            pack_s[HEADS + 1 : HEADS + 2, at] = dgq
            pack_s[HEADS + 2 : HEADS + 3, at] = dgk
        xn_load.wait()
        dgate_t = dgate_s[...].astype(F32).T[:HEADS].astype(BF16)

        def weights(n, carry):
            c = block_of(n)
            xn_cols = xn_s[:, c]
            dw_s[c, :] = mm_tn(xn_cols, dlin_s[...]).astype(BF16)
            pack_s[:HEADS, c] = mm(dgate_t, xn_cols)
            return carry

        lax.fori_loop(0, width // ROWS, weights, 0)
        for k in range(1, n_head):
            w_copy(k).start()
            g_copy(k).start()
        w_in[0] = dw_s[of_head(h), :]
        g_in[0] = pack_s[:, pl.ds(pl.multiple_of(h * lanes, 128), lanes)]

        def finish_layer(r, value):
            layer_out[r, :] = (middle_ref[r, :] + value).astype(BF16)

        mlp.total(finish_layer)
        for tau in range(1, chips - 2):
            dxn.step(tau)
        for k in range(1, n_head):
            g_copy(k).wait_recv()
        g_sum[...] = sum(g_in[k] for k in range(n_head))
        g_last[b] = g_sum[:, tile_of(b)]
        for k in range(1, n_blk):
            pack_copy(k).start()
        for k in range(1, n_head):
            o_copy(k).wait_recv()

        def add_out(r):
            o_sum[r, :] = sum(o_in[k, r, :].astype(F32) for k in range(n_head)).astype(BF16)

        by_rows(rows_here, 16, add_out)

        @pl.when(stays)
        def _():
            keep_out.start()

        @pl.when(moves)
        def _():
            move_out.start()

        for k in range(1, n_head):
            w_copy(k).wait_recv()

        def add(r):
            w_sum[r, :] = sum(w_in[k, r, :].astype(F32) for k in range(n_head)).astype(BF16)

        by_rows(lanes, 64, add)
        for one in own_blocks:
            one.start()
        for k in range(1, n_blk):
            for copy in block_copies(k):
                copy.start()
        dxn.step(chips - 2)

        def consume(r, value):
            unit, factor = unit_of(x_ref[r, :].astype(F32))
            back = unit_back(value * vec_ref[0:1, :], unit, factor)
            input_grad[r, :] = dmid_ref[r, :] + back

        dxn.total(consume)
        for k in range(1, n_blk):
            pack_copy(k).wait_recv()
        g_out[...] = sum(g_last[k] for k in range(n_blk))
        mlp.finish()
        dxn.finish()
        for one in own_blocks:
            one.wait()
        for k in range(1, n_head):
            g_copy(k).wait_send()
            o_copy(k).wait_send()
            w_copy(k).wait_send()
        for k in range(1, n_blk):
            pack_copy(k).wait_send()
            for copy in block_copies(k):
                copy.wait()
        for hop in hops:
            hop.wait()

        @pl.when(stays)
        def _():
            keep_out.wait()

        @pl.when(moves)
        def _():
            move_out.wait()

    dma = pltpu.SemaphoreType.DMA
    kv = spec_of((copies, rows_here, n_blk // copies * HEAD_DIM), BF16)
    return pl.pallas_call(
        kernel,
        out_shape=(
            spec_of((count, width), BF16),
            spec_of((count, width), F32),
            spec_of((PACK_ROWS, 128), F32),
            spec_of((rows_here, n_blk * q_cols), BF16),
            kv,
            kv,
            spec_of((rows_here, width), BF16),
            *(spec_of(one.shape[1:], BF16) for one in ff_sums),
        ),
        in_specs=[ANYWHERE] * 7 + [IN_VMEM] * 17,
        out_specs=[IN_VMEM] * 3 + [ANYWHERE] * 7,
        scratch_shapes=[
            pltpu.VMEM((pack, width), BF16),
            pltpu.VMEM((pack, width), BF16),
            pltpu.VMEM((q_here, pack, pack), BF16),
            pltpu.VMEM((pack, q_cols), BF16),
            pltpu.VMEM((pack, GATE_PAD), F32),
            pltpu.VMEM((pack, GATE_PAD), BF16),
            pltpu.VMEM((pack, columns), BF16),
            pltpu.VMEM((HEAD_DIM, pack), F32),
            pltpu.VMEM((HEAD_DIM, pack), F32),
            pltpu.VMEM((8, HEAD_DIM), F32),
            pltpu.VMEM((width, columns), BF16),
            pltpu.VMEM((PACK_ROWS, width), F32),
            pltpu.VMEM((q_cols, width), BF16),
            pltpu.VMEM((n_head, lanes, columns), BF16),
            pltpu.VMEM((lanes, columns), BF16),
            pltpu.VMEM((n_head, rows_here, width), BF16),
            pltpu.VMEM((rows_here, width), BF16),
            pltpu.VMEM((n_head, PACK_ROWS, lanes), F32),
            pltpu.VMEM((PACK_ROWS, lanes), F32),
            pltpu.VMEM((n_blk, PACK_ROWS, 128), F32),
            *scatter_bufs(chips, count, width),
            *scatter_bufs(chips, count, width)[1:],
            dma((blocks,)),
            dma,
            dma((q_here, blocks)),
            pair_sems(n_head),
            dma((3, 2, n_blk)),
            pair_sems(n_head),
            pair_sems(n_head),
            pair_sems(n_blk),
            dma((3,)),
            pair_sems(len(entries)),
            dma((3,)),
        ],
        compiler_params=local_params(collective_id),
        cost_estimate=comm_cost(2 * pack * width),
        name="attention_end",
    )(
        dy,
        xn,
        p,
        mlp_part.reshape(chips, 2, count, width),
        *ff_sums,
        *saved,
        w_attn,
        vec,
        gates,
        *tables,
        *token_rows,
    )


def feed_forward(attn_part, ff, halfway, cot, inputs, to_mlp, to_attention, n_head, n_blk, collective_id):
    total_rows, width = attn_part.shape
    chips, count = n_blk // 2, total_rows // n_blk
    size, half = count // CHUNKS, total_rows // CHUNKS
    rows_ff = ff[0].shape[0]
    units = n_head * rows_ff
    entries = ff_entries(rows_ff, n_head)
    n_in = len(inputs)

    def kernel(part, cot_hbm, *refs):
        refs = list(refs)

        def take(n):
            taken = refs[:n]
            del refs[:n]
            return taken

        sources = take(3), take(3)
        ins = take(n_in)
        middle, dmid, gain_part, dy_hbm, mlp_hbm, *sum_hbm = take(8)
        made, hn_s, cot_s, dhn_s, u_s, da_s, db_s, stage = take(8)
        inboxes, weights = take(3), take(3)
        chunk_scratch = [take(8) for _ in range(CHUNKS)]
        load_sems, hop_sems, cot_sems, stage_sems, sum_sems, grad_sems, late_sems = refs
        line = Line(n_blk)
        across = Exchange("head", n_head)
        greet_all((across,), line)
        gain_part[...] = jnp.zeros_like(gain_part)

        def place(key, span):
            return pl.ds(key * rows_ff + span.start, span.size)

        loads, hops = [], []
        for e, (w, span, order) in enumerate(entries):
            first, second = 1 << order[0], 1 << order[1]
            for at, key in enumerate((0, first)):
                src = sources[at][w].at[span]
                loads.append(
                    pltpu.make_async_copy(src, weights[w].at[place(key, span)], load_sems.at[e, at])
                )
                there = weights[w].at[place(key ^ second, span)]
                hops.append(flip_copy(src, there, order[1], hop_sems, e, at))

        def cot_loads():
            for j in range(chips):
                for c in range(2):
                    yield pltpu.make_async_copy(
                        cot_hbm.at[j, c],
                        Rows(cot_s, 0, size, chips)[j, c],
                        cot_sems.at[2 * j + c],
                    )

        first, gather1, second, gather2 = [], [], [], []
        for q in range(CHUNKS):
            own, sib, inn, outgoing, sems, g_sems, sems2, g_sems2 = chunk_scratch[q]
            rows = pl.ds(q * size, size)
            first.append(Scatter(line, View(part, rows), (own, sib, inn, outgoing), sems))
            gather1.append(Gather(line, made.at[rows], Rows(hn_s, q, size, chips), g_sems))
            second.append(
                LocalScatter(line, Rows(dhn_s, q, size, chips), (sib, inn, outgoing), sems2)
            )
            gather2.append(Gather(line, made.at[rows], View(dy_hbm, rows), g_sems2))

        late = [
            Gather(
                line,
                ins[1].at[pl.ds(q * size, size)],
                Rows(cot_s, q, size, chips),
                late_sems.at[q - 1],
            )
            for q in range(1, CHUNKS)
        ]

        def turn(q, scatter, between, outs, gather):
            def consume(r, value):
                r = pl.ds(pl.multiple_of(r.start + q * size, 16), r.size)
                made[r, :] = between(r, value, ins, outs).astype(BF16)

            scatter[q].total(consume)
            gather[q].start()

        def loop(steps, body):
            lax.fori_loop(0, steps, lambda k, carry: body(k) or carry, 0)

        def span_of(q):
            return pl.ds(q * half, half)

        def unit_block(q, f):
            r, fr = span_of(q), block_of(f)
            a = mm_nt(hn_s[r, :], weights[0][fr, :])
            b = mm_nt(hn_s[r, :], weights[1][fr, :])
            du = mm_nt(cot_s[r, :], weights[2][fr, :])
            sig = jax.nn.sigmoid(a)
            silu = a * sig
            u_s[r, fr] = (silu * b).astype(BF16)
            da_s[r, fr] = (du * b * sig * (1.0 + a * (1.0 - sig))).astype(BF16)
            db_s[r, fr] = (du * silu).astype(BF16)

        def back(q):
            r = span_of(q)

            def body(n):
                cols = block_of(n, 512)
                dhn = mm(da_s[r, :], weights[0][:, cols]) + mm(db_s[r, :], weights[1][:, cols])
                dhn_s[r, cols] = dhn.astype(BF16)

            loop(width // 512, body)

        def stage_stores(q):
            for j in range(chips):
                for c in range(2):
                    yield pltpu.make_async_copy(
                        Rows(stage, 0, size, chips)[j, c],
                        mlp_hbm.at[j, c, pl.ds(q * size, size)],
                        stage_sems.at[2 * j + c],
                    )

        def mlp_out(q):
            if q:
                for store in stage_stores(q - 1):
                    store.wait()
            r = span_of(q)

            def body(n):
                cols = block_of(n, 512)
                stage[:, cols] = mm(u_s[r, :], weights[2][:, cols]).astype(BF16)

            loop(width // 512, body)
            for store in stage_stores(q):
                store.start()

        def grad(w):
            left, right = ((da_s, hn_s), (db_s, hn_s), (u_s, cot_s))[w]

            def body(f):
                fr = block_of(f)
                weights[w][fr, :] = mm_tn(left[:, fr], right[...]).astype(BF16)

            loop(units // ROWS, body)

        def sum_copies(w):
            for e, (weight, span, order) in enumerate(entries):
                if weight == w:
                    for at, key in enumerate((0, 1 << order[0])):
                        yield flip_copy(
                            weights[w].at[place(key ^ (1 << order[1]), span)],
                            inboxes[w].at[at, span],
                            order[1],
                            sum_sems,
                            e,
                            at,
                        )

        def sum_stores(w):
            for e, (weight, span, order) in enumerate(entries):
                if weight == w:
                    for at, key in enumerate((0, 1 << order[0])):
                        yield pltpu.make_async_copy(
                            weights[w].at[place(key, span)],
                            sum_hbm[w].at[at, span],
                            grad_sems.at[e, at],
                        )

        def send_grad(w):
            grad(w)
            for copy in sum_copies(w):
                copy.start()

        def add_grad(w):
            for copy in sum_copies(w):
                copy.wait()
            for weight, span, order in entries:
                if weight == w:
                    for at, key in enumerate((0, 1 << order[0])):

                        def body(r, span=span, at=at, key=key):
                            r = pl.ds(pl.multiple_of(r.start + span.start, 16), r.size)
                            mine = pl.ds(pl.multiple_of(r.start + key * rows_ff, 16), r.size)
                            value = weights[w][mine, :].astype(F32)
                            value += inboxes[w][at, r, :].astype(F32)
                            weights[w][mine, :] = value.astype(BF16)

                        by_rows(span.size, 16, body)
            for store in sum_stores(w):
                store.start()

        first[0].start()
        for hop in hops:
            hop.start()
        for q in range(1, CHUNKS):
            first[q].start()
        for one in late:
            one.start()
        for load in loads:
            load.start()
        for load in cot_loads():
            load.start()
        steps = chips - 1
        for tau in range(steps):
            first[0].step(tau)
            for one in late:
                one.step(tau + 1)
        turn(0, first, to_mlp, (middle,), gather1)
        for tau in range(steps):
            first[1].step(tau)
            gather1[0].step(tau + 1)
        turn(1, first, to_mlp, (middle,), gather1)
        for q in range(CHUNKS):
            first[q].finish()
        gather1[0].finish()
        gather1[1].step(1)
        for load in loads:
            load.wait()
        for load in cot_loads():
            load.wait()
        for hop in hops:
            hop.wait()
        blocks = units // ROWS
        unit_block(0, 0)
        for s in range(2, chips):
            gather1[1].step(s)
            if s == 2:
                unit_block(0, 1)
        for f in range(2, blocks):
            unit_block(0, f)
        back(0)
        second[0].start()
        gather1[1].finish()
        for one in late:
            one.finish()
        second[0].step(0)
        loop(blocks, lambda f: unit_block(1, f))
        second[0].step(1)
        back(1)
        second[1].start()
        send_grad(0)
        for tau in range(2, steps):
            second[0].step(tau)
        second[1].step(0)
        send_grad(1)
        turn(0, second, to_attention, (middle, dmid, gain_part), gather2)
        second[1].step(1)
        mlp_out(0)
        mlp_out(1)
        gather2[0].step(1)
        send_grad(2)
        for tau in range(2, steps):
            second[1].step(tau)
            gather2[0].step(tau)
        turn(1, second, to_attention, (middle, dmid, gain_part), gather2)
        gather2[0].step(chips - 1)
        for s in range(1, chips):
            gather2[1].step(s)
        for w in range(3):
            add_grad(w)
        for q in range(CHUNKS):
            second[q].finish()
            gather2[q].finish()
        for store in stage_stores(CHUNKS - 1):
            store.wait()
        for w in range(3):
            for store in sum_stores(w):
                store.wait()

    per_chunk = []
    for _ in range(CHUNKS):
        own, sib, inn, outgoing, sems = scatter_bufs(chips, size, width)
        per_chunk += [own, sib, inn, outgoing, sems, gather_sems(chips), sems, gather_sems(chips)]
    sums = jax.ShapeDtypeStruct((2, rows_ff, width), BF16)
    shards_ = jax.ShapeDtypeStruct((chips, 2, count, width), BF16)
    dma = pltpu.SemaphoreType.DMA
    middle, dmid, gain_part, dy, mlp_part, *ff_sums = pl.pallas_call(
        kernel,
        out_shape=(
            jax.ShapeDtypeStruct((count, width), F32),
            jax.ShapeDtypeStruct((count, width), F32),
            jax.ShapeDtypeStruct((8, width), F32),
            shards_,
            shards_,
            *[sums] * 3,
        ),
        in_specs=[ANYWHERE] * 8 + [IN_VMEM] * n_in,
        out_specs=[IN_VMEM] * 3 + [ANYWHERE] * 5,
        scratch_shapes=[
            pltpu.VMEM((count, width), BF16),
            *[pltpu.VMEM((total_rows, width), BF16)] * 3,
            *[pltpu.VMEM((total_rows, units), BF16)] * 3,
            pltpu.VMEM((half, width), BF16),
            *[pltpu.VMEM((2, rows_ff, width), BF16)] * 3,
            *[pltpu.VMEM((units, width), BF16)] * 3,
            *per_chunk,
            dma((len(entries), 2)),
            dma((2, len(entries), 2)),
            dma((n_blk,)),
            dma((n_blk,)),
            dma((2, len(entries), 2)),
            dma((len(entries), 2)),
            dma((CHUNKS - 1, 7, chips, PIECES)),
        ],
        compiler_params=pltpu.CompilerParams(
            collective_id=collective_id, has_side_effects=True, vmem_limit_bytes=62 * 2**20
        ),
        cost_estimate=comm_cost(2 * total_rows * width),
        name="feed_forward",
    )(
        attn_part.reshape(chips, 2, count, width),
        cot,
        *ff,
        *halfway,
        *inputs,
    )
    return (
        middle,
        dmid,
        gain_part,
        dy.reshape(total_rows, width),
        mlp_part.reshape(total_rows, width),
        ff_sums,
    )


def padded(values, size):
    return jnp.pad(values, [(0, 0)] * (values.ndim - 1) + [(0, size - values.shape[-1])])


def shards(
    hidden,
    segment_ids,
    block_ids,
    positions,
    attn_gain,
    w_query,
    key_weight_matrix,
    value_weight_matrix,
    q_gain,
    k_gain,
    w_head_gate,
    w_out,
    mlp_gain,
    w_gate,
    w_up,
    w_down,
    cotangent,
):
    n_head = lax.axis_size("head")
    n_blk = lax.axis_size("blk")
    n_all = n_head * n_blk
    my_head = lax.axis_index("head")
    my_blk = lax.axis_index("blk")
    tokens = hidden.shape[1]
    pack = tokens * n_blk
    rows_here = w_query.shape[0]
    rows_ff = w_gate.shape[0]
    q_here = HEADS // n_blk
    q_cols = q_here * HEAD_DIM
    kv_copies = max(1, n_blk // KV_HEADS)
    kv_here = max(1, KV_HEADS // n_blk)
    kv_cols = kv_here * HEAD_DIM
    device = my_head * n_blk + my_blk
    together = 128 // rows_here
    lane = jnp.arange(128)
    here = (lane // rows_here == device % together)[None]
    mine = jnp.concatenate(
        [
            attn_gain[None],
            mlp_gain[None],
            jnp.zeros((6, rows_here), BF16),
            w_head_gate.T,
        ]
    )
    small = jnp.where(here, jnp.tile(mine, (1, together)), 0).astype(F32)
    share = q_gain.shape[0]
    head_gains = jnp.stack([jnp.tile(q_gain, n_all), jnp.tile(k_gain, n_all)]).astype(F32)
    head_gains = jnp.where(lane // share == device, head_gains, 0)
    small = small + jnp.pad(head_gains, ((2, PACK_ROWS - 4), (0, 0)))
    ids = [
        lax.dynamic_slice_in_dim(ids_, my_head, 1, 0) for ids_ in (positions, segment_ids, block_ids)
    ]
    fused = n_head == 4 and pack <= 1024
    ff = (w_gate, w_up, w_down)
    attn_part, xn, prob, cot, *rest = attention_forward(
        hidden[0],
        (w_query, key_weight_matrix, value_weight_matrix),
        small,
        w_out,
        ids,
        cotangent[0, : tokens // CHUNKS] if fused else cotangent[0],
        ff,
        q_cols,
        kv_copies,
        n_head,
        n_blk,
        0,
    )
    halfway, (w_attn, vec, gates), tables, saved = rest[:3], rest[3:6], rest[6:8], rest[8:]

    def to_mlp(r, total, ins, outs):
        x_ref, gain_ref = ins
        mid = x_ref[r, :].astype(F32) + total
        outs[0][r, :] = mid
        unit, _ = unit_of(mid)
        return unit * gain_ref[1:2, :]

    def to_attention(r, dhn, ins, outs):
        mid_ref, cot_ref, gain_ref = ins
        unit, factor = unit_of(mid_ref[r, :])
        product = dhn * unit
        seen = outs[1]
        seen[...] += product[:8] + product[8:]
        back = cot_ref[r, :].astype(F32) + unit_back(dhn * gain_ref[1:2, :], unit, factor)
        outs[0][r, :] = back
        return back

    if fused:

        def into_mlp(r, total, ins, outs):
            return to_mlp(r, total, (ins[0], ins[2]), outs)

        def into_attention(r, dhn, ins, outs):
            return to_attention(r, dhn, (outs[0], ins[1], ins[2]), outs[1:])

        middle, dmid, mlp_gain_part, dy, mlp_part, ff_sums = feed_forward(
            attn_part,
            ff,
            halfway,
            cot,
            (hidden[0], cotangent[0], vec),
            into_mlp,
            into_attention,
            n_head,
            n_blk,
            1,
        )
    else:
        cot = cot.reshape(pack, MODEL_WIDTH)
        ff_full = []
        for w, (own, other) in enumerate(zip(ff, halfway)):
            full = jnp.zeros((n_head, *own.shape), BF16).at[0].set(own)
            for weight, part, order in ff_entries(rows_ff, n_head):
                if weight == w:
                    span = slice(part.start, part.start + part.size)
                    full = full.at[1 << order[0], span].set(other[span])
            ff_full.append(full)
        middle, hn, *ff_rows = scatter_gather(
            attn_part,
            lambda outs: None,
            to_mlp,
            (hidden[0], vec),
            (jax.ShapeDtypeStruct(hidden.shape[1:], F32),),
            spread_beside(ff_full, n_head),
            n_head,
            n_blk,
            1,
        )
        gate_rows, up_rows, down_rows = (one.reshape(n_head * rows_ff, MODEL_WIDTH) for one in ff_rows)

        a = mm_nt(hn, gate_rows)
        b = mm_nt(hn, up_rows)
        sig = jax.nn.sigmoid(a)
        silu = a * sig
        u = (silu * b).astype(BF16)
        mlp_part = mm(u, down_rows).astype(BF16)
        du = mm_nt(cot, down_rows)
        da = (du * b * sig * (1.0 + a * (1.0 - sig))).astype(BF16)
        db = (du * silu).astype(BF16)
        ff_parts = [
            mm_tn(left, right).astype(BF16).reshape(n_head, rows_ff, MODEL_WIDTH)
            for left, right in ((da, hn), (db, hn), (u, cot))
        ]

        def clear(outs):
            outs[1][...] = jnp.zeros_like(outs[1])

        dmid, mlp_gain_part, dy, *ff_sums, mlp_part = scatter_gather(
            mm(da, gate_rows) + mm(db, up_rows),
            clear,
            to_attention,
            (middle, cotangent[0], vec),
            (
                jax.ShapeDtypeStruct(hidden.shape[1:], F32),
                jax.ShapeDtypeStruct((8, MODEL_WIDTH), F32),
            ),
            collect_beside(ff_parts, mlp_part, n_head),
            n_head,
            n_blk,
            2,
        )

    if fused:
        layer_output, input_grad, small_sums, query_grad, key_grad, value_grad, out_grad, *ff_last = (
            attention_end(
                dy,
                xn,
                prob,
                mlp_part,
                ff_sums,
                saved,
                w_attn,
                vec,
                gates,
                tables,
                (hidden[0], middle, dmid, mlp_gain_part),
                q_here,
                kv_copies,
                n_head,
                n_blk,
                2,
            )
        )
        layer_output, input_grad = layer_output[None], input_grad[None]
    else:
        layer_output = (
            middle + lax.psum_scatter(mlp_part, "blk", scatter_dimension=0, tiled=True).astype(F32)
        ).astype(BF16)[None]
        dxn_part, attn_grad, small_parts, out_grad = attention_backward(
            dy,
            xn,
            prob,
            saved,
            w_attn,
            vec,
            gates,
            tables,
            mlp_gain_part,
            q_here,
            None,
        )
        back_x, query_grad, key_grad, value_grad, out_grad, small_sums, *ff_last = last_scatter(
            dxn_part,
            attn_grad.reshape(n_head, n_blk, rows_here, -1),
            out_grad,
            small_parts,
            ff_sums,
            hidden[0],
            vec,
            q_cols,
            kv_copies,
            n_head,
            n_blk,
            3,
        )
        input_grad = (dmid + back_x)[None]
    ff_grads = [one[0].astype(F32) + two.astype(F32) for one, two in zip(ff_sums, ff_last)]

    query_grad = query_grad.astype(F32)
    key_grad = jnp.sum(key_grad.astype(F32), axis=0)
    value_grad = jnp.sum(value_grad.astype(F32), axis=0)
    small_sums = jnp.sum(
        jnp.where(
            jnp.arange(together)[None, :, None] == device % together,
            small_sums.reshape(PACK_ROWS, together, rows_here),
            0.0,
        ),
        axis=1,
    ), small_sums[HEADS + 1 : HEADS + 3]
    small_sums, head_sums = small_sums
    head_sums = lax.dynamic_slice_in_dim(head_sums, device * share, share, 1)
    head_gate_grad = small_sums[:HEADS].T
    attn_gain_grad = (
        jnp.sum(w_query.astype(F32) * query_grad, axis=1)
        + jnp.sum(key_weight_matrix.astype(F32) * key_grad, axis=1)
        + jnp.sum(value_weight_matrix.astype(F32) * value_grad, axis=1)
        + jnp.sum(w_head_gate.astype(F32) * head_gate_grad, axis=1)
    ) / attn_gain.astype(F32)
    return (
        layer_output,
        input_grad,
        attn_gain_grad,
        query_grad,
        key_grad,
        value_grad,
        head_sums[0],
        head_sums[1],
        head_gate_grad,
        out_grad.astype(F32),
        small_sums[HEADS],
        ff_grads[0],
        ff_grads[1],
        ff_grads[2],
    )


def solution(mesh):
    rows = P(("head", "blk"), None)
    vector = P(("head", "blk"))
    token = P("head", "blk", None)
    return jax.shard_map(
        shards,
        mesh=mesh,
        in_specs=(
            token, P(), P(), P(), vector, rows, rows, rows, vector, vector, rows, rows, vector,
            rows, rows, rows, token,
        ),
        out_specs=(
            token, token, vector, rows, rows, rows, vector, vector, rows, rows, vector,
            rows, rows, rows,
        ),
        check_vma=False,
    )
```

```python
import math

import jax
import jax.numpy as jnp
from jax import lax
from jax.experimental import pallas as pl
from jax.experimental.pallas import tpu as pltpu
from jax.sharding import PartitionSpec as P

MODEL_WIDTH = 2048
HEADS = 16
KV_HEADS = 8
HEAD_DIM = 128
GATE_PAD = 128
EPSILON = 1e-06
ROPE_BASE = 1000000.0
MASKED = -1e30
F32 = jnp.float32
BF16 = jnp.bfloat16
MESH = pl.DeviceIdType.MESH


def mm(a, b):
    return jnp.dot(a, b, preferred_element_type=F32)


def mm_nt(a, b):
    return lax.dot_general(a, b, (((1,), (1,)), ((), ())), preferred_element_type=F32)


def mm_tn(a, b):
    return lax.dot_general(a, b, (((0,), (0,)), ((), ())), preferred_element_type=F32)


def unit_of(values):
    factor = lax.rsqrt(jnp.mean(values * values, axis=-1, keepdims=True) + EPSILON)
    return values * factor, factor


def unit_back(scaled, unit, factor):
    return factor * (scaled - unit * jnp.mean(scaled * unit, axis=-1, keepdims=True))


def signal_to(semaphore, target):
    pl.semaphore_signal(semaphore, inc=1, device_id=target, device_id_type=MESH)


class Line:
    def __init__(self, n_blk):
        self.me = lax.axis_index("blk")
        self.chips = n_blk // 2
        self.i = self.me // 2
        self.c = self.me % 2
        self.right = {"blk": self.me + 2}
        self.left = {"blk": self.me - 2}
        self.sibling = {"blk": self.me + 1 - 2 * self.c}
        self.has_right = self.i < self.chips - 1
        self.has_left = self.i > 0

    def greet(self, barrier):
        signal_to(barrier, self.sibling)

        @pl.when(self.has_right)
        def _():
            signal_to(barrier, self.right)

        @pl.when(self.has_left)
        def _():
            signal_to(barrier, self.left)

        return 1 + self.has_right.astype(jnp.int32) + self.has_left.astype(jnp.int32)


class Gather:
    def __init__(self, line, src, out, sems):
        self.line, self.src, self.out, self.sems = line, src, out, sems
        self.pieces = sems.shape[2]
        self.rows = src.shape[0] // self.pieces

    def part(self, p):
        return pl.ds(p * self.rows, self.rows)

    def move(self, kind, src, j, p, target):
        return pltpu.make_async_remote_copy(
            src_ref=src.at[self.part(p)],
            dst_ref=self.out.at[j, self.line.c, self.part(p)],
            send_sem=self.sems.at[kind, j, p],
            recv_sem=self.sems.at[3 + kind, j, p],
            device_id=target,
            device_id_type=MESH,
        )

    def arrived(self, kind, j, p, core):
        there = self.out.at[j, core, self.part(p)]
        pltpu.make_async_remote_copy(
            src_ref=there,
            dst_ref=there,
            send_sem=self.sems.at[kind, j, p],
            recv_sem=self.sems.at[3 + kind, j, p],
            device_id=self.line.sibling,
            device_id_type=MESH,
        ).wait_recv()

    def send(self, src, j, p, right, left):
        line = self.line
        if right is not None:

            @pl.when(right)
            def _():
                self.move(0, src, j, p, line.right).start()

        if left is not None:

            @pl.when(left)
            def _():
                self.move(1, src, j, p, line.left).start()

        self.move(2, src, j, p, line.sibling).start()

    def own_copy(self):
        return pltpu.make_async_copy(
            self.src, self.out.at[self.line.i, self.line.c], self.sems.at[6, 0, 0]
        )

    def start(self):
        line = self.line
        for p in range(self.pieces):
            self.send(self.src, line.i, p, line.has_right, line.has_left)
        self.own_copy().start()

    def step(self, s):
        line = self.line
        from_left, from_right = line.i - s, line.i + s
        for p in range(self.pieces):

            @pl.when(from_left >= 0)
            def _(p=p):
                self.arrived(0, from_left, p, line.c)
                self.send(self.out.at[from_left, line.c], from_left, p, line.has_right, None)

            @pl.when(from_right < line.chips)
            def _(p=p):
                self.arrived(1, from_right, p, line.c)
                self.send(self.out.at[from_right, line.c], from_right, p, None, line.has_left)

    def finish(self):
        line = self.line
        for j in range(line.chips):
            mine = self.out.at[j, line.c]
            for p in range(self.pieces):
                self.arrived(2, j, p, 1 - line.c)
                self.move(2, mine, j, p, line.sibling).wait_send()

                @pl.when((line.i >= j) & line.has_right)
                def _(j=j, p=p, mine=mine):
                    self.move(0, mine, j, p, line.right).wait_send()

                @pl.when((line.i <= j) & line.has_left)
                def _(j=j, p=p, mine=mine):
                    self.move(1, mine, j, p, line.left).wait_send()

        self.own_copy().wait()

    def run(self):
        self.start()
        for s in range(1, self.line.chips):
            self.step(s)
        self.finish()


def by_rows(rows, step, body):
    def one(k, carry):
        body(pl.ds(pl.multiple_of(k * step, step), step))
        return carry

    lax.fori_loop(0, rows // step, one, 0)


SUMS = 2


class Scatter:
    def __init__(self, line, part, bufs, sems):
        self.line, self.part, self.sems = line, part, sems
        self.own, self.sib, self.inn, self.out = bufs

    def copy(self, kind, src, dst, slot, target):
        return pltpu.make_async_remote_copy(
            src_ref=src,
            dst_ref=dst,
            send_sem=self.sems.at[(kind, *slot)],
            recv_sem=self.sems.at[(3 + kind, *slot)],
            device_id=target,
            device_id_type=MESH,
        )

    def to_sibling(self, j):
        line = self.line
        return self.copy(2, self.part.at[j, 1 - line.c], self.sib.at[j], (j, 0), line.sibling)

    def to_own(self, j):
        return pltpu.make_async_copy(
            self.part.at[j, self.line.c], self.own.at[j], self.sems.at[6, j, 0]
        )

    @property
    def size(self):
        return self.own.shape[1] // SUMS

    def along(self, way, j, p):
        line = self.line
        target = line.left if way else line.right
        span = pl.ds(p * self.size, self.size)
        return self.copy(way, self.out.at[j, span], self.inn.at[way, j, span], (j, p), target)

    def start(self):
        chips = self.line.chips
        order = []
        for k in range((chips + 1) // 2):
            order += [chips - 1 - k, k]
        for j in order[:chips]:
            self.to_sibling(j).start()
            self.to_own(j).start()

    def ready(self, j):
        self.to_sibling(j).wait_recv()
        self.to_own(j).wait()

    def rows_of(self, p, body):
        def shifted(r):
            body(pl.ds(pl.multiple_of(r.start + p * self.size, 16), r.size))

        by_rows(self.size, 16, shifted)

    def pass_on(self, way, j, first):
        self.ready(j)
        for p in range(SUMS):

            @pl.when(first)
            def _(p=p):
                def body(r):
                    total = self.own[j, r, :].astype(F32) + self.sib[j, r, :].astype(F32)
                    self.out[j, r, :] = total.astype(BF16)

                self.rows_of(p, body)

            @pl.when(jnp.logical_not(first))
            def _(p=p):
                self.along(way, j, p).wait_recv()

                def body(r):
                    total = self.own[j, r, :].astype(F32) + self.sib[j, r, :].astype(F32)
                    total += self.inn[way, j, r, :].astype(F32)
                    self.out[j, r, :] = total.astype(BF16)

                self.rows_of(p, body)

            self.along(way, j, p).start()

    def step(self, tau):
        line = self.line

        @pl.when((line.i <= tau) & line.has_right)
        def _():
            self.pass_on(0, line.chips - 1 - tau + line.i, line.i == 0)

        @pl.when((line.chips - 1 - line.i <= tau) & line.has_left)
        def _():
            self.pass_on(1, tau - (line.chips - 1 - line.i), line.i == line.chips - 1)

    def total(self, consume):
        line, i = self.line, self.line.i
        self.ready(i)
        for p in range(SUMS):

            @pl.when(line.has_left)
            def _(p=p):
                self.along(0, i, p).wait_recv()

            @pl.when(line.has_right)
            def _(p=p):
                self.along(1, i, p).wait_recv()

        rows = self.own.shape[1]

        def add(r, with_left, with_right):
            total = self.own[i, r, :].astype(F32) + self.sib[i, r, :].astype(F32)
            if with_left:
                total += self.inn[0, i, r, :].astype(F32)
            if with_right:
                total += self.inn[1, i, r, :].astype(F32)
            consume(r, total)

        @pl.when(line.has_left & line.has_right)
        def _():
            by_rows(rows, 16, lambda r: add(r, True, True))

        @pl.when(line.has_left & jnp.logical_not(line.has_right))
        def _():
            by_rows(rows, 16, lambda r: add(r, True, False))

        @pl.when(line.has_right & jnp.logical_not(line.has_left))
        def _():
            by_rows(rows, 16, lambda r: add(r, False, True))

    def finish(self):
        line = self.line
        for j in range(line.chips):
            self.to_sibling(j).wait_send()
            for p in range(SUMS):

                @pl.when(j > line.i)
                def _(j=j, p=p):
                    self.along(0, j, p).wait_send()

                @pl.when(j < line.i)
                def _(j=j, p=p):
                    self.along(1, j, p).wait_send()


PIECES = 2


def gather_sems(chips):
    return pltpu.SemaphoreType.DMA((7, chips, PIECES))


def scatter_bufs(chips, rows, width):
    return [
        pltpu.VMEM((chips, rows, width), BF16),
        pltpu.VMEM((chips, rows, width), BF16),
        pltpu.VMEM((2, chips, rows, width), BF16),
        pltpu.VMEM((chips, rows, width), BF16),
        pltpu.SemaphoreType.DMA((7, chips, SUMS)),
    ]


ANYWHERE = pl.BlockSpec(memory_space=pl.ANY)
IN_VMEM = pl.BlockSpec(memory_space=pltpu.VMEM)


def params(collective_id):
    return pltpu.CompilerParams(
        collective_id=collective_id, has_side_effects=True, vmem_limit_bytes=56 * 2**20
    )


def comm_cost(byte_count):
    return pl.CostEstimate(flops=0, transcendentals=0, bytes_accessed=40 * byte_count)


class Exchange:
    def __init__(self, axis, size):
        self.axis, self.size = axis, size
        self.me = lax.axis_index(axis)

    def peer(self, k):
        return lax.rem(self.me + k, self.size)

    def greet(self, barrier):
        for k in range(1, self.size):
            signal_to(barrier, {self.axis: self.peer(k)})

    def copy(self, k, src, dst, sems):
        return pltpu.make_async_remote_copy(
            src_ref=src,
            dst_ref=dst,
            send_sem=sems.at[0, k],
            recv_sem=sems.at[1, k],
            device_id={self.axis: self.peer(k)},
            device_id_type=MESH,
        )

    def sems(self):
        return pltpu.SemaphoreType.DMA((2, self.size))


def pair_sems(size):
    return pltpu.SemaphoreType.DMA((2, size))


def greet_all(exchanges, line=None, moves=None):
    barrier = pltpu.get_barrier_semaphore()
    count = 0
    for exchange in exchanges:
        exchange.greet(barrier)
        count += exchange.size - 1
    if line is not None:
        count += line.greet(barrier)
    if moves is not None:
        whether, source = moves

        @pl.when(whether)
        def _():
            signal_to(barrier, source)

        count += whether.astype(jnp.int32)
    pl.semaphore_wait(barrier, count)


def flip_copy(src, dst, bit, sems, *index):
    return pltpu.make_async_remote_copy(
        src_ref=src,
        dst_ref=dst,
        send_sem=sems.at[(0, *index)],
        recv_sem=sems.at[(1, *index)],
        device_id={"head": lax.axis_index("head") ^ (1 << bit)},
        device_id_type=MESH,
    )


def ff_entries(rows, n_head):
    bits = tuple(range(n_head.bit_length() - 1))
    back, half = bits[::-1], rows // 2
    return (
        (0, pl.ds(0, rows), bits),
        (1, pl.ds(0, rows), back),
        (2, pl.ds(0, half), bits),
        (2, pl.ds(half, half), back),
    )


def place_of_out_rows(n_head, n_blk):
    h, b = lax.axis_index("head"), lax.axis_index("blk")
    d = h * n_blk + b
    source = b * n_head + h
    return (d % n_head, d // n_head), (source // n_blk, source % n_blk)


PACK_ROWS = 24


def weight_pieces(b, q_cols, copies):
    kv = b // copies * HEAD_DIM
    return (
        (0, pl.ds(pl.multiple_of(b * q_cols, HEAD_DIM), q_cols), pl.ds(0, q_cols)),
        (1, pl.ds(pl.multiple_of(kv, HEAD_DIM), HEAD_DIM), pl.ds(q_cols, HEAD_DIM)),
        (2, pl.ds(pl.multiple_of(kv, HEAD_DIM), HEAD_DIM), pl.ds(q_cols + HEAD_DIM, HEAD_DIM)),
    )


PACK_ROWS = 24


def weight_pieces(b, q_cols, copies):
    kv = b // copies * HEAD_DIM
    return (
        (0, pl.ds(pl.multiple_of(b * q_cols, HEAD_DIM), q_cols), pl.ds(0, q_cols)),
        (1, pl.ds(pl.multiple_of(kv, HEAD_DIM), HEAD_DIM), pl.ds(q_cols, HEAD_DIM)),
        (2, pl.ds(pl.multiple_of(kv, HEAD_DIM), HEAD_DIM), pl.ds(q_cols + HEAD_DIM, HEAD_DIM)),
    )


class Spread:
    def __init__(self, full, entries, n_head, sems):
        self.full, self.entries, self.n_head, self.sems = full, entries, n_head, sems

    def copies(self, e, level):
        weight, part, order = self.entries[e]
        full = self.full[weight]
        bit = order[level]
        keys = [0]
        for low in order[:level]:
            keys += [key ^ (1 << low) for key in keys]
        for key in keys:
            there = key ^ (1 << bit)
            yield flip_copy(
                full.at[key, part], full.at[there, part], bit, self.sems, e, there
            )

    def level(self, level):
        for e in range(len(self.entries)):
            if level > 1:
                for copy in self.copies(e, level - 1):
                    copy.wait_recv()
            for copy in self.copies(e, level):
                copy.start()

    def start(self):
        self.level(1)

    def finish(self):
        levels = self.n_head.bit_length() - 1
        for level in range(2, levels):
            self.level(level)
        for e in range(len(self.entries)):
            for level in range(1, levels):
                for copy in self.copies(e, level):
                    copy.wait_send()
                    if level == levels - 1:
                        copy.wait_recv()

    @staticmethod
    def sem_shape(n_head):
        return pltpu.SemaphoreType.DMA((2, 4, n_head))


class Collect:
    def __init__(self, have, kept, inbox, total, entries, n_head, sems):
        self.have, self.kept, self.inbox, self.total = have, kept, inbox, total
        self.entries, self.n_head, self.sems = entries, n_head, sems

    def keys(self, order, level):
        keys = [0]
        for low in order[: len(order) - 1 - level]:
            keys += [key ^ (1 << low) for key in keys]
        return keys

    def slot(self, order, key):
        return self.keys(order, 0).index(key)

    def copies(self, e, level):
        weight, part, order = self.entries[e]
        bit = order[len(order) - 1 - level]
        for key in self.keys(order, level):
            slot = self.slot(order, key)
            if level == 0:
                src = self.have[weight].at[key ^ (1 << bit), part]
            else:
                src = self.kept[weight].at[self.slot(order, key ^ (1 << bit)), part]
            yield flip_copy(src, self.inbox[weight].at[level, slot, part], bit, self.sems, e, level, slot)

    def locals_(self):
        for e, (weight, part, order) in enumerate(self.entries):
            for key in self.keys(order, 0):
                slot = self.slot(order, key)
                yield pltpu.make_async_copy(
                    self.have[weight].at[key, part],
                    self.kept[weight].at[slot, part],
                    self.sems.at[2, e, 0, slot],
                )

    def start(self):
        for copy in self.locals_():
            copy.start()
        for e in range(len(self.entries)):
            for copy in self.copies(e, 0):
                copy.start()

    def finish(self):
        for copy in self.locals_():
            copy.wait()
        levels = self.n_head.bit_length() - 2
        for level in range(levels):
            last = level == levels - 1
            for e, (weight, part, order) in enumerate(self.entries):
                for copy in self.copies(e, level):
                    copy.wait_recv()
                for at, key in enumerate(self.keys(order, level)):
                    slot = self.slot(order, key)
                    kept, inbox = self.kept[weight], self.inbox[weight]
                    into = self.total[weight] if last else kept
                    where = at if last else slot

                    def body(r, part=part, slot=slot, kept=kept, inbox=inbox, into=into, where=where):
                        r = pl.ds(pl.multiple_of(r.start + part.start, 16), r.size)
                        value = kept[slot, r, :].astype(F32) + inbox[level, slot, r, :].astype(F32)
                        into[where, r, :] = value.astype(BF16)

                    by_rows(part.size, 16, body)
            for e in range(len(self.entries)):
                if not last:
                    for copy in self.copies(e, level + 1):
                        copy.start()
        for level in range(levels):
            for e in range(len(self.entries)):
                for copy in self.copies(e, level):
                    copy.wait_send()

    @staticmethod
    def sem_shape(n_head):
        levels = n_head.bit_length() - 2
        return pltpu.SemaphoreType.DMA((3, 4, levels, n_head // 2))


def last_scatter(
    partial_rows, w_grad, out_grad, pack, sums, hidden, gain, q_cols, copies, n_head, n_blk, collective_id
):
    total_rows, width = partial_rows.shape
    chips, count = n_blk // 2, total_rows // n_blk
    _, _, rows_here, columns = w_grad.shape
    n_sums = len(sums)
    entries = ff_entries(sums[0].shape[1], n_head) if sums else ()

    def kernel(part, w_src, o_src, g_src, *refs):
        ff_src, (x_ref, gain_ref), refs = refs[:n_sums], refs[n_sums : n_sums + 2], refs[n_sums + 2 :]
        out, wq_out, wk_out, wv_out, o_out, g_out = refs[:6]
        ff_out, refs = refs[6 : 6 + n_sums], refs[6 + n_sums :]
        bufs, sems = refs[:4], refs[4]
        w_in, w_sum, o_in, o_sum, g_in, g_sum, g_last = refs[5:12]
        w_sems, block_sems, o_sems, g_sems, pack_sems, moved, ff_sems, local = refs[12:]
        line = Line(n_blk)
        across, along = Exchange("head", n_head), Exchange("blk", n_blk)
        h, b = across.me, along.me
        (sh, sb), (th, tb) = place_of_out_rows(n_head, n_blk)
        stays = (th == h) & (tb == b)
        moves = jnp.logical_not(stays)
        greet_all((across, along), moves=(moves, {"head": sh, "blk": sb}))

        def w_copy(k):
            return across.copy(k, w_src.at[across.peer(k)], w_in.at[k], w_sems)

        def o_copy(k):
            return across.copy(k, o_src.at[across.peer(k)], o_in.at[k], o_sems)

        lanes = n_blk * rows_here

        def g_part(head):
            return g_src.at[:, pl.ds(pl.multiple_of(head * lanes, 128), lanes)]

        def g_copy(k):
            return across.copy(k, g_part(across.peer(k)), g_in.at[k], g_sems)

        def landings():
            kv = pl.ds(pl.multiple_of(b // copies * HEAD_DIM, HEAD_DIM), HEAD_DIM)
            return (
                wq_out.at[:, pl.ds(pl.multiple_of(b * q_cols, HEAD_DIM), q_cols)],
                wk_out.at[b % copies, :, kv],
                wv_out.at[b % copies, :, kv],
            )

        spans = (
            pl.ds(0, q_cols),
            pl.ds(q_cols, HEAD_DIM),
            pl.ds(q_cols + HEAD_DIM, HEAD_DIM),
        )

        def block_copies(k):
            for w, there in enumerate(landings()):
                yield along.copy(
                    k, w_sum.at[along.peer(k), :, spans[w]], there, block_sems.at[w]
                )

        def pack_copy(k):
            tile = along.peer(k) * rows_here // 128 * 128
            part = g_sum.at[:, pl.ds(pl.multiple_of(tile, 128), 128)]
            return along.copy(k, part, g_last.at[b], pack_sems)

        move_out = pltpu.make_async_remote_copy(
            src_ref=o_sum,
            dst_ref=o_out,
            send_sem=moved.at[0],
            recv_sem=moved.at[1],
            device_id={"head": th, "blk": tb},
            device_id_type=MESH,
        )
        keep_out = pltpu.make_async_copy(o_sum, o_out, moved.at[2])

        def hop(e):
            weight, part, order = entries[e]
            return flip_copy(
                ff_src[weight].at[1, part], ff_out[weight].at[part], order[0], ff_sems, e
            )

        own_w = pltpu.make_async_copy(w_src.at[h], w_in.at[0], local.at[0])
        own_g = pltpu.make_async_copy(g_part(h), g_in.at[0], local.at[1])
        own_blocks = [
            pltpu.make_async_copy(w_sum.at[b, :, spans[w]], there, local.at[4 + w])
            for w, there in enumerate(landings())
        ]
        own_o = pltpu.make_async_copy(o_src.at[h], o_in.at[0], local.at[3])
        scatter = Scatter(line, part, bufs, sems)
        scatter.start()
        own_w.start()
        own_g.start()
        own_o.start()
        for k in range(1, n_head):
            g_copy(k).start()
            w_copy(k).start()
        for k in range(1, n_head):
            o_copy(k).start()
        for e in range(len(entries)):
            hop(e).start()
        scatter.step(0)
        own_g.wait()
        for k in range(1, n_head):
            g_copy(k).wait_recv()
        g_sum[...] = sum(g_in[k] for k in range(n_head))
        own_tile = b * rows_here // 128 * 128
        g_last[b] = g_sum[:, pl.ds(pl.multiple_of(own_tile, 128), 128)]
        for k in range(1, n_blk):
            pack_copy(k).start()
        for tau in range(1, chips - 2):
            scatter.step(tau)
        own_w.wait()
        for k in range(1, n_head):
            w_copy(k).wait_recv()

        def add(j, carry):
            total = w_in[0, j].astype(F32)
            for k in range(1, n_head):
                total += w_in[k, j].astype(F32)
            w_sum[j] = total.astype(BF16)
            return carry

        lax.fori_loop(0, n_blk, add, 0)
        for one in own_blocks:
            one.start()
        for k in range(1, n_blk):
            for copy in block_copies(k):
                copy.start()

        scatter.step(chips - 2)
        own_o.wait()
        for k in range(1, n_head):
            o_copy(k).wait_recv()

        def add_out(r):
            total = o_in[0, r, :].astype(F32)
            for k in range(1, n_head):
                total += o_in[k, r, :].astype(F32)
            o_sum[r, :] = total.astype(BF16)

        by_rows(rows_here, 16, add_out)

        @pl.when(stays)
        def _():
            keep_out.start()

        @pl.when(jnp.logical_not(stays))
        def _():
            move_out.start()

        def consume(r, dxn):
            unit, factor = unit_of(x_ref[r, :].astype(F32))
            out[r, :] = unit_back(dxn * gain_ref[0:1, :], unit, factor)

        scatter.total(consume)
        for k in range(1, n_blk):
            pack_copy(k).wait_recv()
        g_out[...] = sum(g_last[k] for k in range(n_blk))
        scatter.finish()
        for one in own_blocks:
            one.wait()
        for k in range(1, n_head):
            g_copy(k).wait_send()
            o_copy(k).wait_send()
            w_copy(k).wait_send()
        for k in range(1, n_blk):
            pack_copy(k).wait_send()
            for copy in block_copies(k):
                copy.wait()
        for e in range(len(entries)):
            hop(e).wait()

        @pl.when(stays)
        def _():
            keep_out.wait()

        @pl.when(jnp.logical_not(stays))
        def _():
            move_out.wait()

    return pl.pallas_call(
        kernel,
        out_shape=(
            jax.ShapeDtypeStruct((count, width), F32),
            jax.ShapeDtypeStruct((rows_here, n_blk * q_cols), BF16),
            *[jax.ShapeDtypeStruct((copies, rows_here, n_blk // copies * HEAD_DIM), BF16)] * 2,
            jax.ShapeDtypeStruct((rows_here, width), BF16),
            jax.ShapeDtypeStruct((pack.shape[0], 128), F32),
            *(jax.ShapeDtypeStruct(one.shape[1:], BF16) for one in sums),
        ),
        in_specs=[ANYWHERE] * (4 + n_sums) + [IN_VMEM] * 2,
        out_specs=[IN_VMEM] + [ANYWHERE] * 4 + [IN_VMEM] + [ANYWHERE] * n_sums,
        scratch_shapes=[
            *scatter_bufs(chips, count, width),
            pltpu.VMEM((n_head, n_blk, rows_here, columns), BF16),
            pltpu.VMEM((n_blk, rows_here, columns), BF16),
            pltpu.VMEM((n_head, rows_here, width), BF16),
            pltpu.VMEM((rows_here, width), BF16),
            pltpu.VMEM((n_head, pack.shape[0], n_blk * rows_here), F32),
            pltpu.VMEM((pack.shape[0], n_blk * rows_here), F32),
            pltpu.VMEM((n_blk, pack.shape[0], 128), F32),
            pair_sems(n_head),
            pltpu.SemaphoreType.DMA((3, 2, n_blk)),
            pair_sems(n_head),
            pair_sems(n_head),
            pair_sems(n_blk),
            pltpu.SemaphoreType.DMA((3,)),
            pair_sems(max(1, len(entries))),
            pltpu.SemaphoreType.DMA((7,)),
        ],
        compiler_params=params(collective_id),
        cost_estimate=comm_cost(total_rows * width),
        name="last_scatter",
    )(
        partial_rows.astype(BF16).reshape(chips, 2, count, width),
        w_grad,
        out_grad.reshape(n_head, rows_here, width),
        pack,
        *sums,
        hidden,
        gain,
    )


ROWS = 256
CHUNKS = 2


def block_of(k, size=ROWS):
    return pl.ds(pl.multiple_of(k * size, size), size)


class View:
    def __init__(self, ref, rows):
        self.ref, self.rows = ref, rows
        self.at = self

    def __getitem__(self, index):
        if len(index) == 3:
            j, core, inner = index
            return self.ref.at[j, core, pl.ds(self.rows.start + inner.start, inner.size)]
        j, core = index
        return self.ref.at[j, core, self.rows]


def scatter_gather(
    partial_rows, prepare, between, inputs, outputs, beside, n_head, n_blk, collective_id
):
    total_rows, width = partial_rows.shape
    chips, count = n_blk // 2, total_rows // n_blk
    size = count // CHUNKS
    operands, results, result_specs, more_scratch, aliases, make = beside
    n_in, n_out, n_op, n_res = len(inputs), len(outputs), len(operands), len(results)

    def kernel(part, *refs):
        refs = list(refs)

        def take(n):
            taken = refs[:n]
            del refs[:n]
            return taken

        ins, ops, outs = take(n_in), take(n_op), take(n_out)
        (gathered,) = take(1)
        ress = take(n_res)
        (made,) = take(1)
        chunk_scratch = [take(6) for _ in range(CHUNKS)]
        line = Line(n_blk)
        across = Exchange("head", n_head)
        greet_all((across,), line)
        prepare(outs)
        other = make(ops, ress, refs)
        scatters, gathers = [], []
        for q in range(CHUNKS):
            own, sib, inn, outgoing, sems, g_sems = chunk_scratch[q]
            rows = pl.ds(q * size, size)
            scatters.append(Scatter(line, View(part, rows), (own, sib, inn, outgoing), sems))
            gathers.append(Gather(line, made.at[rows], View(gathered, rows), g_sems))

        def turn(q):
            def consume(r, value):
                r = pl.ds(pl.multiple_of(r.start + q * size, 16), r.size)
                made[r, :] = between(r, value, ins, outs).astype(BF16)

            scatters[q].total(consume)
            gathers[q].start()

        scatters[0].start()
        other.start()
        for q in range(1, CHUNKS):
            scatters[q].start()
        for q in range(CHUNKS):
            for tau in range(chips - 1):
                scatters[q].step(tau)
                if q:
                    gathers[q - 1].step(tau + 1)
            turn(q)
        for s in range(1, chips):
            gathers[-1].step(s)
        for q in range(CHUNKS):
            scatters[q].finish()
            gathers[q].finish()
        other.finish()

    per_chunk = []
    for _ in range(CHUNKS):
        per_chunk += [*scatter_bufs(chips, size, width), gather_sems(chips)]
    given = pl.pallas_call(
        kernel,
        out_shape=(
            *outputs,
            jax.ShapeDtypeStruct((chips, 2, count, width), BF16),
            *results,
        ),
        in_specs=[ANYWHERE] + [IN_VMEM] * n_in + [ANYWHERE] * n_op,
        out_specs=[IN_VMEM] * n_out + [ANYWHERE] + list(result_specs),
        scratch_shapes=[pltpu.VMEM((count, width), BF16), *per_chunk, *more_scratch],
        input_output_aliases={1 + n_in + i: n_out + 1 + o for i, o in aliases.items()},
        compiler_params=params(collective_id),
        cost_estimate=comm_cost(2 * total_rows * width),
        name="scatter_gather",
    )(partial_rows.astype(BF16).reshape(chips, 2, count, width), *inputs, *operands)
    return (
        *given[:n_out],
        given[n_out].reshape(total_rows, width),
        *given[n_out + 1 :],
    )


def spread_beside(full, n_head):
    entries = ff_entries(full[0].shape[1], n_head)

    def make(ops, ress, scratch):
        return Spread(ress, entries, n_head, scratch[0])

    return (
        tuple(full),
        tuple(jax.ShapeDtypeStruct(w.shape, w.dtype) for w in full),
        [ANYWHERE] * 3,
        [Spread.sem_shape(n_head)],
        {0: 0, 1: 1, 2: 2},
        make,
    )


def collect_beside(have, carried, n_head):
    entries = ff_entries(have[0].shape[1], n_head)
    levels = n_head.bit_length() - 2
    shapes = [(n_head // 2, *one.shape[1:]) for one in have]

    def make(ops, ress, scratch):
        kept, inbox = scratch[0:3], scratch[3:6]
        return Collect(ops[:3], kept, inbox, ress[:3], entries, n_head, scratch[6])

    return (
        (*have, carried),
        (
            *(jax.ShapeDtypeStruct((2, *one.shape[1:]), BF16) for one in have),
            jax.ShapeDtypeStruct(carried.shape, carried.dtype),
        ),
        [IN_VMEM] * 3 + [ANYWHERE],
        [
            *(pltpu.VMEM(shape, BF16) for shape in shapes),
            *(pltpu.VMEM((levels, *shape), BF16) for shape in shapes),
            Collect.sem_shape(n_head),
        ],
        {3: 3},
        make,
    )


class Rows:
    def __init__(self, ref, q, size, chips):
        self.ref, self.base, self.size = ref, q * size * chips * 2, size
        self.at = self

    def rows(self, j, core, start=0, count=None):
        first = self.base + (j * 2 + core) * self.size + start
        return pl.ds(pl.multiple_of(first, 16), count or self.size)

    def __getitem__(self, index):
        j, core, *inner = index
        if inner:
            return self.ref.at[self.rows(j, core, inner[0].start, inner[0].size)]
        return self.ref.at[self.rows(j, core)]


class OwnRows:
    def __init__(self, rows, core):
        self.view, self.core = rows, core
        self.shape = (0, rows.size)

    def __getitem__(self, index):
        j, r, _ = index
        return self.view.ref[self.view.rows(j, self.core, r.start, r.size), :]


class LocalScatter(Scatter):
    def __init__(self, line, part, bufs, sems):
        super().__init__(line, part, (OwnRows(part, line.c), *bufs), sems)

    def start(self):
        chips = self.line.chips
        order = []
        for k in range((chips + 1) // 2):
            order += [chips - 1 - k, k]
        for j in order[:chips]:
            self.to_sibling(j).start()

    def ready(self, j):
        self.to_sibling(j).wait_recv()


def turned(values, cosine, sine):
    return values * cosine + pltpu.roll(values, HEAD_DIM // 2, 1) * sine


def local_params(collective_id):
    if collective_id is None:
        return pltpu.CompilerParams(vmem_limit_bytes=60 * 2**20)
    return pltpu.CompilerParams(
        collective_id=collective_id, has_side_effects=True, vmem_limit_bytes=60 * 2**20
    )


def spec_of(shape, dtype):
    return jax.ShapeDtypeStruct(shape, dtype)


def attention_forward(
    rows, weights, small, w_out, ids, cot, cot_rows, ff, q_cols, copies, n_head, n_blk, collective_id
):
    count, width = rows.shape
    chips, pack = n_blk // 2, n_blk * count
    rows_here, rows_ff = w_out.shape[0], ff[0].shape[0]
    entries = ff_entries(rows_ff, n_head)
    columns, q_here = q_cols + 2 * HEAD_DIM, q_cols // HEAD_DIM
    together, n_all = 128 // rows_here, n_head * n_blk
    blocks = pack // ROWS
    scale = 1.0 / math.sqrt(HEAD_DIM)

    def kernel(src, cot_ref, *refs):
        w_src, (pack_src, out_src), ff_src = refs[:3], refs[3:5], refs[5:8]
        pos, seg, blk_ids = refs[8:11]
        part_hbm, xn_hbm, p_hbm, cot_hbm = refs[11:15]
        ff_out, refs = refs[15:18], refs[18:]
        w_ref, vec_ref, gate_ref, cos_ref, sin_ref = refs[:5]
        lin_ref, q_ref, k_ref, v_ref, sig_ref, o_ref, gated_ref, o_rows = refs[5:13]
        x_s, xn_s, p_s, low_ref, code_ref, key_ref, g_all, xn_sem, p_sem, part_sem = refs[13:23]
        sems, block_sems, w_sems, pack_sems, g_sems, moved, local = refs[23:30]
        cot_sems, out_sems, ff_sems = refs[30:]
        line = Line(n_blk)
        across, along = Exchange("head", n_head), Exchange("blk", n_blk)
        h, b = across.me, along.me
        h_me, b_me = h, b
        (th, tb), (sh, sb) = place_of_out_rows(n_head, n_blk)
        stays = (th == h) & (tb == b)
        moves = jnp.logical_not(stays)
        greet_all((across, along), moves=(moves, {"head": sh, "blk": sb}))

        def at_rows(head, blk):
            first = (head * n_blk + blk) * rows_here
            return pl.ds(pl.multiple_of(first, rows_here), rows_here)

        def of_head(head):
            size = n_blk * rows_here
            return pl.ds(pl.multiple_of(head * size, size), size)

        def out_rows_of(head):
            return o_rows.at[pl.ds(pl.multiple_of(head * rows_here, rows_here), rows_here)]

        def block_copies(k):
            for w, there, here in weight_pieces(along.peer(k), q_cols, copies):
                yield along.copy(
                    k, w_src[w].at[:, there], w_ref.at[at_rows(h, b), here], block_sems.at[w]
                )

        def pack_copy(k):
            return along.copy(k, pack_src, g_all.at[h, b], pack_sems)

        def w_copy(k):
            return across.copy(k, w_ref.at[of_head(h)], w_ref.at[of_head(h)], w_sems)

        def g_copy(k):
            return across.copy(k, g_all.at[h], g_all.at[h], g_sems)

        def out_copy(k):
            return across.copy(k, out_rows_of(h), out_rows_of(h), out_sems)

        def hop(e):
            weight, part, order = entries[e]
            return flip_copy(
                ff_src[weight].at[part], ff_out[weight].at[part], order[0], ff_sems, e
            )

        move_out = pltpu.make_async_remote_copy(
            src_ref=out_src,
            dst_ref=out_rows_of(th),
            send_sem=moved.at[0],
            recv_sem=moved.at[1],
            device_id={"head": th, "blk": tb},
            device_id_type=MESH,
        )
        keep_out = pltpu.make_async_copy(out_src, out_rows_of(h), moved.at[2])
        locals_ = [
            pltpu.make_async_copy(
                w_src[w].at[:, there], w_ref.at[at_rows(h, b), here], local.at[w]
            )
            for w, there, here in weight_pieces(b, q_cols, copies)
        ] + [pltpu.make_async_copy(pack_src, g_all.at[h, b], local.at[3])]
        for k in range(1, n_blk):
            for copy in block_copies(k):
                copy.start()
        tokens = Gather(line, src, Rows(x_s, 0, count, chips), sems)
        gather = Gather(line, cot_ref.at[pl.ds(0, cot_rows)], cot_hbm, cot_sems)
        for k in range(1, n_blk):
            pack_copy(k).start()
        for one in locals_:
            one.start()

        @pl.when(stays)
        def _():
            keep_out.start()

        @pl.when(moves)
        def _():
            move_out.start()

        for e in (2, 3):
            hop(e).start()
        half = HEAD_DIM // 2
        index = lax.broadcasted_iota(jnp.int32, (half, ROWS), 0).astype(F32)
        frequency = jnp.exp(index * (-2.0 * math.log(ROPE_BASE) / HEAD_DIM))
        pack_row = pl.ds(h, 1)
        key_ref[...] = (seg[pack_row, :] * pack + blk_ids[pack_row, :]).astype(F32)

        def tables(n, carry):
            r = block_of(n)
            angles = frequency * pos[pack_row, r].astype(F32)
            cosine, sine = jnp.cos(angles), jnp.sin(angles)
            cos_ref[r, :] = jnp.concatenate([cosine, cosine], axis=0).T
            sin_ref[r, :] = jnp.concatenate([-sine, sine], axis=0).T
            low_ref[r, :] = jnp.broadcast_to((seg[pack_row, r] * pack).astype(F32), (128, ROWS)).T
            code_ref[r, :] = jnp.broadcast_to(key_ref[:, r], (128, ROWS)).T
            return carry

        lax.fori_loop(0, pack // ROWS, tables, 0)
        for one in locals_:
            one.wait()
        for k in range(1, n_blk):
            pack_copy(k).wait_recv()
        for k in range(1, n_head):
            g_copy(k).start()
        for k in range(1, n_blk):
            for copy in block_copies(k):
                copy.wait_recv()
        tokens.start()
        for k in range(1, n_head):
            w_copy(k).start()

        @pl.when(stays)
        def _():
            keep_out.wait()

        @pl.when(moves)
        def _():
            move_out.wait_recv()

        for k in range(1, n_head):
            out_copy(k).start()
        for s in range(1, chips):
            tokens.step(s)
        gather.start()
        for e in (0, 1):
            hop(e).start()
        for k in range(1, n_head):
            g_copy(k).wait()
        everyone = [g_all.at[d // n_blk, d % n_blk] for d in range(n_all)]
        vec_ref[...] = jnp.zeros_like(vec_ref)
        for t in range(width // 128):
            tile = sum(one[...] for one in everyone[t * together : (t + 1) * together])
            vec_ref[0:2, t * 128 : (t + 1) * 128] = tile[0:2]
            gate_ref[:, t * 128 : (t + 1) * 128] = tile[8:].astype(BF16)
        vec_ref[2:4, 0:128] = sum(one[2:4, :] for one in everyone)
        tokens.finish()
        for k in range(1, n_head):
            w_copy(k).wait()

        def xn_store(n):
            return pltpu.make_async_copy(
                xn_s.at[block_of(n)], xn_hbm.at[block_of(n)], xn_sem.at[n]
            )

        def p_store(h, n):
            return pltpu.make_async_copy(
                p_s.at[h, block_of(n)], p_hbm.at[h, block_of(n)], p_sem.at[h, n]
            )

        def part_store(n):
            return pltpu.make_async_copy(
                x_s.at[block_of(n)], part_hbm.at[block_of(n)], part_sem.at[n]
            )

        def project(n, carry):
            r = block_of(n)
            unit, _ = unit_of(x_s[r, :].astype(F32))
            xn = (unit * vec_ref[0:1, :]).astype(BF16)
            xn_s[r, :] = xn
            xn_store(n).start()
            lin = mm(xn, w_ref[...])
            lin_ref[r, :] = lin
            gate = mm_nt(xn, gate_ref[...])
            one_of = lax.broadcasted_iota(jnp.int32, (ROWS, HEADS), 1)
            lane = lax.broadcasted_iota(jnp.int32, (ROWS, GATE_PAD), 1)
            sigs = jnp.zeros((ROWS, GATE_PAD), F32)
            for h in range(q_here):
                own = jnp.where(one_of == b_me * q_here + h, gate, 0.0)
                own = jax.nn.sigmoid(jnp.sum(own, axis=1, keepdims=True))
                sigs = jnp.where(lane == h, own, sigs)
            sig_ref[r, :] = sigs
            cosine, sine = cos_ref[r, :], sin_ref[r, :]
            for h in range(q_here):
                at = slice(h * HEAD_DIM, (h + 1) * HEAD_DIM)
                unit_q, _ = unit_of(lin[:, at])
                q_ref[r, at] = turned(unit_q * vec_ref[2:3, :HEAD_DIM], cosine, sine).astype(BF16)
            unit_k, _ = unit_of(lin[:, q_cols : q_cols + HEAD_DIM])
            k_ref[r, :] = turned(unit_k * vec_ref[3:4, :HEAD_DIM], cosine, sine).astype(BF16)
            v_ref[r, :] = lin[:, q_cols + HEAD_DIM :].astype(BF16)
            return carry

        lax.fori_loop(0, blocks, project, 0)
        gather.step(1)
        for k in range(1, n_head):
            out_copy(k).wait_recv()

        def attend(n, carry):
            r = block_of(n)
            visible = (key_ref[...] >= low_ref[r, 0:1]) & (key_ref[...] <= code_ref[r, 0:1])
            for h in range(q_here):
                at = slice(h * HEAD_DIM, (h + 1) * HEAD_DIM)
                scores = mm_nt(q_ref[r, at], k_ref[...]) * scale
                scores = jnp.where(visible, scores, MASKED)
                top = jnp.max(scores, axis=-1, keepdims=True)
                weights = jnp.exp(scores - top)
                weights = weights * (1.0 / jnp.sum(weights, axis=-1, keepdims=True))
                prob = weights.astype(BF16)
                p_s[h, r, :] = prob
                p_store(h, n).start()
                out = mm(prob, v_ref[...]).astype(BF16)
                o_ref[r, at] = out
                gated_ref[r, at] = (out.astype(F32) * sig_ref[r, h : h + 1]).astype(BF16)
            x_s[r, :] = mm(gated_ref[r, :], o_rows[...]).astype(BF16)
            part_store(n).start()
            return carry

        lax.fori_loop(0, blocks - 1, attend, 0)
        gather.step(2)
        lax.fori_loop(blocks - 1, blocks, attend, 0)
        for s in range(3, chips):
            gather.step(s)
        gather.finish()
        for k in range(1, n_head):
            out_copy(k).wait_send()
        for e in range(len(entries)):
            hop(e).wait()
        for k in range(1, n_blk):
            pack_copy(k).wait_send()
            for copy in block_copies(k):
                copy.wait_send()

        @pl.when(moves)
        def _():
            move_out.wait_send()

        for n in range(blocks):
            xn_store(n).wait()
            part_store(n).wait()
            for h in range(q_here):
                p_store(h, n).wait()

    dma = pltpu.SemaphoreType.DMA
    return pl.pallas_call(
        kernel,
        out_shape=(
            spec_of((pack, width), BF16),
            spec_of((pack, width), BF16),
            spec_of((q_here, pack, pack), BF16),
            spec_of((chips, 2, cot_rows, width), BF16),
            *(spec_of(w.shape, BF16) for w in ff),
            spec_of((width, columns), BF16),
            spec_of((8, width), F32),
            spec_of((HEADS, width), BF16),
            spec_of((pack, HEAD_DIM), F32),
            spec_of((pack, HEAD_DIM), F32),
            spec_of((pack, columns), F32),
            spec_of((pack, q_cols), BF16),
            spec_of((pack, HEAD_DIM), BF16),
            spec_of((pack, HEAD_DIM), BF16),
            spec_of((pack, GATE_PAD), F32),
            spec_of((pack, q_cols), BF16),
            spec_of((pack, q_cols), BF16),
            spec_of((q_cols, width), BF16),
        ),
        in_specs=[IN_VMEM] * 2 + [ANYWHERE] * 8 + [IN_VMEM] * 3,
        out_specs=[ANYWHERE] * 7 + [IN_VMEM] * 13,
        scratch_shapes=[
            pltpu.VMEM((pack, width), BF16),
            pltpu.VMEM((pack, width), BF16),
            pltpu.VMEM((q_here, pack, pack), BF16),
            pltpu.VMEM((pack, 128), F32),
            pltpu.VMEM((pack, 128), F32),
            pltpu.VMEM((1, pack), F32),
            pltpu.VMEM((n_head, n_blk, PACK_ROWS, 128), F32),
            dma((blocks,)),
            dma((q_here, blocks)),
            dma((blocks,)),
            gather_sems(chips),
            dma((3, 2, n_blk)),
            pair_sems(n_head),
            pair_sems(n_blk),
            pair_sems(n_head),
            dma((3,)),
            dma((4,)),
            gather_sems(chips),
            pair_sems(n_head),
            pair_sems(len(entries)),
        ],
        compiler_params=local_params(collective_id),
        cost_estimate=comm_cost(pack * width),
        name="attention_forward",
    )(rows, cot, *weights, small, w_out, *ff, *ids)


def attention_backward(
    dy, xn, p, saved, w_attn, vec, gates, tables, mlp_gain_part, q_here, beside=None
):
    pack, width = dy.shape
    columns = w_attn.shape[1]
    q_cols = q_here * HEAD_DIM
    blocks = pack // ROWS
    scale = 1.0 / math.sqrt(HEAD_DIM)

    have, n_head, collective_id = beside or ((), 0, None)
    n_have = len(have)
    sum_scratch = []
    if have:
        entries = ff_entries(have[0].shape[1], n_head)
        sum_scratch = [pair_sems(len(entries))]

    def kernel(dy_hbm, xn_hbm, p_hbm, *refs):
        have_refs, refs = refs[:n_have], refs[n_have:]
        n_plain = 14 + 4
        plain, more = refs[:n_plain], refs[n_plain:]
        got, more = more[:n_have], more[n_have:]
        plain_scratch, sems = more[:14], more[14:]
        if not have:
            return local(dy_hbm, xn_hbm, p_hbm, *plain, *plain_scratch)
        greet_all((Exchange("head", n_head),))
        copies = [
            flip_copy(have_refs[w].at[1, part], got[w].at[part], order[0], sems[0], e)
            for e, (w, part, order) in enumerate(entries)
        ]
        for copy in copies:
            copy.start()
        local(dy_hbm, xn_hbm, p_hbm, *plain, *plain_scratch)
        for copy in copies:
            copy.wait()

    def local(dy_hbm, xn_hbm, p_hbm, lin_ref, q_ref, k_ref, v_ref, sig_ref, o_ref, *refs):
        gated_ref, o_rows, w_ref, vec_ref, gate_ref, cos_ref, sin_ref, mlp_ref = refs[:8]
        dxn_hbm, dw_ref, pack_ref, dout_ref = refs[8:12]
        dy_s, xn_s, p_s, do_s, delta_s, dgate_s, dlin_s, dk_s, dv_s, dgq_s = refs[12:22]
        dy_sem, xn_sem, p_sem, out_sem = refs[22:]
        first_head = lax.axis_index("blk") * q_here

        def dy_load(n):
            return pltpu.make_async_copy(
                dy_hbm.at[block_of(n)], dy_s.at[block_of(n)], dy_sem.at[n]
            )

        def p_load(h, n):
            return pltpu.make_async_copy(
                p_hbm.at[h, block_of(n)], p_s.at[h, block_of(n)], p_sem.at[h, n]
            )

        def dxn_store(n):
            return pltpu.make_async_copy(
                dy_s.at[block_of(n)], dxn_hbm.at[block_of(n)], out_sem.at[n]
            )

        xn_load = pltpu.make_async_copy(xn_hbm, xn_s, xn_sem)
        for n in range(blocks):
            dy_load(n).start()
        for n in range(blocks):
            for h in range(q_here):
                p_load(h, n).start()
        xn_load.start()

        def through_gate(n, carry):
            r = block_of(n)
            dy_load(n).wait()
            dgated = mm_nt(dy_s[r, :], o_rows[...])
            lane = lax.broadcasted_iota(jnp.int32, (ROWS, GATE_PAD), 1)
            dgates = jnp.zeros((ROWS, GATE_PAD), F32)
            deltas = jnp.zeros((ROWS, GATE_PAD), F32)
            for h in range(q_here):
                at = slice(h * HEAD_DIM, (h + 1) * HEAD_DIM)
                sig = sig_ref[r, h : h + 1]
                out = o_ref[r, at].astype(F32)
                do = (dgated[:, at] * sig).astype(BF16)
                do_s[r, at] = do
                dgate = jnp.sum(dgated[:, at] * out, axis=-1, keepdims=True) * sig * (1.0 - sig)
                delta = jnp.sum(do.astype(F32) * out, axis=-1, keepdims=True)
                dgates = jnp.where(lane == first_head + h, dgate, dgates)
                deltas = jnp.where(lane == h, delta, deltas)
            dgate_s[r, :] = dgates.astype(BF16)
            delta_s[r, :] = deltas
            return carry

        lax.fori_loop(0, blocks, through_gate, 0)

        def out_grad(n, carry):
            c = block_of(n)
            dout_ref[:, c] = mm_tn(gated_ref[...], dy_s[:, c]).astype(BF16)
            return carry

        lax.fori_loop(0, width // ROWS, out_grad, 0)
        dk_s[...] = jnp.zeros_like(dk_s)
        dv_s[...] = jnp.zeros_like(dv_s)
        dgq_s[...] = jnp.zeros_like(dgq_s)

        def into_lin(grad, lin, gain, r):
            grad = turned(grad.astype(BF16).astype(F32), cos_ref[r, :], -sin_ref[r, :])
            unit, factor = unit_of(lin)
            return unit_back(grad * gain, unit, factor).astype(BF16), grad * unit

        def attend(n, carry):
            r = block_of(n)
            for h in range(q_here):
                at = slice(h * HEAD_DIM, (h + 1) * HEAD_DIM)
                p_load(h, n).wait()
                do, prob, q = do_s[r, at], p_s[h, r, :], q_ref[r, at]
                dp = mm_nt(do, v_ref[...])
                ds = (prob.astype(F32) * (dp - delta_s[r, h : h + 1])).astype(BF16)
                dq = mm(ds, k_ref[...]) * scale
                dk_s[...] += mm(q.T, ds)
                dv_s[...] += mm(do.T, prob)
                dlin, part = into_lin(dq, lin_ref[r, at], vec_ref[2:3, :HEAD_DIM], r)
                dlin_s[r, at] = dlin
                dgq_s[...] += jnp.sum(part.reshape(ROWS // 8, 8, HEAD_DIM), axis=0)
            return carry

        lax.fori_loop(0, blocks, attend, 0)
        every = pl.ds(0, pack)
        k_cols = slice(q_cols, q_cols + HEAD_DIM)
        dlin, part = into_lin(
            dk_s[...].T * scale, lin_ref[:, k_cols], vec_ref[3:4, :HEAD_DIM], every
        )
        dlin_s[:, k_cols] = dlin
        dgk = jnp.sum(part, axis=0, keepdims=True)
        dgq = jnp.sum(dgq_s[...], axis=0, keepdims=True)
        pack_ref[HEADS:, :] = jnp.zeros((PACK_ROWS - HEADS, width), F32)
        pack_ref[HEADS : HEADS + 1, :] = jnp.sum(mlp_ref[...], axis=0, keepdims=True)
        for t in range(width // HEAD_DIM):
            lanes = slice(t * HEAD_DIM, (t + 1) * HEAD_DIM)
            pack_ref[HEADS + 1 : HEADS + 2, lanes] = dgq
            pack_ref[HEADS + 2 : HEADS + 3, lanes] = dgk
        dlin_s[:, q_cols + HEAD_DIM :] = dv_s[...].T.astype(BF16)

        def into_x(n, carry):
            r = block_of(n)
            dxn = mm_nt(dlin_s[r, :], w_ref[...]) + mm(dgate_s[r, :HEADS], gate_ref[...])
            dy_s[r, :] = dxn.astype(BF16)
            dxn_store(n).start()
            return carry

        lax.fori_loop(0, blocks, into_x, 0)
        xn_load.wait()
        dgate_t = dgate_s[...].astype(F32).T[:HEADS].astype(BF16)

        def weights(n, carry):
            c = block_of(n)
            xn_cols = xn_s[:, c]
            dw_ref[c, :] = mm_tn(xn_cols, dlin_s[...]).astype(BF16)
            pack_ref[:HEADS, c] = mm(dgate_t, xn_cols)
            return carry

        lax.fori_loop(0, width // ROWS, weights, 0)
        for n in range(blocks):
            dxn_store(n).wait()

    return pl.pallas_call(
        kernel,
        out_shape=(
            spec_of((pack, width), BF16),
            spec_of((width, columns), BF16),
            spec_of((PACK_ROWS, width), F32),
            spec_of((q_cols, width), BF16),
            *(spec_of(one.shape[1:], BF16) for one in have),
        ),
        in_specs=[ANYWHERE] * (3 + n_have) + [IN_VMEM] * 14,
        out_specs=[ANYWHERE] + [IN_VMEM] * 3 + [ANYWHERE] * n_have,
        scratch_shapes=[
            pltpu.VMEM((pack, width), BF16),
            pltpu.VMEM((pack, width), BF16),
            pltpu.VMEM((q_here, pack, pack), BF16),
            pltpu.VMEM((pack, q_cols), BF16),
            pltpu.VMEM((pack, GATE_PAD), F32),
            pltpu.VMEM((pack, GATE_PAD), BF16),
            pltpu.VMEM((pack, columns), BF16),
            pltpu.VMEM((HEAD_DIM, pack), F32),
            pltpu.VMEM((HEAD_DIM, pack), F32),
            pltpu.VMEM((8, HEAD_DIM), F32),
            pltpu.SemaphoreType.DMA((blocks,)),
            pltpu.SemaphoreType.DMA,
            pltpu.SemaphoreType.DMA((q_here, blocks)),
            pltpu.SemaphoreType.DMA((blocks,)),
            *sum_scratch,
        ],
        compiler_params=local_params(collective_id),
        name="attention_backward",
    )(dy, xn, p, *have, *saved, w_attn, vec, gates, *tables, mlp_gain_part)


def attention_end(
    dy, xn, p, mlp_part, ff_sums, saved, w_attn, vec, gates, tables, token_rows, q_here, copies,
    n_head, n_blk, collective_id
):
    pack, width = dy.shape
    columns = w_attn.shape[1]
    q_cols = q_here * HEAD_DIM
    blocks = pack // ROWS
    scale = 1.0 / math.sqrt(HEAD_DIM)
    chips, count = n_blk // 2, pack // n_blk
    rows_here = width // (n_head * n_blk)
    lanes = n_blk * rows_here
    entries = ff_entries(ff_sums[0].shape[1], n_head)

    def kernel(dy_hbm, xn_hbm, p_hbm, mlp_hbm, *refs):
        refs = list(refs)

        def take(n):
            taken = refs[:n]
            del refs[:n]
            return taken

        ff_src = take(3)
        lin_ref, q_ref, k_ref, v_ref, sig_ref, o_ref, gated_ref, o_rows = take(8)
        w_ref, vec_ref, gate_ref, cos_ref, sin_ref = take(5)
        x_ref, middle_ref, dmid_ref, mlp_gain_ref = take(4)
        layer_out, input_grad, g_out, wq_out, wk_out, wv_out, o_out = take(7)
        ff_out = take(3)
        dy_s, xn_s, p_s, do_s, delta_s, dgate_s, dlin_s, dk_s, dv_s, dgq_s = take(10)
        dw_s, pack_s, dout_s, w_in, w_sum, o_in, o_sum, g_in, g_sum, g_last = take(10)
        mlp_scratch, dxn_scratch, (xg_s,) = take(5), take(4), take(1)
        dy_sem, xn_sem, p_sem = take(3)
        w_sems, block_sems, o_sems, g_sems, pack_sems, moved, ff_sems, local = refs
        line = Line(n_blk)
        across, along = Exchange("head", n_head), Exchange("blk", n_blk)
        h, b = across.me, along.me
        first_head = b * q_here
        (sh, sb), (th, tb) = place_of_out_rows(n_head, n_blk)
        stays = (th == h) & (tb == b)
        moves = jnp.logical_not(stays)
        greet_all((across, along), moves=(moves, {"head": sh, "blk": sb}))

        def dy_load(n):
            return pltpu.make_async_copy(
                dy_hbm.at[block_of(n)], dy_s.at[block_of(n)], dy_sem.at[n]
            )

        def p_load(head, n):
            return pltpu.make_async_copy(
                p_hbm.at[head, block_of(n)], p_s.at[head, block_of(n)], p_sem.at[head, n]
            )

        def of_head(head):
            return pl.ds(pl.multiple_of(head * lanes, lanes), lanes)

        def of_blk(blk):
            return pl.ds(pl.multiple_of(blk * rows_here, rows_here), rows_here)

        def out_of(head):
            return dout_s.at[pl.ds(pl.multiple_of(head * rows_here, rows_here), rows_here)]

        def w_copy(k):
            return across.copy(k, dw_s.at[of_head(across.peer(k))], w_in.at[k], w_sems)

        def o_copy(k):
            return across.copy(k, out_of(across.peer(k)), o_in.at[k], o_sems)

        def g_part(head):
            return pack_s.at[:, pl.ds(pl.multiple_of(head * lanes, 128), lanes)]

        def g_copy(k):
            return across.copy(k, g_part(across.peer(k)), g_in.at[k], g_sems)

        def landings():
            kv = pl.ds(pl.multiple_of(b // copies * HEAD_DIM, HEAD_DIM), HEAD_DIM)
            return (
                wq_out.at[:, pl.ds(pl.multiple_of(b * q_cols, HEAD_DIM), q_cols)],
                wk_out.at[b % copies, :, kv],
                wv_out.at[b % copies, :, kv],
            )

        spans = (
            pl.ds(0, q_cols),
            pl.ds(q_cols, HEAD_DIM),
            pl.ds(q_cols + HEAD_DIM, HEAD_DIM),
        )

        def block_copies(k):
            for w, there in enumerate(landings()):
                src = w_sum.at[of_blk(along.peer(k)), spans[w]]
                yield along.copy(k, src, there, block_sems.at[w])

        def tile_of(blk):
            return pl.ds(pl.multiple_of(blk * rows_here // 128 * 128, 128), 128)

        def pack_copy(k):
            return along.copy(k, g_sum.at[:, tile_of(along.peer(k))], g_last.at[b], pack_sems)

        move_out = pltpu.make_async_remote_copy(
            src_ref=o_sum,
            dst_ref=o_out,
            send_sem=moved.at[0],
            recv_sem=moved.at[1],
            device_id={"head": th, "blk": tb},
            device_id_type=MESH,
        )
        keep_out = pltpu.make_async_copy(o_sum, o_out, moved.at[2])
        hops = [
            flip_copy(ff_src[w].at[1, part], ff_out[w].at[part], order[0], ff_sems, e)
            for e, (w, part, order) in enumerate(entries)
        ]
        own_blocks = [
            pltpu.make_async_copy(w_sum.at[of_blk(b), spans[w]], there, local.at[w])
            for w, there in enumerate(landings())
        ]
        mlp = Scatter(line, mlp_hbm, mlp_scratch[:4], mlp_scratch[4])
        dxn = LocalScatter(
            line, Rows(dy_s, 0, count, chips), dxn_scratch[:3], dxn_scratch[3]
        )
        xn_load = pltpu.make_async_copy(xn_hbm, xn_s, xn_sem)
        for n in range(blocks):
            dy_load(n).start()
        mlp.start()
        for n in range(blocks):
            for head in range(q_here):
                p_load(head, n).start()
        xn_load.start()
        for hop in hops[2:]:
            hop.start()

        def through_gate(n, carry):
            r = block_of(n)
            dy_load(n).wait()
            dgated = mm_nt(dy_s[r, :], o_rows[...])
            lane = lax.broadcasted_iota(jnp.int32, (ROWS, GATE_PAD), 1)
            dgates = jnp.zeros((ROWS, GATE_PAD), F32)
            deltas = jnp.zeros((ROWS, GATE_PAD), F32)
            for head in range(q_here):
                at = slice(head * HEAD_DIM, (head + 1) * HEAD_DIM)
                sig = sig_ref[r, head : head + 1]
                out = o_ref[r, at].astype(F32)
                do = (dgated[:, at] * sig).astype(BF16)
                do_s[r, at] = do
                dgate = jnp.sum(dgated[:, at] * out, axis=-1, keepdims=True) * sig * (1.0 - sig)
                delta = jnp.sum(do.astype(F32) * out, axis=-1, keepdims=True)
                dgates = jnp.where(lane == first_head + head, dgate, dgates)
                deltas = jnp.where(lane == head, delta, deltas)
            dgate_s[r, :] = dgates.astype(BF16)
            delta_s[r, :] = deltas
            return carry

        lax.fori_loop(0, blocks // 2, through_gate, 0)
        mlp.step(0)
        lax.fori_loop(blocks // 2, blocks, through_gate, 0)

        def out_grad(n, carry):
            c = block_of(n)
            dout_s[:, c] = mm_tn(gated_ref[...], dy_s[:, c]).astype(BF16)
            return carry

        lax.fori_loop(0, width // ROWS, out_grad, 0)
        dk_s[...] = jnp.zeros_like(dk_s)
        dv_s[...] = jnp.zeros_like(dv_s)
        dgq_s[...] = jnp.zeros_like(dgq_s)
        xg_s[...] = jnp.zeros_like(xg_s)
        o_in[0] = dout_s[pl.ds(pl.multiple_of(h * rows_here, rows_here), rows_here), :]
        for k in range(1, n_head):
            o_copy(k).start()

        def into_lin(grad, lin, gain, r):
            grad = turned(grad.astype(BF16).astype(F32), cos_ref[r, :], -sin_ref[r, :])
            unit, factor = unit_of(lin)
            return unit_back(grad * gain, unit, factor).astype(BF16), grad * unit

        def attend(n, carry):
            r = block_of(n)
            for head in range(q_here):
                at = slice(head * HEAD_DIM, (head + 1) * HEAD_DIM)
                p_load(head, n).wait()
                do, prob, q = do_s[r, at], p_s[head, r, :], q_ref[r, at]
                dp = mm_nt(do, v_ref[...])
                ds = (prob.astype(F32) * (dp - delta_s[r, head : head + 1])).astype(BF16)
                dq = mm(ds, k_ref[...]) * scale
                dk_s[...] += mm(q.T, ds)
                dv_s[...] += mm(do.T, prob)
                dlin, part = into_lin(dq, lin_ref[r, at], vec_ref[2:3, :HEAD_DIM], r)
                dlin_s[r, at] = dlin
                dgq_s[...] += jnp.sum(part.reshape(ROWS // 8, 8, HEAD_DIM), axis=0)
            return carry

        lax.fori_loop(0, blocks // 2, attend, 0)
        mlp.step(1)
        lax.fori_loop(blocks // 2, blocks, attend, 0)
        every = pl.ds(0, pack)
        k_cols = slice(q_cols, q_cols + HEAD_DIM)
        dlin, part = into_lin(
            dk_s[...].T * scale, lin_ref[:, k_cols], vec_ref[3:4, :HEAD_DIM], every
        )
        dlin_s[:, k_cols] = dlin
        dlin_s[:, q_cols + HEAD_DIM :] = dv_s[...].T.astype(BF16)

        dgk = jnp.sum(part, axis=0, keepdims=True)
        dgq = jnp.sum(dgq_s[...], axis=0, keepdims=True)
        pack_s[HEADS:, :] = jnp.zeros((PACK_ROWS - HEADS, width), F32)
        pack_s[HEADS : HEADS + 1, :] = jnp.sum(mlp_gain_ref[...], axis=0, keepdims=True)
        for t in range(width // HEAD_DIM):
            at = slice(t * HEAD_DIM, (t + 1) * HEAD_DIM)
            pack_s[HEADS + 1 : HEADS + 2, at] = dgq
            pack_s[HEADS + 2 : HEADS + 3, at] = dgk
        xn_load.wait()
        dgate_t = dgate_s[...].astype(F32).T[:HEADS].astype(BF16)

        def weights(n, carry):
            c = block_of(n)
            xn_cols = xn_s[:, c]
            dw_s[c, :] = mm_tn(xn_cols, dlin_s[...]).astype(BF16)
            pack_s[:HEADS, c] = mm(dgate_t, xn_cols)
            return carry

        lax.fori_loop(0, width // ROWS, weights, 0)
        for k in range(1, n_head):
            w_copy(k).start()
        w_in[0] = dw_s[of_head(h), :]

        def into_x(n, carry):
            r = block_of(n)
            back = mm_nt(dlin_s[r, :], w_ref[...]) + mm(dgate_s[r, :HEADS], gate_ref[...])
            dy_s[r, :] = back.astype(BF16)
            product = back * xn_s[r, :].astype(F32)
            xg_s[...] += jnp.sum(product.reshape(ROWS // 8, 8, width), axis=0)
            return carry

        lax.fori_loop(0, blocks, into_x, 0)
        dxn.start()
        pack_s[HEADS + 3 : HEADS + 4, :] = jnp.sum(xg_s[...], axis=0, keepdims=True)
        for k in range(1, n_head):
            g_copy(k).start()
        for hop in hops[:2]:
            hop.start()
        g_in[0] = pack_s[:, pl.ds(pl.multiple_of(h * lanes, 128), lanes)]
        for tau in range(2, chips - 1):
            mlp.step(tau)
        dxn.step(0)
        def finish_layer(r, value):
            layer_out[r, :] = (middle_ref[r, :] + value).astype(BF16)

        mlp.total(finish_layer)
        for tau in range(1, chips - 2):
            dxn.step(tau)
        for k in range(1, n_head):
            g_copy(k).wait_recv()
        g_sum[...] = sum(g_in[k] for k in range(n_head))
        g_last[b] = g_sum[:, tile_of(b)]
        for k in range(1, n_blk):
            pack_copy(k).start()
        for k in range(1, n_head):
            o_copy(k).wait_recv()

        def add_out(r):
            o_sum[r, :] = sum(o_in[k, r, :].astype(F32) for k in range(n_head)).astype(BF16)

        by_rows(rows_here, 16, add_out)

        @pl.when(stays)
        def _():
            keep_out.start()

        @pl.when(moves)
        def _():
            move_out.start()

        for k in range(1, n_head):
            w_copy(k).wait_recv()

        def add(r):
            w_sum[r, :] = sum(w_in[k, r, :].astype(F32) for k in range(n_head)).astype(BF16)

        by_rows(lanes, 64, add)
        for one in own_blocks:
            one.start()
        for k in range(1, n_blk):
            for copy in block_copies(k):
                copy.start()
        dxn.step(chips - 2)

        def consume(r, value):
            unit, factor = unit_of(x_ref[r, :].astype(F32))
            back = unit_back(value * vec_ref[0:1, :], unit, factor)
            input_grad[r, :] = dmid_ref[r, :] + back

        dxn.total(consume)
        for k in range(1, n_blk):
            pack_copy(k).wait_recv()
        g_out[...] = sum(g_last[k] for k in range(n_blk))
        mlp.finish()
        dxn.finish()
        for one in own_blocks:
            one.wait()
        for k in range(1, n_head):
            g_copy(k).wait_send()
            o_copy(k).wait_send()
            w_copy(k).wait_send()
        for k in range(1, n_blk):
            pack_copy(k).wait_send()
            for copy in block_copies(k):
                copy.wait()
        for hop in hops:
            hop.wait()

        @pl.when(stays)
        def _():
            keep_out.wait()

        @pl.when(moves)
        def _():
            move_out.wait()

    dma = pltpu.SemaphoreType.DMA
    kv = spec_of((copies, rows_here, n_blk // copies * HEAD_DIM), BF16)
    return pl.pallas_call(
        kernel,
        out_shape=(
            spec_of((count, width), BF16),
            spec_of((count, width), F32),
            spec_of((PACK_ROWS, 128), F32),
            spec_of((rows_here, n_blk * q_cols), BF16),
            kv,
            kv,
            spec_of((rows_here, width), BF16),
            *(spec_of(one.shape[1:], BF16) for one in ff_sums),
        ),
        in_specs=[ANYWHERE] * 7 + [IN_VMEM] * 17,
        out_specs=[IN_VMEM] * 3 + [ANYWHERE] * 7,
        scratch_shapes=[
            pltpu.VMEM((pack, width), BF16),
            pltpu.VMEM((pack, width), BF16),
            pltpu.VMEM((q_here, pack, pack), BF16),
            pltpu.VMEM((pack, q_cols), BF16),
            pltpu.VMEM((pack, GATE_PAD), F32),
            pltpu.VMEM((pack, GATE_PAD), BF16),
            pltpu.VMEM((pack, columns), BF16),
            pltpu.VMEM((HEAD_DIM, pack), F32),
            pltpu.VMEM((HEAD_DIM, pack), F32),
            pltpu.VMEM((8, HEAD_DIM), F32),
            pltpu.VMEM((width, columns), BF16),
            pltpu.VMEM((PACK_ROWS, width), F32),
            pltpu.VMEM((q_cols, width), BF16),
            pltpu.VMEM((n_head, lanes, columns), BF16),
            pltpu.VMEM((lanes, columns), BF16),
            pltpu.VMEM((n_head, rows_here, width), BF16),
            pltpu.VMEM((rows_here, width), BF16),
            pltpu.VMEM((n_head, PACK_ROWS, lanes), F32),
            pltpu.VMEM((PACK_ROWS, lanes), F32),
            pltpu.VMEM((n_blk, PACK_ROWS, 128), F32),
            *scatter_bufs(chips, count, width),
            *scatter_bufs(chips, count, width)[1:],
            pltpu.VMEM((8, width), F32),
            dma((blocks,)),
            dma,
            dma((q_here, blocks)),
            pair_sems(n_head),
            dma((3, 2, n_blk)),
            pair_sems(n_head),
            pair_sems(n_head),
            pair_sems(n_blk),
            dma((3,)),
            pair_sems(len(entries)),
            dma((3,)),
        ],
        compiler_params=local_params(collective_id),
        cost_estimate=comm_cost(2 * pack * width),
        name="attention_end",
    )(
        dy,
        xn,
        p,
        mlp_part.reshape(chips, 2, count, width),
        *ff_sums,
        *saved,
        w_attn,
        vec,
        gates,
        *tables,
        *token_rows,
    )


def feed_forward(attn_part, ff, halfway, cot, inputs, to_mlp, to_attention, n_head, n_blk, collective_id):
    total_rows, width = attn_part.shape
    chips, count = n_blk // 2, total_rows // n_blk
    size, half = count // CHUNKS, total_rows // CHUNKS
    rows_ff = ff[0].shape[0]
    units = n_head * rows_ff
    entries = ff_entries(rows_ff, n_head)
    n_in = len(inputs)

    def kernel(part, cot_hbm, *refs):
        refs = list(refs)

        def take(n):
            taken = refs[:n]
            del refs[:n]
            return taken

        sources = take(3), take(3)
        ins = take(n_in)
        middle, dmid, gain_part, dy_hbm, mlp_hbm, *sum_hbm = take(8)
        made, hn_s, cot_s, dhn_s, u_s, da_s, db_s, stage = take(8)
        inboxes, weights = take(3), take(3)
        chunk_scratch = [take(8) for _ in range(CHUNKS)]
        load_sems, hop_sems, cot_sems, stage_sems, sum_sems, grad_sems, late_sems = refs
        line = Line(n_blk)
        across = Exchange("head", n_head)
        greet_all((across,), line)
        gain_part[...] = jnp.zeros_like(gain_part)

        def place(key, span):
            return pl.ds(key * rows_ff + span.start, span.size)

        loads, hops = [], []
        for e, (w, span, order) in enumerate(entries):
            first, second = 1 << order[0], 1 << order[1]
            for at, key in enumerate((0, first)):
                src = sources[at][w].at[span]
                loads.append(
                    pltpu.make_async_copy(src, weights[w].at[place(key, span)], load_sems.at[e, at])
                )
                there = weights[w].at[place(key ^ second, span)]
                hops.append(flip_copy(src, there, order[1], hop_sems, e, at))

        def cot_loads():
            for j in range(chips):
                for c in range(2):
                    yield pltpu.make_async_copy(
                        cot_hbm.at[j, c],
                        Rows(cot_s, 0, size, chips)[j, c],
                        cot_sems.at[2 * j + c],
                    )

        first, gather1, second, gather2 = [], [], [], []
        for q in range(CHUNKS):
            own, sib, inn, outgoing, sems, g_sems, sems2, g_sems2 = chunk_scratch[q]
            rows = pl.ds(q * size, size)
            first.append(Scatter(line, View(part, rows), (own, sib, inn, outgoing), sems))
            gather1.append(Gather(line, made.at[rows], Rows(hn_s, q, size, chips), g_sems))
            second.append(
                LocalScatter(line, Rows(dhn_s, q, size, chips), (sib, inn, outgoing), sems2)
            )
            gather2.append(Gather(line, made.at[rows], View(dy_hbm, rows), g_sems2))

        late = [
            Gather(
                line,
                ins[1].at[pl.ds(q * size, size)],
                Rows(cot_s, q, size, chips),
                late_sems.at[q - 1],
            )
            for q in range(1, CHUNKS)
        ]

        def turn(q, scatter, between, outs, gather):
            def consume(r, value):
                r = pl.ds(pl.multiple_of(r.start + q * size, 16), r.size)
                made[r, :] = between(r, value, ins, outs).astype(BF16)

            scatter[q].total(consume)
            gather[q].start()

        def loop(steps, body):
            lax.fori_loop(0, steps, lambda k, carry: body(k) or carry, 0)

        def span_of(q):
            return pl.ds(q * half, half)

        def unit_block(q, f):
            r, fr = span_of(q), block_of(f)
            a = mm_nt(hn_s[r, :], weights[0][fr, :])
            b = mm_nt(hn_s[r, :], weights[1][fr, :])
            du = mm_nt(cot_s[r, :], weights[2][fr, :])
            sig = jax.nn.sigmoid(a)
            silu = a * sig
            u_s[r, fr] = (silu * b).astype(BF16)
            da_s[r, fr] = (du * b * sig * (1.0 + a * (1.0 - sig))).astype(BF16)
            db_s[r, fr] = (du * silu).astype(BF16)

        def back(q):
            r = span_of(q)

            def body(n):
                cols = block_of(n, 512)
                dhn = mm(da_s[r, :], weights[0][:, cols]) + mm(db_s[r, :], weights[1][:, cols])
                dhn_s[r, cols] = dhn.astype(BF16)

            loop(width // 512, body)

        def stage_stores(q):
            for j in range(chips):
                for c in range(2):
                    yield pltpu.make_async_copy(
                        Rows(stage, 0, size, chips)[j, c],
                        mlp_hbm.at[j, c, pl.ds(q * size, size)],
                        stage_sems.at[2 * j + c],
                    )

        def mlp_out(q):
            if q:
                for store in stage_stores(q - 1):
                    store.wait()
            r = span_of(q)

            def body(n):
                cols = block_of(n, 512)
                stage[:, cols] = mm(u_s[r, :], weights[2][:, cols]).astype(BF16)

            loop(width // 512, body)
            for store in stage_stores(q):
                store.start()

        def grad(w):
            left, right = ((da_s, hn_s), (db_s, hn_s), (u_s, cot_s))[w]

            def body(f):
                fr = block_of(f)
                weights[w][fr, :] = mm_tn(left[:, fr], right[...]).astype(BF16)

            loop(units // ROWS, body)

        def sum_copies(w):
            for e, (weight, span, order) in enumerate(entries):
                if weight == w:
                    for at, key in enumerate((0, 1 << order[0])):
                        yield flip_copy(
                            weights[w].at[place(key ^ (1 << order[1]), span)],
                            inboxes[w].at[at, span],
                            order[1],
                            sum_sems,
                            e,
                            at,
                        )

        def sum_stores(w):
            for e, (weight, span, order) in enumerate(entries):
                if weight == w:
                    for at, key in enumerate((0, 1 << order[0])):
                        yield pltpu.make_async_copy(
                            weights[w].at[place(key, span)],
                            sum_hbm[w].at[at, span],
                            grad_sems.at[e, at],
                        )

        def send_grad(w):
            grad(w)
            for copy in sum_copies(w):
                copy.start()

        def add_grad(w):
            for copy in sum_copies(w):
                copy.wait()
            for weight, span, order in entries:
                if weight == w:
                    for at, key in enumerate((0, 1 << order[0])):

                        def body(r, span=span, at=at, key=key):
                            r = pl.ds(pl.multiple_of(r.start + span.start, 16), r.size)
                            mine = pl.ds(pl.multiple_of(r.start + key * rows_ff, 16), r.size)
                            value = weights[w][mine, :].astype(F32)
                            value += inboxes[w][at, r, :].astype(F32)
                            weights[w][mine, :] = value.astype(BF16)

                        by_rows(span.size, 16, body)
            for store in sum_stores(w):
                store.start()

        first[0].start()
        for hop in hops:
            hop.start()
        for q in range(1, CHUNKS):
            first[q].start()
        for one in late:
            one.start()
        for load in loads:
            load.start()
        for load in cot_loads():
            load.start()
        steps = chips - 1
        for tau in range(steps):
            first[0].step(tau)
            for one in late:
                one.step(tau + 1)
        turn(0, first, to_mlp, (middle,), gather1)
        for tau in range(steps):
            first[1].step(tau)
            gather1[0].step(tau + 1)
        turn(1, first, to_mlp, (middle,), gather1)
        for q in range(CHUNKS):
            first[q].finish()
        gather1[0].finish()
        gather1[1].step(1)
        for load in loads:
            load.wait()
        for load in cot_loads():
            load.wait()
        for hop in hops:
            hop.wait()
        blocks = units // ROWS
        unit_block(0, 0)
        for s in range(2, chips):
            gather1[1].step(s)
            if s == 2:
                unit_block(0, 1)
        for f in range(2, blocks):
            unit_block(0, f)
        back(0)
        second[0].start()
        gather1[1].finish()
        for one in late:
            one.finish()
        second[0].step(0)
        loop(blocks, lambda f: unit_block(1, f))
        second[0].step(1)
        back(1)
        second[1].start()
        send_grad(0)
        for tau in range(2, steps):
            second[0].step(tau)
        second[1].step(0)
        send_grad(1)
        turn(0, second, to_attention, (middle, dmid, gain_part), gather2)
        second[1].step(1)
        mlp_out(0)
        mlp_out(1)
        gather2[0].step(1)
        send_grad(2)
        for tau in range(2, steps):
            second[1].step(tau)
            gather2[0].step(tau)
        turn(1, second, to_attention, (middle, dmid, gain_part), gather2)
        gather2[0].step(chips - 1)
        for s in range(1, chips):
            gather2[1].step(s)
        for w in range(3):
            add_grad(w)
        for q in range(CHUNKS):
            second[q].finish()
            gather2[q].finish()
        for store in stage_stores(CHUNKS - 1):
            store.wait()
        for w in range(3):
            for store in sum_stores(w):
                store.wait()

    per_chunk = []
    for _ in range(CHUNKS):
        own, sib, inn, outgoing, sems = scatter_bufs(chips, size, width)
        per_chunk += [own, sib, inn, outgoing, sems, gather_sems(chips), sems, gather_sems(chips)]
    sums = jax.ShapeDtypeStruct((2, rows_ff, width), BF16)
    shards_ = jax.ShapeDtypeStruct((chips, 2, count, width), BF16)
    dma = pltpu.SemaphoreType.DMA
    middle, dmid, gain_part, dy, mlp_part, *ff_sums = pl.pallas_call(
        kernel,
        out_shape=(
            jax.ShapeDtypeStruct((count, width), F32),
            jax.ShapeDtypeStruct((count, width), F32),
            jax.ShapeDtypeStruct((8, width), F32),
            shards_,
            shards_,
            *[sums] * 3,
        ),
        in_specs=[ANYWHERE] * 8 + [IN_VMEM] * n_in,
        out_specs=[IN_VMEM] * 3 + [ANYWHERE] * 5,
        scratch_shapes=[
            pltpu.VMEM((count, width), BF16),
            *[pltpu.VMEM((total_rows, width), BF16)] * 3,
            *[pltpu.VMEM((total_rows, units), BF16)] * 3,
            pltpu.VMEM((half, width), BF16),
            *[pltpu.VMEM((2, rows_ff, width), BF16)] * 3,
            *[pltpu.VMEM((units, width), BF16)] * 3,
            *per_chunk,
            dma((len(entries), 2)),
            dma((2, len(entries), 2)),
            dma((n_blk,)),
            dma((n_blk,)),
            dma((2, len(entries), 2)),
            dma((len(entries), 2)),
            dma((CHUNKS - 1, 7, chips, PIECES)),
        ],
        compiler_params=pltpu.CompilerParams(
            collective_id=collective_id, has_side_effects=True, vmem_limit_bytes=62 * 2**20
        ),
        cost_estimate=comm_cost(2 * total_rows * width),
        name="feed_forward",
    )(
        attn_part.reshape(chips, 2, count, width),
        cot,
        *ff,
        *halfway,
        *inputs,
    )
    return (
        middle,
        dmid,
        gain_part,
        dy.reshape(total_rows, width),
        mlp_part.reshape(total_rows, width),
        ff_sums,
    )


def padded(values, size):
    return jnp.pad(values, [(0, 0)] * (values.ndim - 1) + [(0, size - values.shape[-1])])


def shards(
    hidden,
    segment_ids,
    block_ids,
    positions,
    attn_gain,
    w_query,
    key_weight_matrix,
    value_weight_matrix,
    q_gain,
    k_gain,
    w_head_gate,
    w_out,
    mlp_gain,
    w_gate,
    w_up,
    w_down,
    cotangent,
):
    n_head = lax.axis_size("head")
    n_blk = lax.axis_size("blk")
    n_all = n_head * n_blk
    my_head = lax.axis_index("head")
    my_blk = lax.axis_index("blk")
    tokens = hidden.shape[1]
    pack = tokens * n_blk
    rows_here = w_query.shape[0]
    rows_ff = w_gate.shape[0]
    q_here = HEADS // n_blk
    q_cols = q_here * HEAD_DIM
    kv_copies = max(1, n_blk // KV_HEADS)
    kv_here = max(1, KV_HEADS // n_blk)
    kv_cols = kv_here * HEAD_DIM
    device = my_head * n_blk + my_blk
    together = 128 // rows_here
    lane = jnp.arange(128)
    here = (lane // rows_here == device % together)[None]
    mine = jnp.concatenate(
        [
            attn_gain[None],
            mlp_gain[None],
            jnp.zeros((6, rows_here), BF16),
            w_head_gate.T,
        ]
    )
    small = jnp.where(here, jnp.tile(mine, (1, together)), 0).astype(F32)
    share = q_gain.shape[0]
    head_gains = jnp.stack([jnp.tile(q_gain, n_all), jnp.tile(k_gain, n_all)]).astype(F32)
    head_gains = jnp.where(lane // share == device, head_gains, 0)
    small = small + jnp.pad(head_gains, ((2, PACK_ROWS - 4), (0, 0)))
    ids = (positions, segment_ids, block_ids)
    fused = n_head == 4 and pack <= 1024
    ff = (w_gate, w_up, w_down)
    attn_part, xn, prob, cot, *rest = attention_forward(
        hidden[0],
        (w_query, key_weight_matrix, value_weight_matrix),
        small,
        w_out,
        ids,
        cotangent[0],
        tokens // CHUNKS if fused else tokens,
        ff,
        q_cols,
        kv_copies,
        n_head,
        n_blk,
        0,
    )
    halfway, (w_attn, vec, gates), tables, saved = rest[:3], rest[3:6], rest[6:8], rest[8:]

    def to_mlp(r, total, ins, outs):
        x_ref, gain_ref = ins
        mid = x_ref[r, :].astype(F32) + total
        outs[0][r, :] = mid
        unit, _ = unit_of(mid)
        return unit * gain_ref[1:2, :]

    def to_attention(r, dhn, ins, outs):
        mid_ref, cot_ref, gain_ref = ins
        unit, factor = unit_of(mid_ref[r, :])
        product = dhn * unit
        seen = outs[1]
        seen[...] += product[:8] + product[8:]
        back = cot_ref[r, :].astype(F32) + unit_back(dhn * gain_ref[1:2, :], unit, factor)
        outs[0][r, :] = back
        return back

    if fused:

        def into_mlp(r, total, ins, outs):
            return to_mlp(r, total, (ins[0], ins[2]), outs)

        def into_attention(r, dhn, ins, outs):
            return to_attention(r, dhn, (outs[0], ins[1], ins[2]), outs[1:])

        middle, dmid, mlp_gain_part, dy, mlp_part, ff_sums = feed_forward(
            attn_part,
            ff,
            halfway,
            cot,
            (hidden[0], cotangent[0], vec),
            into_mlp,
            into_attention,
            n_head,
            n_blk,
            1,
        )
    else:
        cot = cot.reshape(pack, MODEL_WIDTH)
        ff_full = []
        for w, (own, other) in enumerate(zip(ff, halfway)):
            full = jnp.zeros((n_head, *own.shape), BF16).at[0].set(own)
            for weight, part, order in ff_entries(rows_ff, n_head):
                if weight == w:
                    span = slice(part.start, part.start + part.size)
                    full = full.at[1 << order[0], span].set(other[span])
            ff_full.append(full)
        middle, hn, *ff_rows = scatter_gather(
            attn_part,
            lambda outs: None,
            to_mlp,
            (hidden[0], vec),
            (jax.ShapeDtypeStruct(hidden.shape[1:], F32),),
            spread_beside(ff_full, n_head),
            n_head,
            n_blk,
            1,
        )
        gate_rows, up_rows, down_rows = (one.reshape(n_head * rows_ff, MODEL_WIDTH) for one in ff_rows)

        a = mm_nt(hn, gate_rows)
        b = mm_nt(hn, up_rows)
        sig = jax.nn.sigmoid(a)
        silu = a * sig
        u = (silu * b).astype(BF16)
        mlp_part = mm(u, down_rows).astype(BF16)
        du = mm_nt(cot, down_rows)
        da = (du * b * sig * (1.0 + a * (1.0 - sig))).astype(BF16)
        db = (du * silu).astype(BF16)
        ff_parts = [
            mm_tn(left, right).astype(BF16).reshape(n_head, rows_ff, MODEL_WIDTH)
            for left, right in ((da, hn), (db, hn), (u, cot))
        ]

        def clear(outs):
            outs[1][...] = jnp.zeros_like(outs[1])

        dmid, mlp_gain_part, dy, *ff_sums, mlp_part = scatter_gather(
            mm(da, gate_rows) + mm(db, up_rows),
            clear,
            to_attention,
            (middle, cotangent[0], vec),
            (
                jax.ShapeDtypeStruct(hidden.shape[1:], F32),
                jax.ShapeDtypeStruct((8, MODEL_WIDTH), F32),
            ),
            collect_beside(ff_parts, mlp_part, n_head),
            n_head,
            n_blk,
            2,
        )

    if fused:
        layer_output, input_grad, small_sums, query_grad, key_grad, value_grad, out_grad, *ff_last = (
            attention_end(
                dy,
                xn,
                prob,
                mlp_part,
                ff_sums,
                saved,
                w_attn,
                vec,
                gates,
                tables,
                (hidden[0], middle, dmid, mlp_gain_part),
                q_here,
                kv_copies,
                n_head,
                n_blk,
                2,
            )
        )
        layer_output, input_grad = layer_output[None], input_grad[None]
    else:
        layer_output = (
            middle + lax.psum_scatter(mlp_part, "blk", scatter_dimension=0, tiled=True).astype(F32)
        ).astype(BF16)[None]
        dxn_part, attn_grad, small_parts, out_grad = attention_backward(
            dy,
            xn,
            prob,
            saved,
            w_attn,
            vec,
            gates,
            tables,
            mlp_gain_part,
            q_here,
            None,
        )
        back_x, query_grad, key_grad, value_grad, out_grad, small_sums, *ff_last = last_scatter(
            dxn_part,
            attn_grad.reshape(n_head, n_blk, rows_here, -1),
            out_grad,
            small_parts,
            ff_sums,
            hidden[0],
            vec,
            q_cols,
            kv_copies,
            n_head,
            n_blk,
            3,
        )
        input_grad = (dmid + back_x)[None]
    ff_grads = [one[0].astype(F32) + two.astype(F32) for one, two in zip(ff_sums, ff_last)]

    query_grad = query_grad.astype(F32)
    key_grad = jnp.sum(key_grad.astype(F32), axis=0)
    value_grad = jnp.sum(value_grad.astype(F32), axis=0)
    small_sums = jnp.sum(
        jnp.where(
            jnp.arange(together)[None, :, None] == device % together,
            small_sums.reshape(PACK_ROWS, together, rows_here),
            0.0,
        ),
        axis=1,
    ), small_sums[HEADS + 1 : HEADS + 3]
    small_sums, head_sums = small_sums
    head_sums = lax.dynamic_slice_in_dim(head_sums, device * share, share, 1)
    head_gate_grad = small_sums[:HEADS].T
    if fused:
        scaled = small_sums[HEADS + 3]
    else:
        scaled = (
            jnp.sum(w_query.astype(F32) * query_grad, axis=1)
            + jnp.sum(key_weight_matrix.astype(F32) * key_grad, axis=1)
            + jnp.sum(value_weight_matrix.astype(F32) * value_grad, axis=1)
            + jnp.sum(w_head_gate.astype(F32) * head_gate_grad, axis=1)
        )
    attn_gain_grad = scaled / attn_gain.astype(F32)
    return (
        layer_output,
        input_grad,
        attn_gain_grad,
        query_grad,
        key_grad,
        value_grad,
        head_sums[0],
        head_sums[1],
        head_gate_grad,
        out_grad.astype(F32),
        small_sums[HEADS],
        ff_grads[0],
        ff_grads[1],
        ff_grads[2],
    )


def solution(mesh):
    rows = P(("head", "blk"), None)
    vector = P(("head", "blk"))
    token = P("head", "blk", None)
    return jax.shard_map(
        shards,
        mesh=mesh,
        in_specs=(
            token, P(), P(), P(), vector, rows, rows, rows, vector, vector, rows, rows, vector,
            rows, rows, rows, token,
        ),
        out_specs=(
            token, token, vector, rows, rows, rows, vector, vector, rows, rows, vector,
            rows, rows, rows,
        ),
        check_vma=False,
    )
```

```python
import math

import jax
import jax.numpy as jnp
from jax import lax
from jax.experimental import pallas as pl
from jax.experimental.pallas import tpu as pltpu
from jax.sharding import PartitionSpec as P

MODEL_WIDTH = 2048
HEADS = 16
KV_HEADS = 8
HEAD_DIM = 128
GATE_PAD = 128
EPSILON = 1e-06
ROPE_BASE = 1000000.0
MASKED = -1e30
F32 = jnp.float32
BF16 = jnp.bfloat16
MESH = pl.DeviceIdType.MESH


def mm(a, b):
    return jnp.dot(a, b, preferred_element_type=F32)


def mm_nt(a, b):
    return lax.dot_general(a, b, (((1,), (1,)), ((), ())), preferred_element_type=F32)


def mm_tn(a, b):
    return lax.dot_general(a, b, (((0,), (0,)), ((), ())), preferred_element_type=F32)


def unit_of(values):
    factor = lax.rsqrt(jnp.mean(values * values, axis=-1, keepdims=True) + EPSILON)
    return values * factor, factor


def unit_back(scaled, unit, factor):
    return factor * (scaled - unit * jnp.mean(scaled * unit, axis=-1, keepdims=True))


def signal_to(semaphore, target):
    pl.semaphore_signal(semaphore, inc=1, device_id=target, device_id_type=MESH)


class Line:
    def __init__(self, n_blk):
        self.me = lax.axis_index("blk")
        self.chips = n_blk // 2
        self.i = self.me // 2
        self.c = self.me % 2
        self.right = {"blk": self.me + 2}
        self.left = {"blk": self.me - 2}
        self.sibling = {"blk": self.me + 1 - 2 * self.c}
        self.has_right = self.i < self.chips - 1
        self.has_left = self.i > 0

    def greet(self, barrier):
        signal_to(barrier, self.sibling)

        @pl.when(self.has_right)
        def _():
            signal_to(barrier, self.right)

        @pl.when(self.has_left)
        def _():
            signal_to(barrier, self.left)

        return 1 + self.has_right.astype(jnp.int32) + self.has_left.astype(jnp.int32)


class Gather:
    def __init__(self, line, src, out, sems):
        self.line, self.src, self.out, self.sems = line, src, out, sems
        self.pieces = sems.shape[2]
        self.rows = src.shape[0] // self.pieces

    def part(self, p):
        return pl.ds(p * self.rows, self.rows)

    def move(self, kind, src, j, p, target):
        return pltpu.make_async_remote_copy(
            src_ref=src.at[self.part(p)],
            dst_ref=self.out.at[j, self.line.c, self.part(p)],
            send_sem=self.sems.at[kind, j, p],
            recv_sem=self.sems.at[3 + kind, j, p],
            device_id=target,
            device_id_type=MESH,
        )

    def arrived(self, kind, j, p, core):
        there = self.out.at[j, core, self.part(p)]
        pltpu.make_async_remote_copy(
            src_ref=there,
            dst_ref=there,
            send_sem=self.sems.at[kind, j, p],
            recv_sem=self.sems.at[3 + kind, j, p],
            device_id=self.line.sibling,
            device_id_type=MESH,
        ).wait_recv()

    def send(self, src, j, p, right, left):
        line = self.line
        if right is not None:

            @pl.when(right)
            def _():
                self.move(0, src, j, p, line.right).start()

        if left is not None:

            @pl.when(left)
            def _():
                self.move(1, src, j, p, line.left).start()

        self.move(2, src, j, p, line.sibling).start()

    def own_copy(self):
        return pltpu.make_async_copy(
            self.src, self.out.at[self.line.i, self.line.c], self.sems.at[6, 0, 0]
        )

    def start(self):
        line = self.line
        for p in range(self.pieces):
            self.send(self.src, line.i, p, line.has_right, line.has_left)
        self.own_copy().start()

    def step(self, s):
        line = self.line
        from_left, from_right = line.i - s, line.i + s
        for p in range(self.pieces):

            @pl.when(from_left >= 0)
            def _(p=p):
                self.arrived(0, from_left, p, line.c)
                self.send(self.out.at[from_left, line.c], from_left, p, line.has_right, None)

            @pl.when(from_right < line.chips)
            def _(p=p):
                self.arrived(1, from_right, p, line.c)
                self.send(self.out.at[from_right, line.c], from_right, p, None, line.has_left)

    def finish(self):
        line = self.line
        for j in range(line.chips):
            mine = self.out.at[j, line.c]
            for p in range(self.pieces):
                self.arrived(2, j, p, 1 - line.c)
                self.move(2, mine, j, p, line.sibling).wait_send()

                @pl.when((line.i >= j) & line.has_right)
                def _(j=j, p=p, mine=mine):
                    self.move(0, mine, j, p, line.right).wait_send()

                @pl.when((line.i <= j) & line.has_left)
                def _(j=j, p=p, mine=mine):
                    self.move(1, mine, j, p, line.left).wait_send()

        self.own_copy().wait()

    def run(self):
        self.start()
        for s in range(1, self.line.chips):
            self.step(s)
        self.finish()


def by_rows(rows, step, body):
    def one(k, carry):
        body(pl.ds(pl.multiple_of(k * step, step), step))
        return carry

    lax.fori_loop(0, rows // step, one, 0)


SUMS = 2


class Scatter:
    def __init__(self, line, part, bufs, sems):
        self.line, self.part, self.sems = line, part, sems
        self.own, self.sib, self.inn, self.out = bufs

    def copy(self, kind, src, dst, slot, target):
        return pltpu.make_async_remote_copy(
            src_ref=src,
            dst_ref=dst,
            send_sem=self.sems.at[(kind, *slot)],
            recv_sem=self.sems.at[(3 + kind, *slot)],
            device_id=target,
            device_id_type=MESH,
        )

    def to_sibling(self, j):
        line = self.line
        return self.copy(2, self.part.at[j, 1 - line.c], self.sib.at[j], (j, 0), line.sibling)

    def to_own(self, j):
        return pltpu.make_async_copy(
            self.part.at[j, self.line.c], self.own.at[j], self.sems.at[6, j, 0]
        )

    @property
    def size(self):
        return self.own.shape[1] // SUMS

    def along(self, way, j, p):
        line = self.line
        target = line.left if way else line.right
        span = pl.ds(p * self.size, self.size)
        return self.copy(way, self.out.at[j, span], self.inn.at[way, j, span], (j, p), target)

    def start(self):
        chips = self.line.chips
        order = []
        for k in range((chips + 1) // 2):
            order += [chips - 1 - k, k]
        for j in order[:chips]:
            self.to_sibling(j).start()
            self.to_own(j).start()

    def ready(self, j):
        self.to_sibling(j).wait_recv()
        self.to_own(j).wait()

    def rows_of(self, p, body):
        def shifted(r):
            body(pl.ds(pl.multiple_of(r.start + p * self.size, 16), r.size))

        by_rows(self.size, 16, shifted)

    def pass_on(self, way, j, first):
        self.ready(j)
        for p in range(SUMS):

            @pl.when(first)
            def _(p=p):
                def body(r):
                    total = self.own[j, r, :].astype(F32) + self.sib[j, r, :].astype(F32)
                    self.out[j, r, :] = total.astype(BF16)

                self.rows_of(p, body)

            @pl.when(jnp.logical_not(first))
            def _(p=p):
                self.along(way, j, p).wait_recv()

                def body(r):
                    total = self.own[j, r, :].astype(F32) + self.sib[j, r, :].astype(F32)
                    total += self.inn[way, j, r, :].astype(F32)
                    self.out[j, r, :] = total.astype(BF16)

                self.rows_of(p, body)

            self.along(way, j, p).start()

    def step(self, tau):
        line = self.line

        @pl.when((line.i <= tau) & line.has_right)
        def _():
            self.pass_on(0, line.chips - 1 - tau + line.i, line.i == 0)

        @pl.when((line.chips - 1 - line.i <= tau) & line.has_left)
        def _():
            self.pass_on(1, tau - (line.chips - 1 - line.i), line.i == line.chips - 1)

    def total(self, consume):
        line, i = self.line, self.line.i
        self.ready(i)
        for p in range(SUMS):

            @pl.when(line.has_left)
            def _(p=p):
                self.along(0, i, p).wait_recv()

            @pl.when(line.has_right)
            def _(p=p):
                self.along(1, i, p).wait_recv()

        rows = self.own.shape[1]

        def add(r, with_left, with_right):
            total = self.own[i, r, :].astype(F32) + self.sib[i, r, :].astype(F32)
            if with_left:
                total += self.inn[0, i, r, :].astype(F32)
            if with_right:
                total += self.inn[1, i, r, :].astype(F32)
            consume(r, total)

        @pl.when(line.has_left & line.has_right)
        def _():
            by_rows(rows, 16, lambda r: add(r, True, True))

        @pl.when(line.has_left & jnp.logical_not(line.has_right))
        def _():
            by_rows(rows, 16, lambda r: add(r, True, False))

        @pl.when(line.has_right & jnp.logical_not(line.has_left))
        def _():
            by_rows(rows, 16, lambda r: add(r, False, True))

    def finish(self):
        line = self.line
        for j in range(line.chips):
            self.to_sibling(j).wait_send()
            for p in range(SUMS):

                @pl.when(j > line.i)
                def _(j=j, p=p):
                    self.along(0, j, p).wait_send()

                @pl.when(j < line.i)
                def _(j=j, p=p):
                    self.along(1, j, p).wait_send()


PIECES = 2


def gather_sems(chips):
    return pltpu.SemaphoreType.DMA((7, chips, PIECES))


def scatter_bufs(chips, rows, width):
    return [
        pltpu.VMEM((chips, rows, width), BF16),
        pltpu.VMEM((chips, rows, width), BF16),
        pltpu.VMEM((2, chips, rows, width), BF16),
        pltpu.VMEM((chips, rows, width), BF16),
        pltpu.SemaphoreType.DMA((7, chips, SUMS)),
    ]


ANYWHERE = pl.BlockSpec(memory_space=pl.ANY)
IN_VMEM = pl.BlockSpec(memory_space=pltpu.VMEM)


def params(collective_id):
    return pltpu.CompilerParams(
        collective_id=collective_id, has_side_effects=True, vmem_limit_bytes=56 * 2**20
    )


def comm_cost(byte_count):
    return pl.CostEstimate(flops=0, transcendentals=0, bytes_accessed=40 * byte_count)


class Exchange:
    def __init__(self, axis, size):
        self.axis, self.size = axis, size
        self.me = lax.axis_index(axis)

    def peer(self, k):
        return lax.rem(self.me + k, self.size)

    def greet(self, barrier):
        for k in range(1, self.size):
            signal_to(barrier, {self.axis: self.peer(k)})

    def copy(self, k, src, dst, sems):
        return pltpu.make_async_remote_copy(
            src_ref=src,
            dst_ref=dst,
            send_sem=sems.at[0, k],
            recv_sem=sems.at[1, k],
            device_id={self.axis: self.peer(k)},
            device_id_type=MESH,
        )

    def sems(self):
        return pltpu.SemaphoreType.DMA((2, self.size))


def pair_sems(size):
    return pltpu.SemaphoreType.DMA((2, size))


def greet_all(exchanges, line=None, moves=None):
    barrier = pltpu.get_barrier_semaphore()
    count = 0
    for exchange in exchanges:
        exchange.greet(barrier)
        count += exchange.size - 1
    if line is not None:
        count += line.greet(barrier)
    if moves is not None:
        whether, source = moves

        @pl.when(whether)
        def _():
            signal_to(barrier, source)

        count += whether.astype(jnp.int32)
    pl.semaphore_wait(barrier, count)


def flip_copy(src, dst, bit, sems, *index):
    return pltpu.make_async_remote_copy(
        src_ref=src,
        dst_ref=dst,
        send_sem=sems.at[(0, *index)],
        recv_sem=sems.at[(1, *index)],
        device_id={"head": lax.axis_index("head") ^ (1 << bit)},
        device_id_type=MESH,
    )


def ff_entries(rows, n_head):
    bits = tuple(range(n_head.bit_length() - 1))
    back, half = bits[::-1], rows // 2
    return (
        (0, pl.ds(0, rows), bits),
        (1, pl.ds(0, rows), back),
        (2, pl.ds(0, half), bits),
        (2, pl.ds(half, half), back),
    )


def place_of_out_rows(n_head, n_blk):
    h, b = lax.axis_index("head"), lax.axis_index("blk")
    d = h * n_blk + b
    source = b * n_head + h
    return (d % n_head, d // n_head), (source // n_blk, source % n_blk)


PACK_ROWS = 24


def weight_pieces(b, q_cols, copies):
    kv = b // copies * HEAD_DIM
    return (
        (0, pl.ds(pl.multiple_of(b * q_cols, HEAD_DIM), q_cols), pl.ds(0, q_cols)),
        (1, pl.ds(pl.multiple_of(kv, HEAD_DIM), HEAD_DIM), pl.ds(q_cols, HEAD_DIM)),
        (2, pl.ds(pl.multiple_of(kv, HEAD_DIM), HEAD_DIM), pl.ds(q_cols + HEAD_DIM, HEAD_DIM)),
    )


PACK_ROWS = 24


def weight_pieces(b, q_cols, copies):
    kv = b // copies * HEAD_DIM
    return (
        (0, pl.ds(pl.multiple_of(b * q_cols, HEAD_DIM), q_cols), pl.ds(0, q_cols)),
        (1, pl.ds(pl.multiple_of(kv, HEAD_DIM), HEAD_DIM), pl.ds(q_cols, HEAD_DIM)),
        (2, pl.ds(pl.multiple_of(kv, HEAD_DIM), HEAD_DIM), pl.ds(q_cols + HEAD_DIM, HEAD_DIM)),
    )


class Spread:
    def __init__(self, full, entries, n_head, sems):
        self.full, self.entries, self.n_head, self.sems = full, entries, n_head, sems

    def copies(self, e, level):
        weight, part, order = self.entries[e]
        full = self.full[weight]
        bit = order[level]
        keys = [0]
        for low in order[:level]:
            keys += [key ^ (1 << low) for key in keys]
        for key in keys:
            there = key ^ (1 << bit)
            yield flip_copy(
                full.at[key, part], full.at[there, part], bit, self.sems, e, there
            )

    def level(self, level):
        for e in range(len(self.entries)):
            if level > 1:
                for copy in self.copies(e, level - 1):
                    copy.wait_recv()
            for copy in self.copies(e, level):
                copy.start()

    def start(self):
        self.level(1)

    def finish(self):
        levels = self.n_head.bit_length() - 1
        for level in range(2, levels):
            self.level(level)
        for e in range(len(self.entries)):
            for level in range(1, levels):
                for copy in self.copies(e, level):
                    copy.wait_send()
                    if level == levels - 1:
                        copy.wait_recv()

    @staticmethod
    def sem_shape(n_head):
        return pltpu.SemaphoreType.DMA((2, 4, n_head))


class Collect:
    def __init__(self, have, kept, inbox, total, entries, n_head, sems):
        self.have, self.kept, self.inbox, self.total = have, kept, inbox, total
        self.entries, self.n_head, self.sems = entries, n_head, sems

    def keys(self, order, level):
        keys = [0]
        for low in order[: len(order) - 1 - level]:
            keys += [key ^ (1 << low) for key in keys]
        return keys

    def slot(self, order, key):
        return self.keys(order, 0).index(key)

    def copies(self, e, level):
        weight, part, order = self.entries[e]
        bit = order[len(order) - 1 - level]
        for key in self.keys(order, level):
            slot = self.slot(order, key)
            if level == 0:
                src = self.have[weight].at[key ^ (1 << bit), part]
            else:
                src = self.kept[weight].at[self.slot(order, key ^ (1 << bit)), part]
            yield flip_copy(src, self.inbox[weight].at[level, slot, part], bit, self.sems, e, level, slot)

    def locals_(self):
        for e, (weight, part, order) in enumerate(self.entries):
            for key in self.keys(order, 0):
                slot = self.slot(order, key)
                yield pltpu.make_async_copy(
                    self.have[weight].at[key, part],
                    self.kept[weight].at[slot, part],
                    self.sems.at[2, e, 0, slot],
                )

    def start(self):
        for copy in self.locals_():
            copy.start()
        for e in range(len(self.entries)):
            for copy in self.copies(e, 0):
                copy.start()

    def finish(self):
        for copy in self.locals_():
            copy.wait()
        levels = self.n_head.bit_length() - 2
        for level in range(levels):
            last = level == levels - 1
            for e, (weight, part, order) in enumerate(self.entries):
                for copy in self.copies(e, level):
                    copy.wait_recv()
                for at, key in enumerate(self.keys(order, level)):
                    slot = self.slot(order, key)
                    kept, inbox = self.kept[weight], self.inbox[weight]
                    into = self.total[weight] if last else kept
                    where = at if last else slot

                    def body(r, part=part, slot=slot, kept=kept, inbox=inbox, into=into, where=where):
                        r = pl.ds(pl.multiple_of(r.start + part.start, 16), r.size)
                        value = kept[slot, r, :].astype(F32) + inbox[level, slot, r, :].astype(F32)
                        into[where, r, :] = value.astype(BF16)

                    by_rows(part.size, 16, body)
            for e in range(len(self.entries)):
                if not last:
                    for copy in self.copies(e, level + 1):
                        copy.start()
        for level in range(levels):
            for e in range(len(self.entries)):
                for copy in self.copies(e, level):
                    copy.wait_send()

    @staticmethod
    def sem_shape(n_head):
        levels = n_head.bit_length() - 2
        return pltpu.SemaphoreType.DMA((3, 4, levels, n_head // 2))


def last_scatter(
    partial_rows, w_grad, out_grad, pack, sums, hidden, gain, q_cols, copies, n_head, n_blk, collective_id
):
    total_rows, width = partial_rows.shape
    chips, count = n_blk // 2, total_rows // n_blk
    _, _, rows_here, columns = w_grad.shape
    n_sums = len(sums)
    entries = ff_entries(sums[0].shape[1], n_head) if sums else ()

    def kernel(part, w_src, o_src, g_src, *refs):
        ff_src, (x_ref, gain_ref), refs = refs[:n_sums], refs[n_sums : n_sums + 2], refs[n_sums + 2 :]
        out, wq_out, wk_out, wv_out, o_out, g_out = refs[:6]
        ff_out, refs = refs[6 : 6 + n_sums], refs[6 + n_sums :]
        bufs, sems = refs[:4], refs[4]
        w_in, w_sum, o_in, o_sum, g_in, g_sum, g_last = refs[5:12]
        w_sems, block_sems, o_sems, g_sems, pack_sems, moved, ff_sems, local = refs[12:]
        line = Line(n_blk)
        across, along = Exchange("head", n_head), Exchange("blk", n_blk)
        h, b = across.me, along.me
        (sh, sb), (th, tb) = place_of_out_rows(n_head, n_blk)
        stays = (th == h) & (tb == b)
        moves = jnp.logical_not(stays)
        greet_all((across, along), moves=(moves, {"head": sh, "blk": sb}))

        def w_copy(k):
            return across.copy(k, w_src.at[across.peer(k)], w_in.at[k], w_sems)

        def o_copy(k):
            return across.copy(k, o_src.at[across.peer(k)], o_in.at[k], o_sems)

        lanes = n_blk * rows_here

        def g_part(head):
            return g_src.at[:, pl.ds(pl.multiple_of(head * lanes, 128), lanes)]

        def g_copy(k):
            return across.copy(k, g_part(across.peer(k)), g_in.at[k], g_sems)

        def landings():
            kv = pl.ds(pl.multiple_of(b // copies * HEAD_DIM, HEAD_DIM), HEAD_DIM)
            return (
                wq_out.at[:, pl.ds(pl.multiple_of(b * q_cols, HEAD_DIM), q_cols)],
                wk_out.at[b % copies, :, kv],
                wv_out.at[b % copies, :, kv],
            )

        spans = (
            pl.ds(0, q_cols),
            pl.ds(q_cols, HEAD_DIM),
            pl.ds(q_cols + HEAD_DIM, HEAD_DIM),
        )

        def block_copies(k):
            for w, there in enumerate(landings()):
                yield along.copy(
                    k, w_sum.at[along.peer(k), :, spans[w]], there, block_sems.at[w]
                )

        def pack_copy(k):
            tile = along.peer(k) * rows_here // 128 * 128
            part = g_sum.at[:, pl.ds(pl.multiple_of(tile, 128), 128)]
            return along.copy(k, part, g_last.at[b], pack_sems)

        move_out = pltpu.make_async_remote_copy(
            src_ref=o_sum,
            dst_ref=o_out,
            send_sem=moved.at[0],
            recv_sem=moved.at[1],
            device_id={"head": th, "blk": tb},
            device_id_type=MESH,
        )
        keep_out = pltpu.make_async_copy(o_sum, o_out, moved.at[2])

        def hop(e):
            weight, part, order = entries[e]
            return flip_copy(
                ff_src[weight].at[1, part], ff_out[weight].at[part], order[0], ff_sems, e
            )

        own_w = pltpu.make_async_copy(w_src.at[h], w_in.at[0], local.at[0])
        own_g = pltpu.make_async_copy(g_part(h), g_in.at[0], local.at[1])
        own_blocks = [
            pltpu.make_async_copy(w_sum.at[b, :, spans[w]], there, local.at[4 + w])
            for w, there in enumerate(landings())
        ]
        own_o = pltpu.make_async_copy(o_src.at[h], o_in.at[0], local.at[3])
        scatter = Scatter(line, part, bufs, sems)
        scatter.start()
        own_w.start()
        own_g.start()
        own_o.start()
        for k in range(1, n_head):
            g_copy(k).start()
            w_copy(k).start()
        for k in range(1, n_head):
            o_copy(k).start()
        for e in range(len(entries)):
            hop(e).start()
        scatter.step(0)
        own_g.wait()
        for k in range(1, n_head):
            g_copy(k).wait_recv()
        g_sum[...] = sum(g_in[k] for k in range(n_head))
        own_tile = b * rows_here // 128 * 128
        g_last[b] = g_sum[:, pl.ds(pl.multiple_of(own_tile, 128), 128)]
        for k in range(1, n_blk):
            pack_copy(k).start()
        for tau in range(1, chips - 2):
            scatter.step(tau)
        own_w.wait()
        for k in range(1, n_head):
            w_copy(k).wait_recv()

        def add(j, carry):
            total = w_in[0, j].astype(F32)
            for k in range(1, n_head):
                total += w_in[k, j].astype(F32)
            w_sum[j] = total.astype(BF16)
            return carry

        lax.fori_loop(0, n_blk, add, 0)
        for one in own_blocks:
            one.start()
        for k in range(1, n_blk):
            for copy in block_copies(k):
                copy.start()

        scatter.step(chips - 2)
        own_o.wait()
        for k in range(1, n_head):
            o_copy(k).wait_recv()

        def add_out(r):
            total = o_in[0, r, :].astype(F32)
            for k in range(1, n_head):
                total += o_in[k, r, :].astype(F32)
            o_sum[r, :] = total.astype(BF16)

        by_rows(rows_here, 16, add_out)

        @pl.when(stays)
        def _():
            keep_out.start()

        @pl.when(jnp.logical_not(stays))
        def _():
            move_out.start()

        def consume(r, dxn):
            unit, factor = unit_of(x_ref[r, :].astype(F32))
            out[r, :] = unit_back(dxn * gain_ref[0:1, :], unit, factor)

        scatter.total(consume)
        for k in range(1, n_blk):
            pack_copy(k).wait_recv()
        g_out[...] = sum(g_last[k] for k in range(n_blk))
        scatter.finish()
        for one in own_blocks:
            one.wait()
        for k in range(1, n_head):
            g_copy(k).wait_send()
            o_copy(k).wait_send()
            w_copy(k).wait_send()
        for k in range(1, n_blk):
            pack_copy(k).wait_send()
            for copy in block_copies(k):
                copy.wait()
        for e in range(len(entries)):
            hop(e).wait()

        @pl.when(stays)
        def _():
            keep_out.wait()

        @pl.when(jnp.logical_not(stays))
        def _():
            move_out.wait()

    return pl.pallas_call(
        kernel,
        out_shape=(
            jax.ShapeDtypeStruct((count, width), F32),
            jax.ShapeDtypeStruct((rows_here, n_blk * q_cols), BF16),
            *[jax.ShapeDtypeStruct((copies, rows_here, n_blk // copies * HEAD_DIM), BF16)] * 2,
            jax.ShapeDtypeStruct((rows_here, width), BF16),
            jax.ShapeDtypeStruct((pack.shape[0], 128), F32),
            *(jax.ShapeDtypeStruct(one.shape[1:], BF16) for one in sums),
        ),
        in_specs=[ANYWHERE] * (4 + n_sums) + [IN_VMEM] * 2,
        out_specs=[IN_VMEM] + [ANYWHERE] * 4 + [IN_VMEM] + [ANYWHERE] * n_sums,
        scratch_shapes=[
            *scatter_bufs(chips, count, width),
            pltpu.VMEM((n_head, n_blk, rows_here, columns), BF16),
            pltpu.VMEM((n_blk, rows_here, columns), BF16),
            pltpu.VMEM((n_head, rows_here, width), BF16),
            pltpu.VMEM((rows_here, width), BF16),
            pltpu.VMEM((n_head, pack.shape[0], n_blk * rows_here), F32),
            pltpu.VMEM((pack.shape[0], n_blk * rows_here), F32),
            pltpu.VMEM((n_blk, pack.shape[0], 128), F32),
            pair_sems(n_head),
            pltpu.SemaphoreType.DMA((3, 2, n_blk)),
            pair_sems(n_head),
            pair_sems(n_head),
            pair_sems(n_blk),
            pltpu.SemaphoreType.DMA((3,)),
            pair_sems(max(1, len(entries))),
            pltpu.SemaphoreType.DMA((7,)),
        ],
        compiler_params=params(collective_id),
        cost_estimate=comm_cost(total_rows * width),
        name="last_scatter",
    )(
        partial_rows.astype(BF16).reshape(chips, 2, count, width),
        w_grad,
        out_grad.reshape(n_head, rows_here, width),
        pack,
        *sums,
        hidden,
        gain,
    )


ROWS = 256
CHUNKS = 2


def block_of(k, size=ROWS):
    return pl.ds(pl.multiple_of(k * size, size), size)


class View:
    def __init__(self, ref, rows):
        self.ref, self.rows = ref, rows
        self.at = self

    def __getitem__(self, index):
        if len(index) == 3:
            j, core, inner = index
            return self.ref.at[j, core, pl.ds(self.rows.start + inner.start, inner.size)]
        j, core = index
        return self.ref.at[j, core, self.rows]


def scatter_gather(
    partial_rows, prepare, between, inputs, outputs, beside, n_head, n_blk, collective_id
):
    total_rows, width = partial_rows.shape
    chips, count = n_blk // 2, total_rows // n_blk
    size = count // CHUNKS
    operands, results, result_specs, more_scratch, aliases, make = beside
    n_in, n_out, n_op, n_res = len(inputs), len(outputs), len(operands), len(results)

    def kernel(part, *refs):
        refs = list(refs)

        def take(n):
            taken = refs[:n]
            del refs[:n]
            return taken

        ins, ops, outs = take(n_in), take(n_op), take(n_out)
        (gathered,) = take(1)
        ress = take(n_res)
        (made,) = take(1)
        chunk_scratch = [take(6) for _ in range(CHUNKS)]
        line = Line(n_blk)
        across = Exchange("head", n_head)
        greet_all((across,), line)
        prepare(outs)
        other = make(ops, ress, refs)
        scatters, gathers = [], []
        for q in range(CHUNKS):
            own, sib, inn, outgoing, sems, g_sems = chunk_scratch[q]
            rows = pl.ds(q * size, size)
            scatters.append(Scatter(line, View(part, rows), (own, sib, inn, outgoing), sems))
            gathers.append(Gather(line, made.at[rows], View(gathered, rows), g_sems))

        def turn(q):
            def consume(r, value):
                r = pl.ds(pl.multiple_of(r.start + q * size, 16), r.size)
                made[r, :] = between(r, value, ins, outs).astype(BF16)

            scatters[q].total(consume)
            gathers[q].start()

        scatters[0].start()
        other.start()
        for q in range(1, CHUNKS):
            scatters[q].start()
        for q in range(CHUNKS):
            for tau in range(chips - 1):
                scatters[q].step(tau)
                if q:
                    gathers[q - 1].step(tau + 1)
            turn(q)
        for s in range(1, chips):
            gathers[-1].step(s)
        for q in range(CHUNKS):
            scatters[q].finish()
            gathers[q].finish()
        other.finish()

    per_chunk = []
    for _ in range(CHUNKS):
        per_chunk += [*scatter_bufs(chips, size, width), gather_sems(chips)]
    given = pl.pallas_call(
        kernel,
        out_shape=(
            *outputs,
            jax.ShapeDtypeStruct((chips, 2, count, width), BF16),
            *results,
        ),
        in_specs=[ANYWHERE] + [IN_VMEM] * n_in + [ANYWHERE] * n_op,
        out_specs=[IN_VMEM] * n_out + [ANYWHERE] + list(result_specs),
        scratch_shapes=[pltpu.VMEM((count, width), BF16), *per_chunk, *more_scratch],
        input_output_aliases={1 + n_in + i: n_out + 1 + o for i, o in aliases.items()},
        compiler_params=params(collective_id),
        cost_estimate=comm_cost(2 * total_rows * width),
        name="scatter_gather",
    )(partial_rows.astype(BF16).reshape(chips, 2, count, width), *inputs, *operands)
    return (
        *given[:n_out],
        given[n_out].reshape(total_rows, width),
        *given[n_out + 1 :],
    )


def spread_beside(full, n_head):
    entries = ff_entries(full[0].shape[1], n_head)

    def make(ops, ress, scratch):
        return Spread(ress, entries, n_head, scratch[0])

    return (
        tuple(full),
        tuple(jax.ShapeDtypeStruct(w.shape, w.dtype) for w in full),
        [ANYWHERE] * 3,
        [Spread.sem_shape(n_head)],
        {0: 0, 1: 1, 2: 2},
        make,
    )


def collect_beside(have, carried, n_head):
    entries = ff_entries(have[0].shape[1], n_head)
    levels = n_head.bit_length() - 2
    shapes = [(n_head // 2, *one.shape[1:]) for one in have]

    def make(ops, ress, scratch):
        kept, inbox = scratch[0:3], scratch[3:6]
        return Collect(ops[:3], kept, inbox, ress[:3], entries, n_head, scratch[6])

    return (
        (*have, carried),
        (
            *(jax.ShapeDtypeStruct((2, *one.shape[1:]), BF16) for one in have),
            jax.ShapeDtypeStruct(carried.shape, carried.dtype),
        ),
        [IN_VMEM] * 3 + [ANYWHERE],
        [
            *(pltpu.VMEM(shape, BF16) for shape in shapes),
            *(pltpu.VMEM((levels, *shape), BF16) for shape in shapes),
            Collect.sem_shape(n_head),
        ],
        {3: 3},
        make,
    )


class Rows:
    def __init__(self, ref, q, size, chips):
        self.ref, self.base, self.size = ref, q * size * chips * 2, size
        self.at = self

    def rows(self, j, core, start=0, count=None):
        first = self.base + (j * 2 + core) * self.size + start
        return pl.ds(pl.multiple_of(first, 16), count or self.size)

    def __getitem__(self, index):
        j, core, *inner = index
        if inner:
            return self.ref.at[self.rows(j, core, inner[0].start, inner[0].size)]
        return self.ref.at[self.rows(j, core)]


class OwnRows:
    def __init__(self, rows, core):
        self.view, self.core = rows, core
        self.shape = (0, rows.size)

    def __getitem__(self, index):
        j, r, _ = index
        return self.view.ref[self.view.rows(j, self.core, r.start, r.size), :]


class LocalScatter(Scatter):
    def __init__(self, line, part, bufs, sems):
        super().__init__(line, part, (OwnRows(part, line.c), *bufs), sems)

    def start(self):
        chips = self.line.chips
        order = []
        for k in range((chips + 1) // 2):
            order += [chips - 1 - k, k]
        for j in order[:chips]:
            self.to_sibling(j).start()

    def ready(self, j):
        self.to_sibling(j).wait_recv()


def turned(values, cosine, sine):
    return values * cosine + pltpu.roll(values, HEAD_DIM // 2, 1) * sine


def local_params(collective_id):
    if collective_id is None:
        return pltpu.CompilerParams(vmem_limit_bytes=60 * 2**20)
    return pltpu.CompilerParams(
        collective_id=collective_id, has_side_effects=True, vmem_limit_bytes=60 * 2**20
    )


def spec_of(shape, dtype):
    return jax.ShapeDtypeStruct(shape, dtype)


def attention_forward(
    rows, weights, small, w_out, ids, cot, cot_rows, ff, q_cols, copies, n_head, n_blk, collective_id
):
    count, width = rows.shape
    chips, pack = n_blk // 2, n_blk * count
    rows_here, rows_ff = w_out.shape[0], ff[0].shape[0]
    entries = ff_entries(rows_ff, n_head)
    columns, q_here = q_cols + 2 * HEAD_DIM, q_cols // HEAD_DIM
    together, n_all = 128 // rows_here, n_head * n_blk
    blocks = pack // ROWS
    scale = 1.0 / math.sqrt(HEAD_DIM)

    def kernel(src, cot_ref, *refs):
        w_src, (pack_src, out_src), ff_src = refs[:3], refs[3:5], refs[5:8]
        pos, seg, blk_ids = refs[8:11]
        part_hbm, xn_hbm, p_hbm, cot_hbm = refs[11:15]
        ff_out, refs = refs[15:18], refs[18:]
        w_ref, vec_ref, gate_ref, cos_ref, sin_ref = refs[:5]
        lin_ref, q_ref, k_ref, v_ref, sig_ref, o_ref, gated_ref, o_rows = refs[5:13]
        x_s, xn_s, p_s, low_ref, code_ref, key_ref, g_all, xn_sem, p_sem, part_sem = refs[13:23]
        sems, block_sems, w_sems, pack_sems, g_sems, moved, local = refs[23:30]
        cot_sems, out_sems, ff_sems = refs[30:]
        line = Line(n_blk)
        across, along = Exchange("head", n_head), Exchange("blk", n_blk)
        h, b = across.me, along.me
        h_me, b_me = h, b
        (th, tb), (sh, sb) = place_of_out_rows(n_head, n_blk)
        stays = (th == h) & (tb == b)
        moves = jnp.logical_not(stays)
        greet_all((across, along), moves=(moves, {"head": sh, "blk": sb}))

        def at_rows(head, blk):
            first = (head * n_blk + blk) * rows_here
            return pl.ds(pl.multiple_of(first, rows_here), rows_here)

        def of_head(head):
            size = n_blk * rows_here
            return pl.ds(pl.multiple_of(head * size, size), size)

        def out_rows_of(head):
            return o_rows.at[pl.ds(pl.multiple_of(head * rows_here, rows_here), rows_here)]

        def block_copies(k):
            for w, there, here in weight_pieces(along.peer(k), q_cols, copies):
                yield along.copy(
                    k, w_src[w].at[:, there], w_ref.at[at_rows(h, b), here], block_sems.at[w]
                )

        def pack_copy(k):
            return along.copy(k, pack_src, g_all.at[h, b], pack_sems)

        def w_copy(k):
            return across.copy(k, w_ref.at[of_head(h)], w_ref.at[of_head(h)], w_sems)

        def g_copy(k):
            return across.copy(k, g_all.at[h], g_all.at[h], g_sems)

        def out_copy(k):
            return across.copy(k, out_rows_of(h), out_rows_of(h), out_sems)

        def hop(e):
            weight, part, order = entries[e]
            return flip_copy(
                ff_src[weight].at[part], ff_out[weight].at[part], order[0], ff_sems, e
            )

        move_out = pltpu.make_async_remote_copy(
            src_ref=out_src,
            dst_ref=out_rows_of(th),
            send_sem=moved.at[0],
            recv_sem=moved.at[1],
            device_id={"head": th, "blk": tb},
            device_id_type=MESH,
        )
        keep_out = pltpu.make_async_copy(out_src, out_rows_of(h), moved.at[2])
        locals_ = [
            pltpu.make_async_copy(
                w_src[w].at[:, there], w_ref.at[at_rows(h, b), here], local.at[w]
            )
            for w, there, here in weight_pieces(b, q_cols, copies)
        ] + [pltpu.make_async_copy(pack_src, g_all.at[h, b], local.at[3])]
        for k in range(1, n_blk):
            for copy in block_copies(k):
                copy.start()
        tokens = Gather(line, src, Rows(x_s, 0, count, chips), sems)
        gather = Gather(line, cot_ref.at[pl.ds(0, cot_rows)], cot_hbm, cot_sems)
        for k in range(1, n_blk):
            pack_copy(k).start()
        for one in locals_:
            one.start()

        @pl.when(stays)
        def _():
            keep_out.start()

        @pl.when(moves)
        def _():
            move_out.start()

        for e in (2, 3):
            hop(e).start()
        half = HEAD_DIM // 2
        index = lax.broadcasted_iota(jnp.int32, (half, ROWS), 0).astype(F32)
        frequency = jnp.exp(index * (-2.0 * math.log(ROPE_BASE) / HEAD_DIM))
        pack_row = pl.ds(h, 1)
        key_ref[...] = (seg[pack_row, :] * pack + blk_ids[pack_row, :]).astype(F32)

        def tables(n, carry):
            r = block_of(n)
            angles = frequency * pos[pack_row, r].astype(F32)
            cosine, sine = jnp.cos(angles), jnp.sin(angles)
            cos_ref[r, :] = jnp.concatenate([cosine, cosine], axis=0).T
            sin_ref[r, :] = jnp.concatenate([-sine, sine], axis=0).T
            low_ref[r, :] = jnp.broadcast_to((seg[pack_row, r] * pack).astype(F32), (128, ROWS)).T
            code_ref[r, :] = jnp.broadcast_to(key_ref[:, r], (128, ROWS)).T
            return carry

        lax.fori_loop(0, pack // ROWS, tables, 0)
        for one in locals_:
            one.wait()
        for k in range(1, n_blk):
            pack_copy(k).wait_recv()
        for k in range(1, n_head):
            g_copy(k).start()
        for k in range(1, n_blk):
            for copy in block_copies(k):
                copy.wait_recv()
        tokens.start()
        for k in range(1, n_head):
            w_copy(k).start()

        @pl.when(stays)
        def _():
            keep_out.wait()

        @pl.when(moves)
        def _():
            move_out.wait_recv()

        for k in range(1, n_head):
            out_copy(k).start()
        for s in range(1, chips):
            tokens.step(s)
        gather.start()
        for e in (0, 1):
            hop(e).start()
        for k in range(1, n_head):
            g_copy(k).wait()
        everyone = [g_all.at[d // n_blk, d % n_blk] for d in range(n_all)]
        vec_ref[...] = jnp.zeros_like(vec_ref)
        for t in range(width // 128):
            tile = sum(one[...] for one in everyone[t * together : (t + 1) * together])
            vec_ref[0:2, t * 128 : (t + 1) * 128] = tile[0:2]
            gate_ref[:, t * 128 : (t + 1) * 128] = tile[8:].astype(BF16)
        vec_ref[2:4, 0:128] = sum(one[2:4, :] for one in everyone)
        tokens.finish()
        for k in range(1, n_head):
            w_copy(k).wait()

        def xn_store(n):
            return pltpu.make_async_copy(
                xn_s.at[block_of(n)], xn_hbm.at[block_of(n)], xn_sem.at[n]
            )

        def p_store(h, n):
            return pltpu.make_async_copy(
                p_s.at[h, block_of(n)], p_hbm.at[h, block_of(n)], p_sem.at[h, n]
            )

        def part_store(n):
            return pltpu.make_async_copy(
                x_s.at[block_of(n)], part_hbm.at[block_of(n)], part_sem.at[n]
            )

        def project(n, carry):
            r = block_of(n)
            unit, _ = unit_of(x_s[r, :].astype(F32))
            xn = (unit * vec_ref[0:1, :]).astype(BF16)
            xn_s[r, :] = xn
            xn_store(n).start()
            lin = mm(xn, w_ref[...])
            lin_ref[r, :] = lin
            gate = mm_nt(xn, gate_ref[...])
            one_of = lax.broadcasted_iota(jnp.int32, (ROWS, HEADS), 1)
            lane = lax.broadcasted_iota(jnp.int32, (ROWS, GATE_PAD), 1)
            sigs = jnp.zeros((ROWS, GATE_PAD), F32)
            for h in range(q_here):
                own = jnp.where(one_of == b_me * q_here + h, gate, 0.0)
                own = jax.nn.sigmoid(jnp.sum(own, axis=1, keepdims=True))
                sigs = jnp.where(lane == h, own, sigs)
            sig_ref[r, :] = sigs
            cosine, sine = cos_ref[r, :], sin_ref[r, :]
            for h in range(q_here):
                at = slice(h * HEAD_DIM, (h + 1) * HEAD_DIM)
                unit_q, _ = unit_of(lin[:, at])
                q_ref[r, at] = turned(unit_q * vec_ref[2:3, :HEAD_DIM], cosine, sine).astype(BF16)
            unit_k, _ = unit_of(lin[:, q_cols : q_cols + HEAD_DIM])
            k_ref[r, :] = turned(unit_k * vec_ref[3:4, :HEAD_DIM], cosine, sine).astype(BF16)
            v_ref[r, :] = lin[:, q_cols + HEAD_DIM :].astype(BF16)
            return carry

        lax.fori_loop(0, blocks, project, 0)
        gather.step(1)
        for k in range(1, n_head):
            out_copy(k).wait_recv()

        def attend(n, carry):
            @pl.when(n == blocks - 1)
            def _():
                gather.step(2)

            r = block_of(n)
            visible = (key_ref[...] >= low_ref[r, 0:1]) & (key_ref[...] <= code_ref[r, 0:1])
            for h in range(q_here):
                at = slice(h * HEAD_DIM, (h + 1) * HEAD_DIM)
                scores = mm_nt(q_ref[r, at], k_ref[...]) * scale
                scores = jnp.where(visible, scores, MASKED)
                top = jnp.max(scores, axis=-1, keepdims=True)
                weights = jnp.exp(scores - top)
                weights = weights * (1.0 / jnp.sum(weights, axis=-1, keepdims=True))
                prob = weights.astype(BF16)
                p_s[h, r, :] = prob
                p_store(h, n).start()
                out = mm(prob, v_ref[...]).astype(BF16)
                o_ref[r, at] = out
                gated_ref[r, at] = (out.astype(F32) * sig_ref[r, h : h + 1]).astype(BF16)
            x_s[r, :] = mm(gated_ref[r, :], o_rows[...]).astype(BF16)
            part_store(n).start()
            return carry

        lax.fori_loop(0, blocks, attend, 0)
        for s in range(3, chips):
            gather.step(s)
        gather.finish()
        for k in range(1, n_head):
            out_copy(k).wait_send()
        for e in range(len(entries)):
            hop(e).wait()
        for k in range(1, n_blk):
            pack_copy(k).wait_send()
            for copy in block_copies(k):
                copy.wait_send()

        @pl.when(moves)
        def _():
            move_out.wait_send()

        for n in range(blocks):
            xn_store(n).wait()
            part_store(n).wait()
            for h in range(q_here):
                p_store(h, n).wait()

    dma = pltpu.SemaphoreType.DMA
    return pl.pallas_call(
        kernel,
        out_shape=(
            spec_of((pack, width), BF16),
            spec_of((pack, width), BF16),
            spec_of((q_here, pack, pack), BF16),
            spec_of((chips, 2, cot_rows, width), BF16),
            *(spec_of(w.shape, BF16) for w in ff),
            spec_of((width, columns), BF16),
            spec_of((8, width), F32),
            spec_of((HEADS, width), BF16),
            spec_of((pack, HEAD_DIM), F32),
            spec_of((pack, HEAD_DIM), F32),
            spec_of((pack, columns), F32),
            spec_of((pack, q_cols), BF16),
            spec_of((pack, HEAD_DIM), BF16),
            spec_of((pack, HEAD_DIM), BF16),
            spec_of((pack, GATE_PAD), F32),
            spec_of((pack, q_cols), BF16),
            spec_of((pack, q_cols), BF16),
            spec_of((q_cols, width), BF16),
        ),
        in_specs=[IN_VMEM] * 2 + [ANYWHERE] * 8 + [IN_VMEM] * 3,
        out_specs=[ANYWHERE] * 7 + [IN_VMEM] * 13,
        scratch_shapes=[
            pltpu.VMEM((pack, width), BF16),
            pltpu.VMEM((pack, width), BF16),
            pltpu.VMEM((q_here, pack, pack), BF16),
            pltpu.VMEM((pack, 128), F32),
            pltpu.VMEM((pack, 128), F32),
            pltpu.VMEM((1, pack), F32),
            pltpu.VMEM((n_head, n_blk, PACK_ROWS, 128), F32),
            dma((blocks,)),
            dma((q_here, blocks)),
            dma((blocks,)),
            gather_sems(chips),
            dma((3, 2, n_blk)),
            pair_sems(n_head),
            pair_sems(n_blk),
            pair_sems(n_head),
            dma((3,)),
            dma((4,)),
            gather_sems(chips),
            pair_sems(n_head),
            pair_sems(len(entries)),
        ],
        compiler_params=local_params(collective_id),
        cost_estimate=comm_cost(pack * width),
        name="attention_forward",
    )(rows, cot, *weights, small, w_out, *ff, *ids)


def attention_backward(
    dy, xn, p, saved, w_attn, vec, gates, tables, mlp_gain_part, q_here, beside=None
):
    pack, width = dy.shape
    columns = w_attn.shape[1]
    q_cols = q_here * HEAD_DIM
    blocks = pack // ROWS
    scale = 1.0 / math.sqrt(HEAD_DIM)

    have, n_head, collective_id = beside or ((), 0, None)
    n_have = len(have)
    sum_scratch = []
    if have:
        entries = ff_entries(have[0].shape[1], n_head)
        sum_scratch = [pair_sems(len(entries))]

    def kernel(dy_hbm, xn_hbm, p_hbm, *refs):
        have_refs, refs = refs[:n_have], refs[n_have:]
        n_plain = 14 + 4
        plain, more = refs[:n_plain], refs[n_plain:]
        got, more = more[:n_have], more[n_have:]
        plain_scratch, sems = more[:14], more[14:]
        if not have:
            return local(dy_hbm, xn_hbm, p_hbm, *plain, *plain_scratch)
        greet_all((Exchange("head", n_head),))
        copies = [
            flip_copy(have_refs[w].at[1, part], got[w].at[part], order[0], sems[0], e)
            for e, (w, part, order) in enumerate(entries)
        ]
        for copy in copies:
            copy.start()
        local(dy_hbm, xn_hbm, p_hbm, *plain, *plain_scratch)
        for copy in copies:
            copy.wait()

    def local(dy_hbm, xn_hbm, p_hbm, lin_ref, q_ref, k_ref, v_ref, sig_ref, o_ref, *refs):
        gated_ref, o_rows, w_ref, vec_ref, gate_ref, cos_ref, sin_ref, mlp_ref = refs[:8]
        dxn_hbm, dw_ref, pack_ref, dout_ref = refs[8:12]
        dy_s, xn_s, p_s, do_s, delta_s, dgate_s, dlin_s, dk_s, dv_s, dgq_s = refs[12:22]
        dy_sem, xn_sem, p_sem, out_sem = refs[22:]
        first_head = lax.axis_index("blk") * q_here

        def dy_load(n):
            return pltpu.make_async_copy(
                dy_hbm.at[block_of(n)], dy_s.at[block_of(n)], dy_sem.at[n]
            )

        def p_load(h, n):
            return pltpu.make_async_copy(
                p_hbm.at[h, block_of(n)], p_s.at[h, block_of(n)], p_sem.at[h, n]
            )

        def dxn_store(n):
            return pltpu.make_async_copy(
                dy_s.at[block_of(n)], dxn_hbm.at[block_of(n)], out_sem.at[n]
            )

        xn_load = pltpu.make_async_copy(xn_hbm, xn_s, xn_sem)
        for n in range(blocks):
            dy_load(n).start()
        for n in range(blocks):
            for h in range(q_here):
                p_load(h, n).start()
        xn_load.start()

        def through_gate(n, carry):
            r = block_of(n)
            dy_load(n).wait()
            dgated = mm_nt(dy_s[r, :], o_rows[...])
            lane = lax.broadcasted_iota(jnp.int32, (ROWS, GATE_PAD), 1)
            dgates = jnp.zeros((ROWS, GATE_PAD), F32)
            deltas = jnp.zeros((ROWS, GATE_PAD), F32)
            for h in range(q_here):
                at = slice(h * HEAD_DIM, (h + 1) * HEAD_DIM)
                sig = sig_ref[r, h : h + 1]
                out = o_ref[r, at].astype(F32)
                do = (dgated[:, at] * sig).astype(BF16)
                do_s[r, at] = do
                dgate = jnp.sum(dgated[:, at] * out, axis=-1, keepdims=True) * sig * (1.0 - sig)
                delta = jnp.sum(do.astype(F32) * out, axis=-1, keepdims=True)
                dgates = jnp.where(lane == first_head + h, dgate, dgates)
                deltas = jnp.where(lane == h, delta, deltas)
            dgate_s[r, :] = dgates.astype(BF16)
            delta_s[r, :] = deltas
            return carry

        lax.fori_loop(0, blocks, through_gate, 0)

        def out_grad(n, carry):
            c = block_of(n)
            dout_ref[:, c] = mm_tn(gated_ref[...], dy_s[:, c]).astype(BF16)
            return carry

        lax.fori_loop(0, width // ROWS, out_grad, 0)
        dk_s[...] = jnp.zeros_like(dk_s)
        dv_s[...] = jnp.zeros_like(dv_s)
        dgq_s[...] = jnp.zeros_like(dgq_s)

        def into_lin(grad, lin, gain, r):
            grad = turned(grad.astype(BF16).astype(F32), cos_ref[r, :], -sin_ref[r, :])
            unit, factor = unit_of(lin)
            return unit_back(grad * gain, unit, factor).astype(BF16), grad * unit

        def attend(n, carry):
            r = block_of(n)
            for h in range(q_here):
                at = slice(h * HEAD_DIM, (h + 1) * HEAD_DIM)
                p_load(h, n).wait()
                do, prob, q = do_s[r, at], p_s[h, r, :], q_ref[r, at]
                dp = mm_nt(do, v_ref[...])
                ds = (prob.astype(F32) * (dp - delta_s[r, h : h + 1])).astype(BF16)
                dq = mm(ds, k_ref[...]) * scale
                dk_s[...] += mm(q.T, ds)
                dv_s[...] += mm(do.T, prob)
                dlin, part = into_lin(dq, lin_ref[r, at], vec_ref[2:3, :HEAD_DIM], r)
                dlin_s[r, at] = dlin
                dgq_s[...] += jnp.sum(part.reshape(ROWS // 8, 8, HEAD_DIM), axis=0)
            return carry

        lax.fori_loop(0, blocks, attend, 0)
        every = pl.ds(0, pack)
        k_cols = slice(q_cols, q_cols + HEAD_DIM)
        dlin, part = into_lin(
            dk_s[...].T * scale, lin_ref[:, k_cols], vec_ref[3:4, :HEAD_DIM], every
        )
        dlin_s[:, k_cols] = dlin
        dgk = jnp.sum(part, axis=0, keepdims=True)
        dgq = jnp.sum(dgq_s[...], axis=0, keepdims=True)
        pack_ref[HEADS:, :] = jnp.zeros((PACK_ROWS - HEADS, width), F32)
        pack_ref[HEADS : HEADS + 1, :] = jnp.sum(mlp_ref[...], axis=0, keepdims=True)
        for t in range(width // HEAD_DIM):
            lanes = slice(t * HEAD_DIM, (t + 1) * HEAD_DIM)
            pack_ref[HEADS + 1 : HEADS + 2, lanes] = dgq
            pack_ref[HEADS + 2 : HEADS + 3, lanes] = dgk
        dlin_s[:, q_cols + HEAD_DIM :] = dv_s[...].T.astype(BF16)

        def into_x(n, carry):
            r = block_of(n)
            dxn = mm_nt(dlin_s[r, :], w_ref[...]) + mm(dgate_s[r, :HEADS], gate_ref[...])
            dy_s[r, :] = dxn.astype(BF16)
            dxn_store(n).start()
            return carry

        lax.fori_loop(0, blocks, into_x, 0)
        xn_load.wait()
        dgate_t = dgate_s[...].astype(F32).T[:HEADS].astype(BF16)

        def weights(n, carry):
            c = block_of(n)
            xn_cols = xn_s[:, c]
            dw_ref[c, :] = mm_tn(xn_cols, dlin_s[...]).astype(BF16)
            pack_ref[:HEADS, c] = mm(dgate_t, xn_cols)
            return carry

        lax.fori_loop(0, width // ROWS, weights, 0)
        for n in range(blocks):
            dxn_store(n).wait()

    return pl.pallas_call(
        kernel,
        out_shape=(
            spec_of((pack, width), BF16),
            spec_of((width, columns), BF16),
            spec_of((PACK_ROWS, width), F32),
            spec_of((q_cols, width), BF16),
            *(spec_of(one.shape[1:], BF16) for one in have),
        ),
        in_specs=[ANYWHERE] * (3 + n_have) + [IN_VMEM] * 14,
        out_specs=[ANYWHERE] + [IN_VMEM] * 3 + [ANYWHERE] * n_have,
        scratch_shapes=[
            pltpu.VMEM((pack, width), BF16),
            pltpu.VMEM((pack, width), BF16),
            pltpu.VMEM((q_here, pack, pack), BF16),
            pltpu.VMEM((pack, q_cols), BF16),
            pltpu.VMEM((pack, GATE_PAD), F32),
            pltpu.VMEM((pack, GATE_PAD), BF16),
            pltpu.VMEM((pack, columns), BF16),
            pltpu.VMEM((HEAD_DIM, pack), F32),
            pltpu.VMEM((HEAD_DIM, pack), F32),
            pltpu.VMEM((8, HEAD_DIM), F32),
            pltpu.SemaphoreType.DMA((blocks,)),
            pltpu.SemaphoreType.DMA,
            pltpu.SemaphoreType.DMA((q_here, blocks)),
            pltpu.SemaphoreType.DMA((blocks,)),
            *sum_scratch,
        ],
        compiler_params=local_params(collective_id),
        name="attention_backward",
    )(dy, xn, p, *have, *saved, w_attn, vec, gates, *tables, mlp_gain_part)


def attention_end(
    dy, xn, p, mlp_part, ff_sums, saved, w_attn, vec, gates, tables, token_rows, q_here, copies,
    n_head, n_blk, collective_id
):
    pack, width = dy.shape
    columns = w_attn.shape[1]
    q_cols = q_here * HEAD_DIM
    blocks = pack // ROWS
    scale = 1.0 / math.sqrt(HEAD_DIM)
    chips, count = n_blk // 2, pack // n_blk
    rows_here = width // (n_head * n_blk)
    lanes = n_blk * rows_here
    entries = ff_entries(ff_sums[0].shape[1], n_head)

    def kernel(dy_hbm, xn_hbm, p_hbm, mlp_hbm, *refs):
        refs = list(refs)

        def take(n):
            taken = refs[:n]
            del refs[:n]
            return taken

        ff_src = take(3)
        lin_ref, q_ref, k_ref, v_ref, sig_ref, o_ref, gated_ref, o_rows = take(8)
        w_ref, vec_ref, gate_ref, cos_ref, sin_ref = take(5)
        x_ref, middle_ref, dmid_ref, mlp_gain_ref = take(4)
        layer_out, input_grad, g_out, wq_out, wk_out, wv_out, o_out = take(7)
        ff_out = take(3)
        dy_s, xn_s, p_s, do_s, delta_s, dgate_s, dlin_s, dk_s, dv_s, dgq_s = take(10)
        dw_s, pack_s, dout_s, w_in, w_sum, o_in, o_sum, g_in, g_sum, g_last = take(10)
        mlp_scratch, dxn_scratch, (xg_s,) = take(5), take(4), take(1)
        dy_sem, xn_sem, p_sem = take(3)
        w_sems, block_sems, o_sems, g_sems, pack_sems, moved, ff_sems, local = refs
        line = Line(n_blk)
        across, along = Exchange("head", n_head), Exchange("blk", n_blk)
        h, b = across.me, along.me
        first_head = b * q_here
        (sh, sb), (th, tb) = place_of_out_rows(n_head, n_blk)
        stays = (th == h) & (tb == b)
        moves = jnp.logical_not(stays)
        greet_all((across, along), moves=(moves, {"head": sh, "blk": sb}))

        def dy_load(n):
            return pltpu.make_async_copy(
                dy_hbm.at[block_of(n)], dy_s.at[block_of(n)], dy_sem.at[n]
            )

        def p_load(head, n):
            return pltpu.make_async_copy(
                p_hbm.at[head, block_of(n)], p_s.at[head, block_of(n)], p_sem.at[head, n]
            )

        def of_head(head):
            return pl.ds(pl.multiple_of(head * lanes, lanes), lanes)

        def of_blk(blk):
            return pl.ds(pl.multiple_of(blk * rows_here, rows_here), rows_here)

        def out_of(head):
            return dout_s.at[pl.ds(pl.multiple_of(head * rows_here, rows_here), rows_here)]

        def w_copy(k):
            return across.copy(k, dw_s.at[of_head(across.peer(k))], w_in.at[k], w_sems)

        def o_copy(k):
            return across.copy(k, out_of(across.peer(k)), o_in.at[k], o_sems)

        def g_part(head):
            return pack_s.at[:, pl.ds(pl.multiple_of(head * lanes, 128), lanes)]

        def g_copy(k):
            return across.copy(k, g_part(across.peer(k)), g_in.at[k], g_sems)

        def landings():
            kv = pl.ds(pl.multiple_of(b // copies * HEAD_DIM, HEAD_DIM), HEAD_DIM)
            return (
                wq_out.at[:, pl.ds(pl.multiple_of(b * q_cols, HEAD_DIM), q_cols)],
                wk_out.at[b % copies, :, kv],
                wv_out.at[b % copies, :, kv],
            )

        spans = (
            pl.ds(0, q_cols),
            pl.ds(q_cols, HEAD_DIM),
            pl.ds(q_cols + HEAD_DIM, HEAD_DIM),
        )

        def block_copies(k):
            for w, there in enumerate(landings()):
                src = w_sum.at[of_blk(along.peer(k)), spans[w]]
                yield along.copy(k, src, there, block_sems.at[w])

        def tile_of(blk):
            return pl.ds(pl.multiple_of(blk * rows_here // 128 * 128, 128), 128)

        def pack_copy(k):
            return along.copy(k, g_sum.at[:, tile_of(along.peer(k))], g_last.at[b], pack_sems)

        move_out = pltpu.make_async_remote_copy(
            src_ref=o_sum,
            dst_ref=o_out,
            send_sem=moved.at[0],
            recv_sem=moved.at[1],
            device_id={"head": th, "blk": tb},
            device_id_type=MESH,
        )
        keep_out = pltpu.make_async_copy(o_sum, o_out, moved.at[2])
        hops = [
            flip_copy(ff_src[w].at[1, part], ff_out[w].at[part], order[0], ff_sems, e)
            for e, (w, part, order) in enumerate(entries)
        ]
        own_blocks = [
            pltpu.make_async_copy(w_sum.at[of_blk(b), spans[w]], there, local.at[w])
            for w, there in enumerate(landings())
        ]
        mlp = Scatter(line, mlp_hbm, mlp_scratch[:4], mlp_scratch[4])
        dxn = LocalScatter(
            line, Rows(dy_s, 0, count, chips), dxn_scratch[:3], dxn_scratch[3]
        )
        xn_load = pltpu.make_async_copy(xn_hbm, xn_s, xn_sem)
        for n in range(blocks):
            dy_load(n).start()
        mlp.start()
        for n in range(blocks):
            for head in range(q_here):
                p_load(head, n).start()
        xn_load.start()
        for hop in hops[2:]:
            hop.start()

        def through_gate(n, carry):
            @pl.when(n == blocks // 2)
            def _():
                mlp.step(0)

            r = block_of(n)
            dy_load(n).wait()
            dgated = mm_nt(dy_s[r, :], o_rows[...])
            lane = lax.broadcasted_iota(jnp.int32, (ROWS, GATE_PAD), 1)
            dgates = jnp.zeros((ROWS, GATE_PAD), F32)
            deltas = jnp.zeros((ROWS, GATE_PAD), F32)
            for head in range(q_here):
                at = slice(head * HEAD_DIM, (head + 1) * HEAD_DIM)
                sig = sig_ref[r, head : head + 1]
                out = o_ref[r, at].astype(F32)
                do = (dgated[:, at] * sig).astype(BF16)
                do_s[r, at] = do
                dgate = jnp.sum(dgated[:, at] * out, axis=-1, keepdims=True) * sig * (1.0 - sig)
                delta = jnp.sum(do.astype(F32) * out, axis=-1, keepdims=True)
                dgates = jnp.where(lane == first_head + head, dgate, dgates)
                deltas = jnp.where(lane == head, delta, deltas)
            dgate_s[r, :] = dgates.astype(BF16)
            delta_s[r, :] = deltas
            return carry

        lax.fori_loop(0, blocks, through_gate, 0)

        def out_grad(n, carry):
            c = block_of(n)
            dout_s[:, c] = mm_tn(gated_ref[...], dy_s[:, c]).astype(BF16)
            return carry

        lax.fori_loop(0, width // ROWS, out_grad, 0)
        dk_s[...] = jnp.zeros_like(dk_s)
        dv_s[...] = jnp.zeros_like(dv_s)
        dgq_s[...] = jnp.zeros_like(dgq_s)
        xg_s[...] = jnp.zeros_like(xg_s)
        o_in[0] = dout_s[pl.ds(pl.multiple_of(h * rows_here, rows_here), rows_here), :]
        for k in range(1, n_head):
            o_copy(k).start()

        def into_lin(grad, lin, gain, r):
            grad = turned(grad.astype(BF16).astype(F32), cos_ref[r, :], -sin_ref[r, :])
            unit, factor = unit_of(lin)
            return unit_back(grad * gain, unit, factor).astype(BF16), grad * unit

        def attend(n, carry):
            @pl.when(n == blocks // 2)
            def _():
                mlp.step(1)

            r = block_of(n)
            for head in range(q_here):
                at = slice(head * HEAD_DIM, (head + 1) * HEAD_DIM)
                p_load(head, n).wait()
                do, prob, q = do_s[r, at], p_s[head, r, :], q_ref[r, at]
                dp = mm_nt(do, v_ref[...])
                ds = (prob.astype(F32) * (dp - delta_s[r, head : head + 1])).astype(BF16)
                dq = mm(ds, k_ref[...]) * scale
                dk_s[...] += mm(q.T, ds)
                dv_s[...] += mm(do.T, prob)
                dlin, part = into_lin(dq, lin_ref[r, at], vec_ref[2:3, :HEAD_DIM], r)
                dlin_s[r, at] = dlin
                dgq_s[...] += jnp.sum(part.reshape(ROWS // 8, 8, HEAD_DIM), axis=0)
            return carry

        lax.fori_loop(0, blocks, attend, 0)
        every = pl.ds(0, pack)
        k_cols = slice(q_cols, q_cols + HEAD_DIM)
        dlin, part = into_lin(
            dk_s[...].T * scale, lin_ref[:, k_cols], vec_ref[3:4, :HEAD_DIM], every
        )
        dlin_s[:, k_cols] = dlin
        dlin_s[:, q_cols + HEAD_DIM :] = dv_s[...].T.astype(BF16)

        dgk = jnp.sum(part, axis=0, keepdims=True)
        dgq = jnp.sum(dgq_s[...], axis=0, keepdims=True)
        pack_s[HEADS:, :] = jnp.zeros((PACK_ROWS - HEADS, width), F32)
        pack_s[HEADS : HEADS + 1, :] = jnp.sum(mlp_gain_ref[...], axis=0, keepdims=True)
        for t in range(width // HEAD_DIM):
            at = slice(t * HEAD_DIM, (t + 1) * HEAD_DIM)
            pack_s[HEADS + 1 : HEADS + 2, at] = dgq
            pack_s[HEADS + 2 : HEADS + 3, at] = dgk
        xn_load.wait()
        dgate_t = dgate_s[...].astype(F32).T[:HEADS].astype(BF16)

        def weights(n, carry):
            c = block_of(n)
            xn_cols = xn_s[:, c]
            dw_s[c, :] = mm_tn(xn_cols, dlin_s[...]).astype(BF16)
            pack_s[:HEADS, c] = mm(dgate_t, xn_cols)
            return carry

        lax.fori_loop(0, width // ROWS, weights, 0)
        for k in range(1, n_head):
            w_copy(k).start()
        w_in[0] = dw_s[of_head(h), :]

        def into_x(n, carry):
            r = block_of(n)
            back = mm_nt(dlin_s[r, :], w_ref[...]) + mm(dgate_s[r, :HEADS], gate_ref[...])
            dy_s[r, :] = back.astype(BF16)
            product = back * xn_s[r, :].astype(F32)
            xg_s[...] += jnp.sum(product.reshape(ROWS // 8, 8, width), axis=0)
            return carry

        lax.fori_loop(0, blocks, into_x, 0)
        dxn.start()
        pack_s[HEADS + 3 : HEADS + 4, :] = jnp.sum(xg_s[...], axis=0, keepdims=True)
        for k in range(1, n_head):
            g_copy(k).start()
        for hop in hops[:2]:
            hop.start()
        g_in[0] = pack_s[:, pl.ds(pl.multiple_of(h * lanes, 128), lanes)]
        for tau in range(2, chips - 1):
            mlp.step(tau)
        dxn.step(0)
        def finish_layer(r, value):
            layer_out[r, :] = (middle_ref[r, :] + value).astype(BF16)

        mlp.total(finish_layer)
        for tau in range(1, chips - 2):
            dxn.step(tau)
        for k in range(1, n_head):
            g_copy(k).wait_recv()
        g_sum[...] = sum(g_in[k] for k in range(n_head))
        g_last[b] = g_sum[:, tile_of(b)]
        for k in range(1, n_blk):
            pack_copy(k).start()
        for k in range(1, n_head):
            o_copy(k).wait_recv()

        def add_out(r):
            o_sum[r, :] = sum(o_in[k, r, :].astype(F32) for k in range(n_head)).astype(BF16)

        by_rows(rows_here, 16, add_out)

        @pl.when(stays)
        def _():
            keep_out.start()

        @pl.when(moves)
        def _():
            move_out.start()

        for k in range(1, n_head):
            w_copy(k).wait_recv()

        def add(r):
            w_sum[r, :] = sum(w_in[k, r, :].astype(F32) for k in range(n_head)).astype(BF16)

        by_rows(lanes, 64, add)
        for one in own_blocks:
            one.start()
        for k in range(1, n_blk):
            for copy in block_copies(k):
                copy.start()
        dxn.step(chips - 2)

        def consume(r, value):
            unit, factor = unit_of(x_ref[r, :].astype(F32))
            back = unit_back(value * vec_ref[0:1, :], unit, factor)
            input_grad[r, :] = dmid_ref[r, :] + back

        dxn.total(consume)
        for k in range(1, n_blk):
            pack_copy(k).wait_recv()
        g_out[...] = sum(g_last[k] for k in range(n_blk))
        mlp.finish()
        dxn.finish()
        for one in own_blocks:
            one.wait()
        for k in range(1, n_head):
            g_copy(k).wait_send()
            o_copy(k).wait_send()
            w_copy(k).wait_send()
        for k in range(1, n_blk):
            pack_copy(k).wait_send()
            for copy in block_copies(k):
                copy.wait()
        for hop in hops:
            hop.wait()

        @pl.when(stays)
        def _():
            keep_out.wait()

        @pl.when(moves)
        def _():
            move_out.wait()

    dma = pltpu.SemaphoreType.DMA
    kv = spec_of((copies, rows_here, n_blk // copies * HEAD_DIM), BF16)
    return pl.pallas_call(
        kernel,
        out_shape=(
            spec_of((count, width), BF16),
            spec_of((count, width), F32),
            spec_of((PACK_ROWS, 128), F32),
            spec_of((rows_here, n_blk * q_cols), BF16),
            kv,
            kv,
            spec_of((rows_here, width), BF16),
            *(spec_of(one.shape[1:], BF16) for one in ff_sums),
        ),
        in_specs=[ANYWHERE] * 7 + [IN_VMEM] * 17,
        out_specs=[IN_VMEM] * 3 + [ANYWHERE] * 7,
        scratch_shapes=[
            pltpu.VMEM((pack, width), BF16),
            pltpu.VMEM((pack, width), BF16),
            pltpu.VMEM((q_here, pack, pack), BF16),
            pltpu.VMEM((pack, q_cols), BF16),
            pltpu.VMEM((pack, GATE_PAD), F32),
            pltpu.VMEM((pack, GATE_PAD), BF16),
            pltpu.VMEM((pack, columns), BF16),
            pltpu.VMEM((HEAD_DIM, pack), F32),
            pltpu.VMEM((HEAD_DIM, pack), F32),
            pltpu.VMEM((8, HEAD_DIM), F32),
            pltpu.VMEM((width, columns), BF16),
            pltpu.VMEM((PACK_ROWS, width), F32),
            pltpu.VMEM((q_cols, width), BF16),
            pltpu.VMEM((n_head, lanes, columns), BF16),
            pltpu.VMEM((lanes, columns), BF16),
            pltpu.VMEM((n_head, rows_here, width), BF16),
            pltpu.VMEM((rows_here, width), BF16),
            pltpu.VMEM((n_head, PACK_ROWS, lanes), F32),
            pltpu.VMEM((PACK_ROWS, lanes), F32),
            pltpu.VMEM((n_blk, PACK_ROWS, 128), F32),
            *scatter_bufs(chips, count, width),
            *scatter_bufs(chips, count, width)[1:],
            pltpu.VMEM((8, width), F32),
            dma((blocks,)),
            dma,
            dma((q_here, blocks)),
            pair_sems(n_head),
            dma((3, 2, n_blk)),
            pair_sems(n_head),
            pair_sems(n_head),
            pair_sems(n_blk),
            dma((3,)),
            pair_sems(len(entries)),
            dma((3,)),
        ],
        compiler_params=local_params(collective_id),
        cost_estimate=comm_cost(2 * pack * width),
        name="attention_end",
    )(
        dy,
        xn,
        p,
        mlp_part.reshape(chips, 2, count, width),
        *ff_sums,
        *saved,
        w_attn,
        vec,
        gates,
        *tables,
        *token_rows,
    )


def feed_forward(attn_part, ff, halfway, cot, inputs, to_mlp, to_attention, n_head, n_blk, collective_id):
    total_rows, width = attn_part.shape
    chips, count = n_blk // 2, total_rows // n_blk
    size, half = count // CHUNKS, total_rows // CHUNKS
    rows_ff = ff[0].shape[0]
    units = n_head * rows_ff
    entries = ff_entries(rows_ff, n_head)
    n_in = len(inputs)

    def kernel(part, cot_hbm, *refs):
        refs = list(refs)

        def take(n):
            taken = refs[:n]
            del refs[:n]
            return taken

        sources = take(3), take(3)
        ins = take(n_in)
        middle, dmid, gain_part, dy_hbm, mlp_hbm, *sum_hbm = take(8)
        made, hn_s, cot_s, dhn_s, u_s, da_s, db_s, stage = take(8)
        inboxes, weights = take(3), take(3)
        chunk_scratch = [take(8) for _ in range(CHUNKS)]
        load_sems, hop_sems, cot_sems, stage_sems, sum_sems, grad_sems, late_sems = refs
        line = Line(n_blk)
        across = Exchange("head", n_head)
        greet_all((across,), line)
        gain_part[...] = jnp.zeros_like(gain_part)

        def place(key, span):
            return pl.ds(key * rows_ff + span.start, span.size)

        loads, hops = [], []
        for e, (w, span, order) in enumerate(entries):
            first, second = 1 << order[0], 1 << order[1]
            for at, key in enumerate((0, first)):
                src = sources[at][w].at[span]
                loads.append(
                    pltpu.make_async_copy(src, weights[w].at[place(key, span)], load_sems.at[e, at])
                )
                there = weights[w].at[place(key ^ second, span)]
                hops.append(flip_copy(src, there, order[1], hop_sems, e, at))

        def cot_loads():
            for j in range(chips):
                for c in range(2):
                    yield pltpu.make_async_copy(
                        cot_hbm.at[j, c],
                        Rows(cot_s, 0, size, chips)[j, c],
                        cot_sems.at[2 * j + c],
                    )

        first, gather1, second, gather2 = [], [], [], []
        for q in range(CHUNKS):
            own, sib, inn, outgoing, sems, g_sems, sems2, g_sems2 = chunk_scratch[q]
            rows = pl.ds(q * size, size)
            first.append(Scatter(line, View(part, rows), (own, sib, inn, outgoing), sems))
            gather1.append(Gather(line, made.at[rows], Rows(hn_s, q, size, chips), g_sems))
            second.append(
                LocalScatter(line, Rows(dhn_s, q, size, chips), (sib, inn, outgoing), sems2)
            )
            gather2.append(Gather(line, made.at[rows], View(dy_hbm, rows), g_sems2))

        late = [
            Gather(
                line,
                ins[1].at[pl.ds(q * size, size)],
                Rows(cot_s, q, size, chips),
                late_sems.at[q - 1],
            )
            for q in range(1, CHUNKS)
        ]

        def turn(q, scatter, between, outs, gather):
            def consume(r, value):
                r = pl.ds(pl.multiple_of(r.start + q * size, 16), r.size)
                made[r, :] = between(r, value, ins, outs).astype(BF16)

            scatter[q].total(consume)
            gather[q].start()

        def loop(steps, body):
            lax.fori_loop(0, steps, lambda k, carry: body(k) or carry, 0)

        def span_of(q):
            return pl.ds(q * half, half)

        def unit_block(q, f):
            r, fr = span_of(q), block_of(f)
            a = mm_nt(hn_s[r, :], weights[0][fr, :])
            b = mm_nt(hn_s[r, :], weights[1][fr, :])
            du = mm_nt(cot_s[r, :], weights[2][fr, :])
            sig = jax.nn.sigmoid(a)
            silu = a * sig
            u_s[r, fr] = (silu * b).astype(BF16)
            da_s[r, fr] = (du * b * sig * (1.0 + a * (1.0 - sig))).astype(BF16)
            db_s[r, fr] = (du * silu).astype(BF16)

        def back(q):
            r = span_of(q)

            def body(n):
                cols = block_of(n, 512)
                dhn = mm(da_s[r, :], weights[0][:, cols]) + mm(db_s[r, :], weights[1][:, cols])
                dhn_s[r, cols] = dhn.astype(BF16)

            loop(width // 512, body)

        def stage_stores(q):
            for j in range(chips):
                for c in range(2):
                    yield pltpu.make_async_copy(
                        Rows(stage, 0, size, chips)[j, c],
                        mlp_hbm.at[j, c, pl.ds(q * size, size)],
                        stage_sems.at[2 * j + c],
                    )

        def mlp_out(q):
            if q:
                for store in stage_stores(q - 1):
                    store.wait()
            r = span_of(q)

            def body(n):
                cols = block_of(n, 512)
                stage[:, cols] = mm(u_s[r, :], weights[2][:, cols]).astype(BF16)

            loop(width // 512, body)
            for store in stage_stores(q):
                store.start()

        def grad(w):
            left, right = ((da_s, hn_s), (db_s, hn_s), (u_s, cot_s))[w]

            def body(f):
                fr = block_of(f)
                weights[w][fr, :] = mm_tn(left[:, fr], right[...]).astype(BF16)

            loop(units // ROWS, body)

        def sum_copies(w):
            for e, (weight, span, order) in enumerate(entries):
                if weight == w:
                    for at, key in enumerate((0, 1 << order[0])):
                        yield flip_copy(
                            weights[w].at[place(key ^ (1 << order[1]), span)],
                            inboxes[w].at[at, span],
                            order[1],
                            sum_sems,
                            e,
                            at,
                        )

        def sum_stores(w):
            for e, (weight, span, order) in enumerate(entries):
                if weight == w:
                    for at, key in enumerate((0, 1 << order[0])):
                        yield pltpu.make_async_copy(
                            weights[w].at[place(key, span)],
                            sum_hbm[w].at[at, span],
                            grad_sems.at[e, at],
                        )

        def send_grad(w):
            grad(w)
            for copy in sum_copies(w):
                copy.start()

        def add_grad(w):
            for copy in sum_copies(w):
                copy.wait()
            for weight, span, order in entries:
                if weight == w:
                    for at, key in enumerate((0, 1 << order[0])):

                        def body(r, span=span, at=at, key=key):
                            r = pl.ds(pl.multiple_of(r.start + span.start, 16), r.size)
                            mine = pl.ds(pl.multiple_of(r.start + key * rows_ff, 16), r.size)
                            value = weights[w][mine, :].astype(F32)
                            value += inboxes[w][at, r, :].astype(F32)
                            weights[w][mine, :] = value.astype(BF16)

                        by_rows(span.size, 16, body)
            for store in sum_stores(w):
                store.start()

        first[0].start()
        for hop in hops:
            hop.start()
        for q in range(1, CHUNKS):
            first[q].start()
        for one in late:
            one.start()
        for load in loads:
            load.start()
        for load in cot_loads():
            load.start()
        steps = chips - 1
        for tau in range(steps):
            first[0].step(tau)
            for one in late:
                one.step(tau + 1)
        turn(0, first, to_mlp, (middle,), gather1)
        for tau in range(steps):
            first[1].step(tau)
            gather1[0].step(tau + 1)
        turn(1, first, to_mlp, (middle,), gather1)
        for q in range(CHUNKS):
            first[q].finish()
        gather1[0].finish()
        gather1[1].step(1)
        for load in loads:
            load.wait()
        for load in cot_loads():
            load.wait()
        for hop in hops:
            hop.wait()
        blocks = units // ROWS

        def first_units(f):
            unit_block(0, f)
            for s in range(2, chips):

                @pl.when(f == s - 2)
                def _(s=s):
                    gather1[1].step(s)

        loop(blocks, first_units)
        for s in range(blocks + 2, chips):
            gather1[1].step(s)
        back(0)
        second[0].start()
        gather1[1].finish()
        for one in late:
            one.finish()
        second[0].step(0)
        loop(blocks, lambda f: unit_block(1, f))
        second[0].step(1)
        back(1)
        second[1].start()
        send_grad(0)
        for tau in range(2, steps):
            second[0].step(tau)
        second[1].step(0)
        send_grad(1)
        turn(0, second, to_attention, (middle, dmid, gain_part), gather2)
        second[1].step(1)
        mlp_out(0)
        mlp_out(1)
        gather2[0].step(1)
        send_grad(2)
        for tau in range(2, steps):
            second[1].step(tau)
            gather2[0].step(tau)
        turn(1, second, to_attention, (middle, dmid, gain_part), gather2)
        gather2[0].step(chips - 1)
        for s in range(1, chips):
            gather2[1].step(s)
        for w in range(3):
            add_grad(w)
        for q in range(CHUNKS):
            second[q].finish()
            gather2[q].finish()
        for store in stage_stores(CHUNKS - 1):
            store.wait()
        for w in range(3):
            for store in sum_stores(w):
                store.wait()

    per_chunk = []
    for _ in range(CHUNKS):
        own, sib, inn, outgoing, sems = scatter_bufs(chips, size, width)
        per_chunk += [own, sib, inn, outgoing, sems, gather_sems(chips), sems, gather_sems(chips)]
    sums = jax.ShapeDtypeStruct((2, rows_ff, width), BF16)
    shards_ = jax.ShapeDtypeStruct((chips, 2, count, width), BF16)
    dma = pltpu.SemaphoreType.DMA
    middle, dmid, gain_part, dy, mlp_part, *ff_sums = pl.pallas_call(
        kernel,
        out_shape=(
            jax.ShapeDtypeStruct((count, width), F32),
            jax.ShapeDtypeStruct((count, width), F32),
            jax.ShapeDtypeStruct((8, width), F32),
            shards_,
            shards_,
            *[sums] * 3,
        ),
        in_specs=[ANYWHERE] * 8 + [IN_VMEM] * n_in,
        out_specs=[IN_VMEM] * 3 + [ANYWHERE] * 5,
        scratch_shapes=[
            pltpu.VMEM((count, width), BF16),
            *[pltpu.VMEM((total_rows, width), BF16)] * 3,
            *[pltpu.VMEM((total_rows, units), BF16)] * 3,
            pltpu.VMEM((half, width), BF16),
            *[pltpu.VMEM((2, rows_ff, width), BF16)] * 3,
            *[pltpu.VMEM((units, width), BF16)] * 3,
            *per_chunk,
            dma((len(entries), 2)),
            dma((2, len(entries), 2)),
            dma((n_blk,)),
            dma((n_blk,)),
            dma((2, len(entries), 2)),
            dma((len(entries), 2)),
            dma((CHUNKS - 1, 7, chips, PIECES)),
        ],
        compiler_params=pltpu.CompilerParams(
            collective_id=collective_id, has_side_effects=True, vmem_limit_bytes=62 * 2**20
        ),
        cost_estimate=comm_cost(2 * total_rows * width),
        name="feed_forward",
    )(
        attn_part.reshape(chips, 2, count, width),
        cot,
        *ff,
        *halfway,
        *inputs,
    )
    return (
        middle,
        dmid,
        gain_part,
        dy.reshape(total_rows, width),
        mlp_part.reshape(total_rows, width),
        ff_sums,
    )


def padded(values, size):
    return jnp.pad(values, [(0, 0)] * (values.ndim - 1) + [(0, size - values.shape[-1])])


def shards(
    hidden,
    segment_ids,
    block_ids,
    positions,
    attn_gain,
    w_query,
    key_weight_matrix,
    value_weight_matrix,
    q_gain,
    k_gain,
    w_head_gate,
    w_out,
    mlp_gain,
    w_gate,
    w_up,
    w_down,
    cotangent,
):
    n_head = lax.axis_size("head")
    n_blk = lax.axis_size("blk")
    n_all = n_head * n_blk
    my_head = lax.axis_index("head")
    my_blk = lax.axis_index("blk")
    tokens = hidden.shape[1]
    pack = tokens * n_blk
    rows_here = w_query.shape[0]
    rows_ff = w_gate.shape[0]
    q_here = HEADS // n_blk
    q_cols = q_here * HEAD_DIM
    kv_copies = max(1, n_blk // KV_HEADS)
    kv_here = max(1, KV_HEADS // n_blk)
    kv_cols = kv_here * HEAD_DIM
    device = my_head * n_blk + my_blk
    together = 128 // rows_here
    lane = jnp.arange(128)
    here = (lane // rows_here == device % together)[None]
    mine = jnp.concatenate(
        [
            attn_gain[None],
            mlp_gain[None],
            jnp.zeros((6, rows_here), BF16),
            w_head_gate.T,
        ]
    )
    small = jnp.where(here, jnp.tile(mine, (1, together)), 0).astype(F32)
    share = q_gain.shape[0]
    head_gains = jnp.stack([jnp.tile(q_gain, n_all), jnp.tile(k_gain, n_all)]).astype(F32)
    head_gains = jnp.where(lane // share == device, head_gains, 0)
    small = small + jnp.pad(head_gains, ((2, PACK_ROWS - 4), (0, 0)))
    ids = (positions, segment_ids, block_ids)
    fused = n_head == 4 and pack <= 1024
    ff = (w_gate, w_up, w_down)
    attn_part, xn, prob, cot, *rest = attention_forward(
        hidden[0],
        (w_query, key_weight_matrix, value_weight_matrix),
        small,
        w_out,
        ids,
        cotangent[0],
        tokens // CHUNKS if fused else tokens,
        ff,
        q_cols,
        kv_copies,
        n_head,
        n_blk,
        0,
    )
    halfway, (w_attn, vec, gates), tables, saved = rest[:3], rest[3:6], rest[6:8], rest[8:]

    def to_mlp(r, total, ins, outs):
        x_ref, gain_ref = ins
        mid = x_ref[r, :].astype(F32) + total
        outs[0][r, :] = mid
        unit, _ = unit_of(mid)
        return unit * gain_ref[1:2, :]

    def to_attention(r, dhn, ins, outs):
        mid_ref, cot_ref, gain_ref = ins
        unit, factor = unit_of(mid_ref[r, :])
        product = dhn * unit
        seen = outs[1]
        seen[...] += product[:8] + product[8:]
        back = cot_ref[r, :].astype(F32) + unit_back(dhn * gain_ref[1:2, :], unit, factor)
        outs[0][r, :] = back
        return back

    if fused:

        def into_mlp(r, total, ins, outs):
            return to_mlp(r, total, (ins[0], ins[2]), outs)

        def into_attention(r, dhn, ins, outs):
            return to_attention(r, dhn, (outs[0], ins[1], ins[2]), outs[1:])

        middle, dmid, mlp_gain_part, dy, mlp_part, ff_sums = feed_forward(
            attn_part,
            ff,
            halfway,
            cot,
            (hidden[0], cotangent[0], vec),
            into_mlp,
            into_attention,
            n_head,
            n_blk,
            1,
        )
    else:
        cot = cot.reshape(pack, MODEL_WIDTH)
        ff_full = []
        for w, (own, other) in enumerate(zip(ff, halfway)):
            full = jnp.zeros((n_head, *own.shape), BF16).at[0].set(own)
            for weight, part, order in ff_entries(rows_ff, n_head):
                if weight == w:
                    span = slice(part.start, part.start + part.size)
                    full = full.at[1 << order[0], span].set(other[span])
            ff_full.append(full)
        middle, hn, *ff_rows = scatter_gather(
            attn_part,
            lambda outs: None,
            to_mlp,
            (hidden[0], vec),
            (jax.ShapeDtypeStruct(hidden.shape[1:], F32),),
            spread_beside(ff_full, n_head),
            n_head,
            n_blk,
            1,
        )
        gate_rows, up_rows, down_rows = (one.reshape(n_head * rows_ff, MODEL_WIDTH) for one in ff_rows)

        a = mm_nt(hn, gate_rows)
        b = mm_nt(hn, up_rows)
        sig = jax.nn.sigmoid(a)
        silu = a * sig
        u = (silu * b).astype(BF16)
        mlp_part = mm(u, down_rows).astype(BF16)
        du = mm_nt(cot, down_rows)
        da = (du * b * sig * (1.0 + a * (1.0 - sig))).astype(BF16)
        db = (du * silu).astype(BF16)
        ff_parts = [
            mm_tn(left, right).astype(BF16).reshape(n_head, rows_ff, MODEL_WIDTH)
            for left, right in ((da, hn), (db, hn), (u, cot))
        ]

        def clear(outs):
            outs[1][...] = jnp.zeros_like(outs[1])

        dmid, mlp_gain_part, dy, *ff_sums, mlp_part = scatter_gather(
            mm(da, gate_rows) + mm(db, up_rows),
            clear,
            to_attention,
            (middle, cotangent[0], vec),
            (
                jax.ShapeDtypeStruct(hidden.shape[1:], F32),
                jax.ShapeDtypeStruct((8, MODEL_WIDTH), F32),
            ),
            collect_beside(ff_parts, mlp_part, n_head),
            n_head,
            n_blk,
            2,
        )

    if fused:
        layer_output, input_grad, small_sums, query_grad, key_grad, value_grad, out_grad, *ff_last = (
            attention_end(
                dy,
                xn,
                prob,
                mlp_part,
                ff_sums,
                saved,
                w_attn,
                vec,
                gates,
                tables,
                (hidden[0], middle, dmid, mlp_gain_part),
                q_here,
                kv_copies,
                n_head,
                n_blk,
                2,
            )
        )
        layer_output, input_grad = layer_output[None], input_grad[None]
    else:
        layer_output = (
            middle + lax.psum_scatter(mlp_part, "blk", scatter_dimension=0, tiled=True).astype(F32)
        ).astype(BF16)[None]
        dxn_part, attn_grad, small_parts, out_grad = attention_backward(
            dy,
            xn,
            prob,
            saved,
            w_attn,
            vec,
            gates,
            tables,
            mlp_gain_part,
            q_here,
            None,
        )
        back_x, query_grad, key_grad, value_grad, out_grad, small_sums, *ff_last = last_scatter(
            dxn_part,
            attn_grad.reshape(n_head, n_blk, rows_here, -1),
            out_grad,
            small_parts,
            ff_sums,
            hidden[0],
            vec,
            q_cols,
            kv_copies,
            n_head,
            n_blk,
            3,
        )
        input_grad = (dmid + back_x)[None]
    ff_grads = [one[0].astype(F32) + two.astype(F32) for one, two in zip(ff_sums, ff_last)]

    query_grad = query_grad.astype(F32)
    key_grad = jnp.sum(key_grad.astype(F32), axis=0)
    value_grad = jnp.sum(value_grad.astype(F32), axis=0)
    small_sums = jnp.sum(
        jnp.where(
            jnp.arange(together)[None, :, None] == device % together,
            small_sums.reshape(PACK_ROWS, together, rows_here),
            0.0,
        ),
        axis=1,
    ), small_sums[HEADS + 1 : HEADS + 3]
    small_sums, head_sums = small_sums
    head_sums = lax.dynamic_slice_in_dim(head_sums, device * share, share, 1)
    head_gate_grad = small_sums[:HEADS].T
    if fused:
        scaled = small_sums[HEADS + 3]
    else:
        scaled = (
            jnp.sum(w_query.astype(F32) * query_grad, axis=1)
            + jnp.sum(key_weight_matrix.astype(F32) * key_grad, axis=1)
            + jnp.sum(value_weight_matrix.astype(F32) * value_grad, axis=1)
            + jnp.sum(w_head_gate.astype(F32) * head_gate_grad, axis=1)
        )
    attn_gain_grad = scaled / attn_gain.astype(F32)
    return (
        layer_output,
        input_grad,
        attn_gain_grad,
        query_grad,
        key_grad,
        value_grad,
        head_sums[0],
        head_sums[1],
        head_gate_grad,
        out_grad.astype(F32),
        small_sums[HEADS],
        ff_grads[0],
        ff_grads[1],
        ff_grads[2],
    )


def solution(mesh):
    rows = P(("head", "blk"), None)
    vector = P(("head", "blk"))
    token = P("head", "blk", None)
    return jax.shard_map(
        shards,
        mesh=mesh,
        in_specs=(
            token, P(), P(), P(), vector, rows, rows, rows, vector, vector, rows, rows, vector,
            rows, rows, rows, token,
        ),
        out_specs=(
            token, token, vector, rows, rows, rows, vector, vector, rows, rows, vector,
            rows, rows, rows,
        ),
        check_vma=False,
    )
```

```python
import math

import jax
import jax.numpy as jnp
from jax import lax
from jax.experimental import pallas as pl
from jax.experimental.pallas import tpu as pltpu
from jax.sharding import PartitionSpec as P

MODEL_WIDTH = 2048
HEADS = 16
KV_HEADS = 8
HEAD_DIM = 128
GATE_PAD = 128
EPSILON = 1e-06
ROPE_BASE = 1000000.0
MASKED = -1e30
F32 = jnp.float32
BF16 = jnp.bfloat16
MESH = pl.DeviceIdType.MESH


def mm(a, b):
    return jnp.dot(a, b, preferred_element_type=F32)


def mm_nt(a, b):
    return lax.dot_general(a, b, (((1,), (1,)), ((), ())), preferred_element_type=F32)


def mm_tn(a, b):
    return lax.dot_general(a, b, (((0,), (0,)), ((), ())), preferred_element_type=F32)


def unit_of(values):
    factor = lax.rsqrt(jnp.mean(values * values, axis=-1, keepdims=True) + EPSILON)
    return values * factor, factor


def unit_back(scaled, unit, factor):
    return factor * (scaled - unit * jnp.mean(scaled * unit, axis=-1, keepdims=True))


def signal_to(semaphore, target):
    pl.semaphore_signal(semaphore, inc=1, device_id=target, device_id_type=MESH)


class Line:
    def __init__(self, n_blk):
        self.me = lax.axis_index("blk")
        self.chips = n_blk // 2
        self.i = self.me // 2
        self.c = self.me % 2
        self.right = {"blk": self.me + 2}
        self.left = {"blk": self.me - 2}
        self.sibling = {"blk": self.me + 1 - 2 * self.c}
        self.has_right = self.i < self.chips - 1
        self.has_left = self.i > 0

    def greet(self, barrier):
        signal_to(barrier, self.sibling)

        @pl.when(self.has_right)
        def _():
            signal_to(barrier, self.right)

        @pl.when(self.has_left)
        def _():
            signal_to(barrier, self.left)

        return 1 + self.has_right.astype(jnp.int32) + self.has_left.astype(jnp.int32)


class Gather:
    def __init__(self, line, src, out, sems):
        self.line, self.src, self.out, self.sems = line, src, out, sems
        self.pieces = sems.shape[2]
        self.rows = src.shape[0] // self.pieces

    def part(self, p):
        return pl.ds(p * self.rows, self.rows)

    def move(self, kind, src, j, p, target):
        return pltpu.make_async_remote_copy(
            src_ref=src.at[self.part(p)],
            dst_ref=self.out.at[j, self.line.c, self.part(p)],
            send_sem=self.sems.at[kind, j, p],
            recv_sem=self.sems.at[3 + kind, j, p],
            device_id=target,
            device_id_type=MESH,
        )

    def arrived(self, kind, j, p, core):
        there = self.out.at[j, core, self.part(p)]
        pltpu.make_async_remote_copy(
            src_ref=there,
            dst_ref=there,
            send_sem=self.sems.at[kind, j, p],
            recv_sem=self.sems.at[3 + kind, j, p],
            device_id=self.line.sibling,
            device_id_type=MESH,
        ).wait_recv()

    def send(self, src, j, p, right, left):
        line = self.line
        if right is not None:

            @pl.when(right)
            def _():
                self.move(0, src, j, p, line.right).start()

        if left is not None:

            @pl.when(left)
            def _():
                self.move(1, src, j, p, line.left).start()

        self.move(2, src, j, p, line.sibling).start()

    def own_copy(self):
        return pltpu.make_async_copy(
            self.src, self.out.at[self.line.i, self.line.c], self.sems.at[6, 0, 0]
        )

    def start(self):
        line = self.line
        for p in range(self.pieces):
            self.send(self.src, line.i, p, line.has_right, line.has_left)
        self.own_copy().start()

    def step(self, s):
        line = self.line
        from_left, from_right = line.i - s, line.i + s
        for p in range(self.pieces):

            @pl.when(from_left >= 0)
            def _(p=p):
                self.arrived(0, from_left, p, line.c)
                self.send(self.out.at[from_left, line.c], from_left, p, line.has_right, None)

            @pl.when(from_right < line.chips)
            def _(p=p):
                self.arrived(1, from_right, p, line.c)
                self.send(self.out.at[from_right, line.c], from_right, p, None, line.has_left)

    def finish(self):
        line = self.line
        for j in range(line.chips):
            mine = self.out.at[j, line.c]
            for p in range(self.pieces):
                self.arrived(2, j, p, 1 - line.c)
                self.move(2, mine, j, p, line.sibling).wait_send()

                @pl.when((line.i >= j) & line.has_right)
                def _(j=j, p=p, mine=mine):
                    self.move(0, mine, j, p, line.right).wait_send()

                @pl.when((line.i <= j) & line.has_left)
                def _(j=j, p=p, mine=mine):
                    self.move(1, mine, j, p, line.left).wait_send()

        self.own_copy().wait()

    def run(self):
        self.start()
        for s in range(1, self.line.chips):
            self.step(s)
        self.finish()


def by_rows(rows, step, body):
    def one(k, carry):
        body(pl.ds(pl.multiple_of(k * step, step), step))
        return carry

    lax.fori_loop(0, rows // step, one, 0)


SUMS = 2


class Scatter:
    def __init__(self, line, part, bufs, sems):
        self.line, self.part, self.sems = line, part, sems
        self.own, self.sib, self.inn, self.out = bufs

    def copy(self, kind, src, dst, slot, target):
        return pltpu.make_async_remote_copy(
            src_ref=src,
            dst_ref=dst,
            send_sem=self.sems.at[(kind, *slot)],
            recv_sem=self.sems.at[(3 + kind, *slot)],
            device_id=target,
            device_id_type=MESH,
        )

    def to_sibling(self, j):
        line = self.line
        return self.copy(2, self.part.at[j, 1 - line.c], self.sib.at[j], (j, 0), line.sibling)

    def to_own(self, j):
        return pltpu.make_async_copy(
            self.part.at[j, self.line.c], self.own.at[j], self.sems.at[6, j, 0]
        )

    @property
    def size(self):
        return self.own.shape[1] // SUMS

    def along(self, way, j, p):
        line = self.line
        target = line.left if way else line.right
        span = pl.ds(p * self.size, self.size)
        return self.copy(way, self.out.at[j, span], self.inn.at[way, j, span], (j, p), target)

    def start(self):
        chips = self.line.chips
        order = []
        for k in range((chips + 1) // 2):
            order += [chips - 1 - k, k]
        for j in order[:chips]:
            self.to_sibling(j).start()
            self.to_own(j).start()

    def ready(self, j):
        self.to_sibling(j).wait_recv()
        self.to_own(j).wait()

    def rows_of(self, p, body):
        def shifted(r):
            body(pl.ds(pl.multiple_of(r.start + p * self.size, 16), r.size))

        by_rows(self.size, 16, shifted)

    def pass_on(self, way, j, first):
        self.ready(j)
        for p in range(SUMS):

            @pl.when(first)
            def _(p=p):
                def body(r):
                    total = self.own[j, r, :].astype(F32) + self.sib[j, r, :].astype(F32)
                    self.out[j, r, :] = total.astype(BF16)

                self.rows_of(p, body)

            @pl.when(jnp.logical_not(first))
            def _(p=p):
                self.along(way, j, p).wait_recv()

                def body(r):
                    total = self.own[j, r, :].astype(F32) + self.sib[j, r, :].astype(F32)
                    total += self.inn[way, j, r, :].astype(F32)
                    self.out[j, r, :] = total.astype(BF16)

                self.rows_of(p, body)

            self.along(way, j, p).start()

    def step(self, tau):
        line = self.line

        @pl.when((line.i <= tau) & line.has_right)
        def _():
            self.pass_on(0, line.chips - 1 - tau + line.i, line.i == 0)

        @pl.when((line.chips - 1 - line.i <= tau) & line.has_left)
        def _():
            self.pass_on(1, tau - (line.chips - 1 - line.i), line.i == line.chips - 1)

    def total(self, consume):
        line, i = self.line, self.line.i
        self.ready(i)
        for p in range(SUMS):

            @pl.when(line.has_left)
            def _(p=p):
                self.along(0, i, p).wait_recv()

            @pl.when(line.has_right)
            def _(p=p):
                self.along(1, i, p).wait_recv()

        rows = self.own.shape[1]

        def add(r, with_left, with_right):
            total = self.own[i, r, :].astype(F32) + self.sib[i, r, :].astype(F32)
            if with_left:
                total += self.inn[0, i, r, :].astype(F32)
            if with_right:
                total += self.inn[1, i, r, :].astype(F32)
            consume(r, total)

        @pl.when(line.has_left & line.has_right)
        def _():
            by_rows(rows, 16, lambda r: add(r, True, True))

        @pl.when(line.has_left & jnp.logical_not(line.has_right))
        def _():
            by_rows(rows, 16, lambda r: add(r, True, False))

        @pl.when(line.has_right & jnp.logical_not(line.has_left))
        def _():
            by_rows(rows, 16, lambda r: add(r, False, True))

    def finish(self):
        line = self.line
        for j in range(line.chips):
            self.to_sibling(j).wait_send()
            for p in range(SUMS):

                @pl.when(j > line.i)
                def _(j=j, p=p):
                    self.along(0, j, p).wait_send()

                @pl.when(j < line.i)
                def _(j=j, p=p):
                    self.along(1, j, p).wait_send()


PIECES = 2


def gather_sems(chips):
    return pltpu.SemaphoreType.DMA((7, chips, PIECES))


def scatter_bufs(chips, rows, width):
    return [
        pltpu.VMEM((chips, rows, width), BF16),
        pltpu.VMEM((chips, rows, width), BF16),
        pltpu.VMEM((2, chips, rows, width), BF16),
        pltpu.VMEM((chips, rows, width), BF16),
        pltpu.SemaphoreType.DMA((7, chips, SUMS)),
    ]


ANYWHERE = pl.BlockSpec(memory_space=pl.ANY)
IN_VMEM = pl.BlockSpec(memory_space=pltpu.VMEM)


def params(collective_id):
    return pltpu.CompilerParams(
        collective_id=collective_id, has_side_effects=True, vmem_limit_bytes=56 * 2**20
    )


def comm_cost(byte_count):
    return pl.CostEstimate(flops=0, transcendentals=0, bytes_accessed=40 * byte_count)


class Exchange:
    def __init__(self, axis, size):
        self.axis, self.size = axis, size
        self.me = lax.axis_index(axis)

    def peer(self, k):
        return lax.rem(self.me + k, self.size)

    def greet(self, barrier):
        for k in range(1, self.size):
            signal_to(barrier, {self.axis: self.peer(k)})

    def copy(self, k, src, dst, sems):
        return pltpu.make_async_remote_copy(
            src_ref=src,
            dst_ref=dst,
            send_sem=sems.at[0, k],
            recv_sem=sems.at[1, k],
            device_id={self.axis: self.peer(k)},
            device_id_type=MESH,
        )

    def sems(self):
        return pltpu.SemaphoreType.DMA((2, self.size))


def pair_sems(size):
    return pltpu.SemaphoreType.DMA((2, size))


def greet_all(exchanges, line=None, moves=None):
    barrier = pltpu.get_barrier_semaphore()
    count = 0
    for exchange in exchanges:
        exchange.greet(barrier)
        count += exchange.size - 1
    if line is not None:
        count += line.greet(barrier)
    if moves is not None:
        whether, source = moves

        @pl.when(whether)
        def _():
            signal_to(barrier, source)

        count += whether.astype(jnp.int32)
    pl.semaphore_wait(barrier, count)


def flip_copy(src, dst, bit, sems, *index):
    return pltpu.make_async_remote_copy(
        src_ref=src,
        dst_ref=dst,
        send_sem=sems.at[(0, *index)],
        recv_sem=sems.at[(1, *index)],
        device_id={"head": lax.axis_index("head") ^ (1 << bit)},
        device_id_type=MESH,
    )


def ff_entries(rows, n_head):
    bits = tuple(range(n_head.bit_length() - 1))
    back, half = bits[::-1], rows // 2
    return (
        (0, pl.ds(0, rows), bits),
        (1, pl.ds(0, rows), back),
        (2, pl.ds(0, half), bits),
        (2, pl.ds(half, half), back),
    )


def place_of_out_rows(n_head, n_blk):
    h, b = lax.axis_index("head"), lax.axis_index("blk")
    d = h * n_blk + b
    source = b * n_head + h
    return (d % n_head, d // n_head), (source // n_blk, source % n_blk)


PACK_ROWS = 24


def weight_pieces(b, q_cols, copies):
    kv = b // copies * HEAD_DIM
    return (
        (0, pl.ds(pl.multiple_of(b * q_cols, HEAD_DIM), q_cols), pl.ds(0, q_cols)),
        (1, pl.ds(pl.multiple_of(kv, HEAD_DIM), HEAD_DIM), pl.ds(q_cols, HEAD_DIM)),
        (2, pl.ds(pl.multiple_of(kv, HEAD_DIM), HEAD_DIM), pl.ds(q_cols + HEAD_DIM, HEAD_DIM)),
    )


PACK_ROWS = 24


def weight_pieces(b, q_cols, copies):
    kv = b // copies * HEAD_DIM
    return (
        (0, pl.ds(pl.multiple_of(b * q_cols, HEAD_DIM), q_cols), pl.ds(0, q_cols)),
        (1, pl.ds(pl.multiple_of(kv, HEAD_DIM), HEAD_DIM), pl.ds(q_cols, HEAD_DIM)),
        (2, pl.ds(pl.multiple_of(kv, HEAD_DIM), HEAD_DIM), pl.ds(q_cols + HEAD_DIM, HEAD_DIM)),
    )


class Spread:
    def __init__(self, full, entries, n_head, sems):
        self.full, self.entries, self.n_head, self.sems = full, entries, n_head, sems

    def copies(self, e, level):
        weight, part, order = self.entries[e]
        full = self.full[weight]
        bit = order[level]
        keys = [0]
        for low in order[:level]:
            keys += [key ^ (1 << low) for key in keys]
        for key in keys:
            there = key ^ (1 << bit)
            yield flip_copy(
                full.at[key, part], full.at[there, part], bit, self.sems, e, there
            )

    def level(self, level):
        for e in range(len(self.entries)):
            if level > 1:
                for copy in self.copies(e, level - 1):
                    copy.wait_recv()
            for copy in self.copies(e, level):
                copy.start()

    def start(self):
        self.level(1)

    def finish(self):
        levels = self.n_head.bit_length() - 1
        for level in range(2, levels):
            self.level(level)
        for e in range(len(self.entries)):
            for level in range(1, levels):
                for copy in self.copies(e, level):
                    copy.wait_send()
                    if level == levels - 1:
                        copy.wait_recv()

    @staticmethod
    def sem_shape(n_head):
        return pltpu.SemaphoreType.DMA((2, 4, n_head))


class Collect:
    def __init__(self, have, kept, inbox, total, entries, n_head, sems):
        self.have, self.kept, self.inbox, self.total = have, kept, inbox, total
        self.entries, self.n_head, self.sems = entries, n_head, sems

    def keys(self, order, level):
        keys = [0]
        for low in order[: len(order) - 1 - level]:
            keys += [key ^ (1 << low) for key in keys]
        return keys

    def slot(self, order, key):
        return self.keys(order, 0).index(key)

    def copies(self, e, level):
        weight, part, order = self.entries[e]
        bit = order[len(order) - 1 - level]
        for key in self.keys(order, level):
            slot = self.slot(order, key)
            if level == 0:
                src = self.have[weight].at[key ^ (1 << bit), part]
            else:
                src = self.kept[weight].at[self.slot(order, key ^ (1 << bit)), part]
            yield flip_copy(src, self.inbox[weight].at[level, slot, part], bit, self.sems, e, level, slot)

    def locals_(self):
        for e, (weight, part, order) in enumerate(self.entries):
            for key in self.keys(order, 0):
                slot = self.slot(order, key)
                yield pltpu.make_async_copy(
                    self.have[weight].at[key, part],
                    self.kept[weight].at[slot, part],
                    self.sems.at[2, e, 0, slot],
                )

    def start(self):
        for copy in self.locals_():
            copy.start()
        for e in range(len(self.entries)):
            for copy in self.copies(e, 0):
                copy.start()

    def finish(self):
        for copy in self.locals_():
            copy.wait()
        levels = self.n_head.bit_length() - 2
        for level in range(levels):
            last = level == levels - 1
            for e, (weight, part, order) in enumerate(self.entries):
                for copy in self.copies(e, level):
                    copy.wait_recv()
                for at, key in enumerate(self.keys(order, level)):
                    slot = self.slot(order, key)
                    kept, inbox = self.kept[weight], self.inbox[weight]
                    into = self.total[weight] if last else kept
                    where = at if last else slot

                    def body(r, part=part, slot=slot, kept=kept, inbox=inbox, into=into, where=where):
                        r = pl.ds(pl.multiple_of(r.start + part.start, 16), r.size)
                        value = kept[slot, r, :].astype(F32) + inbox[level, slot, r, :].astype(F32)
                        into[where, r, :] = value.astype(BF16)

                    by_rows(part.size, 16, body)
            for e in range(len(self.entries)):
                if not last:
                    for copy in self.copies(e, level + 1):
                        copy.start()
        for level in range(levels):
            for e in range(len(self.entries)):
                for copy in self.copies(e, level):
                    copy.wait_send()

    @staticmethod
    def sem_shape(n_head):
        levels = n_head.bit_length() - 2
        return pltpu.SemaphoreType.DMA((3, 4, levels, n_head // 2))


def last_scatter(
    partial_rows, w_grad, out_grad, pack, sums, hidden, gain, q_cols, copies, n_head, n_blk, collective_id
):
    total_rows, width = partial_rows.shape
    chips, count = n_blk // 2, total_rows // n_blk
    _, _, rows_here, columns = w_grad.shape
    n_sums = len(sums)
    entries = ff_entries(sums[0].shape[1], n_head) if sums else ()

    def kernel(part, w_src, o_src, g_src, *refs):
        ff_src, (x_ref, gain_ref), refs = refs[:n_sums], refs[n_sums : n_sums + 2], refs[n_sums + 2 :]
        out, wq_out, wk_out, wv_out, o_out, g_out = refs[:6]
        ff_out, refs = refs[6 : 6 + n_sums], refs[6 + n_sums :]
        bufs, sems = refs[:4], refs[4]
        w_in, w_sum, o_in, o_sum, g_in, g_sum, g_last = refs[5:12]
        w_sems, block_sems, o_sems, g_sems, pack_sems, moved, ff_sems, local = refs[12:]
        line = Line(n_blk)
        across, along = Exchange("head", n_head), Exchange("blk", n_blk)
        h, b = across.me, along.me
        (sh, sb), (th, tb) = place_of_out_rows(n_head, n_blk)
        stays = (th == h) & (tb == b)
        moves = jnp.logical_not(stays)
        greet_all((across, along), moves=(moves, {"head": sh, "blk": sb}))

        def w_copy(k):
            return across.copy(k, w_src.at[across.peer(k)], w_in.at[k], w_sems)

        def o_copy(k):
            return across.copy(k, o_src.at[across.peer(k)], o_in.at[k], o_sems)

        lanes = n_blk * rows_here

        def g_part(head):
            return g_src.at[:, pl.ds(pl.multiple_of(head * lanes, 128), lanes)]

        def g_copy(k):
            return across.copy(k, g_part(across.peer(k)), g_in.at[k], g_sems)

        def landings():
            kv = pl.ds(pl.multiple_of(b // copies * HEAD_DIM, HEAD_DIM), HEAD_DIM)
            return (
                wq_out.at[:, pl.ds(pl.multiple_of(b * q_cols, HEAD_DIM), q_cols)],
                wk_out.at[b % copies, :, kv],
                wv_out.at[b % copies, :, kv],
            )

        spans = (
            pl.ds(0, q_cols),
            pl.ds(q_cols, HEAD_DIM),
            pl.ds(q_cols + HEAD_DIM, HEAD_DIM),
        )

        def block_copies(k):
            for w, there in enumerate(landings()):
                yield along.copy(
                    k, w_sum.at[along.peer(k), :, spans[w]], there, block_sems.at[w]
                )

        def pack_copy(k):
            tile = along.peer(k) * rows_here // 128 * 128
            part = g_sum.at[:, pl.ds(pl.multiple_of(tile, 128), 128)]
            return along.copy(k, part, g_last.at[b], pack_sems)

        move_out = pltpu.make_async_remote_copy(
            src_ref=o_sum,
            dst_ref=o_out,
            send_sem=moved.at[0],
            recv_sem=moved.at[1],
            device_id={"head": th, "blk": tb},
            device_id_type=MESH,
        )
        keep_out = pltpu.make_async_copy(o_sum, o_out, moved.at[2])

        def hop(e):
            weight, part, order = entries[e]
            return flip_copy(
                ff_src[weight].at[1, part], ff_out[weight].at[part], order[0], ff_sems, e
            )

        own_w = pltpu.make_async_copy(w_src.at[h], w_in.at[0], local.at[0])
        own_g = pltpu.make_async_copy(g_part(h), g_in.at[0], local.at[1])
        own_blocks = [
            pltpu.make_async_copy(w_sum.at[b, :, spans[w]], there, local.at[4 + w])
            for w, there in enumerate(landings())
        ]
        own_o = pltpu.make_async_copy(o_src.at[h], o_in.at[0], local.at[3])
        scatter = Scatter(line, part, bufs, sems)
        scatter.start()
        own_w.start()
        own_g.start()
        own_o.start()
        for k in range(1, n_head):
            g_copy(k).start()
            w_copy(k).start()
        for k in range(1, n_head):
            o_copy(k).start()
        for e in range(len(entries)):
            hop(e).start()
        scatter.step(0)
        own_g.wait()
        for k in range(1, n_head):
            g_copy(k).wait_recv()
        g_sum[...] = sum(g_in[k] for k in range(n_head))
        own_tile = b * rows_here // 128 * 128
        g_last[b] = g_sum[:, pl.ds(pl.multiple_of(own_tile, 128), 128)]
        for k in range(1, n_blk):
            pack_copy(k).start()
        for tau in range(1, chips - 2):
            scatter.step(tau)
        own_w.wait()
        for k in range(1, n_head):
            w_copy(k).wait_recv()

        def add(j, carry):
            total = w_in[0, j].astype(F32)
            for k in range(1, n_head):
                total += w_in[k, j].astype(F32)
            w_sum[j] = total.astype(BF16)
            return carry

        lax.fori_loop(0, n_blk, add, 0)
        for one in own_blocks:
            one.start()
        for k in range(1, n_blk):
            for copy in block_copies(k):
                copy.start()

        scatter.step(chips - 2)
        own_o.wait()
        for k in range(1, n_head):
            o_copy(k).wait_recv()

        def add_out(r):
            total = o_in[0, r, :].astype(F32)
            for k in range(1, n_head):
                total += o_in[k, r, :].astype(F32)
            o_sum[r, :] = total.astype(BF16)

        by_rows(rows_here, 16, add_out)

        @pl.when(stays)
        def _():
            keep_out.start()

        @pl.when(jnp.logical_not(stays))
        def _():
            move_out.start()

        def consume(r, dxn):
            unit, factor = unit_of(x_ref[r, :].astype(F32))
            out[r, :] = unit_back(dxn * gain_ref[0:1, :], unit, factor)

        scatter.total(consume)
        for k in range(1, n_blk):
            pack_copy(k).wait_recv()
        g_out[...] = sum(g_last[k] for k in range(n_blk))
        scatter.finish()
        for one in own_blocks:
            one.wait()
        for k in range(1, n_head):
            g_copy(k).wait_send()
            o_copy(k).wait_send()
            w_copy(k).wait_send()
        for k in range(1, n_blk):
            pack_copy(k).wait_send()
            for copy in block_copies(k):
                copy.wait()
        for e in range(len(entries)):
            hop(e).wait()

        @pl.when(stays)
        def _():
            keep_out.wait()

        @pl.when(jnp.logical_not(stays))
        def _():
            move_out.wait()

    return pl.pallas_call(
        kernel,
        out_shape=(
            jax.ShapeDtypeStruct((count, width), F32),
            jax.ShapeDtypeStruct((rows_here, n_blk * q_cols), BF16),
            *[jax.ShapeDtypeStruct((copies, rows_here, n_blk // copies * HEAD_DIM), BF16)] * 2,
            jax.ShapeDtypeStruct((rows_here, width), BF16),
            jax.ShapeDtypeStruct((pack.shape[0], 128), F32),
            *(jax.ShapeDtypeStruct(one.shape[1:], BF16) for one in sums),
        ),
        in_specs=[ANYWHERE] * (4 + n_sums) + [IN_VMEM] * 2,
        out_specs=[IN_VMEM] + [ANYWHERE] * 4 + [IN_VMEM] + [ANYWHERE] * n_sums,
        scratch_shapes=[
            *scatter_bufs(chips, count, width),
            pltpu.VMEM((n_head, n_blk, rows_here, columns), BF16),
            pltpu.VMEM((n_blk, rows_here, columns), BF16),
            pltpu.VMEM((n_head, rows_here, width), BF16),
            pltpu.VMEM((rows_here, width), BF16),
            pltpu.VMEM((n_head, pack.shape[0], n_blk * rows_here), F32),
            pltpu.VMEM((pack.shape[0], n_blk * rows_here), F32),
            pltpu.VMEM((n_blk, pack.shape[0], 128), F32),
            pair_sems(n_head),
            pltpu.SemaphoreType.DMA((3, 2, n_blk)),
            pair_sems(n_head),
            pair_sems(n_head),
            pair_sems(n_blk),
            pltpu.SemaphoreType.DMA((3,)),
            pair_sems(max(1, len(entries))),
            pltpu.SemaphoreType.DMA((7,)),
        ],
        compiler_params=params(collective_id),
        cost_estimate=comm_cost(total_rows * width),
        name="last_scatter",
    )(
        partial_rows.astype(BF16).reshape(chips, 2, count, width),
        w_grad,
        out_grad.reshape(n_head, rows_here, width),
        pack,
        *sums,
        hidden,
        gain,
    )


ROWS = 256
CHUNKS = 2


def block_of(k, size=ROWS):
    return pl.ds(pl.multiple_of(k * size, size), size)


class View:
    def __init__(self, ref, rows):
        self.ref, self.rows = ref, rows
        self.at = self

    def __getitem__(self, index):
        if len(index) == 3:
            j, core, inner = index
            return self.ref.at[j, core, pl.ds(self.rows.start + inner.start, inner.size)]
        j, core = index
        return self.ref.at[j, core, self.rows]


def scatter_gather(
    partial_rows, prepare, between, inputs, outputs, beside, n_head, n_blk, collective_id
):
    total_rows, width = partial_rows.shape
    chips, count = n_blk // 2, total_rows // n_blk
    size = count // CHUNKS
    operands, results, result_specs, more_scratch, aliases, make = beside
    n_in, n_out, n_op, n_res = len(inputs), len(outputs), len(operands), len(results)

    def kernel(part, *refs):
        refs = list(refs)

        def take(n):
            taken = refs[:n]
            del refs[:n]
            return taken

        ins, ops, outs = take(n_in), take(n_op), take(n_out)
        (gathered,) = take(1)
        ress = take(n_res)
        (made,) = take(1)
        chunk_scratch = [take(6) for _ in range(CHUNKS)]
        line = Line(n_blk)
        across = Exchange("head", n_head)
        greet_all((across,), line)
        prepare(outs)
        other = make(ops, ress, refs)
        scatters, gathers = [], []
        for q in range(CHUNKS):
            own, sib, inn, outgoing, sems, g_sems = chunk_scratch[q]
            rows = pl.ds(q * size, size)
            scatters.append(Scatter(line, View(part, rows), (own, sib, inn, outgoing), sems))
            gathers.append(Gather(line, made.at[rows], View(gathered, rows), g_sems))

        def turn(q):
            def consume(r, value):
                r = pl.ds(pl.multiple_of(r.start + q * size, 16), r.size)
                made[r, :] = between(r, value, ins, outs).astype(BF16)

            scatters[q].total(consume)
            gathers[q].start()

        scatters[0].start()
        other.start()
        for q in range(1, CHUNKS):
            scatters[q].start()
        for q in range(CHUNKS):
            for tau in range(chips - 1):
                scatters[q].step(tau)
                if q:
                    gathers[q - 1].step(tau + 1)
            turn(q)
        for s in range(1, chips):
            gathers[-1].step(s)
        for q in range(CHUNKS):
            scatters[q].finish()
            gathers[q].finish()
        other.finish()

    per_chunk = []
    for _ in range(CHUNKS):
        per_chunk += [*scatter_bufs(chips, size, width), gather_sems(chips)]
    given = pl.pallas_call(
        kernel,
        out_shape=(
            *outputs,
            jax.ShapeDtypeStruct((chips, 2, count, width), BF16),
            *results,
        ),
        in_specs=[ANYWHERE] + [IN_VMEM] * n_in + [ANYWHERE] * n_op,
        out_specs=[IN_VMEM] * n_out + [ANYWHERE] + list(result_specs),
        scratch_shapes=[pltpu.VMEM((count, width), BF16), *per_chunk, *more_scratch],
        input_output_aliases={1 + n_in + i: n_out + 1 + o for i, o in aliases.items()},
        compiler_params=params(collective_id),
        cost_estimate=comm_cost(2 * total_rows * width),
        name="scatter_gather",
    )(partial_rows.astype(BF16).reshape(chips, 2, count, width), *inputs, *operands)
    return (
        *given[:n_out],
        given[n_out].reshape(total_rows, width),
        *given[n_out + 1 :],
    )


def spread_beside(full, n_head):
    entries = ff_entries(full[0].shape[1], n_head)

    def make(ops, ress, scratch):
        return Spread(ress, entries, n_head, scratch[0])

    return (
        tuple(full),
        tuple(jax.ShapeDtypeStruct(w.shape, w.dtype) for w in full),
        [ANYWHERE] * 3,
        [Spread.sem_shape(n_head)],
        {0: 0, 1: 1, 2: 2},
        make,
    )


def collect_beside(have, carried, n_head):
    entries = ff_entries(have[0].shape[1], n_head)
    levels = n_head.bit_length() - 2
    shapes = [(n_head // 2, *one.shape[1:]) for one in have]

    def make(ops, ress, scratch):
        kept, inbox = scratch[0:3], scratch[3:6]
        return Collect(ops[:3], kept, inbox, ress[:3], entries, n_head, scratch[6])

    return (
        (*have, carried),
        (
            *(jax.ShapeDtypeStruct((2, *one.shape[1:]), BF16) for one in have),
            jax.ShapeDtypeStruct(carried.shape, carried.dtype),
        ),
        [IN_VMEM] * 3 + [ANYWHERE],
        [
            *(pltpu.VMEM(shape, BF16) for shape in shapes),
            *(pltpu.VMEM((levels, *shape), BF16) for shape in shapes),
            Collect.sem_shape(n_head),
        ],
        {3: 3},
        make,
    )


class Rows:
    def __init__(self, ref, q, size, chips):
        self.ref, self.base, self.size = ref, q * size * chips * 2, size
        self.at = self

    def rows(self, j, core, start=0, count=None):
        first = self.base + (j * 2 + core) * self.size + start
        return pl.ds(pl.multiple_of(first, 16), count or self.size)

    def __getitem__(self, index):
        j, core, *inner = index
        if inner:
            return self.ref.at[self.rows(j, core, inner[0].start, inner[0].size)]
        return self.ref.at[self.rows(j, core)]


class OwnRows:
    def __init__(self, rows, core):
        self.view, self.core = rows, core
        self.shape = (0, rows.size)

    def __getitem__(self, index):
        j, r, _ = index
        return self.view.ref[self.view.rows(j, self.core, r.start, r.size), :]


class LocalScatter(Scatter):
    def __init__(self, line, part, bufs, sems):
        super().__init__(line, part, (OwnRows(part, line.c), *bufs), sems)

    def start(self):
        chips = self.line.chips
        order = []
        for k in range((chips + 1) // 2):
            order += [chips - 1 - k, k]
        for j in order[:chips]:
            self.to_sibling(j).start()

    def ready(self, j):
        self.to_sibling(j).wait_recv()


def turned(values, cosine, sine):
    return values * cosine + pltpu.roll(values, HEAD_DIM // 2, 1) * sine


def local_params(collective_id):
    if collective_id is None:
        return pltpu.CompilerParams(vmem_limit_bytes=60 * 2**20)
    return pltpu.CompilerParams(
        collective_id=collective_id, has_side_effects=True, vmem_limit_bytes=60 * 2**20
    )


def spec_of(shape, dtype):
    return jax.ShapeDtypeStruct(shape, dtype)


def attention_forward(
    rows, weights, small, w_out, ids, cot, cot_rows, ff, q_cols, copies, n_head, n_blk, collective_id
):
    count, width = rows.shape
    chips, pack = n_blk // 2, n_blk * count
    rows_here, rows_ff = w_out.shape[0], ff[0].shape[0]
    entries = ff_entries(rows_ff, n_head)
    columns, q_here = q_cols + 2 * HEAD_DIM, q_cols // HEAD_DIM
    together, n_all = 128 // rows_here, n_head * n_blk
    blocks = pack // ROWS
    scale = 1.0 / math.sqrt(HEAD_DIM)

    def kernel(src, cot_ref, *refs):
        w_src, (pack_src, out_src), ff_src = refs[:3], refs[3:5], refs[5:8]
        pos, seg, blk_ids = refs[8:11]
        part_hbm, xn_hbm, p_hbm, cot_hbm = refs[11:15]
        ff_out, refs = refs[15:18], refs[18:]
        w_ref, vec_ref, gate_ref, cos_ref, sin_ref = refs[:5]
        lin_ref, q_ref, k_ref, v_ref, sig_ref, o_ref, gated_ref, o_rows = refs[5:13]
        x_s, xn_s, p_s, low_ref, code_ref, key_ref, g_all, xn_sem, p_sem, part_sem = refs[13:23]
        sems, block_sems, w_sems, pack_sems, g_sems, moved, local = refs[23:30]
        cot_sems, out_sems, ff_sems = refs[30:]
        line = Line(n_blk)
        across, along = Exchange("head", n_head), Exchange("blk", n_blk)
        h, b = across.me, along.me
        h_me, b_me = h, b
        (th, tb), (sh, sb) = place_of_out_rows(n_head, n_blk)
        stays = (th == h) & (tb == b)
        moves = jnp.logical_not(stays)
        greet_all((across, along), moves=(moves, {"head": sh, "blk": sb}))

        def at_rows(head, blk):
            first = (head * n_blk + blk) * rows_here
            return pl.ds(pl.multiple_of(first, rows_here), rows_here)

        def of_head(head):
            size = n_blk * rows_here
            return pl.ds(pl.multiple_of(head * size, size), size)

        def out_rows_of(head):
            return o_rows.at[pl.ds(pl.multiple_of(head * rows_here, rows_here), rows_here)]

        def block_copies(k):
            for w, there, here in weight_pieces(along.peer(k), q_cols, copies):
                yield along.copy(
                    k, w_src[w].at[:, there], w_ref.at[at_rows(h, b), here], block_sems.at[w]
                )

        def pack_copy(k):
            return along.copy(k, pack_src, g_all.at[h, b], pack_sems)

        def w_copy(k):
            return across.copy(k, w_ref.at[of_head(h)], w_ref.at[of_head(h)], w_sems)

        def g_copy(k):
            return across.copy(k, g_all.at[h], g_all.at[h], g_sems)

        def out_copy(k):
            return across.copy(k, out_rows_of(h), out_rows_of(h), out_sems)

        def hop(e):
            weight, part, order = entries[e]
            return flip_copy(
                ff_src[weight].at[part], ff_out[weight].at[part], order[0], ff_sems, e
            )

        move_out = pltpu.make_async_remote_copy(
            src_ref=out_src,
            dst_ref=out_rows_of(th),
            send_sem=moved.at[0],
            recv_sem=moved.at[1],
            device_id={"head": th, "blk": tb},
            device_id_type=MESH,
        )
        keep_out = pltpu.make_async_copy(out_src, out_rows_of(h), moved.at[2])
        locals_ = [
            pltpu.make_async_copy(
                w_src[w].at[:, there], w_ref.at[at_rows(h, b), here], local.at[w]
            )
            for w, there, here in weight_pieces(b, q_cols, copies)
        ] + [pltpu.make_async_copy(pack_src, g_all.at[h, b], local.at[3])]
        for k in range(1, n_blk):
            for copy in block_copies(k):
                copy.start()
        tokens = Gather(line, src, Rows(x_s, 0, count, chips), sems)
        gather = Gather(line, cot_ref.at[pl.ds(0, cot_rows)], cot_hbm, cot_sems)
        for k in range(1, n_blk):
            pack_copy(k).start()
        for one in locals_:
            one.start()

        @pl.when(stays)
        def _():
            keep_out.start()

        @pl.when(moves)
        def _():
            move_out.start()

        for e in (2, 3):
            hop(e).start()
        half = HEAD_DIM // 2
        index = lax.broadcasted_iota(jnp.int32, (half, ROWS), 0).astype(F32)
        frequency = jnp.exp(index * (-2.0 * math.log(ROPE_BASE) / HEAD_DIM))
        pack_row = pl.ds(h, 1)
        key_ref[...] = (seg[pack_row, :] * pack + blk_ids[pack_row, :]).astype(F32)

        def tables(n, carry):
            r = block_of(n)
            angles = frequency * pos[pack_row, r].astype(F32)
            cosine, sine = jnp.cos(angles), jnp.sin(angles)
            cos_ref[r, :] = jnp.concatenate([cosine, cosine], axis=0).T
            sin_ref[r, :] = jnp.concatenate([-sine, sine], axis=0).T
            low_ref[r, :] = jnp.broadcast_to((seg[pack_row, r] * pack).astype(F32), (128, ROWS)).T
            code_ref[r, :] = jnp.broadcast_to(key_ref[:, r], (128, ROWS)).T
            return carry

        lax.fori_loop(0, pack // ROWS, tables, 0)
        for one in locals_:
            one.wait()
        for k in range(1, n_blk):
            for copy in block_copies(k):
                copy.wait_recv()
        tokens.start()
        for k in range(1, n_head):
            w_copy(k).start()
        for k in range(1, n_blk):
            pack_copy(k).wait_recv()
        for k in range(1, n_head):
            g_copy(k).start()

        @pl.when(stays)
        def _():
            keep_out.wait()

        @pl.when(moves)
        def _():
            move_out.wait_recv()

        for k in range(1, n_head):
            out_copy(k).start()
        for s in range(1, chips):
            tokens.step(s)
        gather.start()
        for e in (0, 1):
            hop(e).start()
        for k in range(1, n_head):
            g_copy(k).wait()
        everyone = [g_all.at[d // n_blk, d % n_blk] for d in range(n_all)]
        vec_ref[...] = jnp.zeros_like(vec_ref)
        for t in range(width // 128):
            tile = sum(one[...] for one in everyone[t * together : (t + 1) * together])
            vec_ref[0:2, t * 128 : (t + 1) * 128] = tile[0:2]
            gate_ref[:, t * 128 : (t + 1) * 128] = tile[8:].astype(BF16)
        vec_ref[2:4, 0:128] = sum(one[2:4, :] for one in everyone)
        tokens.finish()
        for k in range(1, n_head):
            w_copy(k).wait()

        def xn_store(n):
            return pltpu.make_async_copy(
                xn_s.at[block_of(n)], xn_hbm.at[block_of(n)], xn_sem.at[n]
            )

        def p_store(h, n):
            return pltpu.make_async_copy(
                p_s.at[h, block_of(n)], p_hbm.at[h, block_of(n)], p_sem.at[h, n]
            )

        def part_store(n):
            return pltpu.make_async_copy(
                x_s.at[block_of(n)], part_hbm.at[block_of(n)], part_sem.at[n]
            )

        def project(n, carry):
            r = block_of(n)
            unit, _ = unit_of(x_s[r, :].astype(F32))
            xn = (unit * vec_ref[0:1, :]).astype(BF16)
            xn_s[r, :] = xn
            xn_store(n).start()
            lin = mm(xn, w_ref[...])
            lin_ref[r, :] = lin
            gate = mm_nt(xn, gate_ref[...])
            one_of = lax.broadcasted_iota(jnp.int32, (ROWS, HEADS), 1)
            lane = lax.broadcasted_iota(jnp.int32, (ROWS, GATE_PAD), 1)
            sigs = jnp.zeros((ROWS, GATE_PAD), F32)
            for h in range(q_here):
                own = jnp.where(one_of == b_me * q_here + h, gate, 0.0)
                own = jax.nn.sigmoid(jnp.sum(own, axis=1, keepdims=True))
                sigs = jnp.where(lane == h, own, sigs)
            sig_ref[r, :] = sigs
            cosine, sine = cos_ref[r, :], sin_ref[r, :]
            for h in range(q_here):
                at = slice(h * HEAD_DIM, (h + 1) * HEAD_DIM)
                unit_q, _ = unit_of(lin[:, at])
                q_ref[r, at] = turned(unit_q * vec_ref[2:3, :HEAD_DIM], cosine, sine).astype(BF16)
            unit_k, _ = unit_of(lin[:, q_cols : q_cols + HEAD_DIM])
            k_ref[r, :] = turned(unit_k * vec_ref[3:4, :HEAD_DIM], cosine, sine).astype(BF16)
            v_ref[r, :] = lin[:, q_cols + HEAD_DIM :].astype(BF16)
            return carry

        lax.fori_loop(0, blocks, project, 0)
        gather.step(1)
        for k in range(1, n_head):
            out_copy(k).wait_recv()

        def attend(n, carry):
            @pl.when(n == blocks - 1)
            def _():
                gather.step(2)

            r = block_of(n)
            visible = (key_ref[...] >= low_ref[r, 0:1]) & (key_ref[...] <= code_ref[r, 0:1])
            for h in range(q_here):
                at = slice(h * HEAD_DIM, (h + 1) * HEAD_DIM)
                scores = mm_nt(q_ref[r, at], k_ref[...]) * scale
                scores = jnp.where(visible, scores, MASKED)
                top = jnp.max(scores, axis=-1, keepdims=True)
                weights = jnp.exp(scores - top)
                weights = weights * (1.0 / jnp.sum(weights, axis=-1, keepdims=True))
                prob = weights.astype(BF16)
                p_s[h, r, :] = prob
                p_store(h, n).start()
                out = mm(prob, v_ref[...]).astype(BF16)
                o_ref[r, at] = out
                gated_ref[r, at] = (out.astype(F32) * sig_ref[r, h : h + 1]).astype(BF16)
            x_s[r, :] = mm(gated_ref[r, :], o_rows[...]).astype(BF16)
            part_store(n).start()
            return carry

        lax.fori_loop(0, blocks, attend, 0)
        for s in range(3, chips):
            gather.step(s)
        gather.finish()
        for k in range(1, n_head):
            out_copy(k).wait_send()
        for e in range(len(entries)):
            hop(e).wait()
        for k in range(1, n_blk):
            pack_copy(k).wait_send()
            for copy in block_copies(k):
                copy.wait_send()

        @pl.when(moves)
        def _():
            move_out.wait_send()

        for n in range(blocks):
            xn_store(n).wait()
            part_store(n).wait()
            for h in range(q_here):
                p_store(h, n).wait()

    dma = pltpu.SemaphoreType.DMA
    return pl.pallas_call(
        kernel,
        out_shape=(
            spec_of((pack, width), BF16),
            spec_of((pack, width), BF16),
            spec_of((q_here, pack, pack), BF16),
            spec_of((chips, 2, cot_rows, width), BF16),
            *(spec_of(w.shape, BF16) for w in ff),
            spec_of((width, columns), BF16),
            spec_of((8, width), F32),
            spec_of((HEADS, width), BF16),
            spec_of((pack, HEAD_DIM), F32),
            spec_of((pack, HEAD_DIM), F32),
            spec_of((pack, columns), F32),
            spec_of((pack, q_cols), BF16),
            spec_of((pack, HEAD_DIM), BF16),
            spec_of((pack, HEAD_DIM), BF16),
            spec_of((pack, GATE_PAD), F32),
            spec_of((pack, q_cols), BF16),
            spec_of((pack, q_cols), BF16),
            spec_of((q_cols, width), BF16),
        ),
        in_specs=[IN_VMEM] * 2 + [ANYWHERE] * 8 + [IN_VMEM] * 3,
        out_specs=[ANYWHERE] * 7 + [IN_VMEM] * 13,
        scratch_shapes=[
            pltpu.VMEM((pack, width), BF16),
            pltpu.VMEM((pack, width), BF16),
            pltpu.VMEM((q_here, pack, pack), BF16),
            pltpu.VMEM((pack, 128), F32),
            pltpu.VMEM((pack, 128), F32),
            pltpu.VMEM((1, pack), F32),
            pltpu.VMEM((n_head, n_blk, PACK_ROWS, 128), F32),
            dma((blocks,)),
            dma((q_here, blocks)),
            dma((blocks,)),
            gather_sems(chips),
            dma((3, 2, n_blk)),
            pair_sems(n_head),
            pair_sems(n_blk),
            pair_sems(n_head),
            dma((3,)),
            dma((4,)),
            gather_sems(chips),
            pair_sems(n_head),
            pair_sems(len(entries)),
        ],
        compiler_params=local_params(collective_id),
        cost_estimate=comm_cost(pack * width),
        name="attention_forward",
    )(rows, cot, *weights, small, w_out, *ff, *ids)


def attention_backward(
    dy, xn, p, saved, w_attn, vec, gates, tables, mlp_gain_part, q_here, beside=None
):
    pack, width = dy.shape
    columns = w_attn.shape[1]
    q_cols = q_here * HEAD_DIM
    blocks = pack // ROWS
    scale = 1.0 / math.sqrt(HEAD_DIM)

    have, n_head, collective_id = beside or ((), 0, None)
    n_have = len(have)
    sum_scratch = []
    if have:
        entries = ff_entries(have[0].shape[1], n_head)
        sum_scratch = [pair_sems(len(entries))]

    def kernel(dy_hbm, xn_hbm, p_hbm, *refs):
        have_refs, refs = refs[:n_have], refs[n_have:]
        n_plain = 14 + 4
        plain, more = refs[:n_plain], refs[n_plain:]
        got, more = more[:n_have], more[n_have:]
        plain_scratch, sems = more[:14], more[14:]
        if not have:
            return local(dy_hbm, xn_hbm, p_hbm, *plain, *plain_scratch)
        greet_all((Exchange("head", n_head),))
        copies = [
            flip_copy(have_refs[w].at[1, part], got[w].at[part], order[0], sems[0], e)
            for e, (w, part, order) in enumerate(entries)
        ]
        for copy in copies:
            copy.start()
        local(dy_hbm, xn_hbm, p_hbm, *plain, *plain_scratch)
        for copy in copies:
            copy.wait()

    def local(dy_hbm, xn_hbm, p_hbm, lin_ref, q_ref, k_ref, v_ref, sig_ref, o_ref, *refs):
        gated_ref, o_rows, w_ref, vec_ref, gate_ref, cos_ref, sin_ref, mlp_ref = refs[:8]
        dxn_hbm, dw_ref, pack_ref, dout_ref = refs[8:12]
        dy_s, xn_s, p_s, do_s, delta_s, dgate_s, dlin_s, dk_s, dv_s, dgq_s = refs[12:22]
        dy_sem, xn_sem, p_sem, out_sem = refs[22:]
        first_head = lax.axis_index("blk") * q_here

        def dy_load(n):
            return pltpu.make_async_copy(
                dy_hbm.at[block_of(n)], dy_s.at[block_of(n)], dy_sem.at[n]
            )

        def p_load(h, n):
            return pltpu.make_async_copy(
                p_hbm.at[h, block_of(n)], p_s.at[h, block_of(n)], p_sem.at[h, n]
            )

        def dxn_store(n):
            return pltpu.make_async_copy(
                dy_s.at[block_of(n)], dxn_hbm.at[block_of(n)], out_sem.at[n]
            )

        xn_load = pltpu.make_async_copy(xn_hbm, xn_s, xn_sem)
        for n in range(blocks):
            dy_load(n).start()
        for n in range(blocks):
            for h in range(q_here):
                p_load(h, n).start()
        xn_load.start()

        def through_gate(n, carry):
            r = block_of(n)
            dy_load(n).wait()
            dgated = mm_nt(dy_s[r, :], o_rows[...])
            lane = lax.broadcasted_iota(jnp.int32, (ROWS, GATE_PAD), 1)
            dgates = jnp.zeros((ROWS, GATE_PAD), F32)
            deltas = jnp.zeros((ROWS, GATE_PAD), F32)
            for h in range(q_here):
                at = slice(h * HEAD_DIM, (h + 1) * HEAD_DIM)
                sig = sig_ref[r, h : h + 1]
                out = o_ref[r, at].astype(F32)
                do = (dgated[:, at] * sig).astype(BF16)
                do_s[r, at] = do
                dgate = jnp.sum(dgated[:, at] * out, axis=-1, keepdims=True) * sig * (1.0 - sig)
                delta = jnp.sum(do.astype(F32) * out, axis=-1, keepdims=True)
                dgates = jnp.where(lane == first_head + h, dgate, dgates)
                deltas = jnp.where(lane == h, delta, deltas)
            dgate_s[r, :] = dgates.astype(BF16)
            delta_s[r, :] = deltas
            return carry

        lax.fori_loop(0, blocks, through_gate, 0)

        def out_grad(n, carry):
            c = block_of(n)
            dout_ref[:, c] = mm_tn(gated_ref[...], dy_s[:, c]).astype(BF16)
            return carry

        lax.fori_loop(0, width // ROWS, out_grad, 0)
        dk_s[...] = jnp.zeros_like(dk_s)
        dv_s[...] = jnp.zeros_like(dv_s)
        dgq_s[...] = jnp.zeros_like(dgq_s)

        def into_lin(grad, lin, gain, r):
            grad = turned(grad.astype(BF16).astype(F32), cos_ref[r, :], -sin_ref[r, :])
            unit, factor = unit_of(lin)
            return unit_back(grad * gain, unit, factor).astype(BF16), grad * unit

        def attend(n, carry):
            r = block_of(n)
            for h in range(q_here):
                at = slice(h * HEAD_DIM, (h + 1) * HEAD_DIM)
                p_load(h, n).wait()
                do, prob, q = do_s[r, at], p_s[h, r, :], q_ref[r, at]
                dp = mm_nt(do, v_ref[...])
                ds = (prob.astype(F32) * (dp - delta_s[r, h : h + 1])).astype(BF16)
                dq = mm(ds, k_ref[...]) * scale
                dk_s[...] += mm(q.T, ds)
                dv_s[...] += mm(do.T, prob)
                dlin, part = into_lin(dq, lin_ref[r, at], vec_ref[2:3, :HEAD_DIM], r)
                dlin_s[r, at] = dlin
                dgq_s[...] += jnp.sum(part.reshape(ROWS // 8, 8, HEAD_DIM), axis=0)
            return carry

        lax.fori_loop(0, blocks, attend, 0)
        every = pl.ds(0, pack)
        k_cols = slice(q_cols, q_cols + HEAD_DIM)
        dlin, part = into_lin(
            dk_s[...].T * scale, lin_ref[:, k_cols], vec_ref[3:4, :HEAD_DIM], every
        )
        dlin_s[:, k_cols] = dlin
        dgk = jnp.sum(part, axis=0, keepdims=True)
        dgq = jnp.sum(dgq_s[...], axis=0, keepdims=True)
        pack_ref[HEADS:, :] = jnp.zeros((PACK_ROWS - HEADS, width), F32)
        pack_ref[HEADS : HEADS + 1, :] = jnp.sum(mlp_ref[...], axis=0, keepdims=True)
        for t in range(width // HEAD_DIM):
            lanes = slice(t * HEAD_DIM, (t + 1) * HEAD_DIM)
            pack_ref[HEADS + 1 : HEADS + 2, lanes] = dgq
            pack_ref[HEADS + 2 : HEADS + 3, lanes] = dgk
        dlin_s[:, q_cols + HEAD_DIM :] = dv_s[...].T.astype(BF16)

        def into_x(n, carry):
            r = block_of(n)
            dxn = mm_nt(dlin_s[r, :], w_ref[...]) + mm(dgate_s[r, :HEADS], gate_ref[...])
            dy_s[r, :] = dxn.astype(BF16)
            dxn_store(n).start()
            return carry

        lax.fori_loop(0, blocks, into_x, 0)
        xn_load.wait()
        dgate_t = dgate_s[...].astype(F32).T[:HEADS].astype(BF16)

        def weights(n, carry):
            c = block_of(n)
            xn_cols = xn_s[:, c]
            dw_ref[c, :] = mm_tn(xn_cols, dlin_s[...]).astype(BF16)
            pack_ref[:HEADS, c] = mm(dgate_t, xn_cols)
            return carry

        lax.fori_loop(0, width // ROWS, weights, 0)
        for n in range(blocks):
            dxn_store(n).wait()

    return pl.pallas_call(
        kernel,
        out_shape=(
            spec_of((pack, width), BF16),
            spec_of((width, columns), BF16),
            spec_of((PACK_ROWS, width), F32),
            spec_of((q_cols, width), BF16),
            *(spec_of(one.shape[1:], BF16) for one in have),
        ),
        in_specs=[ANYWHERE] * (3 + n_have) + [IN_VMEM] * 14,
        out_specs=[ANYWHERE] + [IN_VMEM] * 3 + [ANYWHERE] * n_have,
        scratch_shapes=[
            pltpu.VMEM((pack, width), BF16),
            pltpu.VMEM((pack, width), BF16),
            pltpu.VMEM((q_here, pack, pack), BF16),
            pltpu.VMEM((pack, q_cols), BF16),
            pltpu.VMEM((pack, GATE_PAD), F32),
            pltpu.VMEM((pack, GATE_PAD), BF16),
            pltpu.VMEM((pack, columns), BF16),
            pltpu.VMEM((HEAD_DIM, pack), F32),
            pltpu.VMEM((HEAD_DIM, pack), F32),
            pltpu.VMEM((8, HEAD_DIM), F32),
            pltpu.SemaphoreType.DMA((blocks,)),
            pltpu.SemaphoreType.DMA,
            pltpu.SemaphoreType.DMA((q_here, blocks)),
            pltpu.SemaphoreType.DMA((blocks,)),
            *sum_scratch,
        ],
        compiler_params=local_params(collective_id),
        name="attention_backward",
    )(dy, xn, p, *have, *saved, w_attn, vec, gates, *tables, mlp_gain_part)


def attention_end(
    dy, xn, p, mlp_part, ff_sums, saved, w_attn, vec, gates, tables, token_rows, q_here, copies,
    n_head, n_blk, collective_id
):
    pack, width = dy.shape
    columns = w_attn.shape[1]
    q_cols = q_here * HEAD_DIM
    blocks = pack // ROWS
    scale = 1.0 / math.sqrt(HEAD_DIM)
    chips, count = n_blk // 2, pack // n_blk
    rows_here = width // (n_head * n_blk)
    lanes = n_blk * rows_here
    entries = ff_entries(ff_sums[0].shape[1], n_head)

    def kernel(dy_hbm, xn_hbm, p_hbm, mlp_hbm, *refs):
        refs = list(refs)

        def take(n):
            taken = refs[:n]
            del refs[:n]
            return taken

        ff_src = take(3)
        lin_ref, q_ref, k_ref, v_ref, sig_ref, o_ref, gated_ref, o_rows = take(8)
        w_ref, vec_ref, gate_ref, cos_ref, sin_ref = take(5)
        x_ref, middle_ref, dmid_ref, mlp_gain_ref = take(4)
        layer_out, input_grad, g_out, wq_out, wk_out, wv_out, o_out = take(7)
        ff_out = take(3)
        dy_s, xn_s, p_s, do_s, delta_s, dgate_s, dlin_s, dk_s, dv_s, dgq_s = take(10)
        dw_s, pack_s, dout_s, w_in, w_sum, o_in, o_sum, g_in, g_sum, g_last = take(10)
        mlp_scratch, dxn_scratch, (xg_s,) = take(5), take(4), take(1)
        dy_sem, xn_sem, p_sem = take(3)
        w_sems, block_sems, o_sems, g_sems, pack_sems, moved, ff_sems, local = refs
        line = Line(n_blk)
        across, along = Exchange("head", n_head), Exchange("blk", n_blk)
        h, b = across.me, along.me
        first_head = b * q_here
        (sh, sb), (th, tb) = place_of_out_rows(n_head, n_blk)
        stays = (th == h) & (tb == b)
        moves = jnp.logical_not(stays)
        greet_all((across, along), moves=(moves, {"head": sh, "blk": sb}))

        def dy_load(n):
            return pltpu.make_async_copy(
                dy_hbm.at[block_of(n)], dy_s.at[block_of(n)], dy_sem.at[n]
            )

        def p_load(head, n):
            return pltpu.make_async_copy(
                p_hbm.at[head, block_of(n)], p_s.at[head, block_of(n)], p_sem.at[head, n]
            )

        def of_head(head):
            return pl.ds(pl.multiple_of(head * lanes, lanes), lanes)

        def of_blk(blk):
            return pl.ds(pl.multiple_of(blk * rows_here, rows_here), rows_here)

        def out_of(head):
            return dout_s.at[pl.ds(pl.multiple_of(head * rows_here, rows_here), rows_here)]

        def w_copy(k):
            return across.copy(k, dw_s.at[of_head(across.peer(k))], w_in.at[k], w_sems)

        def o_copy(k):
            return across.copy(k, out_of(across.peer(k)), o_in.at[k], o_sems)

        def g_part(head):
            return pack_s.at[:, pl.ds(pl.multiple_of(head * lanes, 128), lanes)]

        def g_copy(k):
            return across.copy(k, g_part(across.peer(k)), g_in.at[k], g_sems)

        def landings():
            kv = pl.ds(pl.multiple_of(b // copies * HEAD_DIM, HEAD_DIM), HEAD_DIM)
            return (
                wq_out.at[:, pl.ds(pl.multiple_of(b * q_cols, HEAD_DIM), q_cols)],
                wk_out.at[b % copies, :, kv],
                wv_out.at[b % copies, :, kv],
            )

        spans = (
            pl.ds(0, q_cols),
            pl.ds(q_cols, HEAD_DIM),
            pl.ds(q_cols + HEAD_DIM, HEAD_DIM),
        )

        def block_copies(k):
            for w, there in enumerate(landings()):
                src = w_sum.at[of_blk(along.peer(k)), spans[w]]
                yield along.copy(k, src, there, block_sems.at[w])

        def tile_of(blk):
            return pl.ds(pl.multiple_of(blk * rows_here // 128 * 128, 128), 128)

        def pack_copy(k):
            return along.copy(k, g_sum.at[:, tile_of(along.peer(k))], g_last.at[b], pack_sems)

        move_out = pltpu.make_async_remote_copy(
            src_ref=o_sum,
            dst_ref=o_out,
            send_sem=moved.at[0],
            recv_sem=moved.at[1],
            device_id={"head": th, "blk": tb},
            device_id_type=MESH,
        )
        keep_out = pltpu.make_async_copy(o_sum, o_out, moved.at[2])
        hops = [
            flip_copy(ff_src[w].at[1, part], ff_out[w].at[part], order[0], ff_sems, e)
            for e, (w, part, order) in enumerate(entries)
        ]
        own_blocks = [
            pltpu.make_async_copy(w_sum.at[of_blk(b), spans[w]], there, local.at[w])
            for w, there in enumerate(landings())
        ]
        mlp = Scatter(line, mlp_hbm, mlp_scratch[:4], mlp_scratch[4])
        dxn = LocalScatter(
            line, Rows(dy_s, 0, count, chips), dxn_scratch[:3], dxn_scratch[3]
        )
        xn_load = pltpu.make_async_copy(xn_hbm, xn_s, xn_sem)
        for n in range(blocks):
            dy_load(n).start()
        mlp.start()
        for n in range(blocks):
            for head in range(q_here):
                p_load(head, n).start()
        xn_load.start()
        for hop in hops[2:]:
            hop.start()

        def through_gate(n, carry):
            @pl.when(n == blocks // 2)
            def _():
                mlp.step(0)

            r = block_of(n)
            dy_load(n).wait()
            dgated = mm_nt(dy_s[r, :], o_rows[...])
            lane = lax.broadcasted_iota(jnp.int32, (ROWS, GATE_PAD), 1)
            dgates = jnp.zeros((ROWS, GATE_PAD), F32)
            deltas = jnp.zeros((ROWS, GATE_PAD), F32)
            for head in range(q_here):
                at = slice(head * HEAD_DIM, (head + 1) * HEAD_DIM)
                sig = sig_ref[r, head : head + 1]
                out = o_ref[r, at].astype(F32)
                do = (dgated[:, at] * sig).astype(BF16)
                do_s[r, at] = do
                dgate = jnp.sum(dgated[:, at] * out, axis=-1, keepdims=True) * sig * (1.0 - sig)
                delta = jnp.sum(do.astype(F32) * out, axis=-1, keepdims=True)
                dgates = jnp.where(lane == first_head + head, dgate, dgates)
                deltas = jnp.where(lane == head, delta, deltas)
            dgate_s[r, :] = dgates.astype(BF16)
            delta_s[r, :] = deltas
            return carry

        lax.fori_loop(0, blocks, through_gate, 0)

        def out_grad(n, carry):
            c = block_of(n)
            dout_s[:, c] = mm_tn(gated_ref[...], dy_s[:, c]).astype(BF16)
            return carry

        lax.fori_loop(0, width // ROWS, out_grad, 0)
        dk_s[...] = jnp.zeros_like(dk_s)
        dv_s[...] = jnp.zeros_like(dv_s)
        dgq_s[...] = jnp.zeros_like(dgq_s)
        xg_s[...] = jnp.zeros_like(xg_s)
        o_in[0] = dout_s[pl.ds(pl.multiple_of(h * rows_here, rows_here), rows_here), :]
        for k in range(1, n_head):
            o_copy(k).start()

        def into_lin(grad, lin, gain, r):
            grad = turned(grad.astype(BF16).astype(F32), cos_ref[r, :], -sin_ref[r, :])
            unit, factor = unit_of(lin)
            return unit_back(grad * gain, unit, factor).astype(BF16), grad * unit

        def attend(n, carry):
            @pl.when(n == blocks // 2)
            def _():
                mlp.step(1)

            r = block_of(n)
            for head in range(q_here):
                at = slice(head * HEAD_DIM, (head + 1) * HEAD_DIM)
                p_load(head, n).wait()
                do, prob, q = do_s[r, at], p_s[head, r, :], q_ref[r, at]
                dp = mm_nt(do, v_ref[...])
                ds = (prob.astype(F32) * (dp - delta_s[r, head : head + 1])).astype(BF16)
                dq = mm(ds, k_ref[...]) * scale
                dk_s[...] += mm(q.T, ds)
                dv_s[...] += mm(do.T, prob)
                dlin, part = into_lin(dq, lin_ref[r, at], vec_ref[2:3, :HEAD_DIM], r)
                dlin_s[r, at] = dlin
                dgq_s[...] += jnp.sum(part.reshape(ROWS // 8, 8, HEAD_DIM), axis=0)
            return carry

        lax.fori_loop(0, blocks, attend, 0)
        every = pl.ds(0, pack)
        k_cols = slice(q_cols, q_cols + HEAD_DIM)
        dlin, part = into_lin(
            dk_s[...].T * scale, lin_ref[:, k_cols], vec_ref[3:4, :HEAD_DIM], every
        )
        dlin_s[:, k_cols] = dlin
        dlin_s[:, q_cols + HEAD_DIM :] = dv_s[...].T.astype(BF16)

        dgk = jnp.sum(part, axis=0, keepdims=True)
        dgq = jnp.sum(dgq_s[...], axis=0, keepdims=True)
        pack_s[HEADS:, :] = jnp.zeros((PACK_ROWS - HEADS, width), F32)
        pack_s[HEADS : HEADS + 1, :] = jnp.sum(mlp_gain_ref[...], axis=0, keepdims=True)
        for t in range(width // HEAD_DIM):
            at = slice(t * HEAD_DIM, (t + 1) * HEAD_DIM)
            pack_s[HEADS + 1 : HEADS + 2, at] = dgq
            pack_s[HEADS + 2 : HEADS + 3, at] = dgk
        xn_load.wait()
        dgate_t = dgate_s[...].astype(F32).T[:HEADS].astype(BF16)

        def weights(n, carry):
            c = block_of(n)
            xn_cols = xn_s[:, c]
            dw_s[c, :] = mm_tn(xn_cols, dlin_s[...]).astype(BF16)
            pack_s[:HEADS, c] = mm(dgate_t, xn_cols)
            return carry

        lax.fori_loop(0, width // ROWS, weights, 0)
        for k in range(1, n_head):
            w_copy(k).start()
        w_in[0] = dw_s[of_head(h), :]

        def into_x(n, carry):
            r = block_of(n)
            back = mm_nt(dlin_s[r, :], w_ref[...]) + mm(dgate_s[r, :HEADS], gate_ref[...])
            dy_s[r, :] = back.astype(BF16)
            product = back * xn_s[r, :].astype(F32)
            xg_s[...] += jnp.sum(product.reshape(ROWS // 8, 8, width), axis=0)
            return carry

        lax.fori_loop(0, blocks, into_x, 0)
        dxn.start()
        pack_s[HEADS + 3 : HEADS + 4, :] = jnp.sum(xg_s[...], axis=0, keepdims=True)
        for k in range(1, n_head):
            g_copy(k).start()
        for hop in hops[:2]:
            hop.start()
        g_in[0] = pack_s[:, pl.ds(pl.multiple_of(h * lanes, 128), lanes)]
        for tau in range(2, chips - 1):
            mlp.step(tau)
        dxn.step(0)
        def finish_layer(r, value):
            layer_out[r, :] = (middle_ref[r, :] + value).astype(BF16)

        mlp.total(finish_layer)
        for tau in range(1, chips - 2):
            dxn.step(tau)
        for k in range(1, n_head):
            g_copy(k).wait_recv()
        g_sum[...] = sum(g_in[k] for k in range(n_head))
        g_last[b] = g_sum[:, tile_of(b)]
        for k in range(1, n_blk):
            pack_copy(k).start()
        for k in range(1, n_head):
            o_copy(k).wait_recv()

        def add_out(r):
            o_sum[r, :] = sum(o_in[k, r, :].astype(F32) for k in range(n_head)).astype(BF16)

        by_rows(rows_here, 16, add_out)

        @pl.when(stays)
        def _():
            keep_out.start()

        @pl.when(moves)
        def _():
            move_out.start()

        for k in range(1, n_head):
            w_copy(k).wait_recv()

        def add(r):
            w_sum[r, :] = sum(w_in[k, r, :].astype(F32) for k in range(n_head)).astype(BF16)

        by_rows(lanes, 64, add)
        for one in own_blocks:
            one.start()
        for k in range(1, n_blk):
            for copy in block_copies(k):
                copy.start()
        dxn.step(chips - 2)

        def consume(r, value):
            unit, factor = unit_of(x_ref[r, :].astype(F32))
            back = unit_back(value * vec_ref[0:1, :], unit, factor)
            input_grad[r, :] = dmid_ref[r, :] + back

        dxn.total(consume)
        for k in range(1, n_blk):
            pack_copy(k).wait_recv()
        g_out[...] = sum(g_last[k] for k in range(n_blk))
        mlp.finish()
        dxn.finish()
        for one in own_blocks:
            one.wait()
        for k in range(1, n_head):
            g_copy(k).wait_send()
            o_copy(k).wait_send()
            w_copy(k).wait_send()
        for k in range(1, n_blk):
            pack_copy(k).wait_send()
            for copy in block_copies(k):
                copy.wait()
        for hop in hops:
            hop.wait()

        @pl.when(stays)
        def _():
            keep_out.wait()

        @pl.when(moves)
        def _():
            move_out.wait()

    dma = pltpu.SemaphoreType.DMA
    kv = spec_of((copies, rows_here, n_blk // copies * HEAD_DIM), BF16)
    return pl.pallas_call(
        kernel,
        out_shape=(
            spec_of((count, width), BF16),
            spec_of((count, width), F32),
            spec_of((PACK_ROWS, 128), F32),
            spec_of((rows_here, n_blk * q_cols), BF16),
            kv,
            kv,
            spec_of((rows_here, width), BF16),
            *(spec_of(one.shape[1:], BF16) for one in ff_sums),
        ),
        in_specs=[ANYWHERE] * 7 + [IN_VMEM] * 17,
        out_specs=[IN_VMEM] * 3 + [ANYWHERE] * 7,
        scratch_shapes=[
            pltpu.VMEM((pack, width), BF16),
            pltpu.VMEM((pack, width), BF16),
            pltpu.VMEM((q_here, pack, pack), BF16),
            pltpu.VMEM((pack, q_cols), BF16),
            pltpu.VMEM((pack, GATE_PAD), F32),
            pltpu.VMEM((pack, GATE_PAD), BF16),
            pltpu.VMEM((pack, columns), BF16),
            pltpu.VMEM((HEAD_DIM, pack), F32),
            pltpu.VMEM((HEAD_DIM, pack), F32),
            pltpu.VMEM((8, HEAD_DIM), F32),
            pltpu.VMEM((width, columns), BF16),
            pltpu.VMEM((PACK_ROWS, width), F32),
            pltpu.VMEM((q_cols, width), BF16),
            pltpu.VMEM((n_head, lanes, columns), BF16),
            pltpu.VMEM((lanes, columns), BF16),
            pltpu.VMEM((n_head, rows_here, width), BF16),
            pltpu.VMEM((rows_here, width), BF16),
            pltpu.VMEM((n_head, PACK_ROWS, lanes), F32),
            pltpu.VMEM((PACK_ROWS, lanes), F32),
            pltpu.VMEM((n_blk, PACK_ROWS, 128), F32),
            *scatter_bufs(chips, count, width),
            *scatter_bufs(chips, count, width)[1:],
            pltpu.VMEM((8, width), F32),
            dma((blocks,)),
            dma,
            dma((q_here, blocks)),
            pair_sems(n_head),
            dma((3, 2, n_blk)),
            pair_sems(n_head),
            pair_sems(n_head),
            pair_sems(n_blk),
            dma((3,)),
            pair_sems(len(entries)),
            dma((3,)),
        ],
        compiler_params=local_params(collective_id),
        cost_estimate=comm_cost(2 * pack * width),
        name="attention_end",
    )(
        dy,
        xn,
        p,
        mlp_part.reshape(chips, 2, count, width),
        *ff_sums,
        *saved,
        w_attn,
        vec,
        gates,
        *tables,
        *token_rows,
    )


def feed_forward(attn_part, ff, halfway, cot, inputs, to_mlp, to_attention, n_head, n_blk, collective_id):
    total_rows, width = attn_part.shape
    chips, count = n_blk // 2, total_rows // n_blk
    size, half = count // CHUNKS, total_rows // CHUNKS
    rows_ff = ff[0].shape[0]
    units = n_head * rows_ff
    entries = ff_entries(rows_ff, n_head)
    n_in = len(inputs)

    def kernel(part, cot_hbm, *refs):
        refs = list(refs)

        def take(n):
            taken = refs[:n]
            del refs[:n]
            return taken

        sources = take(3), take(3)
        ins = take(n_in)
        middle, dmid, gain_part, dy_hbm, mlp_hbm, *sum_hbm = take(8)
        made, hn_s, cot_s, dhn_s, u_s, da_s, db_s, stage = take(8)
        inboxes, weights = take(3), take(3)
        chunk_scratch = [take(8) for _ in range(CHUNKS)]
        load_sems, hop_sems, cot_sems, stage_sems, sum_sems, grad_sems, late_sems = refs
        line = Line(n_blk)
        across = Exchange("head", n_head)
        greet_all((across,), line)
        gain_part[...] = jnp.zeros_like(gain_part)

        def place(key, span):
            return pl.ds(key * rows_ff + span.start, span.size)

        loads, hops = [], []
        for e, (w, span, order) in enumerate(entries):
            first, second = 1 << order[0], 1 << order[1]
            for at, key in enumerate((0, first)):
                src = sources[at][w].at[span]
                loads.append(
                    pltpu.make_async_copy(src, weights[w].at[place(key, span)], load_sems.at[e, at])
                )
                there = weights[w].at[place(key ^ second, span)]
                hops.append(flip_copy(src, there, order[1], hop_sems, e, at))

        def cot_loads():
            for j in range(chips):
                for c in range(2):
                    yield pltpu.make_async_copy(
                        cot_hbm.at[j, c],
                        Rows(cot_s, 0, size, chips)[j, c],
                        cot_sems.at[2 * j + c],
                    )

        first, gather1, second, gather2 = [], [], [], []
        for q in range(CHUNKS):
            own, sib, inn, outgoing, sems, g_sems, sems2, g_sems2 = chunk_scratch[q]
            rows = pl.ds(q * size, size)
            first.append(Scatter(line, View(part, rows), (own, sib, inn, outgoing), sems))
            gather1.append(Gather(line, made.at[rows], Rows(hn_s, q, size, chips), g_sems))
            second.append(
                LocalScatter(line, Rows(dhn_s, q, size, chips), (sib, inn, outgoing), sems2)
            )
            gather2.append(Gather(line, made.at[rows], View(dy_hbm, rows), g_sems2))

        late = [
            Gather(
                line,
                ins[1].at[pl.ds(q * size, size)],
                Rows(cot_s, q, size, chips),
                late_sems.at[q - 1],
            )
            for q in range(1, CHUNKS)
        ]

        def turn(q, scatter, between, outs, gather):
            def consume(r, value):
                r = pl.ds(pl.multiple_of(r.start + q * size, 16), r.size)
                made[r, :] = between(r, value, ins, outs).astype(BF16)

            scatter[q].total(consume)
            gather[q].start()

        def loop(steps, body):
            lax.fori_loop(0, steps, lambda k, carry: body(k) or carry, 0)

        def span_of(q):
            return pl.ds(q * half, half)

        def unit_block(q, f):
            r, fr = span_of(q), block_of(f)
            a = mm_nt(hn_s[r, :], weights[0][fr, :])
            b = mm_nt(hn_s[r, :], weights[1][fr, :])
            du = mm_nt(cot_s[r, :], weights[2][fr, :])
            sig = jax.nn.sigmoid(a)
            silu = a * sig
            u_s[r, fr] = (silu * b).astype(BF16)
            da_s[r, fr] = (du * b * sig * (1.0 + a * (1.0 - sig))).astype(BF16)
            db_s[r, fr] = (du * silu).astype(BF16)

        def back(q):
            r = span_of(q)

            def body(n):
                cols = block_of(n, 512)
                dhn = mm(da_s[r, :], weights[0][:, cols]) + mm(db_s[r, :], weights[1][:, cols])
                dhn_s[r, cols] = dhn.astype(BF16)

            loop(width // 512, body)

        def stage_stores(q):
            for j in range(chips):
                for c in range(2):
                    yield pltpu.make_async_copy(
                        Rows(stage, 0, size, chips)[j, c],
                        mlp_hbm.at[j, c, pl.ds(q * size, size)],
                        stage_sems.at[2 * j + c],
                    )

        def mlp_out(q):
            if q:
                for store in stage_stores(q - 1):
                    store.wait()
            r = span_of(q)

            def body(n):
                cols = block_of(n, 512)
                stage[:, cols] = mm(u_s[r, :], weights[2][:, cols]).astype(BF16)

            loop(width // 512, body)
            for store in stage_stores(q):
                store.start()

        def grad(w):
            left, right = ((da_s, hn_s), (db_s, hn_s), (u_s, cot_s))[w]

            def body(f):
                fr = block_of(f)
                weights[w][fr, :] = mm_tn(left[:, fr], right[...]).astype(BF16)

            loop(units // ROWS, body)

        def sum_copies(w):
            for e, (weight, span, order) in enumerate(entries):
                if weight == w:
                    for at, key in enumerate((0, 1 << order[0])):
                        yield flip_copy(
                            weights[w].at[place(key ^ (1 << order[1]), span)],
                            inboxes[w].at[at, span],
                            order[1],
                            sum_sems,
                            e,
                            at,
                        )

        def sum_stores(w):
            for e, (weight, span, order) in enumerate(entries):
                if weight == w:
                    for at, key in enumerate((0, 1 << order[0])):
                        yield pltpu.make_async_copy(
                            weights[w].at[place(key, span)],
                            sum_hbm[w].at[at, span],
                            grad_sems.at[e, at],
                        )

        def send_grad(w):
            grad(w)
            for copy in sum_copies(w):
                copy.start()

        def add_grad(w):
            for copy in sum_copies(w):
                copy.wait()
            for weight, span, order in entries:
                if weight == w:
                    for at, key in enumerate((0, 1 << order[0])):

                        def body(r, span=span, at=at, key=key):
                            r = pl.ds(pl.multiple_of(r.start + span.start, 16), r.size)
                            mine = pl.ds(pl.multiple_of(r.start + key * rows_ff, 16), r.size)
                            value = weights[w][mine, :].astype(F32)
                            value += inboxes[w][at, r, :].astype(F32)
                            weights[w][mine, :] = value.astype(BF16)

                        by_rows(span.size, 16, body)
            for store in sum_stores(w):
                store.start()

        first[0].start()
        for hop in hops:
            hop.start()
        for q in range(1, CHUNKS):
            first[q].start()
        for one in late:
            one.start()
        for load in loads:
            load.start()
        for load in cot_loads():
            load.start()
        steps = chips - 1
        for tau in range(steps):
            first[0].step(tau)
            for one in late:
                one.step(tau + 1)
        turn(0, first, to_mlp, (middle,), gather1)
        for tau in range(steps):
            first[1].step(tau)
            gather1[0].step(tau + 1)
        turn(1, first, to_mlp, (middle,), gather1)
        for q in range(CHUNKS):
            first[q].finish()
        gather1[0].finish()
        gather1[1].step(1)
        for load in loads:
            load.wait()
        for load in cot_loads():
            load.wait()
        for hop in hops:
            hop.wait()
        blocks = units // ROWS

        def first_units(f):
            unit_block(0, f)
            for s in range(2, chips):

                @pl.when(f == s - 2)
                def _(s=s):
                    gather1[1].step(s)

        loop(blocks, first_units)
        for s in range(blocks + 2, chips):
            gather1[1].step(s)
        back(0)
        second[0].start()
        gather1[1].finish()
        for one in late:
            one.finish()
        second[0].step(0)
        loop(blocks, lambda f: unit_block(1, f))
        second[0].step(1)
        back(1)
        second[1].start()
        send_grad(0)
        for tau in range(2, steps):
            second[0].step(tau)
        second[1].step(0)
        send_grad(1)
        turn(0, second, to_attention, (middle, dmid, gain_part), gather2)
        second[1].step(1)
        mlp_out(0)
        mlp_out(1)
        gather2[0].step(1)
        send_grad(2)
        for tau in range(2, steps):
            second[1].step(tau)
            gather2[0].step(tau)
        turn(1, second, to_attention, (middle, dmid, gain_part), gather2)
        gather2[0].step(chips - 1)
        for s in range(1, chips):
            gather2[1].step(s)
        for w in range(3):
            add_grad(w)
        for q in range(CHUNKS):
            second[q].finish()
            gather2[q].finish()
        for store in stage_stores(CHUNKS - 1):
            store.wait()
        for w in range(3):
            for store in sum_stores(w):
                store.wait()

    per_chunk = []
    for _ in range(CHUNKS):
        own, sib, inn, outgoing, sems = scatter_bufs(chips, size, width)
        per_chunk += [own, sib, inn, outgoing, sems, gather_sems(chips), sems, gather_sems(chips)]
    sums = jax.ShapeDtypeStruct((2, rows_ff, width), BF16)
    shards_ = jax.ShapeDtypeStruct((chips, 2, count, width), BF16)
    dma = pltpu.SemaphoreType.DMA
    middle, dmid, gain_part, dy, mlp_part, *ff_sums = pl.pallas_call(
        kernel,
        out_shape=(
            jax.ShapeDtypeStruct((count, width), F32),
            jax.ShapeDtypeStruct((count, width), F32),
            jax.ShapeDtypeStruct((8, width), F32),
            shards_,
            shards_,
            *[sums] * 3,
        ),
        in_specs=[ANYWHERE] * 8 + [IN_VMEM] * n_in,
        out_specs=[IN_VMEM] * 3 + [ANYWHERE] * 5,
        scratch_shapes=[
            pltpu.VMEM((count, width), BF16),
            *[pltpu.VMEM((total_rows, width), BF16)] * 3,
            *[pltpu.VMEM((total_rows, units), BF16)] * 3,
            pltpu.VMEM((half, width), BF16),
            *[pltpu.VMEM((2, rows_ff, width), BF16)] * 3,
            *[pltpu.VMEM((units, width), BF16)] * 3,
            *per_chunk,
            dma((len(entries), 2)),
            dma((2, len(entries), 2)),
            dma((n_blk,)),
            dma((n_blk,)),
            dma((2, len(entries), 2)),
            dma((len(entries), 2)),
            dma((CHUNKS - 1, 7, chips, PIECES)),
        ],
        compiler_params=pltpu.CompilerParams(
            collective_id=collective_id, has_side_effects=True, vmem_limit_bytes=62 * 2**20
        ),
        cost_estimate=comm_cost(2 * total_rows * width),
        name="feed_forward",
    )(
        attn_part.reshape(chips, 2, count, width),
        cot,
        *ff,
        *halfway,
        *inputs,
    )
    return (
        middle,
        dmid,
        gain_part,
        dy.reshape(total_rows, width),
        mlp_part.reshape(total_rows, width),
        ff_sums,
    )


def padded(values, size):
    return jnp.pad(values, [(0, 0)] * (values.ndim - 1) + [(0, size - values.shape[-1])])


def shards(
    hidden,
    segment_ids,
    block_ids,
    positions,
    attn_gain,
    w_query,
    key_weight_matrix,
    value_weight_matrix,
    q_gain,
    k_gain,
    w_head_gate,
    w_out,
    mlp_gain,
    w_gate,
    w_up,
    w_down,
    cotangent,
):
    n_head = lax.axis_size("head")
    n_blk = lax.axis_size("blk")
    n_all = n_head * n_blk
    my_head = lax.axis_index("head")
    my_blk = lax.axis_index("blk")
    tokens = hidden.shape[1]
    pack = tokens * n_blk
    rows_here = w_query.shape[0]
    rows_ff = w_gate.shape[0]
    q_here = HEADS // n_blk
    q_cols = q_here * HEAD_DIM
    kv_copies = max(1, n_blk // KV_HEADS)
    kv_here = max(1, KV_HEADS // n_blk)
    kv_cols = kv_here * HEAD_DIM
    device = my_head * n_blk + my_blk
    together = 128 // rows_here
    lane = jnp.arange(128)
    here = (lane // rows_here == device % together)[None]
    mine = jnp.concatenate(
        [
            attn_gain[None],
            mlp_gain[None],
            jnp.zeros((6, rows_here), BF16),
            w_head_gate.T,
        ]
    )
    small = jnp.where(here, jnp.tile(mine, (1, together)), 0).astype(F32)
    share = q_gain.shape[0]
    head_gains = jnp.stack([jnp.tile(q_gain, n_all), jnp.tile(k_gain, n_all)]).astype(F32)
    head_gains = jnp.where(lane // share == device, head_gains, 0)
    small = small + jnp.pad(head_gains, ((2, PACK_ROWS - 4), (0, 0)))
    ids = (positions, segment_ids, block_ids)
    fused = n_head == 4 and pack <= 1024
    ff = (w_gate, w_up, w_down)
    attn_part, xn, prob, cot, *rest = attention_forward(
        hidden[0],
        (w_query, key_weight_matrix, value_weight_matrix),
        small,
        w_out,
        ids,
        cotangent[0],
        tokens // CHUNKS if fused else tokens,
        ff,
        q_cols,
        kv_copies,
        n_head,
        n_blk,
        0,
    )
    halfway, (w_attn, vec, gates), tables, saved = rest[:3], rest[3:6], rest[6:8], rest[8:]

    def to_mlp(r, total, ins, outs):
        x_ref, gain_ref = ins
        mid = x_ref[r, :].astype(F32) + total
        outs[0][r, :] = mid
        unit, _ = unit_of(mid)
        return unit * gain_ref[1:2, :]

    def to_attention(r, dhn, ins, outs):
        mid_ref, cot_ref, gain_ref = ins
        unit, factor = unit_of(mid_ref[r, :])
        product = dhn * unit
        seen = outs[1]
        seen[...] += product[:8] + product[8:]
        back = cot_ref[r, :].astype(F32) + unit_back(dhn * gain_ref[1:2, :], unit, factor)
        outs[0][r, :] = back
        return back

    if fused:

        def into_mlp(r, total, ins, outs):
            return to_mlp(r, total, (ins[0], ins[2]), outs)

        def into_attention(r, dhn, ins, outs):
            return to_attention(r, dhn, (outs[0], ins[1], ins[2]), outs[1:])

        middle, dmid, mlp_gain_part, dy, mlp_part, ff_sums = feed_forward(
            attn_part,
            ff,
            halfway,
            cot,
            (hidden[0], cotangent[0], vec),
            into_mlp,
            into_attention,
            n_head,
            n_blk,
            1,
        )
    else:
        cot = cot.reshape(pack, MODEL_WIDTH)
        ff_full = []
        for w, (own, other) in enumerate(zip(ff, halfway)):
            full = jnp.zeros((n_head, *own.shape), BF16).at[0].set(own)
            for weight, part, order in ff_entries(rows_ff, n_head):
                if weight == w:
                    span = slice(part.start, part.start + part.size)
                    full = full.at[1 << order[0], span].set(other[span])
            ff_full.append(full)
        middle, hn, *ff_rows = scatter_gather(
            attn_part,
            lambda outs: None,
            to_mlp,
            (hidden[0], vec),
            (jax.ShapeDtypeStruct(hidden.shape[1:], F32),),
            spread_beside(ff_full, n_head),
            n_head,
            n_blk,
            1,
        )
        gate_rows, up_rows, down_rows = (one.reshape(n_head * rows_ff, MODEL_WIDTH) for one in ff_rows)

        a = mm_nt(hn, gate_rows)
        b = mm_nt(hn, up_rows)
        sig = jax.nn.sigmoid(a)
        silu = a * sig
        u = (silu * b).astype(BF16)
        mlp_part = mm(u, down_rows).astype(BF16)
        du = mm_nt(cot, down_rows)
        da = (du * b * sig * (1.0 + a * (1.0 - sig))).astype(BF16)
        db = (du * silu).astype(BF16)
        ff_parts = [
            mm_tn(left, right).astype(BF16).reshape(n_head, rows_ff, MODEL_WIDTH)
            for left, right in ((da, hn), (db, hn), (u, cot))
        ]

        def clear(outs):
            outs[1][...] = jnp.zeros_like(outs[1])

        dmid, mlp_gain_part, dy, *ff_sums, mlp_part = scatter_gather(
            mm(da, gate_rows) + mm(db, up_rows),
            clear,
            to_attention,
            (middle, cotangent[0], vec),
            (
                jax.ShapeDtypeStruct(hidden.shape[1:], F32),
                jax.ShapeDtypeStruct((8, MODEL_WIDTH), F32),
            ),
            collect_beside(ff_parts, mlp_part, n_head),
            n_head,
            n_blk,
            2,
        )

    if fused:
        layer_output, input_grad, small_sums, query_grad, key_grad, value_grad, out_grad, *ff_last = (
            attention_end(
                dy,
                xn,
                prob,
                mlp_part,
                ff_sums,
                saved,
                w_attn,
                vec,
                gates,
                tables,
                (hidden[0], middle, dmid, mlp_gain_part),
                q_here,
                kv_copies,
                n_head,
                n_blk,
                2,
            )
        )
        layer_output, input_grad = layer_output[None], input_grad[None]
    else:
        layer_output = (
            middle + lax.psum_scatter(mlp_part, "blk", scatter_dimension=0, tiled=True).astype(F32)
        ).astype(BF16)[None]
        dxn_part, attn_grad, small_parts, out_grad = attention_backward(
            dy,
            xn,
            prob,
            saved,
            w_attn,
            vec,
            gates,
            tables,
            mlp_gain_part,
            q_here,
            None,
        )
        back_x, query_grad, key_grad, value_grad, out_grad, small_sums, *ff_last = last_scatter(
            dxn_part,
            attn_grad.reshape(n_head, n_blk, rows_here, -1),
            out_grad,
            small_parts,
            ff_sums,
            hidden[0],
            vec,
            q_cols,
            kv_copies,
            n_head,
            n_blk,
            3,
        )
        input_grad = (dmid + back_x)[None]
    ff_grads = [one[0].astype(F32) + two.astype(F32) for one, two in zip(ff_sums, ff_last)]

    query_grad = query_grad.astype(F32)
    key_grad = jnp.sum(key_grad.astype(F32), axis=0)
    value_grad = jnp.sum(value_grad.astype(F32), axis=0)
    small_sums = jnp.sum(
        jnp.where(
            jnp.arange(together)[None, :, None] == device % together,
            small_sums.reshape(PACK_ROWS, together, rows_here),
            0.0,
        ),
        axis=1,
    ), small_sums[HEADS + 1 : HEADS + 3]
    small_sums, head_sums = small_sums
    head_sums = lax.dynamic_slice_in_dim(head_sums, device * share, share, 1)
    head_gate_grad = small_sums[:HEADS].T
    if fused:
        scaled = small_sums[HEADS + 3]
    else:
        scaled = (
            jnp.sum(w_query.astype(F32) * query_grad, axis=1)
            + jnp.sum(key_weight_matrix.astype(F32) * key_grad, axis=1)
            + jnp.sum(value_weight_matrix.astype(F32) * value_grad, axis=1)
            + jnp.sum(w_head_gate.astype(F32) * head_gate_grad, axis=1)
        )
    attn_gain_grad = scaled / attn_gain.astype(F32)
    return (
        layer_output,
        input_grad,
        attn_gain_grad,
        query_grad,
        key_grad,
        value_grad,
        head_sums[0],
        head_sums[1],
        head_gate_grad,
        out_grad.astype(F32),
        small_sums[HEADS],
        ff_grads[0],
        ff_grads[1],
        ff_grads[2],
    )


def solution(mesh):
    rows = P(("head", "blk"), None)
    vector = P(("head", "blk"))
    token = P("head", "blk", None)
    return jax.shard_map(
        shards,
        mesh=mesh,
        in_specs=(
            token, P(), P(), P(), vector, rows, rows, rows, vector, vector, rows, rows, vector,
            rows, rows, rows, token,
        ),
        out_specs=(
            token, token, vector, rows, rows, rows, vector, vector, rows, rows, vector,
            rows, rows, rows,
        ),
        check_vma=False,
    )
```
